32 devices in a mesh: tp: 4 (over x, core), sp: 8 (over z, y).
Axes of the slice: x: 2, y: 2, z: 4, core: 2. Of those that a mesh axis runs over, the one named last changes fastest.
Arguments:
- hidden: bfloat16 [4096, 2048], P('sp'), may hold values from -6 to 6
- segment_ids: int32 [4096], replicated, may hold values from 0 to 1, as said below
- attn_norm: float32 [2048], replicated, may hold values from 0.5 to 1.5
- query_proj: bfloat16 [2048, 2048], P(None, 'tp'), may hold values from -0.125 to 0.125
- key_proj: bfloat16 [2048, 1024], P(None, 'tp'), may hold values from -0.125 to 0.125
- value_proj: bfloat16 [2048, 1024], P(None, 'tp'), may hold values from -0.125 to 0.125
- gate_proj: bfloat16 [2048, 2048], P(None, 'tp'), may hold values from -0.125 to 0.125
- output_proj: bfloat16 [2048, 2048], P('tp'), may hold values from -1 to 1
- query_norm: float32 [128], replicated, may hold values from 0.5 to 1.5
- key_norm: float32 [128], replicated, may hold values from 0.5 to 1.5
- ffn_norm: float32 [2048], replicated, may hold values from 0.5 to 1.5
- ffn_gate: bfloat16 [2048, 6144], P(None, 'sp'), may hold values from -0.125 to 0.125
- ffn_up: bfloat16 [2048, 6144], P(None, 'sp'), may hold values from -0.125 to 0.125
- ffn_down: bfloat16 [6144, 2048], P('sp'), may hold values from -0.078125 to 0.078125
- upstream: bfloat16 [4096, 2048], P('sp'), may hold values from -6 to 6
Outputs:
- layer_out: bfloat16 [4096, 2048], P('sp')
- hidden_grad: float32 [4096, 2048], P('sp')
- attn_norm_grad: float32 [2048], replicated
- query_grad: float32 [2048, 2048], P(None, 'tp')
- key_grad: float32 [2048, 1024], P(None, 'tp')
- value_grad: float32 [2048, 1024], P(None, 'tp')
- gate_grad: float32 [2048, 2048], P(None, 'tp')
- output_grad: float32 [2048, 2048], P('tp')
- query_norm_grad: float32 [128], replicated
- key_norm_grad: float32 [128], replicated
- ffn_norm_grad: float32 [2048], replicated
- ffn_gate_grad: float32 [2048, 6144], P(None, 'sp')
- ffn_up_grad: float32 [2048, 6144], P(None, 'sp')
- ffn_down_grad: float32 [6144, 2048], P('sp')
The draws below stay inside these ranges and needn't reach their ends.
Inputs may be any that keep to these rules, and one draw needn't show every extreme that they name: `segment_ids`: ids never fall along the tokens and number 2 sequences; one of them holds five eighths to three quarters of the 4096 tokens, the others have near-equal lengths.
All inputs are finite; a program needn't handle non-finite values.
Results may differ from the reference program's by a relative error of at most 0.028.
Values may be sent and summed in bfloat16 or wider, within the bound.
A program may use at most 256 MiB of HBM per device.

```python
import math
from functools import partial
import jax
import jax.numpy as jnp
from jax import lax

D = 2048
HQ = 16
HK = 8
HD = 128
FF = 6144
TOKENS = 4096
NSEQ = 2


def draw_segment_ids(key, part):
    key_extra, key_slot = jax.random.split(key)
    extra = jax.random.randint(key_extra, (), 0, TOKENS // 8 + 1, dtype=jnp.int32)
    longest = 5 * TOKENS // 8 + extra
    shorts = NSEQ - 1
    rest = TOKENS - longest
    base_len = rest // shorts
    short_index = jnp.arange(shorts, dtype=jnp.int32)
    short_lens = base_len + jnp.where(short_index == shorts - 1, rest - base_len * shorts, 0)
    long_slot = jax.random.randint(key_slot, (), 0, NSEQ, dtype=jnp.int32)
    places = jnp.arange(NSEQ, dtype=jnp.int32)
    source = jnp.clip(places - (places > long_slot).astype(jnp.int32), 0, shorts - 1)
    lengths = jnp.where(places == long_slot, longest, short_lens[source])
    bounds = jnp.cumsum(lengths)
    token_index = jnp.arange(TOKENS, dtype=jnp.int32)
    return jnp.sum((token_index[:, None] >= bounds[None, :]).astype(jnp.int32), axis=1)


def block_levels(stream_key, shape, cuts, least, largest):
    level = 1.0
    for axis_at, blocks in cuts:
        steps = jax.random.uniform(jax.random.fold_in(jax.random.fold_in(stream_key, 6), axis_at), (blocks,), jnp.float32, least / len(cuts), largest / len(cuts))
        level = level * jnp.repeat(jnp.exp(steps), shape[axis_at] // blocks).reshape((-1,) + (1,) * (len(shape) - 1 - axis_at))
    return level


def gaussian(own_key, dims, scale, limit, cuts=(), kind=jnp.bfloat16):
    entries = scale * jax.random.normal(own_key, dims, jnp.float32)
    if cuts:
        entries = entries * block_levels(own_key, dims, cuts, -0.22, 0.18)
    return jnp.clip(entries, -limit, limit).astype(kind)


def setup_inputs(seed: int = 0) -> dict:
    key_list = jax.random.split(jax.random.key(seed), 16)
    return {
        "hidden": gaussian(key_list[0], (TOKENS, D), 1.0, 6.0, ((0, 8),)),
        "segment_ids": draw_segment_ids(jax.random.fold_in(key_list[15], 71), 0),
        "attn_norm": jnp.clip(1.0 + 0.1 * jax.random.normal(key_list[2], (D,), jnp.float32), 0.5, 1.5),
        "query_proj": gaussian(key_list[3], (D, HQ * HD), D ** -0.5, 0.125, ((1, 4),)),
        "key_proj": gaussian(key_list[4], (D, HK * HD), D ** -0.5, 0.125, ((1, 4),)),
        "value_proj": gaussian(key_list[5], (D, HK * HD), D ** -0.5, 0.125, ((1, 4),)),
        "gate_proj": gaussian(key_list[6], (D, HQ * HD), D ** -0.5, 0.125, ((1, 4),)),
        "output_proj": gaussian(key_list[7], (HQ * HD, D), (HQ * HD // 64) ** -0.5, 1.0, ((0, 4),)),
        "query_norm": jnp.clip(1.0 + 0.1 * jax.random.normal(key_list[8], (HD,), jnp.float32), 0.5, 1.5),
        "key_norm": jnp.clip(1.0 + 0.1 * jax.random.normal(key_list[9], (HD,), jnp.float32), 0.5, 1.5),
        "ffn_norm": jnp.clip(1.0 + 0.1 * jax.random.normal(key_list[10], (D,), jnp.float32), 0.5, 1.5),
        "ffn_gate": gaussian(key_list[11], (D, FF), D ** -0.5, 0.125, ((1, 8),)),
        "ffn_up": gaussian(key_list[12], (D, FF), D ** -0.5, 0.125, ((1, 8),)),
        "ffn_down": gaussian(key_list[13], (FF, D), FF ** -0.5, 0.078125, ((0, 8),)),
        "upstream": gaussian(key_list[14], (TOKENS, D), 1.0, 6.0, ((0, 8),)),
    }


EPSILON = 1e-06
THETA = 1000000.0
HIGHEST = lax.Precision.HIGHEST

@jax.custom_vjp
def low(v):
    return lax.optimization_barrier(v.astype(jnp.bfloat16)).astype(jnp.float32)

@jax.custom_vjp
def low_back(v):
    return v

def low_keep(v):
    return (low(v), None)

def low_pass(kept, grad):
    return (grad,)

def back_keep(v):
    return (v, None)

def back_low(kept, grad):
    return (low(grad),)
low.defvjp(low_keep, low_pass)
low_back.defvjp(back_keep, back_low)

def product(left, right):
    return jnp.dot(left, right, precision=HIGHEST, preferred_element_type=jnp.float32)

def rms_norm(values, gain):
    return values * lax.rsqrt(lax.optimization_barrier(jnp.mean(values * values, axis=-1, keepdims=True)) + EPSILON) * gain

def frequency_table(head_width):
    steps_half = jnp.arange(head_width // 2, dtype=jnp.float32)
    return jnp.exp(steps_half * (-2.0 * math.log(THETA) / head_width))

def rotary(values, cosine, sine):
    half_width = values.shape[-1] // 2
    front_half = values[..., :half_width]
    back_half = values[..., half_width:]
    return jnp.concatenate([front_half * cosine - back_half * sine, back_half * cosine + front_half * sine], axis=-1)

def token_positions(segment_ids):
    token_count = segment_ids.shape[0]
    row_index = jnp.arange(token_count, dtype=jnp.int32)
    boundary = jnp.concatenate([jnp.ones((1,), jnp.bool_), segment_ids[1:] != segment_ids[:-1]])
    starts = lax.cummax(jnp.where(boundary, row_index, jnp.zeros_like(row_index)), axis=0)
    return (row_index, starts)

def attention(queries, key_rows, value_rows, row_index, segment_ids):
    token_count = queries.shape[0]
    blocking = math.gcd(token_count, 512)
    groups = HQ // HK
    score_scale = 1.0 / math.sqrt(HD)
    blocked = queries.reshape(token_count // blocking, blocking, HK, groups, HD)
    anchors = jnp.arange(token_count // blocking, dtype=jnp.int32) * blocking

    def one_block(inputs):
        query_block, anchor = inputs
        query_index = anchor + jnp.arange(blocking, dtype=jnp.int32)
        scores = low_back(jnp.einsum('qkgd,nkd->kgqn', query_block, key_rows, precision=HIGHEST) * score_scale)
        query_segments = lax.dynamic_slice_in_dim(segment_ids, anchor, blocking)
        allowed = (query_segments[:, None] == segment_ids[None, :]) & (row_index[None, :] <= query_index[:, None])
        masked = jnp.where(allowed, scores, -1e+30)
        maxima = lax.optimization_barrier(jnp.max(masked, axis=-1, keepdims=True))
        exps_kept = jnp.exp(masked - maxima)
        weights_low = low(exps_kept / lax.optimization_barrier(jnp.sum(exps_kept, axis=-1, keepdims=True)))
        return jnp.einsum('kgqn,nkd->qkgd', weights_low, value_rows, precision=HIGHEST)
    mixed_heads = lax.map(jax.checkpoint(one_block), (blocked, anchors))
    return low_back(mixed_heads.reshape(token_count, HQ * HD))

def layer(row_index, segment_ids, cosine, sine, hidden, attn_norm, query_proj, key_proj, value_proj, gate_proj, output_proj, query_norm, key_norm, ffn_norm, ffn_gate, ffn_up, ffn_down):
    token_count = hidden.shape[0]
    normed = low(rms_norm(hidden, attn_norm))
    queries = low_back(product(normed, query_proj)).reshape(token_count, HQ, HD)
    key_rows = low_back(product(normed, key_proj)).reshape(token_count, HK, HD)
    value_rows = low(low_back(product(normed, value_proj))).reshape(token_count, HK, HD)
    gate_raw = low_back(product(normed, gate_proj))
    queries = low(rotary(rms_norm(queries, query_norm), cosine, sine))
    key_rows = low(rotary(rms_norm(key_rows, key_norm), cosine, sine))
    mixed_heads = attention(queries, key_rows, value_rows, row_index, segment_ids)
    gated_heads = low(mixed_heads * jax.nn.sigmoid(gate_raw))
    middle = hidden + low_back(product(gated_heads, output_proj))
    normed_two = low(rms_norm(middle, ffn_norm))
    gate_vals = low_back(product(normed_two, ffn_gate))
    up_vals = low_back(product(normed_two, ffn_up))
    inner_act = low(jax.nn.silu(gate_vals) * up_vals)
    return middle + low_back(product(inner_act, ffn_down))

def reference(hidden, segment_ids, attn_norm, query_proj, key_proj, value_proj, gate_proj, output_proj, query_norm, key_norm, ffn_norm, ffn_gate, ffn_up, ffn_down, upstream):
    row_index, starts = token_positions(segment_ids)
    angles = (row_index - starts).astype(jnp.float32)[:, None] * frequency_table(HD)[None, :]
    cosine = jnp.cos(angles)[:, None, :]
    sine = jnp.sin(angles)[:, None, :]
    inputs = tuple((array.astype(jnp.float32) for array in (hidden, attn_norm, query_proj, key_proj, value_proj, gate_proj, output_proj, query_norm, key_norm, ffn_norm, ffn_gate, ffn_up, ffn_down)))
    result, pullback = jax.vjp(partial(layer, row_index, segment_ids, cosine, sine), *inputs)
    grads = pullback(upstream.astype(jnp.float32))
    return (result.astype(jnp.bfloat16), grads[0], grads[1], grads[2], grads[3], grads[4], grads[5], grads[6], grads[7], grads[8], grads[9], grads[10], grads[11], grads[12])
```

```python
import functools
import math

import jax
import jax.numpy as jnp
from jax import lax
from jax.experimental import pallas as pl
from jax.experimental.pallas import tpu as pltpu
from jax.sharding import PartitionSpec as P

EPSILON = 1e-06
THETA = 1000000.0
LOG2E = 1.4426950408889634
F32 = jnp.float32
BF16 = jnp.bfloat16


def norm_scales(values):
    return lax.rsqrt(jnp.mean(values * values, axis=-1, keepdims=True) + EPSILON)


def norm_rows(values, gain):
    scales = norm_scales(values)
    return (values * scales * gain, scales)


def norm_back(values, scales, gain, incoming):
    weighted = incoming * gain
    inner_sum = jnp.sum(weighted * values, axis=-1, keepdims=True)
    grad_values = (
        scales * weighted - values * (scales * scales * scales) * inner_sum / values.shape[-1]
    )
    return (grad_values, incoming * values * scales)


def rotary(values, cosine, sine):
    half_width = values.shape[-1] // 2
    front_half = values[..., :half_width]
    back_half = values[..., half_width:]
    return jnp.concatenate(
        [front_half * cosine - back_half * sine, back_half * cosine + front_half * sine], axis=-1
    )


def rotary_back(grads, cosine, sine):
    half_width = grads.shape[-1] // 2
    front_half = grads[..., :half_width]
    back_half = grads[..., half_width:]
    return jnp.concatenate(
        [front_half * cosine + back_half * sine, back_half * cosine - front_half * sine], axis=-1
    )


def matmul(left, right):
    return jnp.dot(left, right, preferred_element_type=F32)


def outer_sum(left, right):
    return lax.dot_general(left, right, (((0,), (0,)), ((), ())), preferred_element_type=F32)


def times_transpose(left, right):
    return lax.dot_general(left, right, (((1,), (1,)), ((), ())), preferred_element_type=F32)


def attn_forward_kernel(first, diagonal, scale, info, starts, queries, kv_a, kv_b, *rest):
    if first:
        acc_out, sum_out = rest
    else:
        acc_in, sum_in, acc_out, sum_out = rest
    rows = queries.shape[0]
    keys_n = kv_a.shape[1]
    per_group = queries.shape[1] // kv_a.shape[2]
    width = kv_a.shape[2]
    if first:
        acc_out[...] = jnp.zeros_like(acc_out)
        sum_out[...] = jnp.zeros_like(sum_out)
    else:
        acc_out[...] = acc_in[...]
        sum_out[...] = sum_in[...]
    own_first = info[0]
    for slot, block in enumerate((kv_a, kv_b)):
        key_first = info[1 + slot]
        live = info[3 + slot] > 0

        def work(masked, causal):
            ones = jnp.ones((keys_n, width), BF16)
            values = jnp.concatenate([block[1], ones], axis=1)
            keys = block[0]
            if masked:
                key_index = key_first + lax.broadcasted_iota(jnp.int32, (rows, keys_n), 1)
                allowed = key_index >= starts[...]
                if causal:
                    row_index = own_first + lax.broadcasted_iota(jnp.int32, (rows, keys_n), 0)
                    allowed = allowed & (key_index <= row_index)
            for head in range(per_group):
                cols = slice(head * width, (head + 1) * width)
                scores = times_transpose(queries[:, cols], keys)
                weights = jnp.exp2(scores * (scale * LOG2E))
                if masked:
                    weights = jnp.where(allowed, weights, 0.0)
                both = matmul(weights.astype(BF16), values)
                acc_out[:, cols] += both[:, :width]
                sum_out[:, cols] += both[:, width:]

        if diagonal and slot == 0:
            work(True, True)
        else:
            full = info[5 + slot] > 0
            pl.when(live & full)(functools.partial(work, False, False))
            pl.when(live & jnp.logical_not(full))(functools.partial(work, True, False))


def attn_forward(info, starts, queries, kv_a, kv_b, carried, scale):
    rows, all_width = queries.shape
    width = 128
    groups = kv_a.shape[2] // width
    group_width = all_width // groups
    keys_n = kv_a.shape[1]
    first = carried is None
    spec_q = pl.BlockSpec((rows, group_width), lambda g, info: (0, g))
    spec_kv = pl.BlockSpec((2, keys_n, width), lambda g, info: (0, 0, g))
    specs = [pl.BlockSpec((rows, 1), lambda g, info: (0, 0)), spec_q, spec_kv, spec_kv]
    operands = [starts, queries, kv_a, kv_b]
    if not first:
        specs += [spec_q, spec_q]
        operands += list(carried)
    return pl.pallas_call(
        functools.partial(attn_forward_kernel, first, first, scale),
        grid_spec=pltpu.PrefetchScalarGridSpec(
            num_scalar_prefetch=1,
            grid=(groups,),
            in_specs=specs,
            out_specs=[spec_q, spec_q],
        ),
        out_shape=[jax.ShapeDtypeStruct((rows, all_width), F32)] * 2,
        compiler_params=pltpu.CompilerParams(dimension_semantics=("arbitrary",)),
        cost_estimate=pl.CostEstimate(
            flops=16 * rows * keys_n * all_width,
            transcendentals=2 * rows * keys_n * all_width // width,
            bytes_accessed=8 * rows * all_width,
        ),
        name="attn_forward",
    )(info, *operands)


def attn_backward_kernel(first, diagonal, scale, info, starts, lse, deltas, queries, grads, kv_a, kv_b, *rest):
    if first:
        grad_q, grad_a, grad_b = rest
    else:
        grad_in, grad_q, grad_a, grad_b = rest
    rows = queries.shape[0]
    keys_n = kv_a.shape[1]
    width = kv_a.shape[2]
    per_group = queries.shape[1] // width
    if first:
        grad_q[...] = jnp.zeros_like(grad_q)
    else:
        grad_q[...] = grad_in[...]
    own_first = info[0]
    for slot, (block, out) in enumerate(((kv_a, grad_a), (kv_b, grad_b))):
        key_first = info[1 + slot]
        live = info[3 + slot] > 0

        def work(masked, causal):
            keys = block[0]
            values = block[1]
            keys_t = keys.T
            if masked:
                key_index = key_first + lax.broadcasted_iota(jnp.int32, (keys_n, rows), 0)
                allowed = key_index >= starts[...]
                if causal:
                    row_index = own_first + lax.broadcasted_iota(jnp.int32, (keys_n, rows), 1)
                    allowed = allowed & (key_index <= row_index)
            total_k = jnp.zeros((keys_n, width), F32)
            total_v = jnp.zeros((keys_n, width), F32)
            for head in range(per_group):
                cols = slice(head * width, (head + 1) * width)
                q_head = queries[:, cols]
                g_head = grads[:, cols]
                scores = times_transpose(keys, q_head)
                probs = jnp.exp2(scores * (scale * LOG2E) - lse[0, head : head + 1, :])
                if masked:
                    probs = jnp.where(allowed, probs, 0.0)
                grad_probs = times_transpose(values, g_head)
                grad_scores = (probs * (grad_probs - deltas[0, head : head + 1, :])).astype(BF16)
                total_v += matmul(probs.astype(BF16), g_head)
                total_k += matmul(grad_scores, q_head)
                grad_q[:, cols] += matmul(keys_t, grad_scores).T
            out[0] = (total_k * scale).astype(BF16)
            out[1] = total_v.astype(BF16)

        if diagonal and slot == 0:
            work(True, True)
        else:
            full = info[5 + slot] > 0
            pl.when(live & full)(functools.partial(work, False, False))
            pl.when(live & jnp.logical_not(full))(functools.partial(work, True, False))

            @pl.when(jnp.logical_not(live))
            def _():
                out[...] = jnp.zeros_like(out)


def attn_backward(info, starts_row, lse, deltas, queries, grads, kv_a, kv_b, carried, diagonal, scale):
    rows, all_width = queries.shape
    width = 128
    groups = kv_a.shape[2] // width
    group_width = all_width // groups
    per_group = group_width // width
    keys_n = kv_a.shape[1]
    first = carried is None
    spec_q = pl.BlockSpec((rows, group_width), lambda g, info: (0, g))
    spec_kv = pl.BlockSpec((2, keys_n, width), lambda g, info: (0, 0, g))
    spec_row = pl.BlockSpec((1, per_group, rows), lambda g, info: (g, 0, 0))
    specs = [
        pl.BlockSpec((1, rows), lambda g, info: (0, 0)),
        spec_row,
        spec_row,
        spec_q,
        spec_q,
        spec_kv,
        spec_kv,
    ]
    operands = [starts_row, lse, deltas, queries, grads, kv_a, kv_b]
    if not first:
        specs.append(spec_q)
        operands.append(carried)
    return pl.pallas_call(
        functools.partial(attn_backward_kernel, first, diagonal, scale),
        grid_spec=pltpu.PrefetchScalarGridSpec(
            num_scalar_prefetch=1,
            grid=(groups,),
            in_specs=specs,
            out_specs=[spec_q, spec_kv, spec_kv],
        ),
        out_shape=[
            jax.ShapeDtypeStruct((rows, all_width), F32),
            jax.ShapeDtypeStruct(kv_a.shape, BF16),
            jax.ShapeDtypeStruct(kv_a.shape, BF16),
        ],
        compiler_params=pltpu.CompilerParams(dimension_semantics=("arbitrary",)),
        cost_estimate=pl.CostEstimate(
            flops=20 * rows * keys_n * all_width,
            transcendentals=2 * rows * keys_n * all_width // width,
            bytes_accessed=8 * rows * all_width,
        ),
        name="attn_backward",
    )(info, *operands)


def body(
    hidden,
    segment_ids,
    attn_norm,
    query_proj,
    key_proj,
    value_proj,
    gate_proj,
    output_proj,
    query_norm,
    key_norm,
    ffn_norm,
    ffn_gate,
    ffn_up,
    ffn_down,
    upstream,
):
    rows_dev, model = hidden.shape
    head_width = query_norm.shape[0]
    heads = query_proj.shape[1] // head_width
    groups = key_proj.shape[1] // head_width
    per_group = heads // groups
    group_width = groups * head_width
    sp_n = lax.axis_size("sp")
    tp_n = lax.axis_size("tp")
    outer = sp_n // 2
    sides = tp_n // 2
    quarter = rows_dev // tp_n
    tp_i = lax.axis_index("tp")
    sp_i = lax.axis_index("sp")
    ring_i = sp_i // 2
    pair_i = sp_i % 2
    side_i = tp_i // 2
    core_i = tp_i % 2
    own_first = sp_i * rows_dev
    quarter_first = tp_i * quarter
    scale = 1.0 / math.sqrt(head_width)

    ring_pairs = [(z * 2 + y, ((z + 1) % outer) * 2 + y) for z in range(outer) for y in range(2)]
    pair_pairs = [(i, i ^ 1) for i in range(sp_n)]
    side_pairs = [(i, i ^ 2) for i in range(tp_n)]
    core_pairs = [(i, i ^ 1) for i in range(tp_n)]

    def ring(value):
        return lax.ppermute(value, "sp", ring_pairs)

    def pair(value):
        return lax.ppermute(value, "sp", pair_pairs)

    def side(value):
        return lax.ppermute(value, "tp", side_pairs)

    def core(value):
        return lax.ppermute(value, "tp", core_pairs)

    def gather_sp(block):
        blocks = []
        for k in range(outer):
            blocks.append((block, pair(block)))
            if k < outer - 1:
                block = ring(block)
        return blocks

    def scatter_sp(parts):
        def paired(k):
            return parts[k][0] + pair(parts[k][1].astype(BF16)).astype(F32)

        total = paired(1 % outer)
        for k in range(2, outer + 1):
            total = ring(total.astype(BF16)).astype(F32) + paired(k % outer)
        return total

    first_id = segment_ids[0]
    second_start = jnp.sum((segment_ids == first_id).astype(jnp.int32))
    own_index = own_first + jnp.arange(rows_dev, dtype=jnp.int32)
    own_starts = jnp.where(own_index < second_start, 0, second_start)
    steps_half = jnp.arange(head_width // 2, dtype=F32)
    frequencies = jnp.exp(steps_half * (-2.0 * math.log(THETA) / head_width))
    angles = (own_index - own_starts).astype(F32)[:, None] * frequencies[None, :]
    cosine = jnp.cos(angles)[:, None, :]
    sine = jnp.sin(angles)[:, None, :]

    hidden_full = hidden.astype(F32)
    normed_full, attn_scales = norm_rows(hidden_full, attn_norm)
    normed = normed_full.astype(BF16)
    key_raw = matmul(normed, key_proj).reshape(rows_dev, groups, head_width)
    value_rows = matmul(normed, value_proj).astype(BF16)
    key_normed, key_scales = norm_rows(key_raw, key_norm)
    key_rot = rotary(key_normed, cosine, sine).astype(BF16).reshape(rows_dev, group_width)
    kv_own = jnp.stack([key_rot, value_rows])

    low, high = (outer // 4, 3 * outer // 4) if outer % 4 == 0 else (0, outer)
    reach = high - 1 if low else outer - 1

    def up_pairs(step):
        return [
            (z * 2 + y, (z + 1) * 2 + y)
            for z in range(outer - 1)
            for y in range(2)
            if z + 1 - step >= 0 and (z + 1 - step >= low or z + 1 < high)
        ]

    kv_blocks = []
    travelling = kv_own
    for k in range(reach + 1):
        kv_blocks.append((travelling, pair(travelling)))
        if k < reach:
            travelling = lax.ppermute(travelling, "sp", up_pairs(k + 1))

    query_raw = matmul(normed, query_proj).reshape(rows_dev, heads, head_width)
    gate_raw = matmul(normed, gate_proj)
    query_normed, query_scales = norm_rows(query_raw, query_norm)
    queries = rotary(query_normed, cosine, sine).astype(BF16).reshape(rows_dev, heads * head_width)

    grad_quarter = lax.dynamic_slice_in_dim(upstream, quarter_first, quarter)
    up_blocks = gather_sp(grad_quarter)

    row_start_low = own_starts[0]
    row_start_high = own_starts[-1]

    def block_info(k):
        shards = [(ring_i - k) * 2 + pair_i, (ring_i - k) * 2 + (1 - pair_i)]
        entries = [own_first] + [shard * rows_dev for shard in shards]
        live = []
        full = []
        for shard in shards:
            token = shard * rows_dev
            live.append((shard >= 0) & (shard <= sp_i) & (token + rows_dev - 1 >= row_start_low))
            full.append((token >= row_start_high) & (shard < sp_i))
        return jnp.stack(entries + [v.astype(jnp.int32) for v in live + full]).astype(jnp.int32)

    infos = [block_info(k) for k in range(reach + 1)]
    starts_column = own_starts[:, None]
    starts_row = own_starts[None, :]
    carried = None
    for k in range(reach + 1):
        carried = attn_forward(
            infos[k], starts_column, queries, kv_blocks[k][0], kv_blocks[k][1], carried, scale
        )
    mix_acc, mix_sum = carried
    mixed = mix_acc / mix_sum
    lse = jnp.log2(mix_sum.reshape(rows_dev, heads, head_width)[:, :, 0])
    lse_rows = lse.T.reshape(groups, per_group, rows_dev)
    gate_sig = jax.nn.sigmoid(gate_raw)
    gated = (mixed * gate_sig).astype(BF16)

    def scatter_tp(part):
        part = part.reshape(sides, 2, quarter, model)
        keep = lax.dynamic_index_in_dim(part, core_i, 1, keepdims=False)
        send = lax.dynamic_index_in_dim(part, 1 - core_i, 1, keepdims=False)
        keep = keep + core(send.astype(BF16)).astype(F32)
        mine = lax.dynamic_index_in_dim(keep, side_i, 0, keepdims=False)
        other = lax.dynamic_index_in_dim(keep, 1 - side_i, 0, keepdims=False)
        return mine + side(other.astype(BF16)).astype(F32)

    def gather_tp(block):
        far = side(block)
        swap_side = side_i == 1
        two = jnp.where(swap_side, jnp.stack([far, block]), jnp.stack([block, far]))
        near = core(two)
        swap_core = core_i == 1
        full = jnp.where(
            swap_core, jnp.stack([near, two], axis=1), jnp.stack([two, near], axis=1)
        )
        return full.reshape((rows_dev,) + block.shape[1:])

    attn_quarter = scatter_tp(matmul(gated, output_proj))
    hidden_quarter = lax.dynamic_slice_in_dim(hidden, quarter_first, quarter).astype(F32)
    middle = hidden_quarter + attn_quarter
    normed_two_full, ffn_scales = norm_rows(middle, ffn_norm)
    normed_two = normed_two_full.astype(BF16)

    two_blocks = gather_sp(normed_two)
    rows_list, up_list, inner_list, gate_list, grad_up_list = [None] * outer, [None] * outer, [None] * outer, [None] * outer, [None] * outer
    grad_parts = [None] * outer
    for k in list(range(1, outer)) + [0]:
        rows_k = jnp.concatenate(two_blocks[k])
        up_k = jnp.concatenate(up_blocks[k])
        gate_vals = matmul(rows_k, ffn_gate)
        up_vals = matmul(rows_k, ffn_up)
        sig = jax.nn.sigmoid(gate_vals)
        grad_inner = times_transpose(up_k, ffn_down)
        grad_gate = (grad_inner * up_vals * (sig * (1.0 + gate_vals * (1.0 - sig)))).astype(BF16)
        grad_up = (grad_inner * (gate_vals * sig)).astype(BF16)
        inner = (gate_vals * sig * up_vals).astype(BF16)
        grad_parts[k] = (
            times_transpose(grad_gate, ffn_gate) + times_transpose(grad_up, ffn_up)
        ).reshape(2, quarter, model)
        rows_list[k], up_list[k], inner_list[k] = rows_k, up_k, inner
        gate_list[k], grad_up_list[k] = grad_gate, grad_up
    grad_two = scatter_sp(grad_parts)

    norm_grad_two, ffn_gain_terms = norm_back(middle, ffn_scales, ffn_norm, grad_two)
    grad_middle_quarter = grad_quarter.astype(F32) + norm_grad_two
    grad_branch = gather_tp(grad_middle_quarter.astype(BF16))

    mlp_parts = [matmul(inner_list[k], ffn_down).reshape(2, quarter, model) for k in range(outer)]
    mlp_quarter = scatter_sp(mlp_parts)
    layer_out = gather_tp((middle + mlp_quarter).astype(BF16))

    rows_all = jnp.concatenate(rows_list)
    up_all = jnp.concatenate(up_list)
    inner_all = jnp.concatenate(inner_list)
    gate_all = jnp.concatenate(gate_list)
    grad_up_all = jnp.concatenate(grad_up_list)

    def reduce_tp(part):
        half = part.shape[0] // 2
        keep = lax.dynamic_slice_in_dim(part, core_i * half, half)
        send = lax.dynamic_slice_in_dim(part, (1 - core_i) * half, half)
        keep = (keep + core(send.astype(BF16)).astype(F32)).astype(BF16)
        keep = (keep.astype(F32) + side(keep).astype(F32)).astype(BF16)
        near = core(keep)
        total = jnp.where(
            core_i == 1, jnp.concatenate([near, keep]), jnp.concatenate([keep, near])
        )
        return total.astype(F32)

    ffn_gate_grad = reduce_tp(outer_sum(rows_all, gate_all))
    ffn_up_grad = reduce_tp(outer_sum(rows_all, grad_up_all))
    ffn_down_grad = reduce_tp(outer_sum(inner_all, up_all))

    output_part = outer_sum(gated, grad_branch)
    grad_gated = times_transpose(grad_branch, output_proj)
    grad_mixed = (grad_gated * gate_sig).astype(BF16)
    grad_gate_raw = (grad_gated * mixed * (gate_sig * (1.0 - gate_sig))).astype(BF16)
    deltas = jnp.sum(
        (grad_mixed.astype(F32) * mixed).reshape(rows_dev, heads, head_width), axis=-1
    )
    delta_rows = deltas.T.reshape(groups, per_group, rows_dev)

    def down_pairs(step):
        return [(b, a) for a, b in up_pairs(step)]

    query_acc = None
    travelling = None
    for k in list(range(reach, -1, -1)):
        query_acc, grad_a, grad_b = attn_backward(
            infos[k], starts_row, lse_rows, delta_rows, queries, grad_mixed,
            kv_blocks[k][0], kv_blocks[k][1], query_acc, k == 0, scale,
        )
        total = grad_a.astype(F32) + pair(grad_b).astype(F32)
        if travelling is not None:
            total = total + travelling.astype(F32)
        if k > 0:
            travelling = lax.ppermute(total.astype(BF16), "sp", down_pairs(k))
    grad_key_rot = total[0].reshape(rows_dev, groups, head_width)
    grad_value_low = total[1].astype(BF16)
    grad_query_rot = (query_acc * scale).reshape(rows_dev, heads, head_width)
    grad_query_raw, query_gain_terms = norm_back(
        query_raw, query_scales, query_norm, rotary_back(grad_query_rot, cosine, sine)
    )
    grad_key_raw, key_gain_terms = norm_back(
        key_raw, key_scales, key_norm, rotary_back(grad_key_rot, cosine, sine)
    )
    grad_query_low = grad_query_raw.reshape(rows_dev, heads * head_width).astype(BF16)
    grad_key_low = grad_key_raw.reshape(rows_dev, group_width).astype(BF16)

    def reduce_sp(part):
        count, width = part.shape
        half = count // 2
        chunk = half // outer
        keep = lax.dynamic_slice_in_dim(part, pair_i * half, half)
        send = lax.dynamic_slice_in_dim(part, (1 - pair_i) * half, half)
        keep = keep + pair(send.astype(BF16)).astype(F32)

        def piece(k):
            return lax.dynamic_slice_in_dim(keep, ((ring_i - k) % outer) * chunk, chunk)

        total = piece(1 % outer)
        for k in range(2, outer + 1):
            total = ring(total.astype(BF16)).astype(F32) + piece(k % outer)
        block = total.astype(BF16)
        out = jnp.zeros((count, width), F32)
        for k in range(outer):
            at = ((ring_i - k) % outer) * chunk
            out = lax.dynamic_update_slice(out, block.astype(F32), (pair_i * half + at, 0))
            out = lax.dynamic_update_slice(
                out, pair(block).astype(F32), ((1 - pair_i) * half + at, 0)
            )
            if k < outer - 1:
                block = ring(block)
        return out

    output_grad = reduce_sp(output_part)
    gate_grad = reduce_sp(outer_sum(normed, grad_gate_raw))
    query_grad = reduce_sp(outer_sum(normed, grad_query_low))
    key_grad = reduce_sp(outer_sum(normed, grad_key_low))
    value_grad = reduce_sp(outer_sum(normed, grad_value_low))

    grad_normed_part = (
        times_transpose(grad_query_low, query_proj)
        + times_transpose(grad_key_low, key_proj)
        + times_transpose(grad_value_low, value_proj)
        + times_transpose(grad_gate_raw, gate_proj)
    )
    grad_normed = scatter_tp(grad_normed_part)
    scales_quarter = lax.dynamic_slice_in_dim(attn_scales, quarter_first, quarter)
    norm_grad_one, attn_gain_terms = norm_back(
        hidden_quarter, scales_quarter, attn_norm, grad_normed
    )
    hidden_grad = gather_tp((grad_middle_quarter + norm_grad_one).astype(BF16)).astype(F32)

    gains = jnp.concatenate(
        [
            jnp.sum(attn_gain_terms, axis=0),
            jnp.sum(ffn_gain_terms, axis=0),
            jnp.sum(query_gain_terms, axis=(0, 1)),
            jnp.sum(key_gain_terms, axis=(0, 1)),
        ]
    )
    for axis, size in (("tp", tp_n), ("sp", sp_n)):
        bit = 1
        while bit < size:
            gains = gains + lax.ppermute(gains, axis, [(i, i ^ bit) for i in range(size)])
            bit *= 2
    return (
        layer_out,
        hidden_grad,
        gains[:model],
        query_grad,
        key_grad,
        value_grad,
        gate_grad,
        output_grad,
        gains[2 * model : 2 * model + head_width],
        gains[2 * model + head_width :],
        gains[model : 2 * model],
        ffn_gate_grad,
        ffn_up_grad,
        ffn_down_grad,
    )


def solution(mesh):
    placed = (
        P("sp", None),
        P(),
        P(),
        P(None, "tp"),
        P(None, "tp"),
        P(None, "tp"),
        P(None, "tp"),
        P("tp", None),
        P(),
        P(),
        P(),
        P(None, "sp"),
        P(None, "sp"),
        P("sp", None),
        P("sp", None),
    )
    return jax.shard_map(
        body,
        mesh=mesh,
        in_specs=placed,
        out_specs=(
            P("sp", None),
            P("sp", None),
            P(),
            P(None, "tp"),
            P(None, "tp"),
            P(None, "tp"),
            P(None, "tp"),
            P("tp", None),
            P(),
            P(),
            P(),
            P(None, "sp"),
            P(None, "sp"),
            P("sp", None),
        ),
        check_vma=False,
    )
```

```python
import functools
import math

import jax
import jax.numpy as jnp
from jax import lax
from jax.experimental import pallas as pl
from jax.experimental.pallas import tpu as pltpu
from jax.sharding import PartitionSpec as P

EPSILON = 1e-06
THETA = 1000000.0
LOG2E = 1.4426950408889634
F32 = jnp.float32
BF16 = jnp.bfloat16


def norm_scales(values):
    return lax.rsqrt(jnp.mean(values * values, axis=-1, keepdims=True) + EPSILON)


def norm_rows(values, gain):
    scales = norm_scales(values)
    return (values * scales * gain, scales)


def norm_back(values, scales, gain, incoming):
    weighted = incoming * gain
    inner_sum = jnp.sum(weighted * values, axis=-1, keepdims=True)
    grad_values = (
        scales * weighted - values * (scales * scales * scales) * inner_sum / values.shape[-1]
    )
    return (grad_values, incoming * values * scales)


def rotary(values, cosine, sine):
    half_width = values.shape[-1] // 2
    front_half = values[..., :half_width]
    back_half = values[..., half_width:]
    return jnp.concatenate(
        [front_half * cosine - back_half * sine, back_half * cosine + front_half * sine], axis=-1
    )


def rotary_back(grads, cosine, sine):
    half_width = grads.shape[-1] // 2
    front_half = grads[..., :half_width]
    back_half = grads[..., half_width:]
    return jnp.concatenate(
        [front_half * cosine + back_half * sine, back_half * cosine - front_half * sine], axis=-1
    )


def matmul(left, right):
    return jnp.dot(left, right, preferred_element_type=F32)


def outer_sum(left, right):
    return lax.dot_general(left, right, (((0,), (0,)), ((), ())), preferred_element_type=F32)


def times_transpose(left, right):
    return lax.dot_general(left, right, (((1,), (1,)), ((), ())), preferred_element_type=F32)


def attn_forward_kernel(first, diagonal, scale, info, starts, queries, kv_a, kv_b, *rest):
    if first:
        acc_out, sum_out = rest
    else:
        acc_in, sum_in, acc_out, sum_out = rest
    rows = queries.shape[0]
    keys_n = kv_a.shape[1]
    per_group = queries.shape[1] // kv_a.shape[2]
    width = kv_a.shape[2]
    if first:
        acc_out[...] = jnp.zeros_like(acc_out)
        sum_out[...] = jnp.zeros_like(sum_out)
    else:
        acc_out[...] = acc_in[...]
        sum_out[...] = sum_in[...]
    own_first = info[0]
    for slot, block in enumerate((kv_a, kv_b)):
        key_first = info[1 + slot]
        live = info[3 + slot] > 0

        def work(masked, causal):
            ones = jnp.ones((keys_n, width), BF16)
            values = jnp.concatenate([block[1], ones], axis=1)
            keys = block[0]
            if masked:
                key_index = key_first + lax.broadcasted_iota(jnp.int32, (rows, keys_n), 1)
                allowed = key_index >= starts[...]
                if causal:
                    row_index = own_first + lax.broadcasted_iota(jnp.int32, (rows, keys_n), 0)
                    allowed = allowed & (key_index <= row_index)
            for head in range(per_group):
                cols = slice(head * width, (head + 1) * width)
                scores = times_transpose(queries[:, cols], keys)
                weights = jnp.exp2(scores * (scale * LOG2E))
                if masked:
                    weights = jnp.where(allowed, weights, 0.0)
                both = matmul(weights.astype(BF16), values)
                acc_out[:, cols] += both[:, :width]
                sum_out[:, cols] += both[:, width:]

        if diagonal and slot == 0:
            work(True, True)
        else:
            full = info[5 + slot] > 0
            pl.when(live & full)(functools.partial(work, False, False))
            pl.when(live & jnp.logical_not(full))(functools.partial(work, True, False))


def attn_forward(info, starts, queries, kv_a, kv_b, carried, scale):
    rows, all_width = queries.shape
    width = 128
    groups = kv_a.shape[2] // width
    group_width = all_width // groups
    keys_n = kv_a.shape[1]
    first = carried is None
    spec_q = pl.BlockSpec((rows, group_width), lambda g, info: (0, g))
    spec_kv = pl.BlockSpec((2, keys_n, width), lambda g, info: (0, 0, g))
    specs = [pl.BlockSpec((rows, 1), lambda g, info: (0, 0)), spec_q, spec_kv, spec_kv]
    operands = [starts, queries, kv_a, kv_b]
    if not first:
        specs += [spec_q, spec_q]
        operands += list(carried)
    return pl.pallas_call(
        functools.partial(attn_forward_kernel, first, first, scale),
        grid_spec=pltpu.PrefetchScalarGridSpec(
            num_scalar_prefetch=1,
            grid=(groups,),
            in_specs=specs,
            out_specs=[spec_q, spec_q],
        ),
        out_shape=[jax.ShapeDtypeStruct((rows, all_width), F32)] * 2,
        compiler_params=pltpu.CompilerParams(dimension_semantics=("arbitrary",)),
        cost_estimate=pl.CostEstimate(
            flops=16 * rows * keys_n * all_width,
            transcendentals=2 * rows * keys_n * all_width // width,
            bytes_accessed=8 * rows * all_width,
        ),
        name="attn_forward",
    )(info, *operands)


def attn_backward_kernel(first, diagonal, scale, info, starts, lse, deltas, queries, grads, kv_a, kv_b, *rest):
    if first:
        grad_q, grad_a, grad_b = rest
    else:
        grad_in, grad_q, grad_a, grad_b = rest
    rows = queries.shape[0]
    keys_n = kv_a.shape[1]
    width = kv_a.shape[2]
    per_group = queries.shape[1] // width
    if first:
        grad_q[...] = jnp.zeros_like(grad_q)
    else:
        grad_q[...] = grad_in[...]
    own_first = info[0]
    for slot, (block, out) in enumerate(((kv_a, grad_a), (kv_b, grad_b))):
        key_first = info[1 + slot]
        live = info[3 + slot] > 0

        def work(masked, causal):
            keys = block[0]
            values = block[1]
            keys_t = keys.T
            if masked:
                key_index = key_first + lax.broadcasted_iota(jnp.int32, (keys_n, rows), 0)
                allowed = key_index >= starts[...]
                if causal:
                    row_index = own_first + lax.broadcasted_iota(jnp.int32, (keys_n, rows), 1)
                    allowed = allowed & (key_index <= row_index)
            total_k = jnp.zeros((keys_n, width), F32)
            total_v = jnp.zeros((keys_n, width), F32)
            for head in range(per_group):
                cols = slice(head * width, (head + 1) * width)
                q_head = queries[:, cols]
                g_head = grads[:, cols]
                scores = times_transpose(keys, q_head)
                probs = jnp.exp2(scores * (scale * LOG2E) - lse[0, head : head + 1, :])
                if masked:
                    probs = jnp.where(allowed, probs, 0.0)
                grad_probs = times_transpose(values, g_head)
                grad_scores = (probs * (grad_probs - deltas[0, head : head + 1, :])).astype(BF16)
                total_v += matmul(probs.astype(BF16), g_head)
                total_k += matmul(grad_scores, q_head)
                grad_q[:, cols] += matmul(keys_t, grad_scores).T
            out[0] = (total_k * scale).astype(BF16)
            out[1] = total_v.astype(BF16)

        if diagonal and slot == 0:
            work(True, True)
        else:
            full = info[5 + slot] > 0
            pl.when(live & full)(functools.partial(work, False, False))
            pl.when(live & jnp.logical_not(full))(functools.partial(work, True, False))

            @pl.when(jnp.logical_not(live))
            def _():
                out[...] = jnp.zeros_like(out)


def attn_backward(info, starts_row, lse, deltas, queries, grads, kv_a, kv_b, carried, diagonal, scale):
    rows, all_width = queries.shape
    width = 128
    groups = kv_a.shape[2] // width
    group_width = all_width // groups
    per_group = group_width // width
    keys_n = kv_a.shape[1]
    first = carried is None
    spec_q = pl.BlockSpec((rows, group_width), lambda g, info: (0, g))
    spec_kv = pl.BlockSpec((2, keys_n, width), lambda g, info: (0, 0, g))
    spec_row = pl.BlockSpec((1, per_group, rows), lambda g, info: (g, 0, 0))
    specs = [
        pl.BlockSpec((1, rows), lambda g, info: (0, 0)),
        spec_row,
        spec_row,
        spec_q,
        spec_q,
        spec_kv,
        spec_kv,
    ]
    operands = [starts_row, lse, deltas, queries, grads, kv_a, kv_b]
    if not first:
        specs.append(spec_q)
        operands.append(carried)
    return pl.pallas_call(
        functools.partial(attn_backward_kernel, first, diagonal, scale),
        grid_spec=pltpu.PrefetchScalarGridSpec(
            num_scalar_prefetch=1,
            grid=(groups,),
            in_specs=specs,
            out_specs=[spec_q, spec_kv, spec_kv],
        ),
        out_shape=[
            jax.ShapeDtypeStruct((rows, all_width), F32),
            jax.ShapeDtypeStruct(kv_a.shape, BF16),
            jax.ShapeDtypeStruct(kv_a.shape, BF16),
        ],
        compiler_params=pltpu.CompilerParams(dimension_semantics=("arbitrary",)),
        cost_estimate=pl.CostEstimate(
            flops=20 * rows * keys_n * all_width,
            transcendentals=2 * rows * keys_n * all_width // width,
            bytes_accessed=8 * rows * all_width,
        ),
        name="attn_backward",
    )(info, *operands)


def finish_kernel(
    outer, sides, sp_n, tp_n, streams, width_scale,
    *refs,
):
    MESH = pl.DeviceIdType.MESH
    parts = refs[:streams]
    (part_ref, hidden_ref, scale_ref, gain_ref, middle_ref, sums_ref) = refs[streams : streams + 6]
    outs = refs[streams + 6 : 2 * streams + 6]
    grad_out, sums_out = refs[2 * streams + 6 : 2 * streams + 8]
    rest = refs[2 * streams + 8 :]
    got = rest[:streams]
    staged = rest[streams : 2 * streams]
    (near_got, far_got, keep_buf, far_stage, sums_got, sums_stage) = rest[2 * streams : 2 * streams + 6]
    (reduce_send, reduce_recv, gather_send, gather_recv, pair_send, pair_recv) = rest[
        2 * streams + 6 : 2 * streams + 12
    ]
    tp_send, tp_recv, sums_send, sums_recv = rest[2 * streams + 12 :]

    sp_i = lax.axis_index("sp")
    tp_i = lax.axis_index("tp")
    line = sp_i // 2
    half = sp_i % 2
    side = tp_i // 2
    core = tp_i % 2
    last = outer - 1

    def sp_at(z, y):
        return (tp_i, z * 2 + y)

    pair_dev = sp_at(line, 1 - half)
    core_dev = (side * 2 + (1 - core), sp_i)
    side_dev = ((1 - side) * 2 + core, sp_i)

    tp_bits = []
    bit = 1
    while bit < tp_n:
        tp_bits.append(bit)
        bit *= 2
    sp_bits = []
    bit = 1
    while bit < sp_n:
        sp_bits.append(bit)
        bit *= 2

    def flip(value, bit):
        return value + bit - 2 * bit * ((value // bit) % 2)

    sum_devs = [(flip(tp_i, b), sp_i) for b in tp_bits] + [(tp_i, flip(sp_i, b)) for b in sp_bits]

    barrier = pltpu.get_barrier_semaphore()
    greeted = [sp_at((line + 1) % outer, half), sp_at((line + outer - 1) % outer, half)] + sum_devs
    for device in greeted:
        pl.semaphore_signal(barrier, inc=1, device_id=device, device_id_type=MESH)
    pl.semaphore_wait(barrier, len(greeted))

    def remote(src, dst, send, recv, device):
        return pltpu.make_async_remote_copy(
            src_ref=src, dst_ref=dst, send_sem=send, recv_sem=recv,
            device_id=device, device_id_type=MESH,
        )

    places = (line, last - line)
    nexts = (sp_at(jnp.minimum(line + 1, last), half), sp_at(jnp.maximum(line - 1, 0), half))
    signs = (1, -1)

    def rows_of(stream, index):
        count = parts[stream].shape[0] // outer
        return pl.ds(pl.multiple_of(index * count, count), count)

    def reduce_copy(stream, way, step, src):
        return remote(
            src, got[stream].at[way, step - 1], reduce_send.at[stream, way, step - 1],
            reduce_recv.at[stream, way, step - 1], nexts[way],
        )

    def clamp(index):
        return jnp.clip(index, 0, last)

    def reduce_step(stream, step):
        for way in range(2):
            place, sign = places[way], signs[way]
            target = clamp(line + sign * (outer - step))
            own = parts[stream].at[rows_of(stream, target), :]

            @pl.when(place == 0)
            def _():
                reduce_copy(stream, way, step, own).start()

            if step > 1:

                @pl.when((place > 0) & (place <= step - 1))
                def _():
                    reduce_copy(stream, way, step - 1, own).wait_recv()
                    stage = staged[stream].at[way, step - 2]
                    stage[...] = (
                        got[stream][way, step - 2].astype(F32) + own[...].astype(F32)
                    ).astype(BF16)
                    reduce_copy(stream, way, step, stage).start()

    def gather_copy(stream, way, step, origin):
        block = outs[stream].at[half, rows_of(stream, origin), :]
        return remote(
            block, block, gather_send.at[stream, way, step - 1],
            gather_recv.at[stream, way, step - 1], nexts[way],
        )

    def pair_copy(stream, slot, origin):
        block = outs[stream].at[half, rows_of(stream, origin), :]
        return remote(block, block, pair_send.at[stream, slot], pair_recv.at[stream, slot], pair_dev)

    def reduce_final(stream):
        own = parts[stream].at[rows_of(stream, line), :]
        block = outs[stream].at[half, rows_of(stream, line), :]
        for way in range(2):

            @pl.when(places[way] > 0)
            def _():
                reduce_copy(stream, way, last, own).wait_recv()

        up = jnp.where(line > 0, got[stream][0, last - 1].astype(F32), 0.0)
        down = jnp.where(line < last, got[stream][1, last - 1].astype(F32), 0.0)
        block[...] = (own[...].astype(F32) + up + down).astype(BF16)
        for way in range(2):

            @pl.when(places[way] < last)
            def _():
                gather_copy(stream, way, 1, line).start()

        pair_copy(stream, 0, line).start()

    def gather_step(stream, step):
        for way in range(2):
            place, sign = places[way], signs[way]
            origin = clamp(line - sign * step)

            @pl.when(place >= step)
            def _():
                gather_copy(stream, way, step, origin).wait_recv()
                if step < last:

                    @pl.when(place < last)
                    def _():
                        gather_copy(stream, way, step + 1, origin).start()

                pair_copy(stream, 1 + way * last + step - 1, origin).start()

    def drain(stream):
        pair_copy(stream, 0, line).wait()
        for way in range(2):
            place, sign = places[way], signs[way]
            for step in range(1, outer):
                origin = clamp(line - sign * step)

                @pl.when(place <= step - 1)
                def _():
                    reduce_copy(stream, way, step, parts[stream].at[rows_of(stream, 0), :]).wait_send()

                @pl.when((place >= step - 1) & (place < last))
                def _():
                    gather_copy(stream, way, step, origin).wait_send()

                @pl.when(place >= step)
                def _():
                    pair_copy(stream, 1 + way * last + step - 1, origin).wait()

    def near_copy(index):
        return remote(
            part_ref.at[index, 1 - core], near_got.at[index], tp_send.at[index], tp_recv.at[index],
            core_dev,
        )

    def far_copy():
        return remote(far_stage, far_got, tp_send.at[sides], tp_recv.at[sides], side_dev)

    def spread_copy(slot, s, device):
        block = grad_out.at[s, core]
        return remote(block, block, tp_send.at[sides + slot], tp_recv.at[sides + slot], device)

    def input_step(step):
        if step == 0:
            for index in range(sides):
                near_copy(index).start()
        if step == 1:
            for index in range(sides):
                near_copy(index).wait_recv()
            keep_buf[...] = part_ref[side, core].astype(F32) + near_got[side].astype(F32)
            far_stage[...] = (
                part_ref[1 - side, core].astype(F32) + near_got[1 - side].astype(F32)
            ).astype(BF16)
            far_copy().start()
        if step == 2:
            far_copy().wait_recv()
            incoming = keep_buf[...] + far_got[...].astype(F32)
            values = hidden_ref[...].astype(F32)
            scales = scale_ref[...]
            weighted = incoming * gain_ref[...]
            inner_sum = jnp.sum(weighted * values, axis=-1, keepdims=True)
            grads = scales * weighted - values * (scales * scales * scales) * inner_sum * width_scale
            grad_out[side, core] = (middle_ref[...] + grads).astype(BF16)
            spread_copy(1, side, side_dev).start()
            spread_copy(2, side, core_dev).start()
        if step == 3:
            spread_copy(1, side, side_dev).wait_recv()
            spread_copy(3, 1 - side, core_dev).start()
        if step == 4:
            spread_copy(2, side, core_dev).wait_recv()
            spread_copy(3, 1 - side, core_dev).wait_recv()
            for index in range(sides):
                near_copy(index).wait_send()
            far_copy().wait_send()
            spread_copy(1, side, side_dev).wait_send()
            spread_copy(2, side, core_dev).wait_send()
            spread_copy(3, 1 - side, core_dev).wait_send()

    rounds = len(sum_devs)

    def sums_copy(step):
        src = sums_ref if step == 0 else sums_stage.at[step - 1]
        return remote(
            src, sums_got.at[step], sums_send.at[step], sums_recv.at[step], sum_devs[step]
        )

    def sums_step(step):
        if step > 0:
            sums_copy(step - 1).wait_recv()
            before = sums_ref[...] if step == 1 else sums_stage[step - 2]
            total = before + sums_got[step - 1]
            if step == rounds:
                sums_out[...] = total
            else:
                sums_stage[step - 1] = total
        if step < rounds:
            sums_copy(step).start()
        if step == rounds:
            for index in range(rounds):
                sums_copy(index).wait_send()

    extra = []
    for index in range(5):
        extra.append(functools.partial(input_step, index))
    for index in range(rounds + 1):
        extra.append(functools.partial(sums_step, index))
    for turn in range(streams + 1):
        for step in range(1, outer + 1):
            if turn < streams:
                if step < outer:
                    reduce_step(turn, step)
                else:
                    reduce_final(turn)
            if turn > 0 and step < outer:
                gather_step(turn - 1, step)
            if extra:
                extra.pop(0)()
    for step in extra:
        step()
    for stream in range(streams):
        drain(stream)


def finish(parts, part, hidden, scales, gain, middle, sums, outer, sp_n, tp_n):
    streams = len(parts)
    sides = tp_n // 2
    quarter, model = hidden.shape
    last = outer - 1
    rounds = (tp_n - 1).bit_length() + (sp_n - 1).bit_length()
    vmem = pl.BlockSpec(memory_space=pltpu.VMEM)
    chunk = [(2, last, p.shape[0] // outer, p.shape[1]) for p in parts]
    dma = pltpu.SemaphoreType.DMA
    return pl.pallas_call(
        functools.partial(finish_kernel, outer, sides, sp_n, tp_n, streams, 1.0 / model),
        out_shape=[jax.ShapeDtypeStruct((2,) + p.shape, BF16) for p in parts]
        + [
            jax.ShapeDtypeStruct((sides, 2, quarter, model), BF16),
            jax.ShapeDtypeStruct(sums.shape, F32),
        ],
        in_specs=[vmem] * (streams + 6),
        out_specs=[vmem] * (streams + 2),
        scratch_shapes=[pltpu.VMEM(c, BF16) for c in chunk]
        + [pltpu.VMEM(c, BF16) for c in chunk]
        + [
            pltpu.VMEM((sides, quarter, model), BF16),
            pltpu.VMEM((quarter, model), BF16),
            pltpu.VMEM((quarter, model), F32),
            pltpu.VMEM((quarter, model), BF16),
            pltpu.VMEM((rounds,) + sums.shape, F32),
            pltpu.VMEM((rounds,) + sums.shape, F32),
        ]
        + [dma((streams, 2, last))] * 4
        + [dma((streams, 1 + 2 * last))] * 2
        + [dma((sides + 4,))] * 2
        + [dma((rounds,))] * 2,
        compiler_params=pltpu.CompilerParams(
            collective_id=1, has_side_effects=True, vmem_limit_bytes=60 * 1024 * 1024
        ),
        cost_estimate=pl.CostEstimate(flops=10**9, bytes_accessed=10**8, transcendentals=0),
        name="finish",
    )(*parts, part, hidden, scales, gain, middle, sums)


def body(
    hidden,
    segment_ids,
    attn_norm,
    query_proj,
    key_proj,
    value_proj,
    gate_proj,
    output_proj,
    query_norm,
    key_norm,
    ffn_norm,
    ffn_gate,
    ffn_up,
    ffn_down,
    upstream,
):
    rows_dev, model = hidden.shape
    head_width = query_norm.shape[0]
    heads = query_proj.shape[1] // head_width
    groups = key_proj.shape[1] // head_width
    per_group = heads // groups
    group_width = groups * head_width
    sp_n = lax.axis_size("sp")
    tp_n = lax.axis_size("tp")
    outer = sp_n // 2
    sides = tp_n // 2
    quarter = rows_dev // tp_n
    tp_i = lax.axis_index("tp")
    sp_i = lax.axis_index("sp")
    ring_i = sp_i // 2
    pair_i = sp_i % 2
    side_i = tp_i // 2
    core_i = tp_i % 2
    own_first = sp_i * rows_dev
    quarter_first = tp_i * quarter
    scale = 1.0 / math.sqrt(head_width)

    ring_pairs = [(z * 2 + y, ((z + 1) % outer) * 2 + y) for z in range(outer) for y in range(2)]
    pair_pairs = [(i, i ^ 1) for i in range(sp_n)]
    side_pairs = [(i, i ^ 2) for i in range(tp_n)]
    core_pairs = [(i, i ^ 1) for i in range(tp_n)]

    def ring(value):
        return lax.ppermute(value, "sp", ring_pairs)

    def pair(value):
        return lax.ppermute(value, "sp", pair_pairs)

    def side(value):
        return lax.ppermute(value, "tp", side_pairs)

    def core(value):
        return lax.ppermute(value, "tp", core_pairs)

    def gather_sp(block):
        blocks = []
        for k in range(outer):
            blocks.append((block, pair(block)))
            if k < outer - 1:
                block = ring(block)
        return blocks

    def scatter_sp(parts):
        def paired(k):
            return parts[k][0] + pair(parts[k][1].astype(BF16)).astype(F32)

        total = paired(1 % outer)
        for k in range(2, outer + 1):
            total = ring(total.astype(BF16)).astype(F32) + paired(k % outer)
        return total

    first_id = segment_ids[0]
    second_start = jnp.sum((segment_ids == first_id).astype(jnp.int32))
    own_index = own_first + jnp.arange(rows_dev, dtype=jnp.int32)
    own_starts = jnp.where(own_index < second_start, 0, second_start)
    steps_half = jnp.arange(head_width // 2, dtype=F32)
    frequencies = jnp.exp(steps_half * (-2.0 * math.log(THETA) / head_width))
    angles = (own_index - own_starts).astype(F32)[:, None] * frequencies[None, :]
    cosine = jnp.cos(angles)[:, None, :]
    sine = jnp.sin(angles)[:, None, :]

    hidden_full = hidden.astype(F32)
    normed_full, attn_scales = norm_rows(hidden_full, attn_norm)
    normed = normed_full.astype(BF16)
    key_raw = matmul(normed, key_proj).reshape(rows_dev, groups, head_width)
    value_rows = matmul(normed, value_proj).astype(BF16)
    key_normed, key_scales = norm_rows(key_raw, key_norm)
    key_rot = rotary(key_normed, cosine, sine).astype(BF16).reshape(rows_dev, group_width)
    kv_own = jnp.stack([key_rot, value_rows])

    low, high = (outer // 4, 3 * outer // 4) if outer % 4 == 0 else (0, outer)
    reach = high - 1 if low else outer - 1

    def up_pairs(step):
        return [
            (z * 2 + y, (z + 1) * 2 + y)
            for z in range(outer - 1)
            for y in range(2)
            if z + 1 - step >= 0 and (z + 1 - step >= low or z + 1 < high)
        ]

    kv_blocks = []
    travelling = kv_own
    for k in range(reach + 1):
        kv_blocks.append((travelling, pair(travelling)))
        if k < reach:
            travelling = lax.ppermute(travelling, "sp", up_pairs(k + 1))

    query_raw = matmul(normed, query_proj).reshape(rows_dev, heads, head_width)
    gate_raw = matmul(normed, gate_proj)
    query_normed, query_scales = norm_rows(query_raw, query_norm)
    queries = rotary(query_normed, cosine, sine).astype(BF16).reshape(rows_dev, heads * head_width)

    def swap_half(value):
        piece = model // 4
        mine = pair(lax.dynamic_slice_in_dim(value, ((1 - pair_i) * 2 + core_i) * piece, piece, 1))
        near = core(mine)
        return jnp.where(
            core_i == 1, jnp.concatenate([near, mine], 1), jnp.concatenate([mine, near], 1)
        )

    normed_own = lax.dynamic_slice_in_dim(normed, pair_i * (model // 2), model // 2, 1)
    both_normed = jnp.concatenate([normed_own, swap_half(normed)])

    grad_quarter = lax.dynamic_slice_in_dim(upstream, quarter_first, quarter)
    up_blocks = gather_sp(grad_quarter)

    row_start_low = own_starts[0]
    row_start_high = own_starts[-1]

    def block_info(k):
        shards = [(ring_i - k) * 2 + pair_i, (ring_i - k) * 2 + (1 - pair_i)]
        entries = [own_first] + [shard * rows_dev for shard in shards]
        live = []
        full = []
        for shard in shards:
            token = shard * rows_dev
            live.append((shard >= 0) & (shard <= sp_i) & (token + rows_dev - 1 >= row_start_low))
            full.append((token >= row_start_high) & (shard < sp_i))
        return jnp.stack(entries + [v.astype(jnp.int32) for v in live + full]).astype(jnp.int32)

    infos = [block_info(k) for k in range(reach + 1)]
    starts_column = own_starts[:, None]
    starts_row = own_starts[None, :]
    carried = None
    for k in range(reach + 1):
        carried = attn_forward(
            infos[k], starts_column, queries, kv_blocks[k][0], kv_blocks[k][1], carried, scale
        )
    mix_acc, mix_sum = carried
    mixed = mix_acc / mix_sum
    lse = jnp.log2(mix_sum.reshape(rows_dev, heads, head_width)[:, :, 0])
    lse_rows = lse.T.reshape(groups, per_group, rows_dev)
    gate_sig = jax.nn.sigmoid(gate_raw)
    gated = (mixed * gate_sig).astype(BF16)
    gated_other = pair(gated)

    def scatter_tp(part):
        part = part.reshape(sides, 2, quarter, model)
        keep = lax.dynamic_index_in_dim(part, core_i, 1, keepdims=False)
        send = lax.dynamic_index_in_dim(part, 1 - core_i, 1, keepdims=False)
        keep = keep + core(send.astype(BF16)).astype(F32)
        mine = lax.dynamic_index_in_dim(keep, side_i, 0, keepdims=False)
        other = lax.dynamic_index_in_dim(keep, 1 - side_i, 0, keepdims=False)
        return mine + side(other.astype(BF16)).astype(F32)

    def gather_tp(block):
        far = side(block)
        swap_side = side_i == 1
        two = jnp.where(swap_side, jnp.stack([far, block]), jnp.stack([block, far]))
        near = core(two)
        swap_core = core_i == 1
        full = jnp.where(
            swap_core, jnp.stack([near, two], axis=1), jnp.stack([two, near], axis=1)
        )
        return full.reshape((rows_dev,) + block.shape[1:])

    attn_quarter = scatter_tp(matmul(gated, output_proj))
    hidden_quarter = lax.dynamic_slice_in_dim(hidden, quarter_first, quarter).astype(F32)
    middle = hidden_quarter + attn_quarter
    normed_two_full, ffn_scales = norm_rows(middle, ffn_norm)
    normed_two = normed_two_full.astype(BF16)

    two_blocks = gather_sp(normed_two)
    rows_list, up_list, inner_list, gate_list, grad_up_list = [None] * outer, [None] * outer, [None] * outer, [None] * outer, [None] * outer
    grad_parts = [None] * outer
    for k in list(range(1, outer)) + [0]:
        rows_k = jnp.concatenate(two_blocks[k])
        up_k = jnp.concatenate(up_blocks[k])
        gate_vals = matmul(rows_k, ffn_gate)
        up_vals = matmul(rows_k, ffn_up)
        sig = jax.nn.sigmoid(gate_vals)
        grad_inner = times_transpose(up_k, ffn_down)
        grad_gate = (grad_inner * up_vals * (sig * (1.0 + gate_vals * (1.0 - sig)))).astype(BF16)
        grad_up = (grad_inner * (gate_vals * sig)).astype(BF16)
        inner = (gate_vals * sig * up_vals).astype(BF16)
        grad_parts[k] = (
            times_transpose(grad_gate, ffn_gate) + times_transpose(grad_up, ffn_up)
        ).reshape(2, quarter, model)
        rows_list[k], up_list[k], inner_list[k] = rows_k, up_k, inner
        gate_list[k], grad_up_list[k] = grad_gate, grad_up
    grad_two = scatter_sp(grad_parts)

    norm_grad_two, ffn_gain_terms = norm_back(middle, ffn_scales, ffn_norm, grad_two)
    grad_middle_quarter = grad_quarter.astype(F32) + norm_grad_two
    grad_branch = gather_tp(grad_middle_quarter.astype(BF16))

    mlp_parts = [matmul(inner_list[k], ffn_down).reshape(2, quarter, model) for k in range(outer)]
    mlp_quarter = scatter_sp(mlp_parts)
    layer_out = gather_tp((middle + mlp_quarter).astype(BF16))

    rows_all = jnp.concatenate(rows_list)
    up_all = jnp.concatenate(up_list)
    inner_all = jnp.concatenate(inner_list)
    gate_all = jnp.concatenate(gate_list)
    grad_up_all = jnp.concatenate(grad_up_list)

    def reduce_tp(part):
        half = part.shape[0] // 2
        keep = lax.dynamic_slice_in_dim(part, core_i * half, half)
        send = lax.dynamic_slice_in_dim(part, (1 - core_i) * half, half)
        keep = (keep + core(send.astype(BF16)).astype(F32)).astype(BF16)
        keep = (keep.astype(F32) + side(keep).astype(F32)).astype(BF16)
        near = core(keep)
        total = jnp.where(
            core_i == 1, jnp.concatenate([near, keep]), jnp.concatenate([keep, near])
        )
        return total.astype(F32)

    ffn_gate_grad = reduce_tp(outer_sum(rows_all, gate_all))
    ffn_up_grad = reduce_tp(outer_sum(rows_all, grad_up_all))
    ffn_down_grad = reduce_tp(outer_sum(inner_all, up_all))

    branch_other = swap_half(grad_branch)
    branch_own = lax.dynamic_slice_in_dim(grad_branch, pair_i * (model // 2), model // 2, 1)
    output_half = outer_sum(
        jnp.concatenate([gated, gated_other]), jnp.concatenate([branch_own, branch_other])
    )
    grad_gated = times_transpose(grad_branch, output_proj)
    grad_mixed = (grad_gated * gate_sig).astype(BF16)
    grad_gate_raw = (grad_gated * mixed * (gate_sig * (1.0 - gate_sig))).astype(BF16)
    gate_half = outer_sum(both_normed, jnp.concatenate([grad_gate_raw, pair(grad_gate_raw)]))
    deltas = jnp.sum(
        (grad_mixed.astype(F32) * mixed).reshape(rows_dev, heads, head_width), axis=-1
    )
    delta_rows = deltas.T.reshape(groups, per_group, rows_dev)

    def down_pairs(step):
        return [(b, a) for a, b in up_pairs(step)]

    query_acc = None
    travelling = None
    for k in list(range(reach, -1, -1)):
        query_acc, grad_a, grad_b = attn_backward(
            infos[k], starts_row, lse_rows, delta_rows, queries, grad_mixed,
            kv_blocks[k][0], kv_blocks[k][1], query_acc, k == 0, scale,
        )
        total = grad_a.astype(F32) + pair(grad_b).astype(F32)
        if travelling is not None:
            total = total + travelling.astype(F32)
        if k > 0:
            travelling = lax.ppermute(total.astype(BF16), "sp", down_pairs(k))
    grad_key_rot = total[0].reshape(rows_dev, groups, head_width)
    grad_value_low = total[1].astype(BF16)
    grad_query_rot = (query_acc * scale).reshape(rows_dev, heads, head_width)
    grad_query_raw, query_gain_terms = norm_back(
        query_raw, query_scales, query_norm, rotary_back(grad_query_rot, cosine, sine)
    )
    grad_key_raw, key_gain_terms = norm_back(
        key_raw, key_scales, key_norm, rotary_back(grad_key_rot, cosine, sine)
    )
    grad_query_low = grad_query_raw.reshape(rows_dev, heads * head_width).astype(BF16)
    grad_key_low = grad_key_raw.reshape(rows_dev, group_width).astype(BF16)
    grad_kv_low = jnp.concatenate([grad_key_low, grad_value_low], axis=1)

    both_queries = jnp.concatenate([grad_query_low, pair(grad_query_low)])
    both_kv = jnp.concatenate([grad_kv_low, pair(grad_kv_low)])
    parts = [
        output_half.astype(BF16),
        gate_half.astype(BF16),
        outer_sum(both_normed, both_queries).astype(BF16),
        outer_sum(both_normed, both_kv).astype(BF16),
    ]

    grad_normed_part = (
        times_transpose(grad_query_low, query_proj)
        + times_transpose(grad_key_low, key_proj)
        + times_transpose(grad_value_low, value_proj)
        + times_transpose(grad_gate_raw, gate_proj)
    )
    gains = jnp.concatenate(
        [
            jnp.sum(grad_normed_part * hidden_full * attn_scales, axis=0),
            jnp.sum(ffn_gain_terms, axis=0),
            jnp.sum(query_gain_terms, axis=(0, 1)),
            jnp.sum(key_gain_terms, axis=(0, 1)),
        ]
    )
    gains_at = 2 * model + 2 * head_width
    gains = jnp.pad(gains, (0, -gains_at % 1024)).reshape(-1, 128)
    scales_quarter = lax.dynamic_slice_in_dim(attn_scales, quarter_first, quarter)
    finished = finish(
        parts,
        grad_normed_part.astype(BF16).reshape(sides, 2, quarter, model),
        lax.dynamic_slice_in_dim(hidden, quarter_first, quarter),
        scales_quarter,
        attn_norm[None, :],
        grad_middle_quarter,
        gains,
        outer,
        sp_n,
        tp_n,
    )
    output_all, gate_all_w, query_all, kv_all, input_all, gains = finished
    output_grad = jnp.concatenate([output_all[0], output_all[1]], axis=1).astype(F32)
    gate_grad = gate_all_w.reshape(model, heads * head_width).astype(F32)
    query_grad = query_all.reshape(model, heads * head_width).astype(F32)
    kv_all = kv_all.reshape(model, 2 * group_width)
    key_grad = kv_all[:, :group_width].astype(F32)
    value_grad = kv_all[:, group_width:].astype(F32)
    hidden_grad = input_all.reshape(rows_dev, model).astype(F32)
    gains = gains.reshape(-1)
    return (
        layer_out,
        hidden_grad,
        gains[:model],
        query_grad,
        key_grad,
        value_grad,
        gate_grad,
        output_grad,
        gains[2 * model : 2 * model + head_width],
        gains[2 * model + head_width : gains_at],
        gains[model : 2 * model],
        ffn_gate_grad,
        ffn_up_grad,
        ffn_down_grad,
    )


def solution(mesh):
    placed = (
        P("sp", None),
        P(),
        P(),
        P(None, "tp"),
        P(None, "tp"),
        P(None, "tp"),
        P(None, "tp"),
        P("tp", None),
        P(),
        P(),
        P(),
        P(None, "sp"),
        P(None, "sp"),
        P("sp", None),
        P("sp", None),
    )
    return jax.shard_map(
        body,
        mesh=mesh,
        in_specs=placed,
        out_specs=(
            P("sp", None),
            P("sp", None),
            P(),
            P(None, "tp"),
            P(None, "tp"),
            P(None, "tp"),
            P(None, "tp"),
            P("tp", None),
            P(),
            P(),
            P(),
            P(None, "sp"),
            P(None, "sp"),
            P("sp", None),
        ),
        check_vma=False,
    )
```

```python
import functools
import math

import jax
import jax.numpy as jnp
from jax import lax
from jax.experimental import pallas as pl
from jax.experimental.pallas import tpu as pltpu
from jax.sharding import PartitionSpec as P

EPSILON = 1e-06
THETA = 1000000.0
LOG2E = 1.4426950408889634
F32 = jnp.float32
BF16 = jnp.bfloat16


def norm_scales(values):
    return lax.rsqrt(jnp.mean(values * values, axis=-1, keepdims=True) + EPSILON)


def norm_rows(values, gain):
    scales = norm_scales(values)
    return (values * scales * gain, scales)


def norm_back(values, scales, gain, incoming):
    weighted = incoming * gain
    inner_sum = jnp.sum(weighted * values, axis=-1, keepdims=True)
    grad_values = (
        scales * weighted - values * (scales * scales * scales) * inner_sum / values.shape[-1]
    )
    return (grad_values, incoming * values * scales)


def rotary(values, cosine, sine):
    half_width = values.shape[-1] // 2
    front_half = values[..., :half_width]
    back_half = values[..., half_width:]
    return jnp.concatenate(
        [front_half * cosine - back_half * sine, back_half * cosine + front_half * sine], axis=-1
    )


def rotary_back(grads, cosine, sine):
    half_width = grads.shape[-1] // 2
    front_half = grads[..., :half_width]
    back_half = grads[..., half_width:]
    return jnp.concatenate(
        [front_half * cosine + back_half * sine, back_half * cosine - front_half * sine], axis=-1
    )


def matmul(left, right):
    return jnp.dot(left, right, preferred_element_type=F32)


def outer_sum(left, right):
    return lax.dot_general(left, right, (((0,), (0,)), ((), ())), preferred_element_type=F32)


def times_transpose(left, right):
    return lax.dot_general(left, right, (((1,), (1,)), ((), ())), preferred_element_type=F32)


def attn_forward_kernel(first, diagonal, scale, info, starts, queries, kv_a, kv_b, *rest):
    if first:
        acc_out, sum_out = rest
    else:
        acc_in, sum_in, acc_out, sum_out = rest
    rows = queries.shape[0]
    keys_n = kv_a.shape[1]
    per_group = queries.shape[1] // kv_a.shape[2]
    width = kv_a.shape[2]
    if first:
        acc_out[...] = jnp.zeros_like(acc_out)
        sum_out[...] = jnp.zeros_like(sum_out)
    else:
        acc_out[...] = acc_in[...]
        sum_out[...] = sum_in[...]
    own_first = info[0]
    for slot, block in enumerate((kv_a, kv_b)):
        key_first = info[1 + slot]
        live = info[3 + slot] > 0

        def work(masked, causal):
            ones = jnp.ones((keys_n, width), BF16)
            values = jnp.concatenate([block[1], ones], axis=1)
            keys = block[0]
            if masked:
                key_index = key_first + lax.broadcasted_iota(jnp.int32, (rows, keys_n), 1)
                allowed = key_index >= starts[...]
                if causal:
                    row_index = own_first + lax.broadcasted_iota(jnp.int32, (rows, keys_n), 0)
                    allowed = allowed & (key_index <= row_index)
            for head in range(per_group):
                cols = slice(head * width, (head + 1) * width)
                scores = times_transpose(queries[:, cols], keys)
                weights = jnp.exp2(scores * (scale * LOG2E))
                if masked:
                    weights = jnp.where(allowed, weights, 0.0)
                both = matmul(weights.astype(BF16), values)
                acc_out[:, cols] += both[:, :width]
                sum_out[:, cols] += both[:, width:]

        if diagonal and slot == 0:
            work(True, True)
        else:
            full = info[5 + slot] > 0
            pl.when(live & full)(functools.partial(work, False, False))
            pl.when(live & jnp.logical_not(full))(functools.partial(work, True, False))


def attn_forward(info, starts, queries, kv_a, kv_b, carried, scale):
    rows, all_width = queries.shape
    width = 128
    groups = kv_a.shape[2] // width
    group_width = all_width // groups
    keys_n = kv_a.shape[1]
    first = carried is None
    spec_q = pl.BlockSpec((rows, group_width), lambda g, info: (0, g))
    spec_kv = pl.BlockSpec((2, keys_n, width), lambda g, info: (0, 0, g))
    specs = [pl.BlockSpec((rows, 1), lambda g, info: (0, 0)), spec_q, spec_kv, spec_kv]
    operands = [starts, queries, kv_a, kv_b]
    if not first:
        specs += [spec_q, spec_q]
        operands += list(carried)
    return pl.pallas_call(
        functools.partial(attn_forward_kernel, first, first, scale),
        grid_spec=pltpu.PrefetchScalarGridSpec(
            num_scalar_prefetch=1,
            grid=(groups,),
            in_specs=specs,
            out_specs=[spec_q, spec_q],
        ),
        out_shape=[jax.ShapeDtypeStruct((rows, all_width), F32)] * 2,
        compiler_params=pltpu.CompilerParams(dimension_semantics=("arbitrary",)),
        cost_estimate=pl.CostEstimate(
            flops=16 * rows * keys_n * all_width,
            transcendentals=2 * rows * keys_n * all_width // width,
            bytes_accessed=8 * rows * all_width,
        ),
        name="attn_forward",
    )(info, *operands)


def attn_backward_kernel(first, diagonal, scale, info, starts, lse, deltas, queries, grads, kv_a, kv_b, *rest):
    if first:
        grad_q, grad_a, grad_b = rest
    else:
        grad_in, grad_q, grad_a, grad_b = rest
    rows = queries.shape[0]
    keys_n = kv_a.shape[1]
    width = kv_a.shape[2]
    per_group = queries.shape[1] // width
    if first:
        grad_q[...] = jnp.zeros_like(grad_q)
    else:
        grad_q[...] = grad_in[...]
    own_first = info[0]
    for slot, (block, out) in enumerate(((kv_a, grad_a), (kv_b, grad_b))):
        key_first = info[1 + slot]
        live = info[3 + slot] > 0

        def work(masked, causal):
            keys = block[0]
            values = block[1]
            keys_t = keys.T
            if masked:
                key_index = key_first + lax.broadcasted_iota(jnp.int32, (keys_n, rows), 0)
                allowed = key_index >= starts[...]
                if causal:
                    row_index = own_first + lax.broadcasted_iota(jnp.int32, (keys_n, rows), 1)
                    allowed = allowed & (key_index <= row_index)
            total_k = jnp.zeros((keys_n, width), F32)
            total_v = jnp.zeros((keys_n, width), F32)
            for head in range(per_group):
                cols = slice(head * width, (head + 1) * width)
                q_head = queries[:, cols]
                g_head = grads[:, cols]
                scores = times_transpose(keys, q_head)
                probs = jnp.exp2(scores * (scale * LOG2E) - lse[0, head : head + 1, :])
                if masked:
                    probs = jnp.where(allowed, probs, 0.0)
                grad_probs = times_transpose(values, g_head)
                grad_scores = (probs * (grad_probs - deltas[0, head : head + 1, :])).astype(BF16)
                total_v += matmul(probs.astype(BF16), g_head)
                total_k += matmul(grad_scores, q_head)
                grad_q[:, cols] += matmul(keys_t, grad_scores).T
            out[0] = (total_k * scale).astype(BF16)
            out[1] = total_v.astype(BF16)

        if diagonal and slot == 0:
            work(True, True)
        else:
            full = info[5 + slot] > 0
            pl.when(live & full)(functools.partial(work, False, False))
            pl.when(live & jnp.logical_not(full))(functools.partial(work, True, False))

            @pl.when(jnp.logical_not(live))
            def _():
                out[...] = jnp.zeros_like(out)


def attn_backward(info, starts_row, lse, deltas, queries, grads, kv_a, kv_b, carried, diagonal, scale):
    rows, all_width = queries.shape
    width = 128
    groups = kv_a.shape[2] // width
    group_width = all_width // groups
    per_group = group_width // width
    keys_n = kv_a.shape[1]
    first = carried is None
    spec_q = pl.BlockSpec((rows, group_width), lambda g, info: (0, g))
    spec_kv = pl.BlockSpec((2, keys_n, width), lambda g, info: (0, 0, g))
    spec_row = pl.BlockSpec((1, per_group, rows), lambda g, info: (g, 0, 0))
    specs = [
        pl.BlockSpec((1, rows), lambda g, info: (0, 0)),
        spec_row,
        spec_row,
        spec_q,
        spec_q,
        spec_kv,
        spec_kv,
    ]
    operands = [starts_row, lse, deltas, queries, grads, kv_a, kv_b]
    if not first:
        specs.append(spec_q)
        operands.append(carried)
    return pl.pallas_call(
        functools.partial(attn_backward_kernel, first, diagonal, scale),
        grid_spec=pltpu.PrefetchScalarGridSpec(
            num_scalar_prefetch=1,
            grid=(groups,),
            in_specs=specs,
            out_specs=[spec_q, spec_kv, spec_kv],
        ),
        out_shape=[
            jax.ShapeDtypeStruct((rows, all_width), F32),
            jax.ShapeDtypeStruct(kv_a.shape, BF16),
            jax.ShapeDtypeStruct(kv_a.shape, BF16),
        ],
        compiler_params=pltpu.CompilerParams(dimension_semantics=("arbitrary",)),
        cost_estimate=pl.CostEstimate(
            flops=20 * rows * keys_n * all_width,
            transcendentals=2 * rows * keys_n * all_width // width,
            bytes_accessed=8 * rows * all_width,
        ),
        name="attn_backward",
    )(info, *operands)


def middle_kernel(outer, *refs):
    MESH = pl.DeviceIdType.MESH
    blocks = 2 * outer
    (gated, out_proj, hidden_ref, gain_ref, gate_in, up_in, down_in) = refs[:7]
    ups_in = refs[7 : 7 + blocks]
    (middle_out, grad_out, gain_out, branch, inner_out, dw_gate, dw_up, dw_down) = refs[
        7 + blocks : 15 + blocks
    ]
    (
        w_gate, w_up, w_down, ups, rows, grad_inner, inner, grad_gate, grad_up,
        near_stage, near_got, far_stage, far_got, far_keep, own_keep,
        keep, y_stage, y_got, z_stage, z_got,
        load_sem, store_sem, tp_send, tp_recv, zs, zr, ys, yr, rys, ryr, rzs, rzr,
    ) = refs[15 + blocks :]
    stage_gate, stage_up, stage_down = w_gate, w_up, w_down
    quarter, model = hidden_ref.shape
    group = 2 * quarter
    chunk = model // outer
    last = outer - 1

    sp_i = lax.axis_index("sp")
    tp_i = lax.axis_index("tp")
    line = sp_i // 2
    half = sp_i % 2
    side = tp_i // 2
    core = tp_i % 2

    def sp_at(z, y):
        return (tp_i, z * 2 + y)

    pair_dev = sp_at(line, 1 - half)
    core_dev = (side * 2 + (1 - core), sp_i)
    side_dev = ((1 - side) * 2 + core, sp_i)
    nexts = (sp_at(jnp.minimum(line + 1, last), half), sp_at(jnp.maximum(line - 1, 0), half))

    loads = [
        pltpu.make_async_copy(src, dst, load_sem.at[index])
        for index, (src, dst) in enumerate(
            [(down_in, w_down)]
            + [(ups_in[b], ups.at[pl.ds(b * quarter, quarter), :]) for b in range(blocks)]
            + [(gate_in, w_gate), (up_in, w_up)]
        )
    ]
    for load in loads:
        load.start()

    barrier = pltpu.get_barrier_semaphore()
    greeted = [
        sp_at((line + 1) % outer, half), sp_at((line + outer - 1) % outer, half),
        pair_dev, core_dev, side_dev,
    ]
    for device in greeted:
        pl.semaphore_signal(barrier, inc=1, device_id=device, device_id_type=MESH)
    pl.semaphore_wait(barrier, len(greeted))

    def remote(src, dst, send, recv, device):
        return pltpu.make_async_remote_copy(
            src_ref=src, dst_ref=dst, send_sem=send, recv_sem=recv,
            device_id=device, device_id_type=MESH,
        )

    def aligned(index, count):
        return pl.ds(pl.multiple_of(index * count, count), count)

    def near_copy(j):
        return remote(near_stage.at[j], near_got.at[j], tp_send.at[j], tp_recv.at[j], core_dev)

    def far_copy():
        return remote(far_stage, far_got, tp_send.at[2], tp_recv.at[2], side_dev)

    def projected(s, c):
        return matmul(gated[aligned(s * 2 + c, quarter), :], out_proj[...])

    near_stage[0] = projected(1 - side, 1 - core).astype(BF16)
    near_copy(0).start()
    near_stage[1] = projected(side, 1 - core).astype(BF16)
    near_copy(1).start()
    far_keep[...] = projected(1 - side, core)
    near_copy(0).wait_recv()
    far_stage[...] = (far_keep[...] + near_got[0].astype(F32)).astype(BF16)
    far_copy().start()
    own_keep[...] = projected(side, core)

    for load in loads[: 1 + blocks]:
        load.wait()

    def grad_inner_of(k, carry):
        at = aligned(k, group)
        grad_inner[at, :] = times_transpose(ups[at, :], w_down[...])
        return carry

    lax.fori_loop(0, outer, grad_inner_of, 0)
    near_copy(1).wait_recv()
    far_copy().wait_recv()
    middle = hidden_ref[...].astype(F32) + (
        own_keep[...] + near_got[1].astype(F32) + far_got[...].astype(F32)
    )
    middle_out[...] = middle
    rows[0:quarter, :] = (middle * norm_scales(middle) * gain_ref[...]).astype(BF16)

    def entry(k, j):
        return pl.ds(pl.multiple_of((k * 2 + j) * quarter, quarter), quarter)

    def wrap(k):
        return (k + outer) % outer

    def z_copy(way, k):
        to = wrap(k + 1 - 2 * way)
        return remote(
            rows.at[entry(k, 0), :], rows.at[entry(to, 0), :], zs.at[way, k], zr.at[to], nexts[way]
        )

    def z_arrived(k):
        return remote(
            rows.at[entry(k, 0), :], rows.at[entry(k, 0), :], zs.at[0, k], zr.at[k], nexts[0]
        )

    def y_copy(k):
        return remote(
            rows.at[entry(k, 0), :], rows.at[entry(k, 1), :], ys.at[k], yr.at[k], pair_dev
        )

    short = jnp.minimum(line, last - line)

    def delta_of(i):
        near = jnp.where(i % 2 == 1, -((i + 1) // 2), (i + 1) // 2)
        far = jnp.where(line < last - line, i - short, short - i)
        return jnp.where(i <= 2 * short, near, far)

    def slot_of(delta):
        return jnp.where(delta <= 0, -delta, outer - delta)

    for way, exists in ((0, line < last), (1, line > 0)):
        pl.when(exists)(z_copy(way, 0).start)
    y_copy(0).start()

    def goes_on(delta):
        return ((delta < 0) & (line < last), (delta > 0) & (line > 0))

    def forward(i):
        delta = delta_of(i)
        k = slot_of(delta)
        z_arrived(k).wait_recv()
        for way, exists in enumerate(goes_on(delta)):
            pl.when(exists)(z_copy(way, k).start)
        y_copy(k).start()

    for load in loads[1 + blocks :]:
        load.wait()
    forward(1)

    def turn_forward(i, carry):
        @pl.when(i + 2 < outer)
        def _():
            forward(i + 2)

        k = slot_of(delta_of(i))
        y_copy(k).wait_recv()
        at = aligned(k, group)
        rows_k = rows[at, :]
        gate_vals = matmul(rows_k, w_gate[...])
        up_vals = matmul(rows_k, w_up[...])
        incoming = grad_inner[at, :]
        sig = jax.nn.sigmoid(gate_vals)
        silu = gate_vals * sig
        grad_gate[at, :] = (incoming * up_vals * (sig * (1.0 + gate_vals * (1.0 - sig)))).astype(BF16)
        grad_up[at, :] = (incoming * silu).astype(BF16)
        inner[at, :] = (silu * up_vals).astype(BF16)
        return carry

    lax.fori_loop(0, outer, turn_forward, 0)
    inner_store = pltpu.make_async_copy(inner, inner_out, store_sem.at[0])
    inner_store.start()

    def y_sum(k):
        at = aligned(k, quarter)
        return remote(y_stage.at[at, :], y_got.at[at, :], rys.at[k], ryr.at[k], pair_dev)

    def turn_parts(step, carry):
        k = slot_of(delta_of(last - step))
        at = aligned(k, group)
        part = times_transpose(grad_gate[at, :], w_gate[...]) + times_transpose(
            grad_up[at, :], w_up[...]
        )
        y_stage[aligned(k, quarter), :] = part[quarter:].astype(BF16)
        y_sum(k).start()
        keep[aligned(k, quarter), :] = part[:quarter]
        return carry

    lax.fori_loop(0, outer, turn_parts, 0)

    def z_sum(way, k):
        to = wrap(k + 1 - 2 * way)
        return remote(
            z_stage.at[aligned(k, quarter), :],
            z_got.at[pl.ds(pl.multiple_of((way * outer + to) * quarter, quarter), quarter), :],
            rzs.at[k], rzr.at[way, to], nexts[way],
        )

    def z_got_at(way, k):
        return z_got[pl.ds(pl.multiple_of((way * outer + k) * quarter, quarter), quarter), :]

    def z_sum_arrived(way, k):
        return remote(
            z_stage.at[aligned(k, quarter), :], z_stage.at[aligned(k, quarter), :],
            rzs.at[k], rzr.at[way, k], nexts[way],
        )

    def gate_up_stores(c):
        at = aligned(c, chunk)
        return (
            pltpu.make_async_copy(stage_gate.at[at, :], dw_gate.at[at, :], store_sem.at[1 + 2 * c]),
            pltpu.make_async_copy(stage_up.at[at, :], dw_up.at[at, :], store_sem.at[2 + 2 * c]),
        )

    def weight_chunk(c):
        at = aligned(c, chunk)
        some = rows[:, at]
        stage_gate[at, :] = outer_sum(some, grad_gate[...]).astype(BF16)
        stage_up[at, :] = outer_sum(some, grad_up[...]).astype(BF16)
        for store in gate_up_stores(c):
            store.start()

    def turn_sums(step, carry):
        weight_chunk(step)
        delta = delta_of(last - step)
        k = slot_of(delta)
        at = aligned(k, quarter)
        y_sum(k).wait_recv()
        own = keep[at, :] + y_got[at, :].astype(F32)
        for way, (here, before) in enumerate(
            ((delta > 0, line > 0), (delta < 0, line < last))
        ):

            @pl.when(here & before)
            def _():
                z_sum_arrived(way, k).wait_recv()
                z_stage[at, :] = (own + z_got_at(way, k).astype(F32)).astype(BF16)

            @pl.when(here & jnp.logical_not(before))
            def _():
                z_stage[at, :] = own.astype(BF16)

            pl.when(here)(z_sum(way, k).start)
        return carry

    lax.fori_loop(0, last, turn_sums, 0)
    weight_chunk(last)
    y_sum(0).wait_recv()
    for way, exists in ((0, line > 0), (1, line < last)):
        pl.when(exists)(z_sum_arrived(way, 0).wait_recv)
    below = jnp.where(line > 0, z_got_at(0, 0).astype(F32), 0.0)
    above = jnp.where(line < last, z_got_at(1, 0).astype(F32), 0.0)
    grad_two = keep[0:quarter, :] + y_got[0:quarter, :].astype(F32) + below + above

    values = middle_out[...]
    back, gain_terms = norm_back(values, norm_scales(values), gain_ref[...], grad_two)
    grads = ups[0:quarter, :].astype(F32) + back
    branch[side, core] = grads.astype(BF16)

    def spread_copy(slot, s, device):
        block = branch.at[s, core]
        return remote(block, block, tp_send.at[3 + slot], tp_recv.at[3 + slot], device)

    spread_copy(0, side, side_dev).start()
    spread_copy(1, side, core_dev).start()
    grad_out[...] = grads
    gain_out[...] = jnp.sum(gain_terms, axis=0, keepdims=True)

    def down_store(c):
        at = aligned(c, chunk)
        return pltpu.make_async_copy(
            stage_down.at[:, at], dw_down.at[:, at], store_sem.at[1 + 2 * outer + c]
        )

    def turn_down(c, carry):
        at = aligned(c, chunk)
        stage_down[:, at] = outer_sum(inner[...], ups[:, at]).astype(BF16)
        down_store(c).start()
        return carry

    lax.fori_loop(0, outer, turn_down, 0)
    spread_copy(0, side, side_dev).wait_recv()
    spread_copy(2, 1 - side, core_dev).start()
    spread_copy(1, side, core_dev).wait_recv()

    inner_store.wait()
    near_copy(0).wait_send()
    near_copy(1).wait_send()
    far_copy().wait_send()
    for way, exists in ((0, line < last), (1, line > 0)):
        pl.when(exists)(z_copy(way, 0).wait_send)

    def turn_drain(i, carry):
        delta = delta_of(i)
        k = slot_of(delta)
        y_copy(k).wait_send()
        y_sum(k).wait_send()
        for store in gate_up_stores(i):
            store.wait()
        down_store(i).wait()
        for way, exists in enumerate(goes_on(delta)):
            pl.when(exists)(z_copy(way, k).wait_send)
        pl.when(delta != 0)(z_sum(0, k).wait_send)
        return carry

    lax.fori_loop(0, outer, turn_drain, 0)
    spread_copy(0, side, side_dev).wait_send()
    spread_copy(1, side, core_dev).wait_send()
    spread_copy(2, 1 - side, core_dev).wait()


def middle_layer(gated, out_proj, hidden, gain, w_gate, w_up, w_down, ups, outer, sides):
    quarter, model = hidden.shape
    units = w_down.shape[0]
    rows_n = 2 * outer * quarter
    vmem = pl.BlockSpec(memory_space=pltpu.VMEM)
    anywhere = pl.BlockSpec(memory_space=pl.ANY)
    dma = pltpu.SemaphoreType.DMA
    line_rows = outer * quarter
    return pl.pallas_call(
        functools.partial(middle_kernel, outer),
        out_shape=[
            jax.ShapeDtypeStruct((quarter, model), F32),
            jax.ShapeDtypeStruct((quarter, model), F32),
            jax.ShapeDtypeStruct((1, model), F32),
            jax.ShapeDtypeStruct((sides, 2, quarter, model), BF16),
            jax.ShapeDtypeStruct((rows_n, units), BF16),
            jax.ShapeDtypeStruct((model, units), BF16),
            jax.ShapeDtypeStruct((model, units), BF16),
            jax.ShapeDtypeStruct((units, model), BF16),
        ],
        in_specs=[vmem] * 4 + [anywhere] * (3 + len(ups)),
        out_specs=[vmem] * 4 + [anywhere] * 4,
        scratch_shapes=[
            pltpu.VMEM((model, units), BF16),
            pltpu.VMEM((model, units), BF16),
            pltpu.VMEM((units, model), BF16),
            pltpu.VMEM((rows_n, model), BF16),
            pltpu.VMEM((rows_n, model), BF16),
            pltpu.VMEM((rows_n, units), F32),
            pltpu.VMEM((rows_n, units), BF16),
            pltpu.VMEM((rows_n, units), BF16),
            pltpu.VMEM((rows_n, units), BF16),
            pltpu.VMEM((2, quarter, model), BF16),
            pltpu.VMEM((2, quarter, model), BF16),
            pltpu.VMEM((quarter, model), BF16),
            pltpu.VMEM((quarter, model), BF16),
            pltpu.VMEM((quarter, model), F32),
            pltpu.VMEM((quarter, model), F32),
            pltpu.VMEM((line_rows, model), F32),
            pltpu.VMEM((line_rows, model), BF16),
            pltpu.VMEM((line_rows, model), BF16),
            pltpu.VMEM((line_rows, model), BF16),
            pltpu.VMEM((2 * line_rows, model), BF16),
            dma((3 + len(ups),)),
            dma((1 + 3 * outer,)),
            dma((6,)),
            dma((6,)),
            dma((2, outer)),
            dma((outer,)),
            dma((outer,)),
            dma((outer,)),
            dma((outer,)),
            dma((outer,)),
            dma((outer,)),
            dma((2, outer)),
        ],
        compiler_params=pltpu.CompilerParams(
            collective_id=2, has_side_effects=True, vmem_limit_bytes=58 * 1024 * 1024
        ),
        cost_estimate=pl.CostEstimate(flops=3 * 10**10, bytes_accessed=4 * 10**7, transcendentals=0),
        name="middle",
    )(gated, out_proj, hidden, gain, w_gate, w_up, w_down, *ups)


def finish_kernel(
    outer, sides, sp_n, tp_n, streams, width_scale,
    *refs,
):
    MESH = pl.DeviceIdType.MESH
    parts = refs[:streams]
    (part_ref, hidden_ref, scale_ref, gain_ref, middle_ref, sums_ref) = refs[streams : streams + 6]
    outs = refs[streams + 6 : 2 * streams + 6]
    grad_out, sums_out = refs[2 * streams + 6 : 2 * streams + 8]
    rest = refs[2 * streams + 8 :]
    got = rest[:streams]
    staged = rest[streams : 2 * streams]
    (near_got, far_got, keep_buf, far_stage, sums_got, sums_stage) = rest[2 * streams : 2 * streams + 6]
    (reduce_send, reduce_recv, gather_send, gather_recv, pair_send, pair_recv) = rest[
        2 * streams + 6 : 2 * streams + 12
    ]
    tp_send, tp_recv, sums_send, sums_recv = rest[2 * streams + 12 :]

    sp_i = lax.axis_index("sp")
    tp_i = lax.axis_index("tp")
    line = sp_i // 2
    half = sp_i % 2
    side = tp_i // 2
    core = tp_i % 2
    last = outer - 1

    def sp_at(z, y):
        return (tp_i, z * 2 + y)

    pair_dev = sp_at(line, 1 - half)
    core_dev = (side * 2 + (1 - core), sp_i)
    side_dev = ((1 - side) * 2 + core, sp_i)

    tp_bits = []
    bit = 1
    while bit < tp_n:
        tp_bits.append(bit)
        bit *= 2
    sp_bits = []
    bit = 1
    while bit < sp_n:
        sp_bits.append(bit)
        bit *= 2

    def flip(value, bit):
        return value + bit - 2 * bit * ((value // bit) % 2)

    sum_devs = [(flip(tp_i, b), sp_i) for b in tp_bits] + [(tp_i, flip(sp_i, b)) for b in sp_bits]

    barrier = pltpu.get_barrier_semaphore()
    greeted = [sp_at((line + 1) % outer, half), sp_at((line + outer - 1) % outer, half)] + sum_devs
    for device in greeted:
        pl.semaphore_signal(barrier, inc=1, device_id=device, device_id_type=MESH)
    pl.semaphore_wait(barrier, len(greeted))

    def remote(src, dst, send, recv, device):
        return pltpu.make_async_remote_copy(
            src_ref=src, dst_ref=dst, send_sem=send, recv_sem=recv,
            device_id=device, device_id_type=MESH,
        )

    places = (line, last - line)
    nexts = (sp_at(jnp.minimum(line + 1, last), half), sp_at(jnp.maximum(line - 1, 0), half))
    signs = (1, -1)

    def rows_of(stream, index):
        count = parts[stream].shape[0] // outer
        return pl.ds(pl.multiple_of(index * count, count), count)

    def reduce_copy(stream, way, step, src):
        return remote(
            src, got[stream].at[way, step - 1], reduce_send.at[stream, way, step - 1],
            reduce_recv.at[stream, way, step - 1], nexts[way],
        )

    def clamp(index):
        return jnp.clip(index, 0, last)

    def reduce_step(stream, step):
        for way in range(2):
            place, sign = places[way], signs[way]
            target = clamp(line + sign * (outer - step))
            own = parts[stream].at[rows_of(stream, target), :]

            @pl.when(place == 0)
            def _():
                reduce_copy(stream, way, step, own).start()

            if step > 1:

                @pl.when((place > 0) & (place <= step - 1))
                def _():
                    reduce_copy(stream, way, step - 1, own).wait_recv()
                    stage = staged[stream].at[way, step - 2]
                    stage[...] = (
                        got[stream][way, step - 2].astype(F32) + own[...].astype(F32)
                    ).astype(BF16)
                    reduce_copy(stream, way, step, stage).start()

    def gather_copy(stream, way, step, origin):
        block = outs[stream].at[half, rows_of(stream, origin), :]
        return remote(
            block, block, gather_send.at[stream, way, step - 1],
            gather_recv.at[stream, way, step - 1], nexts[way],
        )

    def pair_copy(stream, slot, origin):
        block = outs[stream].at[half, rows_of(stream, origin), :]
        return remote(block, block, pair_send.at[stream, slot], pair_recv.at[stream, slot], pair_dev)

    def reduce_final(stream):
        own = parts[stream].at[rows_of(stream, line), :]
        block = outs[stream].at[half, rows_of(stream, line), :]
        for way in range(2):

            @pl.when(places[way] > 0)
            def _():
                reduce_copy(stream, way, last, own).wait_recv()

        up = jnp.where(line > 0, got[stream][0, last - 1].astype(F32), 0.0)
        down = jnp.where(line < last, got[stream][1, last - 1].astype(F32), 0.0)
        block[...] = (own[...].astype(F32) + up + down).astype(BF16)
        for way in range(2):

            @pl.when(places[way] < last)
            def _():
                gather_copy(stream, way, 1, line).start()

        pair_copy(stream, 0, line).start()

    def gather_step(stream, step):
        for way in range(2):
            place, sign = places[way], signs[way]
            origin = clamp(line - sign * step)

            @pl.when(place >= step)
            def _():
                gather_copy(stream, way, step, origin).wait_recv()
                if step < last:

                    @pl.when(place < last)
                    def _():
                        gather_copy(stream, way, step + 1, origin).start()

                pair_copy(stream, 1 + way * last + step - 1, origin).start()

    def drain(stream):
        pair_copy(stream, 0, line).wait()
        for way in range(2):
            place, sign = places[way], signs[way]
            for step in range(1, outer):
                origin = clamp(line - sign * step)

                @pl.when(place <= step - 1)
                def _():
                    reduce_copy(stream, way, step, parts[stream].at[rows_of(stream, 0), :]).wait_send()

                @pl.when((place >= step - 1) & (place < last))
                def _():
                    gather_copy(stream, way, step, origin).wait_send()

                @pl.when(place >= step)
                def _():
                    pair_copy(stream, 1 + way * last + step - 1, origin).wait()

    def near_copy(index):
        return remote(
            part_ref.at[index, 1 - core], near_got.at[index], tp_send.at[index], tp_recv.at[index],
            core_dev,
        )

    def far_copy():
        return remote(far_stage, far_got, tp_send.at[sides], tp_recv.at[sides], side_dev)

    def spread_copy(slot, s, device):
        block = grad_out.at[s, core]
        return remote(block, block, tp_send.at[sides + slot], tp_recv.at[sides + slot], device)

    def input_step(step):
        if step == 0:
            for index in range(sides):
                near_copy(index).start()
        if step == 1:
            for index in range(sides):
                near_copy(index).wait_recv()
            keep_buf[...] = part_ref[side, core].astype(F32) + near_got[side].astype(F32)
            far_stage[...] = (
                part_ref[1 - side, core].astype(F32) + near_got[1 - side].astype(F32)
            ).astype(BF16)
            far_copy().start()
        if step == 2:
            far_copy().wait_recv()
            incoming = keep_buf[...] + far_got[...].astype(F32)
            values = hidden_ref[...].astype(F32)
            scales = scale_ref[...]
            weighted = incoming * gain_ref[...]
            inner_sum = jnp.sum(weighted * values, axis=-1, keepdims=True)
            grads = scales * weighted - values * (scales * scales * scales) * inner_sum * width_scale
            grad_out[side, core] = (middle_ref[...] + grads).astype(BF16)
            spread_copy(1, side, side_dev).start()
            spread_copy(2, side, core_dev).start()
        if step == 3:
            spread_copy(1, side, side_dev).wait_recv()
            spread_copy(3, 1 - side, core_dev).start()
        if step == 4:
            spread_copy(2, side, core_dev).wait_recv()
            spread_copy(3, 1 - side, core_dev).wait_recv()
            for index in range(sides):
                near_copy(index).wait_send()
            far_copy().wait_send()
            spread_copy(1, side, side_dev).wait_send()
            spread_copy(2, side, core_dev).wait_send()
            spread_copy(3, 1 - side, core_dev).wait_send()

    rounds = len(sum_devs)

    def sums_copy(step):
        src = sums_ref if step == 0 else sums_stage.at[step - 1]
        return remote(
            src, sums_got.at[step], sums_send.at[step], sums_recv.at[step], sum_devs[step]
        )

    def sums_step(step):
        if step > 0:
            sums_copy(step - 1).wait_recv()
            before = sums_ref[...] if step == 1 else sums_stage[step - 2]
            total = before + sums_got[step - 1]
            if step == rounds:
                sums_out[...] = total
            else:
                sums_stage[step - 1] = total
        if step < rounds:
            sums_copy(step).start()
        if step == rounds:
            for index in range(rounds):
                sums_copy(index).wait_send()

    extra = []
    for index in range(5):
        extra.append(functools.partial(input_step, index))
    for index in range(rounds + 1):
        extra.append(functools.partial(sums_step, index))
    for turn in range(streams + 1):
        for step in range(1, outer + 1):
            if turn < streams:
                if step < outer:
                    reduce_step(turn, step)
                else:
                    reduce_final(turn)
            if turn > 0 and step < outer:
                gather_step(turn - 1, step)
            if extra:
                extra.pop(0)()
    for step in extra:
        step()
    for stream in range(streams):
        drain(stream)


def finish(parts, part, hidden, scales, gain, middle, sums, outer, sp_n, tp_n):
    streams = len(parts)
    sides = tp_n // 2
    quarter, model = hidden.shape
    last = outer - 1
    rounds = (tp_n - 1).bit_length() + (sp_n - 1).bit_length()
    vmem = pl.BlockSpec(memory_space=pltpu.VMEM)
    chunk = [(2, last, p.shape[0] // outer, p.shape[1]) for p in parts]
    dma = pltpu.SemaphoreType.DMA
    return pl.pallas_call(
        functools.partial(finish_kernel, outer, sides, sp_n, tp_n, streams, 1.0 / model),
        out_shape=[jax.ShapeDtypeStruct((2,) + p.shape, BF16) for p in parts]
        + [
            jax.ShapeDtypeStruct((sides, 2, quarter, model), BF16),
            jax.ShapeDtypeStruct(sums.shape, F32),
        ],
        in_specs=[vmem] * (streams + 6),
        out_specs=[vmem] * (streams + 2),
        scratch_shapes=[pltpu.VMEM(c, BF16) for c in chunk]
        + [pltpu.VMEM(c, BF16) for c in chunk]
        + [
            pltpu.VMEM((sides, quarter, model), BF16),
            pltpu.VMEM((quarter, model), BF16),
            pltpu.VMEM((quarter, model), F32),
            pltpu.VMEM((quarter, model), BF16),
            pltpu.VMEM((rounds,) + sums.shape, F32),
            pltpu.VMEM((rounds,) + sums.shape, F32),
        ]
        + [dma((streams, 2, last))] * 4
        + [dma((streams, 1 + 2 * last))] * 2
        + [dma((sides + 4,))] * 2
        + [dma((rounds,))] * 2,
        compiler_params=pltpu.CompilerParams(
            collective_id=1, has_side_effects=True, vmem_limit_bytes=60 * 1024 * 1024
        ),
        cost_estimate=pl.CostEstimate(flops=10**9, bytes_accessed=10**8, transcendentals=0),
        name="finish",
    )(*parts, part, hidden, scales, gain, middle, sums)


def body(
    hidden,
    segment_ids,
    attn_norm,
    query_proj,
    key_proj,
    value_proj,
    gate_proj,
    output_proj,
    query_norm,
    key_norm,
    ffn_norm,
    ffn_gate,
    ffn_up,
    ffn_down,
    upstream,
):
    rows_dev, model = hidden.shape
    head_width = query_norm.shape[0]
    heads = query_proj.shape[1] // head_width
    groups = key_proj.shape[1] // head_width
    per_group = heads // groups
    group_width = groups * head_width
    sp_n = lax.axis_size("sp")
    tp_n = lax.axis_size("tp")
    outer = sp_n // 2
    sides = tp_n // 2
    quarter = rows_dev // tp_n
    tp_i = lax.axis_index("tp")
    sp_i = lax.axis_index("sp")
    ring_i = sp_i // 2
    pair_i = sp_i % 2
    side_i = tp_i // 2
    core_i = tp_i % 2
    own_first = sp_i * rows_dev
    quarter_first = tp_i * quarter
    scale = 1.0 / math.sqrt(head_width)

    ring_pairs = [(z * 2 + y, ((z + 1) % outer) * 2 + y) for z in range(outer) for y in range(2)]
    pair_pairs = [(i, i ^ 1) for i in range(sp_n)]
    side_pairs = [(i, i ^ 2) for i in range(tp_n)]
    core_pairs = [(i, i ^ 1) for i in range(tp_n)]

    def ring(value):
        return lax.ppermute(value, "sp", ring_pairs)

    def pair(value):
        return lax.ppermute(value, "sp", pair_pairs)

    def side(value):
        return lax.ppermute(value, "tp", side_pairs)

    def core(value):
        return lax.ppermute(value, "tp", core_pairs)

    def gather_sp(block):
        blocks = []
        for k in range(outer):
            blocks.append((block, pair(block)))
            if k < outer - 1:
                block = ring(block)
        return blocks

    def scatter_sp(parts):
        def paired(k):
            return parts[k][0] + pair(parts[k][1].astype(BF16)).astype(F32)

        total = paired(1 % outer)
        for k in range(2, outer + 1):
            total = ring(total.astype(BF16)).astype(F32) + paired(k % outer)
        return total

    first_id = segment_ids[0]
    second_start = jnp.sum((segment_ids == first_id).astype(jnp.int32))
    own_index = own_first + jnp.arange(rows_dev, dtype=jnp.int32)
    own_starts = jnp.where(own_index < second_start, 0, second_start)
    steps_half = jnp.arange(head_width // 2, dtype=F32)
    frequencies = jnp.exp(steps_half * (-2.0 * math.log(THETA) / head_width))
    angles = (own_index - own_starts).astype(F32)[:, None] * frequencies[None, :]
    cosine = jnp.cos(angles)[:, None, :]
    sine = jnp.sin(angles)[:, None, :]

    hidden_full = hidden.astype(F32)
    normed_full, attn_scales = norm_rows(hidden_full, attn_norm)
    normed = normed_full.astype(BF16)
    key_raw = matmul(normed, key_proj).reshape(rows_dev, groups, head_width)
    value_rows = matmul(normed, value_proj).astype(BF16)
    key_normed, key_scales = norm_rows(key_raw, key_norm)
    key_rot = rotary(key_normed, cosine, sine).astype(BF16).reshape(rows_dev, group_width)
    kv_own = jnp.stack([key_rot, value_rows])

    low, high = (outer // 4, 3 * outer // 4) if outer % 4 == 0 else (0, outer)
    reach = high - 1 if low else outer - 1

    def up_pairs(step):
        return [
            (z * 2 + y, (z + 1) * 2 + y)
            for z in range(outer - 1)
            for y in range(2)
            if z + 1 - step >= 0 and (z + 1 - step >= low or z + 1 < high)
        ]

    kv_blocks = []
    travelling = kv_own
    for k in range(reach + 1):
        kv_blocks.append((travelling, pair(travelling)))
        if k < reach:
            travelling = lax.ppermute(travelling, "sp", up_pairs(k + 1))

    query_raw = matmul(normed, query_proj).reshape(rows_dev, heads, head_width)
    gate_raw = matmul(normed, gate_proj)
    query_normed, query_scales = norm_rows(query_raw, query_norm)
    queries = rotary(query_normed, cosine, sine).astype(BF16).reshape(rows_dev, heads * head_width)

    def swap_half(value):
        piece = model // 4
        mine = pair(lax.dynamic_slice_in_dim(value, ((1 - pair_i) * 2 + core_i) * piece, piece, 1))
        near = core(mine)
        return jnp.where(
            core_i == 1, jnp.concatenate([near, mine], 1), jnp.concatenate([mine, near], 1)
        )

    normed_own = lax.dynamic_slice_in_dim(normed, pair_i * (model // 2), model // 2, 1)
    both_normed = jnp.concatenate([normed_own, swap_half(normed)])

    grad_quarter = lax.dynamic_slice_in_dim(upstream, quarter_first, quarter)
    up_blocks = gather_sp(grad_quarter)

    row_start_low = own_starts[0]
    row_start_high = own_starts[-1]

    def block_info(k):
        shards = [(ring_i - k) * 2 + pair_i, (ring_i - k) * 2 + (1 - pair_i)]
        entries = [own_first] + [shard * rows_dev for shard in shards]
        live = []
        full = []
        for shard in shards:
            token = shard * rows_dev
            live.append((shard >= 0) & (shard <= sp_i) & (token + rows_dev - 1 >= row_start_low))
            full.append((token >= row_start_high) & (shard < sp_i))
        return jnp.stack(entries + [v.astype(jnp.int32) for v in live + full]).astype(jnp.int32)

    infos = [block_info(k) for k in range(reach + 1)]
    starts_column = own_starts[:, None]
    starts_row = own_starts[None, :]
    carried = None
    for k in range(reach + 1):
        carried = attn_forward(
            infos[k], starts_column, queries, kv_blocks[k][0], kv_blocks[k][1], carried, scale
        )
    mix_acc, mix_sum = carried
    mixed = mix_acc / mix_sum
    lse = jnp.log2(mix_sum.reshape(rows_dev, heads, head_width)[:, :, 0])
    lse_rows = lse.T.reshape(groups, per_group, rows_dev)
    gate_sig = jax.nn.sigmoid(gate_raw)
    gated = (mixed * gate_sig).astype(BF16)
    gated_other = pair(gated)

    def scatter_tp(part):
        part = part.reshape(sides, 2, quarter, model)
        keep = lax.dynamic_index_in_dim(part, core_i, 1, keepdims=False)
        send = lax.dynamic_index_in_dim(part, 1 - core_i, 1, keepdims=False)
        keep = keep + core(send.astype(BF16)).astype(F32)
        mine = lax.dynamic_index_in_dim(keep, side_i, 0, keepdims=False)
        other = lax.dynamic_index_in_dim(keep, 1 - side_i, 0, keepdims=False)
        return mine + side(other.astype(BF16)).astype(F32)

    def gather_tp(block):
        far = side(block)
        swap_side = side_i == 1
        two = jnp.where(swap_side, jnp.stack([far, block]), jnp.stack([block, far]))
        near = core(two)
        swap_core = core_i == 1
        full = jnp.where(
            swap_core, jnp.stack([near, two], axis=1), jnp.stack([two, near], axis=1)
        )
        return full.reshape((rows_dev,) + block.shape[1:])

    fused = outer * quarter <= 512 and outer > 1 and tp_n == 4
    if fused:
        middle, grad_middle_quarter, ffn_gain_sum, branch, inner_rows, *ffn_parts = middle_layer(
            gated,
            output_proj,
            lax.dynamic_slice_in_dim(hidden, quarter_first, quarter),
            ffn_norm[None, :],
            ffn_gate,
            ffn_up,
            ffn_down,
            [block for both in up_blocks for block in both],
            outer,
            sides,
        )
        grad_branch = branch.reshape(rows_dev, model)
        ffn_gain_sum = ffn_gain_sum[0]
        inner_list = [
            inner_rows[k * 2 * quarter : (k + 1) * 2 * quarter] for k in range(outer)
        ]
    else:
        attn_quarter = scatter_tp(matmul(gated, output_proj))
        hidden_quarter = lax.dynamic_slice_in_dim(hidden, quarter_first, quarter).astype(F32)
        middle = hidden_quarter + attn_quarter
        normed_two_full, ffn_scales = norm_rows(middle, ffn_norm)
        normed_two = normed_two_full.astype(BF16)

        two_blocks = gather_sp(normed_two)
        rows_list, up_list, inner_list, gate_list, grad_up_list = [None] * outer, [None] * outer, [None] * outer, [None] * outer, [None] * outer
        grad_parts = [None] * outer
        for k in list(range(1, outer)) + [0]:
            rows_k = jnp.concatenate(two_blocks[k])
            up_k = jnp.concatenate(up_blocks[k])
            gate_vals = matmul(rows_k, ffn_gate)
            up_vals = matmul(rows_k, ffn_up)
            sig = jax.nn.sigmoid(gate_vals)
            grad_inner = times_transpose(up_k, ffn_down)
            grad_gate = (grad_inner * up_vals * (sig * (1.0 + gate_vals * (1.0 - sig)))).astype(BF16)
            grad_up = (grad_inner * (gate_vals * sig)).astype(BF16)
            inner = (gate_vals * sig * up_vals).astype(BF16)
            grad_parts[k] = (
                times_transpose(grad_gate, ffn_gate) + times_transpose(grad_up, ffn_up)
            ).reshape(2, quarter, model)
            rows_list[k], up_list[k], inner_list[k] = rows_k, up_k, inner
            gate_list[k], grad_up_list[k] = grad_gate, grad_up
        grad_two = scatter_sp(grad_parts)

        norm_grad_two, ffn_gain_terms = norm_back(middle, ffn_scales, ffn_norm, grad_two)
        grad_middle_quarter = grad_quarter.astype(F32) + norm_grad_two
        grad_branch = gather_tp(grad_middle_quarter.astype(BF16))
        ffn_gain_sum = jnp.sum(ffn_gain_terms, axis=0)

    mlp_parts = [matmul(inner_list[k], ffn_down).reshape(2, quarter, model) for k in range(outer)]
    mlp_quarter = scatter_sp(mlp_parts)
    layer_out = gather_tp((middle + mlp_quarter).astype(BF16))

    def reduce_tp(part):
        half = part.shape[0] // 2
        keep = lax.dynamic_slice_in_dim(part, core_i * half, half)
        send = lax.dynamic_slice_in_dim(part, (1 - core_i) * half, half)
        keep = (keep.astype(F32) + core(send.astype(BF16)).astype(F32)).astype(BF16)
        keep = (keep.astype(F32) + side(keep).astype(F32)).astype(BF16)
        near = core(keep)
        total = jnp.where(
            core_i == 1, jnp.concatenate([near, keep]), jnp.concatenate([keep, near])
        )
        return total.astype(F32)

    if not fused:
        rows_all = jnp.concatenate(rows_list)
        up_all = jnp.concatenate(up_list)
        inner_all = jnp.concatenate(inner_list)
        gate_all = jnp.concatenate(gate_list)
        grad_up_all = jnp.concatenate(grad_up_list)
        ffn_parts = [
            outer_sum(rows_all, gate_all),
            outer_sum(rows_all, grad_up_all),
            outer_sum(inner_all, up_all),
        ]
    ffn_gate_grad, ffn_up_grad, ffn_down_grad = [reduce_tp(part) for part in ffn_parts]

    branch_other = swap_half(grad_branch)
    branch_own = lax.dynamic_slice_in_dim(grad_branch, pair_i * (model // 2), model // 2, 1)
    output_half = outer_sum(
        jnp.concatenate([gated, gated_other]), jnp.concatenate([branch_own, branch_other])
    )
    grad_gated = times_transpose(grad_branch, output_proj)
    grad_mixed = (grad_gated * gate_sig).astype(BF16)
    grad_gate_raw = (grad_gated * mixed * (gate_sig * (1.0 - gate_sig))).astype(BF16)
    gate_half = outer_sum(both_normed, jnp.concatenate([grad_gate_raw, pair(grad_gate_raw)]))
    deltas = jnp.sum(
        (grad_mixed.astype(F32) * mixed).reshape(rows_dev, heads, head_width), axis=-1
    )
    delta_rows = deltas.T.reshape(groups, per_group, rows_dev)

    def down_pairs(step):
        return [(b, a) for a, b in up_pairs(step)]

    query_acc = None
    travelling = None
    for k in list(range(reach, -1, -1)):
        query_acc, grad_a, grad_b = attn_backward(
            infos[k], starts_row, lse_rows, delta_rows, queries, grad_mixed,
            kv_blocks[k][0], kv_blocks[k][1], query_acc, k == 0, scale,
        )
        total = grad_a.astype(F32) + pair(grad_b).astype(F32)
        if travelling is not None:
            total = total + travelling.astype(F32)
        if k > 0:
            travelling = lax.ppermute(total.astype(BF16), "sp", down_pairs(k))
    grad_key_rot = total[0].reshape(rows_dev, groups, head_width)
    grad_value_low = total[1].astype(BF16)
    grad_query_rot = (query_acc * scale).reshape(rows_dev, heads, head_width)
    grad_query_raw, query_gain_terms = norm_back(
        query_raw, query_scales, query_norm, rotary_back(grad_query_rot, cosine, sine)
    )
    grad_key_raw, key_gain_terms = norm_back(
        key_raw, key_scales, key_norm, rotary_back(grad_key_rot, cosine, sine)
    )
    grad_query_low = grad_query_raw.reshape(rows_dev, heads * head_width).astype(BF16)
    grad_key_low = grad_key_raw.reshape(rows_dev, group_width).astype(BF16)
    grad_kv_low = jnp.concatenate([grad_key_low, grad_value_low], axis=1)

    both_queries = jnp.concatenate([grad_query_low, pair(grad_query_low)])
    both_kv = jnp.concatenate([grad_kv_low, pair(grad_kv_low)])
    parts = [
        output_half.astype(BF16),
        gate_half.astype(BF16),
        outer_sum(both_normed, both_queries).astype(BF16),
        outer_sum(both_normed, both_kv).astype(BF16),
    ]

    grad_normed_part = (
        times_transpose(grad_query_low, query_proj)
        + times_transpose(grad_key_low, key_proj)
        + times_transpose(grad_value_low, value_proj)
        + times_transpose(grad_gate_raw, gate_proj)
    )
    gains = jnp.concatenate(
        [
            jnp.sum(grad_normed_part * hidden_full * attn_scales, axis=0),
            ffn_gain_sum,
            jnp.sum(query_gain_terms, axis=(0, 1)),
            jnp.sum(key_gain_terms, axis=(0, 1)),
        ]
    )
    gains_at = 2 * model + 2 * head_width
    gains = jnp.pad(gains, (0, -gains_at % 1024)).reshape(-1, 128)
    scales_quarter = lax.dynamic_slice_in_dim(attn_scales, quarter_first, quarter)
    finished = finish(
        parts,
        grad_normed_part.astype(BF16).reshape(sides, 2, quarter, model),
        lax.dynamic_slice_in_dim(hidden, quarter_first, quarter),
        scales_quarter,
        attn_norm[None, :],
        grad_middle_quarter,
        gains,
        outer,
        sp_n,
        tp_n,
    )
    output_all, gate_all_w, query_all, kv_all, input_all, gains = finished
    output_grad = jnp.concatenate([output_all[0], output_all[1]], axis=1).astype(F32)
    gate_grad = gate_all_w.reshape(model, heads * head_width).astype(F32)
    query_grad = query_all.reshape(model, heads * head_width).astype(F32)
    kv_all = kv_all.reshape(model, 2 * group_width)
    key_grad = kv_all[:, :group_width].astype(F32)
    value_grad = kv_all[:, group_width:].astype(F32)
    hidden_grad = input_all.reshape(rows_dev, model).astype(F32)
    gains = gains.reshape(-1)
    return (
        layer_out,
        hidden_grad,
        gains[:model],
        query_grad,
        key_grad,
        value_grad,
        gate_grad,
        output_grad,
        gains[2 * model : 2 * model + head_width],
        gains[2 * model + head_width : gains_at],
        gains[model : 2 * model],
        ffn_gate_grad,
        ffn_up_grad,
        ffn_down_grad,
    )


def solution(mesh):
    placed = (
        P("sp", None),
        P(),
        P(),
        P(None, "tp"),
        P(None, "tp"),
        P(None, "tp"),
        P(None, "tp"),
        P("tp", None),
        P(),
        P(),
        P(),
        P(None, "sp"),
        P(None, "sp"),
        P("sp", None),
        P("sp", None),
    )
    return jax.shard_map(
        body,
        mesh=mesh,
        in_specs=placed,
        out_specs=(
            P("sp", None),
            P("sp", None),
            P(),
            P(None, "tp"),
            P(None, "tp"),
            P(None, "tp"),
            P(None, "tp"),
            P("tp", None),
            P(),
            P(),
            P(),
            P(None, "sp"),
            P(None, "sp"),
            P("sp", None),
        ),
        check_vma=False,
    )
```

```python
import functools
import math

import jax
import jax.numpy as jnp
from jax import lax
from jax.experimental import pallas as pl
from jax.experimental.pallas import tpu as pltpu
from jax.sharding import PartitionSpec as P

EPSILON = 1e-06
THETA = 1000000.0
LOG2E = 1.4426950408889634
F32 = jnp.float32
BF16 = jnp.bfloat16


def norm_scales(values):
    return lax.rsqrt(jnp.mean(values * values, axis=-1, keepdims=True) + EPSILON)


def norm_rows(values, gain):
    scales = norm_scales(values)
    return (values * scales * gain, scales)


def norm_back(values, scales, gain, incoming):
    weighted = incoming * gain
    inner_sum = jnp.sum(weighted * values, axis=-1, keepdims=True)
    grad_values = (
        scales * weighted - values * (scales * scales * scales) * inner_sum / values.shape[-1]
    )
    return (grad_values, incoming * values * scales)


def rotary(values, cosine, sine):
    half_width = values.shape[-1] // 2
    front_half = values[..., :half_width]
    back_half = values[..., half_width:]
    return jnp.concatenate(
        [front_half * cosine - back_half * sine, back_half * cosine + front_half * sine], axis=-1
    )


def rotary_back(grads, cosine, sine):
    half_width = grads.shape[-1] // 2
    front_half = grads[..., :half_width]
    back_half = grads[..., half_width:]
    return jnp.concatenate(
        [front_half * cosine + back_half * sine, back_half * cosine - front_half * sine], axis=-1
    )


def matmul(left, right):
    return jnp.dot(left, right, preferred_element_type=F32)


def outer_sum(left, right):
    return lax.dot_general(left, right, (((0,), (0,)), ((), ())), preferred_element_type=F32)


def times_transpose(left, right):
    return lax.dot_general(left, right, (((1,), (1,)), ((), ())), preferred_element_type=F32)


def attn_forward_kernel(first, diagonal, scale, info, starts, queries, kv_a, kv_b, *rest):
    if first:
        acc_out, sum_out = rest
    else:
        acc_in, sum_in, acc_out, sum_out = rest
    rows = queries.shape[0]
    keys_n = kv_a.shape[1]
    per_group = queries.shape[1] // kv_a.shape[2]
    width = kv_a.shape[2]
    if first:
        acc_out[...] = jnp.zeros_like(acc_out)
        sum_out[...] = jnp.zeros_like(sum_out)
    else:
        acc_out[...] = acc_in[...]
        sum_out[...] = sum_in[...]
    own_first = info[0]
    for slot, block in enumerate((kv_a, kv_b)):
        key_first = info[1 + slot]
        live = info[3 + slot] > 0

        def work(masked, causal):
            ones = jnp.ones((keys_n, width), BF16)
            values = jnp.concatenate([block[1], ones], axis=1)
            keys = block[0]
            if masked:
                key_index = key_first + lax.broadcasted_iota(jnp.int32, (rows, keys_n), 1)
                allowed = key_index >= starts[...]
                if causal:
                    row_index = own_first + lax.broadcasted_iota(jnp.int32, (rows, keys_n), 0)
                    allowed = allowed & (key_index <= row_index)
            for head in range(per_group):
                cols = slice(head * width, (head + 1) * width)
                scores = times_transpose(queries[:, cols], keys)
                weights = jnp.exp2(scores * (scale * LOG2E))
                if masked:
                    weights = jnp.where(allowed, weights, 0.0)
                both = matmul(weights.astype(BF16), values)
                acc_out[:, cols] += both[:, :width]
                sum_out[:, cols] += both[:, width:]

        if diagonal and slot == 0:
            work(True, True)
        else:
            full = info[5 + slot] > 0
            pl.when(live & full)(functools.partial(work, False, False))
            pl.when(live & jnp.logical_not(full))(functools.partial(work, True, False))


def attn_forward(info, starts, queries, kv_a, kv_b, carried, scale):
    rows, all_width = queries.shape
    width = 128
    groups = kv_a.shape[2] // width
    group_width = all_width // groups
    keys_n = kv_a.shape[1]
    first = carried is None
    spec_q = pl.BlockSpec((rows, group_width), lambda g, info: (0, g))
    spec_kv = pl.BlockSpec((2, keys_n, width), lambda g, info: (0, 0, g))
    specs = [pl.BlockSpec((rows, 1), lambda g, info: (0, 0)), spec_q, spec_kv, spec_kv]
    operands = [starts, queries, kv_a, kv_b]
    if not first:
        specs += [spec_q, spec_q]
        operands += list(carried)
    return pl.pallas_call(
        functools.partial(attn_forward_kernel, first, first, scale),
        grid_spec=pltpu.PrefetchScalarGridSpec(
            num_scalar_prefetch=1,
            grid=(groups,),
            in_specs=specs,
            out_specs=[spec_q, spec_q],
        ),
        out_shape=[jax.ShapeDtypeStruct((rows, all_width), F32)] * 2,
        compiler_params=pltpu.CompilerParams(dimension_semantics=("arbitrary",)),
        cost_estimate=pl.CostEstimate(
            flops=16 * rows * keys_n * all_width,
            transcendentals=2 * rows * keys_n * all_width // width,
            bytes_accessed=8 * rows * all_width,
        ),
        name="attn_forward",
    )(info, *operands)


def attn_backward_kernel(first, diagonal, scale, info, starts, lse, deltas, queries, grads, kv_a, kv_b, *rest):
    if first:
        grad_q, grad_a, grad_b = rest
    else:
        grad_in, grad_q, grad_a, grad_b = rest
    rows = queries.shape[0]
    keys_n = kv_a.shape[1]
    width = kv_a.shape[2]
    per_group = queries.shape[1] // width
    if first:
        grad_q[...] = jnp.zeros_like(grad_q)
    else:
        grad_q[...] = grad_in[...]
    own_first = info[0]
    for slot, (block, out) in enumerate(((kv_a, grad_a), (kv_b, grad_b))):
        key_first = info[1 + slot]
        live = info[3 + slot] > 0

        def work(masked, causal):
            keys = block[0]
            values = block[1]
            keys_t = keys.T
            if masked:
                key_index = key_first + lax.broadcasted_iota(jnp.int32, (keys_n, rows), 0)
                allowed = key_index >= starts[...]
                if causal:
                    row_index = own_first + lax.broadcasted_iota(jnp.int32, (keys_n, rows), 1)
                    allowed = allowed & (key_index <= row_index)
            total_k = jnp.zeros((keys_n, width), F32)
            total_v = jnp.zeros((keys_n, width), F32)
            for head in range(per_group):
                cols = slice(head * width, (head + 1) * width)
                q_head = queries[:, cols]
                g_head = grads[:, cols]
                scores = times_transpose(keys, q_head)
                probs = jnp.exp2(scores * (scale * LOG2E) - lse[0, head : head + 1, :])
                if masked:
                    probs = jnp.where(allowed, probs, 0.0)
                grad_probs = times_transpose(values, g_head)
                grad_scores = (probs * (grad_probs - deltas[0, head : head + 1, :])).astype(BF16)
                total_v += matmul(probs.astype(BF16), g_head)
                total_k += matmul(grad_scores, q_head)
                grad_q[:, cols] += matmul(keys_t, grad_scores).T
            out[0] = (total_k * scale).astype(BF16)
            out[1] = total_v.astype(BF16)

        if diagonal and slot == 0:
            work(True, True)
        else:
            full = info[5 + slot] > 0
            pl.when(live & full)(functools.partial(work, False, False))
            pl.when(live & jnp.logical_not(full))(functools.partial(work, True, False))

            @pl.when(jnp.logical_not(live))
            def _():
                out[...] = jnp.zeros_like(out)


def attn_backward(info, starts_row, lse, deltas, queries, grads, kv_a, kv_b, carried, diagonal, scale):
    rows, all_width = queries.shape
    width = 128
    groups = kv_a.shape[2] // width
    group_width = all_width // groups
    per_group = group_width // width
    keys_n = kv_a.shape[1]
    first = carried is None
    spec_q = pl.BlockSpec((rows, group_width), lambda g, info: (0, g))
    spec_kv = pl.BlockSpec((2, keys_n, width), lambda g, info: (0, 0, g))
    spec_row = pl.BlockSpec((1, per_group, rows), lambda g, info: (g, 0, 0))
    specs = [
        pl.BlockSpec((1, rows), lambda g, info: (0, 0)),
        spec_row,
        spec_row,
        spec_q,
        spec_q,
        spec_kv,
        spec_kv,
    ]
    operands = [starts_row, lse, deltas, queries, grads, kv_a, kv_b]
    if not first:
        specs.append(spec_q)
        operands.append(carried)
    return pl.pallas_call(
        functools.partial(attn_backward_kernel, first, diagonal, scale),
        grid_spec=pltpu.PrefetchScalarGridSpec(
            num_scalar_prefetch=1,
            grid=(groups,),
            in_specs=specs,
            out_specs=[spec_q, spec_kv, spec_kv],
        ),
        out_shape=[
            jax.ShapeDtypeStruct((rows, all_width), F32),
            jax.ShapeDtypeStruct(kv_a.shape, BF16),
            jax.ShapeDtypeStruct(kv_a.shape, BF16),
        ],
        compiler_params=pltpu.CompilerParams(dimension_semantics=("arbitrary",)),
        cost_estimate=pl.CostEstimate(
            flops=20 * rows * keys_n * all_width,
            transcendentals=2 * rows * keys_n * all_width // width,
            bytes_accessed=8 * rows * all_width,
        ),
        name="attn_backward",
    )(info, *operands)


def middle_kernel(outer, *refs):
    MESH = pl.DeviceIdType.MESH
    blocks = 2 * outer
    (gated, out_proj, hidden_ref, gain_ref, gate_in, up_in, down_in) = refs[:7]
    ups_in = refs[7 : 7 + blocks]
    (middle_out, grad_out, gain_out, branch, inner_out, dw_both, dw_down) = refs[
        7 + blocks : 14 + blocks
    ]
    (
        w_gate, w_up, w_down, ups, rows, grad_inner, inner, grad_gate, grad_up,
        near_stage, near_got, far_stage, far_got, far_keep, own_keep,
        keep, y_stage, y_got, z_stage, z_got,
        load_sem, store_sem, tp_send, tp_recv, zs, zr, ys, yr, rys, ryr, rzs, rzr,
    ) = refs[14 + blocks :]
    stage_gate, stage_up, stage_down = w_gate, w_up, w_down
    quarter, model = hidden_ref.shape
    group = 2 * quarter
    chunk = model // outer
    last = outer - 1

    sp_i = lax.axis_index("sp")
    tp_i = lax.axis_index("tp")
    line = sp_i // 2
    half = sp_i % 2
    side = tp_i // 2
    core = tp_i % 2

    def sp_at(z, y):
        return (tp_i, z * 2 + y)

    pair_dev = sp_at(line, 1 - half)
    core_dev = (side * 2 + (1 - core), sp_i)
    side_dev = ((1 - side) * 2 + core, sp_i)
    nexts = (sp_at(jnp.minimum(line + 1, last), half), sp_at(jnp.maximum(line - 1, 0), half))

    loads = [
        pltpu.make_async_copy(src, dst, load_sem.at[index])
        for index, (src, dst) in enumerate(
            [(down_in, w_down)]
            + [(ups_in[b], ups.at[pl.ds(b * quarter, quarter), :]) for b in range(blocks)]
            + [(gate_in, w_gate), (up_in, w_up)]
        )
    ]
    for load in loads:
        load.start()

    barrier = pltpu.get_barrier_semaphore()
    greeted = [
        sp_at((line + 1) % outer, half), sp_at((line + outer - 1) % outer, half),
        pair_dev, core_dev, side_dev,
    ]
    for device in greeted:
        pl.semaphore_signal(barrier, inc=1, device_id=device, device_id_type=MESH)
    pl.semaphore_wait(barrier, len(greeted))

    def remote(src, dst, send, recv, device):
        return pltpu.make_async_remote_copy(
            src_ref=src, dst_ref=dst, send_sem=send, recv_sem=recv,
            device_id=device, device_id_type=MESH,
        )

    def aligned(index, count):
        return pl.ds(pl.multiple_of(index * count, count), count)

    def near_copy(j):
        return remote(near_stage.at[j], near_got.at[j], tp_send.at[j], tp_recv.at[j], core_dev)

    def far_copy():
        return remote(far_stage, far_got, tp_send.at[2], tp_recv.at[2], side_dev)

    def projected(s, c):
        return matmul(gated[aligned(s * 2 + c, quarter), :], out_proj[...])

    near_stage[0] = projected(1 - side, 1 - core).astype(BF16)
    near_copy(0).start()
    near_stage[1] = projected(side, 1 - core).astype(BF16)
    near_copy(1).start()
    far_keep[...] = projected(1 - side, core)
    near_copy(0).wait_recv()
    far_stage[...] = (far_keep[...] + near_got[0].astype(F32)).astype(BF16)
    far_copy().start()
    own_keep[...] = projected(side, core)

    for load in loads[: 1 + blocks]:
        load.wait()

    def grad_inner_of(k, carry):
        at = aligned(k, group)
        grad_inner[at, :] = times_transpose(ups[at, :], w_down[...])
        return carry

    lax.fori_loop(0, outer, grad_inner_of, 0)
    near_copy(1).wait_recv()
    far_copy().wait_recv()
    middle = hidden_ref[...].astype(F32) + (
        own_keep[...] + near_got[1].astype(F32) + far_got[...].astype(F32)
    )
    middle_out[...] = middle
    rows[0:quarter, :] = (middle * norm_scales(middle) * gain_ref[...]).astype(BF16)

    def entry(k, j):
        return pl.ds(pl.multiple_of((k * 2 + j) * quarter, quarter), quarter)

    def wrap(k):
        return (k + outer) % outer

    def z_copy(way, k):
        to = wrap(k + 1 - 2 * way)
        return remote(
            rows.at[entry(k, 0), :], rows.at[entry(to, 0), :], zs.at[way, k], zr.at[to], nexts[way]
        )

    def z_arrived(k):
        return remote(
            rows.at[entry(k, 0), :], rows.at[entry(k, 0), :], zs.at[0, k], zr.at[k], nexts[0]
        )

    def y_copy(k):
        return remote(
            rows.at[entry(k, 0), :], rows.at[entry(k, 1), :], ys.at[k], yr.at[k], pair_dev
        )

    short = jnp.minimum(line, last - line)

    def delta_of(i):
        near = jnp.where(i % 2 == 1, -((i + 1) // 2), (i + 1) // 2)
        far = jnp.where(line < last - line, i - short, short - i)
        return jnp.where(i <= 2 * short, near, far)

    def slot_of(delta):
        return jnp.where(delta <= 0, -delta, outer - delta)

    for way, exists in ((0, line < last), (1, line > 0)):
        pl.when(exists)(z_copy(way, 0).start)
    y_copy(0).start()

    def goes_on(delta):
        return ((delta < 0) & (line < last), (delta > 0) & (line > 0))

    def forward(i):
        delta = delta_of(i)
        k = slot_of(delta)
        z_arrived(k).wait_recv()
        for way, exists in enumerate(goes_on(delta)):
            pl.when(exists)(z_copy(way, k).start)
        y_copy(k).start()

    for load in loads[1 + blocks :]:
        load.wait()
    forward(1)

    def turn_forward(i, carry):
        @pl.when(i + 2 < outer)
        def _():
            forward(i + 2)

        k = slot_of(delta_of(i))
        y_copy(k).wait_recv()
        at = aligned(k, group)
        rows_k = rows[at, :]
        gate_vals = matmul(rows_k, w_gate[...])
        up_vals = matmul(rows_k, w_up[...])
        incoming = grad_inner[at, :]
        sig = jax.nn.sigmoid(gate_vals)
        silu = gate_vals * sig
        grad_gate[at, :] = (incoming * up_vals * (sig * (1.0 + gate_vals * (1.0 - sig)))).astype(BF16)
        grad_up[at, :] = (incoming * silu).astype(BF16)
        inner[at, :] = (silu * up_vals).astype(BF16)
        return carry

    lax.fori_loop(0, outer, turn_forward, 0)
    inner_store = pltpu.make_async_copy(inner, inner_out, store_sem.at[0])
    inner_store.start()

    def y_sum(k):
        at = aligned(k, quarter)
        return remote(y_stage.at[at, :], y_got.at[at, :], rys.at[k], ryr.at[k], pair_dev)

    def turn_parts(step, carry):
        k = slot_of(delta_of(last - step))
        at = aligned(k, group)
        part = times_transpose(grad_gate[at, :], w_gate[...]) + times_transpose(
            grad_up[at, :], w_up[...]
        )
        y_stage[aligned(k, quarter), :] = part[quarter:].astype(BF16)
        y_sum(k).start()
        keep[aligned(k, quarter), :] = part[:quarter]
        return carry

    lax.fori_loop(0, outer, turn_parts, 0)

    def z_sum(way, k):
        to = wrap(k + 1 - 2 * way)
        return remote(
            z_stage.at[aligned(k, quarter), :],
            z_got.at[pl.ds(pl.multiple_of((way * outer + to) * quarter, quarter), quarter), :],
            rzs.at[k], rzr.at[way, to], nexts[way],
        )

    def z_got_at(way, k):
        return z_got[pl.ds(pl.multiple_of((way * outer + k) * quarter, quarter), quarter), :]

    def z_sum_arrived(way, k):
        return remote(
            z_stage.at[aligned(k, quarter), :], z_stage.at[aligned(k, quarter), :],
            rzs.at[k], rzr.at[way, k], nexts[way],
        )

    def gate_up_stores(c):
        at = aligned(c, chunk)
        return (
            pltpu.make_async_copy(stage_gate.at[at, :], dw_both.at[0, at, :], store_sem.at[1 + 2 * c]),
            pltpu.make_async_copy(stage_up.at[at, :], dw_both.at[1, at, :], store_sem.at[2 + 2 * c]),
        )

    def weight_chunk(c):
        at = aligned(c, chunk)
        some = rows[:, at]
        stage_gate[at, :] = outer_sum(some, grad_gate[...]).astype(BF16)
        stage_up[at, :] = outer_sum(some, grad_up[...]).astype(BF16)
        for store in gate_up_stores(c):
            store.start()

    def turn_sums(step, carry):
        weight_chunk(step)
        delta = delta_of(last - step)
        k = slot_of(delta)
        at = aligned(k, quarter)
        y_sum(k).wait_recv()
        own = keep[at, :] + y_got[at, :].astype(F32)
        for way, (here, before) in enumerate(
            ((delta > 0, line > 0), (delta < 0, line < last))
        ):

            @pl.when(here & before)
            def _():
                z_sum_arrived(way, k).wait_recv()
                z_stage[at, :] = (own + z_got_at(way, k).astype(F32)).astype(BF16)

            @pl.when(here & jnp.logical_not(before))
            def _():
                z_stage[at, :] = own.astype(BF16)

            pl.when(here)(z_sum(way, k).start)
        return carry

    lax.fori_loop(0, last, turn_sums, 0)
    weight_chunk(last)
    y_sum(0).wait_recv()
    for way, exists in ((0, line > 0), (1, line < last)):
        pl.when(exists)(z_sum_arrived(way, 0).wait_recv)
    below = jnp.where(line > 0, z_got_at(0, 0).astype(F32), 0.0)
    above = jnp.where(line < last, z_got_at(1, 0).astype(F32), 0.0)
    grad_two = keep[0:quarter, :] + y_got[0:quarter, :].astype(F32) + below + above

    values = middle_out[...]
    back, gain_terms = norm_back(values, norm_scales(values), gain_ref[...], grad_two)
    grads = ups[0:quarter, :].astype(F32) + back
    branch[side, core] = grads.astype(BF16)

    def spread_copy(slot, s, device):
        block = branch.at[s, core]
        return remote(block, block, tp_send.at[3 + slot], tp_recv.at[3 + slot], device)

    spread_copy(0, side, side_dev).start()
    spread_copy(1, side, core_dev).start()
    grad_out[...] = grads
    gain_out[...] = jnp.sum(gain_terms, axis=0, keepdims=True)

    def down_store(c):
        at = aligned(c, chunk)
        return pltpu.make_async_copy(
            stage_down.at[:, at], dw_down.at[:, at], store_sem.at[1 + 2 * outer + c]
        )

    def turn_down(c, carry):
        at = aligned(c, chunk)
        stage_down[:, at] = outer_sum(inner[...], ups[:, at]).astype(BF16)
        down_store(c).start()
        return carry

    lax.fori_loop(0, outer, turn_down, 0)
    spread_copy(0, side, side_dev).wait_recv()
    spread_copy(2, 1 - side, core_dev).start()
    spread_copy(1, side, core_dev).wait_recv()

    inner_store.wait()
    near_copy(0).wait_send()
    near_copy(1).wait_send()
    far_copy().wait_send()
    for way, exists in ((0, line < last), (1, line > 0)):
        pl.when(exists)(z_copy(way, 0).wait_send)

    def turn_drain(i, carry):
        delta = delta_of(i)
        k = slot_of(delta)
        y_copy(k).wait_send()
        y_sum(k).wait_send()
        for store in gate_up_stores(i):
            store.wait()
        down_store(i).wait()
        for way, exists in enumerate(goes_on(delta)):
            pl.when(exists)(z_copy(way, k).wait_send)
        pl.when(delta != 0)(z_sum(0, k).wait_send)
        return carry

    lax.fori_loop(0, outer, turn_drain, 0)
    spread_copy(0, side, side_dev).wait_send()
    spread_copy(1, side, core_dev).wait_send()
    spread_copy(2, 1 - side, core_dev).wait()


def middle_layer(gated, out_proj, hidden, gain, w_gate, w_up, w_down, ups, outer, sides):
    quarter, model = hidden.shape
    units = w_down.shape[0]
    rows_n = 2 * outer * quarter
    vmem = pl.BlockSpec(memory_space=pltpu.VMEM)
    anywhere = pl.BlockSpec(memory_space=pl.ANY)
    dma = pltpu.SemaphoreType.DMA
    line_rows = outer * quarter
    return pl.pallas_call(
        functools.partial(middle_kernel, outer),
        out_shape=[
            jax.ShapeDtypeStruct((quarter, model), F32),
            jax.ShapeDtypeStruct((quarter, model), F32),
            jax.ShapeDtypeStruct((1, model), F32),
            jax.ShapeDtypeStruct((sides, 2, quarter, model), BF16),
            jax.ShapeDtypeStruct((rows_n, units), BF16),
            jax.ShapeDtypeStruct((2, model, units), BF16),
            jax.ShapeDtypeStruct((units, model), BF16),
        ],
        in_specs=[vmem] * 4 + [anywhere] * (3 + len(ups)),
        out_specs=[vmem] * 4 + [anywhere] * 3,
        scratch_shapes=[
            pltpu.VMEM((model, units), BF16),
            pltpu.VMEM((model, units), BF16),
            pltpu.VMEM((units, model), BF16),
            pltpu.VMEM((rows_n, model), BF16),
            pltpu.VMEM((rows_n, model), BF16),
            pltpu.VMEM((rows_n, units), F32),
            pltpu.VMEM((rows_n, units), BF16),
            pltpu.VMEM((rows_n, units), BF16),
            pltpu.VMEM((rows_n, units), BF16),
            pltpu.VMEM((2, quarter, model), BF16),
            pltpu.VMEM((2, quarter, model), BF16),
            pltpu.VMEM((quarter, model), BF16),
            pltpu.VMEM((quarter, model), BF16),
            pltpu.VMEM((quarter, model), F32),
            pltpu.VMEM((quarter, model), F32),
            pltpu.VMEM((line_rows, model), F32),
            pltpu.VMEM((line_rows, model), BF16),
            pltpu.VMEM((line_rows, model), BF16),
            pltpu.VMEM((line_rows, model), BF16),
            pltpu.VMEM((2 * line_rows, model), BF16),
            dma((3 + len(ups),)),
            dma((1 + 3 * outer,)),
            dma((6,)),
            dma((6,)),
            dma((2, outer)),
            dma((outer,)),
            dma((outer,)),
            dma((outer,)),
            dma((outer,)),
            dma((outer,)),
            dma((outer,)),
            dma((2, outer)),
        ],
        compiler_params=pltpu.CompilerParams(
            collective_id=2, has_side_effects=True, vmem_limit_bytes=58 * 1024 * 1024
        ),
        cost_estimate=pl.CostEstimate(flops=3 * 10**10, bytes_accessed=4 * 10**7, transcendentals=0),
        name="middle",
    )(gated, out_proj, hidden, gain, w_gate, w_up, w_down, *ups)


def finish_kernel(
    outer, sides, sp_n, tp_n, streams, width_scale,
    *refs,
):
    MESH = pl.DeviceIdType.MESH
    parts = refs[:streams]
    (part_ref, hidden_ref, scale_ref, gain_ref, middle_ref, sums_ref) = refs[streams : streams + 6]
    outs = refs[streams + 6 : 2 * streams + 6]
    grad_out, sums_out = refs[2 * streams + 6 : 2 * streams + 8]
    rest = refs[2 * streams + 8 :]
    got = rest[:streams]
    staged = rest[streams : 2 * streams]
    (near_got, far_got, keep_buf, far_stage, sums_got, sums_stage) = rest[2 * streams : 2 * streams + 6]
    (reduce_send, reduce_recv, gather_send, gather_recv, pair_send, pair_recv) = rest[
        2 * streams + 6 : 2 * streams + 12
    ]
    tp_send, tp_recv, sums_send, sums_recv = rest[2 * streams + 12 :]

    sp_i = lax.axis_index("sp")
    tp_i = lax.axis_index("tp")
    line = sp_i // 2
    half = sp_i % 2
    side = tp_i // 2
    core = tp_i % 2
    last = outer - 1

    def sp_at(z, y):
        return (tp_i, z * 2 + y)

    pair_dev = sp_at(line, 1 - half)
    core_dev = (side * 2 + (1 - core), sp_i)
    side_dev = ((1 - side) * 2 + core, sp_i)

    tp_bits = []
    bit = 1
    while bit < tp_n:
        tp_bits.append(bit)
        bit *= 2
    sp_bits = []
    bit = 1
    while bit < sp_n:
        sp_bits.append(bit)
        bit *= 2

    def flip(value, bit):
        return value + bit - 2 * bit * ((value // bit) % 2)

    sum_devs = [(flip(tp_i, b), sp_i) for b in tp_bits] + [(tp_i, flip(sp_i, b)) for b in sp_bits]

    barrier = pltpu.get_barrier_semaphore()
    greeted = [sp_at((line + 1) % outer, half), sp_at((line + outer - 1) % outer, half)] + sum_devs
    for device in greeted:
        pl.semaphore_signal(barrier, inc=1, device_id=device, device_id_type=MESH)
    pl.semaphore_wait(barrier, len(greeted))

    def remote(src, dst, send, recv, device):
        return pltpu.make_async_remote_copy(
            src_ref=src, dst_ref=dst, send_sem=send, recv_sem=recv,
            device_id=device, device_id_type=MESH,
        )

    places = (line, last - line)
    nexts = (sp_at(jnp.minimum(line + 1, last), half), sp_at(jnp.maximum(line - 1, 0), half))
    signs = (1, -1)

    def rows_of(stream, index):
        count = parts[stream].shape[0] // outer
        return pl.ds(pl.multiple_of(index * count, count), count)

    def reduce_copy(stream, way, step, src):
        return remote(
            src, got[stream].at[way, step - 1], reduce_send.at[stream, way, step - 1],
            reduce_recv.at[stream, way, step - 1], nexts[way],
        )

    def clamp(index):
        return jnp.clip(index, 0, last)

    def reduce_step(stream, step):
        for way in range(2):
            place, sign = places[way], signs[way]
            target = clamp(line + sign * (outer - step))
            own = parts[stream].at[rows_of(stream, target), :]

            @pl.when(place == 0)
            def _():
                reduce_copy(stream, way, step, own).start()

            if step > 1:

                @pl.when((place > 0) & (place <= step - 1))
                def _():
                    reduce_copy(stream, way, step - 1, own).wait_recv()
                    stage = staged[stream].at[way, step - 2]
                    stage[...] = (
                        got[stream][way, step - 2].astype(F32) + own[...].astype(F32)
                    ).astype(BF16)
                    reduce_copy(stream, way, step, stage).start()

    def gather_copy(stream, way, step, origin):
        block = outs[stream].at[half, rows_of(stream, origin), :]
        return remote(
            block, block, gather_send.at[stream, way, step - 1],
            gather_recv.at[stream, way, step - 1], nexts[way],
        )

    def pair_copy(stream, slot, origin):
        block = outs[stream].at[half, rows_of(stream, origin), :]
        return remote(block, block, pair_send.at[stream, slot], pair_recv.at[stream, slot], pair_dev)

    def reduce_final(stream):
        own = parts[stream].at[rows_of(stream, line), :]
        block = outs[stream].at[half, rows_of(stream, line), :]
        for way in range(2):

            @pl.when(places[way] > 0)
            def _():
                reduce_copy(stream, way, last, own).wait_recv()

        up = jnp.where(line > 0, got[stream][0, last - 1].astype(F32), 0.0)
        down = jnp.where(line < last, got[stream][1, last - 1].astype(F32), 0.0)
        block[...] = (own[...].astype(F32) + up + down).astype(BF16)
        for way in range(2):

            @pl.when(places[way] < last)
            def _():
                gather_copy(stream, way, 1, line).start()

        pair_copy(stream, 0, line).start()

    def gather_step(stream, step):
        for way in range(2):
            place, sign = places[way], signs[way]
            origin = clamp(line - sign * step)

            @pl.when(place >= step)
            def _():
                gather_copy(stream, way, step, origin).wait_recv()
                if step < last:

                    @pl.when(place < last)
                    def _():
                        gather_copy(stream, way, step + 1, origin).start()

                pair_copy(stream, 1 + way * last + step - 1, origin).start()

    def drain(stream):
        pair_copy(stream, 0, line).wait()
        for way in range(2):
            place, sign = places[way], signs[way]
            for step in range(1, outer):
                origin = clamp(line - sign * step)

                @pl.when(place <= step - 1)
                def _():
                    reduce_copy(stream, way, step, parts[stream].at[rows_of(stream, 0), :]).wait_send()

                @pl.when((place >= step - 1) & (place < last))
                def _():
                    gather_copy(stream, way, step, origin).wait_send()

                @pl.when(place >= step)
                def _():
                    pair_copy(stream, 1 + way * last + step - 1, origin).wait()

    def near_copy(index):
        return remote(
            part_ref.at[index, 1 - core], near_got.at[index], tp_send.at[index], tp_recv.at[index],
            core_dev,
        )

    def far_copy():
        return remote(far_stage, far_got, tp_send.at[sides], tp_recv.at[sides], side_dev)

    def spread_copy(slot, s, device):
        block = grad_out.at[s, core]
        return remote(block, block, tp_send.at[sides + slot], tp_recv.at[sides + slot], device)

    def input_step(step):
        if step == 0:
            for index in range(sides):
                near_copy(index).start()
        if step == 1:
            for index in range(sides):
                near_copy(index).wait_recv()
            keep_buf[...] = part_ref[side, core].astype(F32) + near_got[side].astype(F32)
            far_stage[...] = (
                part_ref[1 - side, core].astype(F32) + near_got[1 - side].astype(F32)
            ).astype(BF16)
            far_copy().start()
        if step == 2:
            far_copy().wait_recv()
            incoming = keep_buf[...] + far_got[...].astype(F32)
            values = hidden_ref[...].astype(F32)
            scales = scale_ref[...]
            weighted = incoming * gain_ref[...]
            inner_sum = jnp.sum(weighted * values, axis=-1, keepdims=True)
            grads = scales * weighted - values * (scales * scales * scales) * inner_sum * width_scale
            grad_out[side, core] = (middle_ref[...] + grads).astype(BF16)
            spread_copy(1, side, side_dev).start()
            spread_copy(2, side, core_dev).start()
        if step == 3:
            spread_copy(1, side, side_dev).wait_recv()
            spread_copy(3, 1 - side, core_dev).start()
        if step == 4:
            spread_copy(2, side, core_dev).wait_recv()
            spread_copy(3, 1 - side, core_dev).wait_recv()
            for index in range(sides):
                near_copy(index).wait_send()
            far_copy().wait_send()
            spread_copy(1, side, side_dev).wait_send()
            spread_copy(2, side, core_dev).wait_send()
            spread_copy(3, 1 - side, core_dev).wait_send()

    rounds = len(sum_devs)

    def sums_copy(step):
        src = sums_ref if step == 0 else sums_stage.at[step - 1]
        return remote(
            src, sums_got.at[step], sums_send.at[step], sums_recv.at[step], sum_devs[step]
        )

    def sums_step(step):
        if step > 0:
            sums_copy(step - 1).wait_recv()
            before = sums_ref[...] if step == 1 else sums_stage[step - 2]
            total = before + sums_got[step - 1]
            if step == rounds:
                sums_out[...] = total
            else:
                sums_stage[step - 1] = total
        if step < rounds:
            sums_copy(step).start()
        if step == rounds:
            for index in range(rounds):
                sums_copy(index).wait_send()

    extra = []
    for index in range(5):
        extra.append(functools.partial(input_step, index))
    for index in range(rounds + 1):
        extra.append(functools.partial(sums_step, index))
    for turn in range(streams + 1):
        for step in range(1, outer + 1):
            if turn < streams:
                if step < outer:
                    reduce_step(turn, step)
                else:
                    reduce_final(turn)
            if turn > 0 and step < outer:
                gather_step(turn - 1, step)
            if extra:
                extra.pop(0)()
    for step in extra:
        step()
    for stream in range(streams):
        drain(stream)


def finish(parts, part, hidden, scales, gain, middle, sums, outer, sp_n, tp_n):
    streams = len(parts)
    sides = tp_n // 2
    quarter, model = hidden.shape
    last = outer - 1
    rounds = (tp_n - 1).bit_length() + (sp_n - 1).bit_length()
    vmem = pl.BlockSpec(memory_space=pltpu.VMEM)
    chunk = [(2, last, p.shape[0] // outer, p.shape[1]) for p in parts]
    dma = pltpu.SemaphoreType.DMA
    return pl.pallas_call(
        functools.partial(finish_kernel, outer, sides, sp_n, tp_n, streams, 1.0 / model),
        out_shape=[jax.ShapeDtypeStruct((2,) + p.shape, BF16) for p in parts]
        + [
            jax.ShapeDtypeStruct((sides, 2, quarter, model), BF16),
            jax.ShapeDtypeStruct(sums.shape, F32),
        ],
        in_specs=[vmem] * (streams + 6),
        out_specs=[vmem] * (streams + 2),
        scratch_shapes=[pltpu.VMEM(c, BF16) for c in chunk]
        + [pltpu.VMEM(c, BF16) for c in chunk]
        + [
            pltpu.VMEM((sides, quarter, model), BF16),
            pltpu.VMEM((quarter, model), BF16),
            pltpu.VMEM((quarter, model), F32),
            pltpu.VMEM((quarter, model), BF16),
            pltpu.VMEM((rounds,) + sums.shape, F32),
            pltpu.VMEM((rounds,) + sums.shape, F32),
        ]
        + [dma((streams, 2, last))] * 4
        + [dma((streams, 1 + 2 * last))] * 2
        + [dma((sides + 4,))] * 2
        + [dma((rounds,))] * 2,
        compiler_params=pltpu.CompilerParams(
            collective_id=1, has_side_effects=True, vmem_limit_bytes=60 * 1024 * 1024
        ),
        cost_estimate=pl.CostEstimate(flops=10**9, bytes_accessed=10**8, transcendentals=0),
        name="finish",
    )(*parts, part, hidden, scales, gain, middle, sums)


def body(
    hidden,
    segment_ids,
    attn_norm,
    query_proj,
    key_proj,
    value_proj,
    gate_proj,
    output_proj,
    query_norm,
    key_norm,
    ffn_norm,
    ffn_gate,
    ffn_up,
    ffn_down,
    upstream,
):
    rows_dev, model = hidden.shape
    head_width = query_norm.shape[0]
    heads = query_proj.shape[1] // head_width
    groups = key_proj.shape[1] // head_width
    per_group = heads // groups
    group_width = groups * head_width
    sp_n = lax.axis_size("sp")
    tp_n = lax.axis_size("tp")
    outer = sp_n // 2
    sides = tp_n // 2
    quarter = rows_dev // tp_n
    tp_i = lax.axis_index("tp")
    sp_i = lax.axis_index("sp")
    ring_i = sp_i // 2
    pair_i = sp_i % 2
    side_i = tp_i // 2
    core_i = tp_i % 2
    own_first = sp_i * rows_dev
    quarter_first = tp_i * quarter
    scale = 1.0 / math.sqrt(head_width)

    ring_pairs = [(z * 2 + y, ((z + 1) % outer) * 2 + y) for z in range(outer) for y in range(2)]
    pair_pairs = [(i, i ^ 1) for i in range(sp_n)]
    side_pairs = [(i, i ^ 2) for i in range(tp_n)]
    core_pairs = [(i, i ^ 1) for i in range(tp_n)]

    def ring(value):
        return lax.ppermute(value, "sp", ring_pairs)

    def pair(value):
        return lax.ppermute(value, "sp", pair_pairs)

    def side(value):
        return lax.ppermute(value, "tp", side_pairs)

    def core(value):
        return lax.ppermute(value, "tp", core_pairs)

    def gather_sp(block):
        blocks = []
        for k in range(outer):
            blocks.append((block, pair(block)))
            if k < outer - 1:
                block = ring(block)
        return blocks

    def scatter_sp(parts):
        def paired(k):
            return parts[k][0] + pair(parts[k][1].astype(BF16)).astype(F32)

        total = paired(1 % outer)
        for k in range(2, outer + 1):
            total = ring(total.astype(BF16)).astype(F32) + paired(k % outer)
        return total

    first_id = segment_ids[0]
    second_start = jnp.sum((segment_ids == first_id).astype(jnp.int32))
    own_index = own_first + jnp.arange(rows_dev, dtype=jnp.int32)
    own_starts = jnp.where(own_index < second_start, 0, second_start)
    steps_half = jnp.arange(head_width // 2, dtype=F32)
    frequencies = jnp.exp(steps_half * (-2.0 * math.log(THETA) / head_width))
    angles = (own_index - own_starts).astype(F32)[:, None] * frequencies[None, :]
    cosine = jnp.cos(angles)[:, None, :]
    sine = jnp.sin(angles)[:, None, :]

    hidden_full = hidden.astype(F32)
    normed_full, attn_scales = norm_rows(hidden_full, attn_norm)
    normed = normed_full.astype(BF16)
    key_raw = matmul(normed, key_proj).reshape(rows_dev, groups, head_width)
    value_rows = matmul(normed, value_proj).astype(BF16)
    key_normed, key_scales = norm_rows(key_raw, key_norm)
    key_rot = rotary(key_normed, cosine, sine).astype(BF16).reshape(rows_dev, group_width)
    kv_own = jnp.stack([key_rot, value_rows])

    low, high = (outer // 4, 3 * outer // 4) if outer % 4 == 0 else (0, outer)
    reach = high - 1 if low else outer - 1

    def up_pairs(step):
        return [
            (z * 2 + y, (z + 1) * 2 + y)
            for z in range(outer - 1)
            for y in range(2)
            if z + 1 - step >= 0 and (z + 1 - step >= low or z + 1 < high)
        ]

    kv_blocks = []
    travelling = kv_own
    for k in range(reach + 1):
        kv_blocks.append((travelling, pair(travelling)))
        if k < reach:
            travelling = lax.ppermute(travelling, "sp", up_pairs(k + 1))

    query_raw = matmul(normed, query_proj).reshape(rows_dev, heads, head_width)
    gate_raw = matmul(normed, gate_proj)
    query_normed, query_scales = norm_rows(query_raw, query_norm)
    queries = rotary(query_normed, cosine, sine).astype(BF16).reshape(rows_dev, heads * head_width)

    def swap_half(value):
        piece = model // 4
        mine = pair(lax.dynamic_slice_in_dim(value, ((1 - pair_i) * 2 + core_i) * piece, piece, 1))
        near = core(mine)
        return jnp.where(
            core_i == 1, jnp.concatenate([near, mine], 1), jnp.concatenate([mine, near], 1)
        )

    normed_own = lax.dynamic_slice_in_dim(normed, pair_i * (model // 2), model // 2, 1)
    both_normed = jnp.concatenate([normed_own, swap_half(normed)])

    grad_quarter = lax.dynamic_slice_in_dim(upstream, quarter_first, quarter)
    up_blocks = gather_sp(grad_quarter)

    row_start_low = own_starts[0]
    row_start_high = own_starts[-1]

    def block_info(k):
        shards = [(ring_i - k) * 2 + pair_i, (ring_i - k) * 2 + (1 - pair_i)]
        entries = [own_first] + [shard * rows_dev for shard in shards]
        live = []
        full = []
        for shard in shards:
            token = shard * rows_dev
            live.append((shard >= 0) & (shard <= sp_i) & (token + rows_dev - 1 >= row_start_low))
            full.append((token >= row_start_high) & (shard < sp_i))
        return jnp.stack(entries + [v.astype(jnp.int32) for v in live + full]).astype(jnp.int32)

    infos = [block_info(k) for k in range(reach + 1)]
    starts_column = own_starts[:, None]
    starts_row = own_starts[None, :]
    carried = None
    for k in range(reach + 1):
        carried = attn_forward(
            infos[k], starts_column, queries, kv_blocks[k][0], kv_blocks[k][1], carried, scale
        )
    mix_acc, mix_sum = carried
    mixed = mix_acc / mix_sum
    lse = jnp.log2(mix_sum.reshape(rows_dev, heads, head_width)[:, :, 0])
    lse_rows = lse.T.reshape(groups, per_group, rows_dev)
    gate_sig = jax.nn.sigmoid(gate_raw)
    gated = (mixed * gate_sig).astype(BF16)
    gated_other = pair(gated)

    def scatter_tp(part):
        part = part.reshape(sides, 2, quarter, model)
        keep = lax.dynamic_index_in_dim(part, core_i, 1, keepdims=False)
        send = lax.dynamic_index_in_dim(part, 1 - core_i, 1, keepdims=False)
        keep = keep + core(send.astype(BF16)).astype(F32)
        mine = lax.dynamic_index_in_dim(keep, side_i, 0, keepdims=False)
        other = lax.dynamic_index_in_dim(keep, 1 - side_i, 0, keepdims=False)
        return mine + side(other.astype(BF16)).astype(F32)

    def gather_tp(block):
        far = side(block)
        swap_side = side_i == 1
        two = jnp.where(swap_side, jnp.stack([far, block]), jnp.stack([block, far]))
        near = core(two)
        swap_core = core_i == 1
        full = jnp.where(
            swap_core, jnp.stack([near, two], axis=1), jnp.stack([two, near], axis=1)
        )
        return full.reshape((rows_dev,) + block.shape[1:])

    fused = outer * quarter <= 512 and outer > 1 and tp_n == 4
    if fused:
        middle, grad_middle_quarter, ffn_gain_sum, branch, inner_rows, *ffn_parts = middle_layer(
            gated,
            output_proj,
            lax.dynamic_slice_in_dim(hidden, quarter_first, quarter),
            ffn_norm[None, :],
            ffn_gate,
            ffn_up,
            ffn_down,
            [block for both in up_blocks for block in both],
            outer,
            sides,
        )
        grad_branch = branch.reshape(rows_dev, model)
        ffn_gain_sum = ffn_gain_sum[0]
        inner_list = [
            inner_rows[k * 2 * quarter : (k + 1) * 2 * quarter] for k in range(outer)
        ]
    else:
        attn_quarter = scatter_tp(matmul(gated, output_proj))
        hidden_quarter = lax.dynamic_slice_in_dim(hidden, quarter_first, quarter).astype(F32)
        middle = hidden_quarter + attn_quarter
        normed_two_full, ffn_scales = norm_rows(middle, ffn_norm)
        normed_two = normed_two_full.astype(BF16)

        two_blocks = gather_sp(normed_two)
        rows_list, up_list, inner_list, gate_list, grad_up_list = [None] * outer, [None] * outer, [None] * outer, [None] * outer, [None] * outer
        grad_parts = [None] * outer
        for k in list(range(1, outer)) + [0]:
            rows_k = jnp.concatenate(two_blocks[k])
            up_k = jnp.concatenate(up_blocks[k])
            gate_vals = matmul(rows_k, ffn_gate)
            up_vals = matmul(rows_k, ffn_up)
            sig = jax.nn.sigmoid(gate_vals)
            grad_inner = times_transpose(up_k, ffn_down)
            grad_gate = (grad_inner * up_vals * (sig * (1.0 + gate_vals * (1.0 - sig)))).astype(BF16)
            grad_up = (grad_inner * (gate_vals * sig)).astype(BF16)
            inner = (gate_vals * sig * up_vals).astype(BF16)
            grad_parts[k] = (
                times_transpose(grad_gate, ffn_gate) + times_transpose(grad_up, ffn_up)
            ).reshape(2, quarter, model)
            rows_list[k], up_list[k], inner_list[k] = rows_k, up_k, inner
            gate_list[k], grad_up_list[k] = grad_gate, grad_up
        grad_two = scatter_sp(grad_parts)

        norm_grad_two, ffn_gain_terms = norm_back(middle, ffn_scales, ffn_norm, grad_two)
        grad_middle_quarter = grad_quarter.astype(F32) + norm_grad_two
        grad_branch = gather_tp(grad_middle_quarter.astype(BF16))
        ffn_gain_sum = jnp.sum(ffn_gain_terms, axis=0)

    mlp_parts = [matmul(inner_list[k], ffn_down).reshape(2, quarter, model) for k in range(outer)]
    mlp_quarter = scatter_sp(mlp_parts)
    layer_out = gather_tp((middle + mlp_quarter).astype(BF16))

    def reduce_tp(part):
        half = part.shape[1] // 2
        keep = lax.dynamic_slice_in_dim(part, core_i * half, half, 1)
        send = lax.dynamic_slice_in_dim(part, (1 - core_i) * half, half, 1)
        return (keep.astype(F32) + core(send.astype(BF16)).astype(F32)).astype(BF16)

    def whole_tp(keep, far):
        keep = (keep.astype(F32) + far.astype(F32)).astype(BF16)
        near = core(keep)
        return jnp.where(
            core_i == 1, jnp.concatenate([near, keep], 1), jnp.concatenate([keep, near], 1)
        ).astype(F32)

    if not fused:
        rows_all = jnp.concatenate(rows_list)
        up_all = jnp.concatenate(up_list)
        inner_all = jnp.concatenate(inner_list)
        gate_all = jnp.concatenate(gate_list)
        grad_up_all = jnp.concatenate(grad_up_list)
        ffn_parts = [
            jnp.stack([outer_sum(rows_all, gate_all), outer_sum(rows_all, grad_up_all)]),
            outer_sum(inner_all, up_all),
        ]
    ffn_halves = [reduce_tp(ffn_parts[0]), reduce_tp(ffn_parts[1][None])]

    branch_other = swap_half(grad_branch)
    branch_own = lax.dynamic_slice_in_dim(grad_branch, pair_i * (model // 2), model // 2, 1)
    output_half = outer_sum(
        jnp.concatenate([gated, gated_other]), jnp.concatenate([branch_own, branch_other])
    )
    grad_gated = times_transpose(grad_branch, output_proj)
    grad_mixed = (grad_gated * gate_sig).astype(BF16)
    grad_gate_raw = (grad_gated * mixed * (gate_sig * (1.0 - gate_sig))).astype(BF16)
    gate_half = outer_sum(both_normed, jnp.concatenate([grad_gate_raw, pair(grad_gate_raw)]))
    deltas = jnp.sum(
        (grad_mixed.astype(F32) * mixed).reshape(rows_dev, heads, head_width), axis=-1
    )
    delta_rows = deltas.T.reshape(groups, per_group, rows_dev)

    def down_pairs(step):
        return [(b, a) for a, b in up_pairs(step)]

    grad_mixed, ffn_halves = lax.optimization_barrier((grad_mixed, ffn_halves))
    ffn_halves = [(keep, side(keep)) for keep in ffn_halves]
    query_acc = None
    travelling = None
    for k in list(range(reach, -1, -1)):
        query_acc, grad_a, grad_b = attn_backward(
            infos[k], starts_row, lse_rows, delta_rows, queries, grad_mixed,
            kv_blocks[k][0], kv_blocks[k][1], query_acc, k == 0, scale,
        )
        total = grad_a.astype(F32) + pair(grad_b).astype(F32)
        if travelling is not None:
            total = total + travelling.astype(F32)
        if k > 0:
            travelling = lax.ppermute(total.astype(BF16), "sp", down_pairs(k))
    grad_key_rot = total[0].reshape(rows_dev, groups, head_width)
    grad_value_low = total[1].astype(BF16)
    grad_query_rot = (query_acc * scale).reshape(rows_dev, heads, head_width)
    grad_query_raw, query_gain_terms = norm_back(
        query_raw, query_scales, query_norm, rotary_back(grad_query_rot, cosine, sine)
    )
    grad_key_raw, key_gain_terms = norm_back(
        key_raw, key_scales, key_norm, rotary_back(grad_key_rot, cosine, sine)
    )
    grad_query_low = grad_query_raw.reshape(rows_dev, heads * head_width).astype(BF16)
    grad_key_low = grad_key_raw.reshape(rows_dev, group_width).astype(BF16)
    grad_kv_low = jnp.concatenate([grad_key_low, grad_value_low], axis=1)
    grad_query_low, grad_kv_low, ffn_halves = lax.optimization_barrier(
        (grad_query_low, grad_kv_low, ffn_halves)
    )
    ffn_grads = [whole_tp(*halves) for halves in ffn_halves]

    both_queries = jnp.concatenate([grad_query_low, pair(grad_query_low)])
    both_kv = jnp.concatenate([grad_kv_low, pair(grad_kv_low)])
    parts = [
        output_half.astype(BF16),
        gate_half.astype(BF16),
        outer_sum(both_normed, both_queries).astype(BF16),
        outer_sum(both_normed, both_kv).astype(BF16),
    ]

    grad_normed_part = (
        times_transpose(grad_query_low, query_proj)
        + times_transpose(grad_key_low, key_proj)
        + times_transpose(grad_value_low, value_proj)
        + times_transpose(grad_gate_raw, gate_proj)
    )
    gains = jnp.concatenate(
        [
            jnp.sum(grad_normed_part * hidden_full * attn_scales, axis=0),
            ffn_gain_sum,
            jnp.sum(query_gain_terms, axis=(0, 1)),
            jnp.sum(key_gain_terms, axis=(0, 1)),
        ]
    )
    parts, ffn_grads = lax.optimization_barrier((parts, ffn_grads))
    gains_at = 2 * model + 2 * head_width
    gains = jnp.pad(gains, (0, -gains_at % 1024)).reshape(-1, 128)
    scales_quarter = lax.dynamic_slice_in_dim(attn_scales, quarter_first, quarter)
    finished = finish(
        parts,
        grad_normed_part.astype(BF16).reshape(sides, 2, quarter, model),
        lax.dynamic_slice_in_dim(hidden, quarter_first, quarter),
        scales_quarter,
        attn_norm[None, :],
        grad_middle_quarter,
        gains,
        outer,
        sp_n,
        tp_n,
    )
    output_all, gate_all_w, query_all, kv_all, input_all, gains = finished
    output_grad = jnp.concatenate([output_all[0], output_all[1]], axis=1).astype(F32)
    gate_grad = gate_all_w.reshape(model, heads * head_width).astype(F32)
    query_grad = query_all.reshape(model, heads * head_width).astype(F32)
    kv_all = kv_all.reshape(model, 2 * group_width)
    key_grad = kv_all[:, :group_width].astype(F32)
    value_grad = kv_all[:, group_width:].astype(F32)
    hidden_grad = input_all.reshape(rows_dev, model).astype(F32)
    gains = gains.reshape(-1)
    return (
        layer_out,
        hidden_grad,
        gains[:model],
        query_grad,
        key_grad,
        value_grad,
        gate_grad,
        output_grad,
        gains[2 * model : 2 * model + head_width],
        gains[2 * model + head_width : gains_at],
        gains[model : 2 * model],
        ffn_grads[0][0],
        ffn_grads[0][1],
        ffn_grads[1][0],
    )


def solution(mesh):
    placed = (
        P("sp", None),
        P(),
        P(),
        P(None, "tp"),
        P(None, "tp"),
        P(None, "tp"),
        P(None, "tp"),
        P("tp", None),
        P(),
        P(),
        P(),
        P(None, "sp"),
        P(None, "sp"),
        P("sp", None),
        P("sp", None),
    )
    return jax.shard_map(
        body,
        mesh=mesh,
        in_specs=placed,
        out_specs=(
            P("sp", None),
            P("sp", None),
            P(),
            P(None, "tp"),
            P(None, "tp"),
            P(None, "tp"),
            P(None, "tp"),
            P("tp", None),
            P(),
            P(),
            P(),
            P(None, "sp"),
            P(None, "sp"),
            P("sp", None),
        ),
        check_vma=False,
    )
```

```python
import functools
import math

import jax
import jax.numpy as jnp
from jax import lax
from jax.experimental import pallas as pl
from jax.experimental.pallas import tpu as pltpu
from jax.sharding import PartitionSpec as P

EPSILON = 1e-06
THETA = 1000000.0
LOG2E = 1.4426950408889634
F32 = jnp.float32
BF16 = jnp.bfloat16


def norm_scales(values):
    return lax.rsqrt(jnp.mean(values * values, axis=-1, keepdims=True) + EPSILON)


def norm_rows(values, gain):
    scales = norm_scales(values)
    return (values * scales * gain, scales)


def norm_back(values, scales, gain, incoming):
    weighted = incoming * gain
    inner_sum = jnp.sum(weighted * values, axis=-1, keepdims=True)
    grad_values = (
        scales * weighted - values * (scales * scales * scales) * inner_sum / values.shape[-1]
    )
    return (grad_values, incoming * values * scales)


def rotary(values, cosine, sine):
    half_width = values.shape[-1] // 2
    front_half = values[..., :half_width]
    back_half = values[..., half_width:]
    return jnp.concatenate(
        [front_half * cosine - back_half * sine, back_half * cosine + front_half * sine], axis=-1
    )


def rotary_back(grads, cosine, sine):
    half_width = grads.shape[-1] // 2
    front_half = grads[..., :half_width]
    back_half = grads[..., half_width:]
    return jnp.concatenate(
        [front_half * cosine + back_half * sine, back_half * cosine - front_half * sine], axis=-1
    )


def matmul(left, right):
    return jnp.dot(left, right, preferred_element_type=F32)


def outer_sum(left, right):
    return lax.dot_general(left, right, (((0,), (0,)), ((), ())), preferred_element_type=F32)


def times_transpose(left, right):
    return lax.dot_general(left, right, (((1,), (1,)), ((), ())), preferred_element_type=F32)


def attn_forward_kernel(first, diagonal, scale, info, starts, queries, kv_a, kv_b, *rest):
    if first:
        acc_out, sum_out = rest
    else:
        acc_in, sum_in, acc_out, sum_out = rest
    rows = queries.shape[0]
    keys_n = kv_a.shape[1]
    per_group = queries.shape[1] // kv_a.shape[2]
    width = kv_a.shape[2]
    if first:
        acc_out[...] = jnp.zeros_like(acc_out)
        sum_out[...] = jnp.zeros_like(sum_out)
    else:
        acc_out[...] = acc_in[...]
        sum_out[...] = sum_in[...]
    own_first = info[0]
    for slot, block in enumerate((kv_a, kv_b)):
        key_first = info[1 + slot]
        live = info[3 + slot] > 0

        def work(masked, causal):
            ones = jnp.ones((keys_n, width), BF16)
            values = jnp.concatenate([block[1], ones], axis=1)
            keys = block[0]
            if masked:
                key_index = key_first + lax.broadcasted_iota(jnp.int32, (rows, keys_n), 1)
                allowed = key_index >= starts[...]
                if causal:
                    row_index = own_first + lax.broadcasted_iota(jnp.int32, (rows, keys_n), 0)
                    allowed = allowed & (key_index <= row_index)
            for head in range(per_group):
                cols = slice(head * width, (head + 1) * width)
                scores = times_transpose(queries[:, cols], keys)
                weights = jnp.exp2(scores * (scale * LOG2E))
                if masked:
                    weights = jnp.where(allowed, weights, 0.0)
                both = matmul(weights.astype(BF16), values)
                acc_out[:, cols] += both[:, :width]
                sum_out[:, cols] += both[:, width:]

        if diagonal and slot == 0:
            work(True, True)
        else:
            full = info[5 + slot] > 0
            pl.when(live & full)(functools.partial(work, False, False))
            pl.when(live & jnp.logical_not(full))(functools.partial(work, True, False))


def attn_forward(info, starts, queries, kv_a, kv_b, carried, scale):
    rows, all_width = queries.shape
    width = 128
    groups = kv_a.shape[2] // width
    group_width = all_width // groups
    keys_n = kv_a.shape[1]
    first = carried is None
    spec_q = pl.BlockSpec((rows, group_width), lambda g, info: (0, g))
    spec_kv = pl.BlockSpec((2, keys_n, width), lambda g, info: (0, 0, g))
    specs = [pl.BlockSpec((rows, 1), lambda g, info: (0, 0)), spec_q, spec_kv, spec_kv]
    operands = [starts, queries, kv_a, kv_b]
    if not first:
        specs += [spec_q, spec_q]
        operands += list(carried)
    return pl.pallas_call(
        functools.partial(attn_forward_kernel, first, first, scale),
        grid_spec=pltpu.PrefetchScalarGridSpec(
            num_scalar_prefetch=1,
            grid=(groups,),
            in_specs=specs,
            out_specs=[spec_q, spec_q],
        ),
        out_shape=[jax.ShapeDtypeStruct((rows, all_width), F32)] * 2,
        compiler_params=pltpu.CompilerParams(dimension_semantics=("arbitrary",)),
        cost_estimate=pl.CostEstimate(
            flops=16 * rows * keys_n * all_width,
            transcendentals=2 * rows * keys_n * all_width // width,
            bytes_accessed=8 * rows * all_width,
        ),
        name="attn_forward",
    )(info, *operands)


def attn_backward_kernel(first, diagonal, scale, info, starts, lse, deltas, queries, grads, kv_a, kv_b, *rest):
    if first:
        grad_q, grad_a, grad_b = rest
    else:
        grad_in, grad_q, grad_a, grad_b = rest
    rows = queries.shape[0]
    keys_n = kv_a.shape[1]
    width = kv_a.shape[2]
    per_group = queries.shape[1] // width
    if first:
        grad_q[...] = jnp.zeros_like(grad_q)
    else:
        grad_q[...] = grad_in[...]
    own_first = info[0]
    for slot, (block, out) in enumerate(((kv_a, grad_a), (kv_b, grad_b))):
        key_first = info[1 + slot]
        live = info[3 + slot] > 0

        def work(masked, causal):
            keys = block[0]
            values = block[1]
            keys_t = keys.T
            if masked:
                key_index = key_first + lax.broadcasted_iota(jnp.int32, (keys_n, rows), 0)
                allowed = key_index >= starts[...]
                if causal:
                    row_index = own_first + lax.broadcasted_iota(jnp.int32, (keys_n, rows), 1)
                    allowed = allowed & (key_index <= row_index)
            total_k = jnp.zeros((keys_n, width), F32)
            total_v = jnp.zeros((keys_n, width), F32)
            for head in range(per_group):
                cols = slice(head * width, (head + 1) * width)
                q_head = queries[:, cols]
                g_head = grads[:, cols]
                scores = times_transpose(keys, q_head)
                probs = jnp.exp2(scores * (scale * LOG2E) - lse[0, head : head + 1, :])
                if masked:
                    probs = jnp.where(allowed, probs, 0.0)
                grad_probs = times_transpose(values, g_head)
                grad_scores = (probs * (grad_probs - deltas[0, head : head + 1, :])).astype(BF16)
                total_v += matmul(probs.astype(BF16), g_head)
                total_k += matmul(grad_scores, q_head)
                grad_q[:, cols] += matmul(keys_t, grad_scores).T
            out[0] = (total_k * scale).astype(BF16)
            out[1] = total_v.astype(BF16)

        if diagonal and slot == 0:
            work(True, True)
        else:
            full = info[5 + slot] > 0
            pl.when(live & full)(functools.partial(work, False, False))
            pl.when(live & jnp.logical_not(full))(functools.partial(work, True, False))

            @pl.when(jnp.logical_not(live))
            def _():
                out[...] = jnp.zeros_like(out)


def attn_backward(info, starts_row, lse, deltas, queries, grads, kv_a, kv_b, carried, diagonal, scale):
    rows, all_width = queries.shape
    width = 128
    groups = kv_a.shape[2] // width
    group_width = all_width // groups
    per_group = group_width // width
    keys_n = kv_a.shape[1]
    first = carried is None
    spec_q = pl.BlockSpec((rows, group_width), lambda g, info: (0, g))
    spec_kv = pl.BlockSpec((2, keys_n, width), lambda g, info: (0, 0, g))
    spec_row = pl.BlockSpec((1, per_group, rows), lambda g, info: (g, 0, 0))
    specs = [
        pl.BlockSpec((1, rows), lambda g, info: (0, 0)),
        spec_row,
        spec_row,
        spec_q,
        spec_q,
        spec_kv,
        spec_kv,
    ]
    operands = [starts_row, lse, deltas, queries, grads, kv_a, kv_b]
    if not first:
        specs.append(spec_q)
        operands.append(carried)
    return pl.pallas_call(
        functools.partial(attn_backward_kernel, first, diagonal, scale),
        grid_spec=pltpu.PrefetchScalarGridSpec(
            num_scalar_prefetch=1,
            grid=(groups,),
            in_specs=specs,
            out_specs=[spec_q, spec_kv, spec_kv],
        ),
        out_shape=[
            jax.ShapeDtypeStruct((rows, all_width), F32),
            jax.ShapeDtypeStruct(kv_a.shape, BF16),
            jax.ShapeDtypeStruct(kv_a.shape, BF16),
        ],
        compiler_params=pltpu.CompilerParams(dimension_semantics=("arbitrary",)),
        cost_estimate=pl.CostEstimate(
            flops=20 * rows * keys_n * all_width,
            transcendentals=2 * rows * keys_n * all_width // width,
            bytes_accessed=8 * rows * all_width,
        ),
        name="attn_backward",
    )(info, *operands)


def middle_kernel(outer, *refs):
    MESH = pl.DeviceIdType.MESH
    blocks = 2 * outer
    (gated, out_proj, hidden_ref, gain_ref, gate_in, up_in, down_in) = refs[:7]
    ups_in = refs[7 : 7 + blocks]
    (middle_out, grad_out, gain_out, branch, inner_out, dw_both, dw_down) = refs[
        7 + blocks : 14 + blocks
    ]
    (
        w_gate, w_up, w_down, ups, rows, grad_inner, inner, grad_gate, grad_up,
        near_stage, near_got, far_stage, far_got, far_keep, own_keep,
        keep, y_stage, y_got, z_stage, z_got,
        load_sem, store_sem, tp_send, tp_recv, zs, zr, ys, yr, rys, ryr, rzs, rzr,
    ) = refs[14 + blocks :]
    stage_gate, stage_up, stage_down = w_gate, w_up, w_down
    quarter, model = hidden_ref.shape
    group = 2 * quarter
    chunk = model // outer
    last = outer - 1

    sp_i = lax.axis_index("sp")
    tp_i = lax.axis_index("tp")
    line = sp_i // 2
    half = sp_i % 2
    side = tp_i // 2
    core = tp_i % 2

    def sp_at(z, y):
        return (tp_i, z * 2 + y)

    pair_dev = sp_at(line, 1 - half)
    core_dev = (side * 2 + (1 - core), sp_i)
    side_dev = ((1 - side) * 2 + core, sp_i)
    nexts = (sp_at(jnp.minimum(line + 1, last), half), sp_at(jnp.maximum(line - 1, 0), half))

    loads = [
        pltpu.make_async_copy(src, dst, load_sem.at[index])
        for index, (src, dst) in enumerate(
            [(down_in, w_down)]
            + [(ups_in[b], ups.at[pl.ds(b * quarter, quarter), :]) for b in range(blocks)]
            + [(gate_in, w_gate), (up_in, w_up)]
        )
    ]
    for load in loads:
        load.start()

    barrier = pltpu.get_barrier_semaphore()
    greeted = [
        sp_at((line + 1) % outer, half), sp_at((line + outer - 1) % outer, half),
        pair_dev, core_dev, side_dev,
    ]
    for device in greeted:
        pl.semaphore_signal(barrier, inc=1, device_id=device, device_id_type=MESH)
    pl.semaphore_wait(barrier, len(greeted))

    def remote(src, dst, send, recv, device):
        return pltpu.make_async_remote_copy(
            src_ref=src, dst_ref=dst, send_sem=send, recv_sem=recv,
            device_id=device, device_id_type=MESH,
        )

    def aligned(index, count):
        return pl.ds(pl.multiple_of(index * count, count), count)

    def near_copy(j):
        return remote(near_stage.at[j], near_got.at[j], tp_send.at[j], tp_recv.at[j], core_dev)

    def far_copy():
        return remote(far_stage, far_got, tp_send.at[2], tp_recv.at[2], side_dev)

    def projected(s, c):
        return matmul(gated[aligned(s * 2 + c, quarter), :], out_proj[...])

    near_stage[0] = projected(1 - side, 1 - core).astype(BF16)
    near_copy(0).start()
    near_stage[1] = projected(side, 1 - core).astype(BF16)
    near_copy(1).start()
    far_keep[...] = projected(1 - side, core)
    near_copy(0).wait_recv()
    far_stage[...] = (far_keep[...] + near_got[0].astype(F32)).astype(BF16)
    far_copy().start()
    own_keep[...] = projected(side, core)

    for load in loads[: 1 + blocks]:
        load.wait()

    def grad_inner_of(k, carry):
        at = aligned(k, group)
        grad_inner[at, :] = times_transpose(ups[at, :], w_down[...])
        return carry

    lax.fori_loop(0, outer, grad_inner_of, 0)
    near_copy(1).wait_recv()
    far_copy().wait_recv()
    middle = hidden_ref[...].astype(F32) + (
        own_keep[...] + near_got[1].astype(F32) + far_got[...].astype(F32)
    )
    middle_out[...] = middle
    rows[0:quarter, :] = (middle * norm_scales(middle) * gain_ref[...]).astype(BF16)

    def entry(k, j):
        return pl.ds(pl.multiple_of((k * 2 + j) * quarter, quarter), quarter)

    def wrap(k):
        return (k + outer) % outer

    def z_copy(way, k):
        to = wrap(k + 1 - 2 * way)
        return remote(
            rows.at[entry(k, 0), :], rows.at[entry(to, 0), :], zs.at[way, k], zr.at[to], nexts[way]
        )

    def z_arrived(k):
        return remote(
            rows.at[entry(k, 0), :], rows.at[entry(k, 0), :], zs.at[0, k], zr.at[k], nexts[0]
        )

    def y_copy(k):
        return remote(
            rows.at[entry(k, 0), :], rows.at[entry(k, 1), :], ys.at[k], yr.at[k], pair_dev
        )

    short = jnp.minimum(line, last - line)

    def delta_of(i):
        near = jnp.where(i % 2 == 1, -((i + 1) // 2), (i + 1) // 2)
        far = jnp.where(line < last - line, i - short, short - i)
        return jnp.where(i <= 2 * short, near, far)

    def slot_of(delta):
        return jnp.where(delta <= 0, -delta, outer - delta)

    for way, exists in ((0, line < last), (1, line > 0)):
        pl.when(exists)(z_copy(way, 0).start)
    y_copy(0).start()

    def goes_on(delta):
        return ((delta < 0) & (line < last), (delta > 0) & (line > 0))

    def forward(i):
        delta = delta_of(i)
        k = slot_of(delta)
        z_arrived(k).wait_recv()
        for way, exists in enumerate(goes_on(delta)):
            pl.when(exists)(z_copy(way, k).start)
        y_copy(k).start()

    for load in loads[1 + blocks :]:
        load.wait()
    forward(1)

    def turn_forward(i, carry):
        @pl.when(i + 2 < outer)
        def _():
            forward(i + 2)

        k = slot_of(delta_of(i))
        y_copy(k).wait_recv()
        at = aligned(k, group)
        rows_k = rows[at, :]
        gate_vals = matmul(rows_k, w_gate[...])
        up_vals = matmul(rows_k, w_up[...])
        incoming = grad_inner[at, :]
        sig = jax.nn.sigmoid(gate_vals)
        silu = gate_vals * sig
        grad_gate[at, :] = (incoming * up_vals * (sig * (1.0 + gate_vals * (1.0 - sig)))).astype(BF16)
        grad_up[at, :] = (incoming * silu).astype(BF16)
        inner[at, :] = (silu * up_vals).astype(BF16)
        return carry

    lax.fori_loop(0, outer, turn_forward, 0)
    inner_store = pltpu.make_async_copy(inner, inner_out, store_sem.at[0])
    inner_store.start()

    def y_sum(k):
        at = aligned(k, quarter)
        return remote(y_stage.at[at, :], y_got.at[at, :], rys.at[k], ryr.at[k], pair_dev)

    def turn_parts(step, carry):
        k = slot_of(delta_of(last - step))
        at = aligned(k, group)
        part = times_transpose(grad_gate[at, :], w_gate[...]) + times_transpose(
            grad_up[at, :], w_up[...]
        )
        y_stage[aligned(k, quarter), :] = part[quarter:].astype(BF16)
        y_sum(k).start()
        keep[aligned(k, quarter), :] = part[:quarter]
        return carry

    lax.fori_loop(0, outer, turn_parts, 0)

    def z_sum(way, k):
        to = wrap(k + 1 - 2 * way)
        return remote(
            z_stage.at[aligned(k, quarter), :],
            z_got.at[pl.ds(pl.multiple_of((way * outer + to) * quarter, quarter), quarter), :],
            rzs.at[k], rzr.at[way, to], nexts[way],
        )

    def z_got_at(way, k):
        return z_got[pl.ds(pl.multiple_of((way * outer + k) * quarter, quarter), quarter), :]

    def z_sum_arrived(way, k):
        return remote(
            z_stage.at[aligned(k, quarter), :], z_stage.at[aligned(k, quarter), :],
            rzs.at[k], rzr.at[way, k], nexts[way],
        )

    def gate_up_stores(c):
        at = aligned(c, chunk)
        return (
            pltpu.make_async_copy(stage_gate.at[at, :], dw_both.at[0, at, :], store_sem.at[1 + 2 * c]),
            pltpu.make_async_copy(stage_up.at[at, :], dw_both.at[1, at, :], store_sem.at[2 + 2 * c]),
        )

    def weight_chunk(c):
        at = aligned(c, chunk)
        some = rows[:, at]
        stage_gate[at, :] = outer_sum(some, grad_gate[...]).astype(BF16)
        stage_up[at, :] = outer_sum(some, grad_up[...]).astype(BF16)
        for store in gate_up_stores(c):
            store.start()

    def turn_sums(step, carry):
        weight_chunk(step)
        delta = delta_of(last - step)
        k = slot_of(delta)
        at = aligned(k, quarter)
        y_sum(k).wait_recv()
        own = keep[at, :] + y_got[at, :].astype(F32)
        for way, (here, before) in enumerate(
            ((delta > 0, line > 0), (delta < 0, line < last))
        ):

            @pl.when(here & before)
            def _():
                z_sum_arrived(way, k).wait_recv()
                z_stage[at, :] = (own + z_got_at(way, k).astype(F32)).astype(BF16)

            @pl.when(here & jnp.logical_not(before))
            def _():
                z_stage[at, :] = own.astype(BF16)

            pl.when(here)(z_sum(way, k).start)
        return carry

    lax.fori_loop(0, last, turn_sums, 0)
    weight_chunk(last)
    y_sum(0).wait_recv()
    for way, exists in ((0, line > 0), (1, line < last)):
        pl.when(exists)(z_sum_arrived(way, 0).wait_recv)
    below = jnp.where(line > 0, z_got_at(0, 0).astype(F32), 0.0)
    above = jnp.where(line < last, z_got_at(1, 0).astype(F32), 0.0)
    grad_two = keep[0:quarter, :] + y_got[0:quarter, :].astype(F32) + below + above

    values = middle_out[...]
    back, gain_terms = norm_back(values, norm_scales(values), gain_ref[...], grad_two)
    grads = ups[0:quarter, :].astype(F32) + back
    branch[side, core] = grads.astype(BF16)

    def spread_copy(slot, s, device):
        block = branch.at[s, core]
        return remote(block, block, tp_send.at[3 + slot], tp_recv.at[3 + slot], device)

    spread_copy(0, side, side_dev).start()
    spread_copy(1, side, core_dev).start()
    grad_out[...] = grads
    gain_out[...] = jnp.sum(gain_terms, axis=0, keepdims=True)

    def down_store(c):
        at = aligned(c, chunk)
        return pltpu.make_async_copy(
            stage_down.at[:, at], dw_down.at[:, at], store_sem.at[1 + 2 * outer + c]
        )

    def turn_down(c, carry):
        at = aligned(c, chunk)
        stage_down[:, at] = outer_sum(inner[...], ups[:, at]).astype(BF16)
        down_store(c).start()
        return carry

    lax.fori_loop(0, outer, turn_down, 0)
    spread_copy(0, side, side_dev).wait_recv()
    spread_copy(2, 1 - side, core_dev).start()
    spread_copy(1, side, core_dev).wait_recv()

    inner_store.wait()
    near_copy(0).wait_send()
    near_copy(1).wait_send()
    far_copy().wait_send()
    for way, exists in ((0, line < last), (1, line > 0)):
        pl.when(exists)(z_copy(way, 0).wait_send)

    def turn_drain(i, carry):
        delta = delta_of(i)
        k = slot_of(delta)
        y_copy(k).wait_send()
        y_sum(k).wait_send()
        for store in gate_up_stores(i):
            store.wait()
        down_store(i).wait()
        for way, exists in enumerate(goes_on(delta)):
            pl.when(exists)(z_copy(way, k).wait_send)
        pl.when(delta != 0)(z_sum(0, k).wait_send)
        return carry

    lax.fori_loop(0, outer, turn_drain, 0)
    spread_copy(0, side, side_dev).wait_send()
    spread_copy(1, side, core_dev).wait_send()
    spread_copy(2, 1 - side, core_dev).wait()


def middle_layer(gated, out_proj, hidden, gain, w_gate, w_up, w_down, ups, outer, sides):
    quarter, model = hidden.shape
    units = w_down.shape[0]
    rows_n = 2 * outer * quarter
    vmem = pl.BlockSpec(memory_space=pltpu.VMEM)
    anywhere = pl.BlockSpec(memory_space=pl.ANY)
    dma = pltpu.SemaphoreType.DMA
    line_rows = outer * quarter
    return pl.pallas_call(
        functools.partial(middle_kernel, outer),
        out_shape=[
            jax.ShapeDtypeStruct((quarter, model), F32),
            jax.ShapeDtypeStruct((quarter, model), F32),
            jax.ShapeDtypeStruct((1, model), F32),
            jax.ShapeDtypeStruct((sides, 2, quarter, model), BF16),
            jax.ShapeDtypeStruct((rows_n, units), BF16),
            jax.ShapeDtypeStruct((2, model, units), BF16),
            jax.ShapeDtypeStruct((units, model), BF16),
        ],
        in_specs=[vmem] * 4 + [anywhere] * (3 + len(ups)),
        out_specs=[vmem] * 4 + [anywhere] * 3,
        scratch_shapes=[
            pltpu.VMEM((model, units), BF16),
            pltpu.VMEM((model, units), BF16),
            pltpu.VMEM((units, model), BF16),
            pltpu.VMEM((rows_n, model), BF16),
            pltpu.VMEM((rows_n, model), BF16),
            pltpu.VMEM((rows_n, units), F32),
            pltpu.VMEM((rows_n, units), BF16),
            pltpu.VMEM((rows_n, units), BF16),
            pltpu.VMEM((rows_n, units), BF16),
            pltpu.VMEM((2, quarter, model), BF16),
            pltpu.VMEM((2, quarter, model), BF16),
            pltpu.VMEM((quarter, model), BF16),
            pltpu.VMEM((quarter, model), BF16),
            pltpu.VMEM((quarter, model), F32),
            pltpu.VMEM((quarter, model), F32),
            pltpu.VMEM((line_rows, model), F32),
            pltpu.VMEM((line_rows, model), BF16),
            pltpu.VMEM((line_rows, model), BF16),
            pltpu.VMEM((line_rows, model), BF16),
            pltpu.VMEM((2 * line_rows, model), BF16),
            dma((3 + len(ups),)),
            dma((1 + 3 * outer,)),
            dma((6,)),
            dma((6,)),
            dma((2, outer)),
            dma((outer,)),
            dma((outer,)),
            dma((outer,)),
            dma((outer,)),
            dma((outer,)),
            dma((outer,)),
            dma((2, outer)),
        ],
        compiler_params=pltpu.CompilerParams(
            collective_id=2, has_side_effects=True, vmem_limit_bytes=58 * 1024 * 1024
        ),
        cost_estimate=pl.CostEstimate(flops=3 * 10**10, bytes_accessed=4 * 10**7, transcendentals=0),
        name="middle",
    )(gated, out_proj, hidden, gain, w_gate, w_up, w_down, *ups)


FFN_CHUNKS = 6


def finish_kernel(
    outer, sides, sp_n, tp_n, streams, width_scale,
    *refs,
):
    MESH = pl.DeviceIdType.MESH
    parts = refs[:streams]
    (part_ref, hidden_ref, scale_ref, gain_ref, middle_ref, sums_ref) = refs[streams : streams + 6]
    both_in, last_in = refs[streams + 6 : streams + 8]
    outs = refs[streams + 8 : 2 * streams + 8]
    grad_out, sums_out, both_out, last_out = refs[2 * streams + 8 : 2 * streams + 12]
    rest = refs[2 * streams + 12 :]
    got = rest[:streams]
    staged = rest[streams : 2 * streams]
    (near_got, far_got, keep_buf, far_stage, sums_got, sums_stage) = rest[2 * streams : 2 * streams + 6]
    rest = rest[2 * streams + 6 :]
    (both_keep, both_got, both_far, last_keep, last_got, last_far) = rest[:6]
    (f_load, f_near_send, f_near_recv, f_far_send, f_far_recv, f_store, f_out_send, f_out_recv) = rest[6:14]
    (reduce_send, reduce_recv, gather_send, gather_recv, pair_send, pair_recv) = rest[14:20]
    tp_send, tp_recv, sums_send, sums_recv = rest[20:]

    sp_i = lax.axis_index("sp")
    tp_i = lax.axis_index("tp")
    line = sp_i // 2
    half = sp_i % 2
    side = tp_i // 2
    core = tp_i % 2
    last = outer - 1

    def sp_at(z, y):
        return (tp_i, z * 2 + y)

    pair_dev = sp_at(line, 1 - half)
    core_dev = (side * 2 + (1 - core), sp_i)
    side_dev = ((1 - side) * 2 + core, sp_i)

    tp_bits = []
    bit = 1
    while bit < tp_n:
        tp_bits.append(bit)
        bit *= 2
    sp_bits = []
    bit = 1
    while bit < sp_n:
        sp_bits.append(bit)
        bit *= 2

    def flip(value, bit):
        return value + bit - 2 * bit * ((value // bit) % 2)

    sum_devs = [(flip(tp_i, b), sp_i) for b in tp_bits] + [(tp_i, flip(sp_i, b)) for b in sp_bits]

    barrier = pltpu.get_barrier_semaphore()
    greeted = [sp_at((line + 1) % outer, half), sp_at((line + outer - 1) % outer, half)] + sum_devs
    for device in greeted:
        pl.semaphore_signal(barrier, inc=1, device_id=device, device_id_type=MESH)
    pl.semaphore_wait(barrier, len(greeted))

    def remote(src, dst, send, recv, device):
        return pltpu.make_async_remote_copy(
            src_ref=src, dst_ref=dst, send_sem=send, recv_sem=recv,
            device_id=device, device_id_type=MESH,
        )

    places = (line, last - line)
    nexts = (sp_at(jnp.minimum(line + 1, last), half), sp_at(jnp.maximum(line - 1, 0), half))
    signs = (1, -1)

    def rows_of(stream, index):
        count = parts[stream].shape[0] // outer
        return pl.ds(pl.multiple_of(index * count, count), count)

    def reduce_copy(stream, way, step, src):
        return remote(
            src, got[stream].at[way, step - 1], reduce_send.at[stream, way, step - 1],
            reduce_recv.at[stream, way, step - 1], nexts[way],
        )

    def clamp(index):
        return jnp.clip(index, 0, last)

    def reduce_step(stream, step):
        for way in range(2):
            place, sign = places[way], signs[way]
            target = clamp(line + sign * (outer - step))
            own = parts[stream].at[rows_of(stream, target), :]

            @pl.when(place == 0)
            def _():
                reduce_copy(stream, way, step, own).start()

            if step > 1:

                @pl.when((place > 0) & (place <= step - 1))
                def _():
                    reduce_copy(stream, way, step - 1, own).wait_recv()
                    stage = staged[stream].at[way, step - 2]
                    stage[...] = (
                        got[stream][way, step - 2].astype(F32) + own[...].astype(F32)
                    ).astype(BF16)
                    reduce_copy(stream, way, step, stage).start()

    def gather_copy(stream, way, step, origin):
        block = outs[stream].at[half, rows_of(stream, origin), :]
        return remote(
            block, block, gather_send.at[stream, way, step - 1],
            gather_recv.at[stream, way, step - 1], nexts[way],
        )

    def pair_copy(stream, slot, origin):
        block = outs[stream].at[half, rows_of(stream, origin), :]
        return remote(block, block, pair_send.at[stream, slot], pair_recv.at[stream, slot], pair_dev)

    def reduce_final(stream):
        own = parts[stream].at[rows_of(stream, line), :]
        block = outs[stream].at[half, rows_of(stream, line), :]
        for way in range(2):

            @pl.when(places[way] > 0)
            def _():
                reduce_copy(stream, way, last, own).wait_recv()

        up = jnp.where(line > 0, got[stream][0, last - 1].astype(F32), 0.0)
        down = jnp.where(line < last, got[stream][1, last - 1].astype(F32), 0.0)
        block[...] = (own[...].astype(F32) + up + down).astype(BF16)
        for way in range(2):

            @pl.when(places[way] < last)
            def _():
                gather_copy(stream, way, 1, line).start()

        pair_copy(stream, 0, line).start()

    def gather_step(stream, step):
        for way in range(2):
            place, sign = places[way], signs[way]
            origin = clamp(line - sign * step)

            @pl.when(place >= step)
            def _():
                gather_copy(stream, way, step, origin).wait_recv()
                if step < last:

                    @pl.when(place < last)
                    def _():
                        gather_copy(stream, way, step + 1, origin).start()

                pair_copy(stream, 1 + way * last + step - 1, origin).start()

    def drain(stream):
        pair_copy(stream, 0, line).wait()
        for way in range(2):
            place, sign = places[way], signs[way]
            for step in range(1, outer):
                origin = clamp(line - sign * step)

                @pl.when(place <= step - 1)
                def _():
                    reduce_copy(stream, way, step, parts[stream].at[rows_of(stream, 0), :]).wait_send()

                @pl.when((place >= step - 1) & (place < last))
                def _():
                    gather_copy(stream, way, step, origin).wait_send()

                @pl.when(place >= step)
                def _():
                    pair_copy(stream, 1 + way * last + step - 1, origin).wait()

    def near_copy(index):
        return remote(
            part_ref.at[index, 1 - core], near_got.at[index], tp_send.at[index], tp_recv.at[index],
            core_dev,
        )

    def far_copy():
        return remote(far_stage, far_got, tp_send.at[sides], tp_recv.at[sides], side_dev)

    def spread_copy(slot, s, device):
        block = grad_out.at[s, core]
        return remote(block, block, tp_send.at[sides + slot], tp_recv.at[sides + slot], device)

    def input_step(step):
        if step == 0:
            for index in range(sides):
                near_copy(index).start()
        if step == 1:
            for index in range(sides):
                near_copy(index).wait_recv()
            keep_buf[...] = part_ref[side, core].astype(F32) + near_got[side].astype(F32)
            far_stage[...] = (
                part_ref[1 - side, core].astype(F32) + near_got[1 - side].astype(F32)
            ).astype(BF16)
            far_copy().start()
        if step == 2:
            far_copy().wait_recv()
            incoming = keep_buf[...] + far_got[...].astype(F32)
            values = hidden_ref[...].astype(F32)
            scales = scale_ref[...]
            weighted = incoming * gain_ref[...]
            inner_sum = jnp.sum(weighted * values, axis=-1, keepdims=True)
            grads = scales * weighted - values * (scales * scales * scales) * inner_sum * width_scale
            grad_out[side, core] = (middle_ref[...] + grads).astype(BF16)
            spread_copy(1, side, side_dev).start()
            spread_copy(2, side, core_dev).start()
        if step == 3:
            spread_copy(1, side, side_dev).wait_recv()
            spread_copy(3, 1 - side, core_dev).start()
        if step == 4:
            spread_copy(2, side, core_dev).wait_recv()
            spread_copy(3, 1 - side, core_dev).wait_recv()
            for index in range(sides):
                near_copy(index).wait_send()
            far_copy().wait_send()
            spread_copy(1, side, side_dev).wait_send()
            spread_copy(2, side, core_dev).wait_send()
            spread_copy(3, 1 - side, core_dev).wait_send()

    both_half = both_keep.shape[1]
    last_half = last_keep.shape[0]

    def ffn_at(j, refs, whole, owner):
        if j < 4:
            count = both_half // 2
            start = (j % 2) * count
            if whole:
                start = pl.multiple_of(owner * both_half + start, count)
            return refs[0].at[j // 2, pl.ds(start, count), :]
        count = last_half // 2
        start = (j - 4) * count
        if whole:
            start = pl.multiple_of(owner * last_half + start, count)
        return refs[1].at[pl.ds(start, count), :]

    ffn_in = (both_in, last_in)
    ffn_out = (both_out, last_out)

    def ffn_keep(j):
        return ffn_at(j, (both_keep, last_keep), False, 0)

    def ffn_got(j):
        return ffn_at(j, (both_got, last_got), False, 0)

    def ffn_far(j):
        return ffn_at(j, (both_far, last_far), False, 0)

    def ffn_load(j):
        return pltpu.make_async_copy(ffn_at(j, ffn_in, True, core), ffn_keep(j), f_load.at[j])

    def ffn_near_copy(j):
        return remote(
            ffn_at(j, ffn_in, True, 1 - core), ffn_got(j), f_near_send.at[j], f_near_recv.at[j], core_dev
        )

    def ffn_far_copy(j):
        return remote(ffn_keep(j), ffn_far(j), f_far_send.at[j], f_far_recv.at[j], side_dev)

    def ffn_store(j):
        return pltpu.make_async_copy(ffn_got(j), ffn_at(j, ffn_out, True, core), f_store.at[j])

    def ffn_out_copy(j):
        return remote(
            ffn_got(j), ffn_at(j, ffn_out, True, core), f_out_send.at[j], f_out_recv.at[j], core_dev
        )

    def ffn_sum(j):
        ffn_load(j).wait()
        ffn_near_copy(j).wait_recv()
        keep = ffn_keep(j)
        keep[...] = (keep[...].astype(F32) + ffn_got(j)[...].astype(F32)).astype(BF16)
        ffn_far_copy(j).start()

    def ffn_total(j):
        ffn_far_copy(j).wait_recv()
        total = ffn_keep(j)[...].astype(F32) + ffn_far(j)[...].astype(F32)
        ffn_got(j)[...] = total.astype(BF16)
        ffn_store(j).start()
        ffn_out_copy(j).start()

    def ffn_drain(j):
        ffn_near_copy(j).wait_send()
        ffn_far_copy(j).wait_send()
        ffn_store(j).wait()
        ffn_out_copy(j).wait()

    rounds = len(sum_devs)

    def sums_copy(step):
        src = sums_ref if step == 0 else sums_stage.at[step - 1]
        return remote(
            src, sums_got.at[step], sums_send.at[step], sums_recv.at[step], sum_devs[step]
        )

    def sums_step(step):
        if step > 0:
            sums_copy(step - 1).wait_recv()
            before = sums_ref[...] if step == 1 else sums_stage[step - 2]
            total = before + sums_got[step - 1]
            if step == rounds:
                sums_out[...] = total
            else:
                sums_stage[step - 1] = total
        if step < rounds:
            sums_copy(step).start()
        if step == rounds:
            for index in range(rounds):
                sums_copy(index).wait_send()

    def later(do, *args):
        return functools.partial(do, *args)

    extra = [
        later(input_step, 0), later(input_step, 1), later(ffn_sum, 0), later(ffn_sum, 1),
        later(input_step, 2), later(ffn_sum, 2), later(ffn_sum, 3), later(input_step, 3),
        later(ffn_sum, 4), later(ffn_sum, 5), later(sums_step, 0), later(ffn_total, 0),
        later(sums_step, 1), later(sums_step, 2), later(ffn_total, 1), later(input_step, 4),
        later(sums_step, 3), later(ffn_total, 2), later(sums_step, 4),
    ]
    extra += [later(sums_step, index) for index in range(5, rounds + 1)]
    extra += [later(ffn_total, index) for index in range(3, FFN_CHUNKS)]
    for index in range(FFN_CHUNKS):
        ffn_near_copy(index).start()
        ffn_load(index).start()
    for turn in range(streams + 1):
        for step in range(1, outer + 1):
            if turn < streams:
                if step < outer:
                    reduce_step(turn, step)
                else:
                    reduce_final(turn)
            if turn > 0 and step < outer:
                gather_step(turn - 1, step)
            if extra:
                extra.pop(0)()
    for step in extra:
        step()
    for stream in range(streams):
        drain(stream)
    for index in range(FFN_CHUNKS):
        ffn_drain(index)


def finish(parts, part, hidden, scales, gain, middle, sums, ffn, outer, sp_n, tp_n):
    streams = len(parts)
    sides = tp_n // 2
    quarter, model = hidden.shape
    last = outer - 1
    rounds = (tp_n - 1).bit_length() + (sp_n - 1).bit_length()
    vmem = pl.BlockSpec(memory_space=pltpu.VMEM)
    anywhere = pl.BlockSpec(memory_space=pl.ANY)
    chunk = [(2, last, p.shape[0] // outer, p.shape[1]) for p in parts]
    dma = pltpu.SemaphoreType.DMA
    return pl.pallas_call(
        functools.partial(finish_kernel, outer, sides, sp_n, tp_n, streams, 1.0 / model),
        out_shape=[jax.ShapeDtypeStruct((2,) + p.shape, BF16) for p in parts]
        + [
            jax.ShapeDtypeStruct((sides, 2, quarter, model), BF16),
            jax.ShapeDtypeStruct(sums.shape, F32),
        ]
        + [jax.ShapeDtypeStruct(f.shape, BF16) for f in ffn],
        in_specs=[vmem] * (streams + 6) + [anywhere] * 2,
        out_specs=[vmem] * (streams + 2) + [anywhere] * 2,
        scratch_shapes=[pltpu.VMEM(c, BF16) for c in chunk]
        + [pltpu.VMEM(c, BF16) for c in chunk]
        + [
            pltpu.VMEM((sides, quarter, model), BF16),
            pltpu.VMEM((quarter, model), BF16),
            pltpu.VMEM((quarter, model), F32),
            pltpu.VMEM((quarter, model), BF16),
            pltpu.VMEM((rounds,) + sums.shape, F32),
            pltpu.VMEM((rounds,) + sums.shape, F32),
        ]
        + [pltpu.VMEM((2, ffn[0].shape[1] // 2, ffn[0].shape[2]), BF16)] * 3
        + [pltpu.VMEM((ffn[1].shape[0] // 2, ffn[1].shape[1]), BF16)] * 3
        + [dma((FFN_CHUNKS,))] * 8
        + [dma((streams, 2, last))] * 4
        + [dma((streams, 1 + 2 * last))] * 2
        + [dma((sides + 4,))] * 2
        + [dma((rounds,))] * 2,
        compiler_params=pltpu.CompilerParams(
            collective_id=1, has_side_effects=True, vmem_limit_bytes=60 * 1024 * 1024
        ),
        cost_estimate=pl.CostEstimate(flops=10**9, bytes_accessed=10**8, transcendentals=0),
        name="finish",
    )(*parts, part, hidden, scales, gain, middle, sums, *ffn)


def body(
    hidden,
    segment_ids,
    attn_norm,
    query_proj,
    key_proj,
    value_proj,
    gate_proj,
    output_proj,
    query_norm,
    key_norm,
    ffn_norm,
    ffn_gate,
    ffn_up,
    ffn_down,
    upstream,
):
    rows_dev, model = hidden.shape
    head_width = query_norm.shape[0]
    heads = query_proj.shape[1] // head_width
    groups = key_proj.shape[1] // head_width
    per_group = heads // groups
    group_width = groups * head_width
    sp_n = lax.axis_size("sp")
    tp_n = lax.axis_size("tp")
    outer = sp_n // 2
    sides = tp_n // 2
    quarter = rows_dev // tp_n
    tp_i = lax.axis_index("tp")
    sp_i = lax.axis_index("sp")
    ring_i = sp_i // 2
    pair_i = sp_i % 2
    side_i = tp_i // 2
    core_i = tp_i % 2
    own_first = sp_i * rows_dev
    quarter_first = tp_i * quarter
    scale = 1.0 / math.sqrt(head_width)

    ring_pairs = [(z * 2 + y, ((z + 1) % outer) * 2 + y) for z in range(outer) for y in range(2)]
    pair_pairs = [(i, i ^ 1) for i in range(sp_n)]
    side_pairs = [(i, i ^ 2) for i in range(tp_n)]
    core_pairs = [(i, i ^ 1) for i in range(tp_n)]

    def ring(value):
        return lax.ppermute(value, "sp", ring_pairs)

    def pair(value):
        return lax.ppermute(value, "sp", pair_pairs)

    def side(value):
        return lax.ppermute(value, "tp", side_pairs)

    def core(value):
        return lax.ppermute(value, "tp", core_pairs)

    def gather_sp(block):
        blocks = []
        for k in range(outer):
            blocks.append((block, pair(block)))
            if k < outer - 1:
                block = ring(block)
        return blocks

    def scatter_sp(parts):
        def paired(k):
            return parts[k][0] + pair(parts[k][1].astype(BF16)).astype(F32)

        total = paired(1 % outer)
        for k in range(2, outer + 1):
            total = ring(total.astype(BF16)).astype(F32) + paired(k % outer)
        return total

    first_id = segment_ids[0]
    second_start = jnp.sum((segment_ids == first_id).astype(jnp.int32))
    own_index = own_first + jnp.arange(rows_dev, dtype=jnp.int32)
    own_starts = jnp.where(own_index < second_start, 0, second_start)
    steps_half = jnp.arange(head_width // 2, dtype=F32)
    frequencies = jnp.exp(steps_half * (-2.0 * math.log(THETA) / head_width))
    angles = (own_index - own_starts).astype(F32)[:, None] * frequencies[None, :]
    cosine = jnp.cos(angles)[:, None, :]
    sine = jnp.sin(angles)[:, None, :]

    hidden_full = hidden.astype(F32)
    normed_full, attn_scales = norm_rows(hidden_full, attn_norm)
    normed = normed_full.astype(BF16)
    key_raw = matmul(normed, key_proj).reshape(rows_dev, groups, head_width)
    value_rows = matmul(normed, value_proj).astype(BF16)
    key_normed, key_scales = norm_rows(key_raw, key_norm)
    key_rot = rotary(key_normed, cosine, sine).astype(BF16).reshape(rows_dev, group_width)
    kv_own = jnp.stack([key_rot, value_rows])

    low, high = (outer // 4, 3 * outer // 4) if outer % 4 == 0 else (0, outer)
    reach = high - 1 if low else outer - 1

    def up_pairs(step):
        return [
            (z * 2 + y, (z + 1) * 2 + y)
            for z in range(outer - 1)
            for y in range(2)
            if z + 1 - step >= 0 and (z + 1 - step >= low or z + 1 < high)
        ]

    kv_blocks = []
    travelling = kv_own
    for k in range(reach + 1):
        kv_blocks.append((travelling, pair(travelling)))
        if k < reach:
            travelling = lax.ppermute(travelling, "sp", up_pairs(k + 1))

    query_raw = matmul(normed, query_proj).reshape(rows_dev, heads, head_width)
    gate_raw = matmul(normed, gate_proj)
    query_normed, query_scales = norm_rows(query_raw, query_norm)
    queries = rotary(query_normed, cosine, sine).astype(BF16).reshape(rows_dev, heads * head_width)

    def swap_half(value):
        piece = model // 4
        mine = pair(lax.dynamic_slice_in_dim(value, ((1 - pair_i) * 2 + core_i) * piece, piece, 1))
        near = core(mine)
        return jnp.where(
            core_i == 1, jnp.concatenate([near, mine], 1), jnp.concatenate([mine, near], 1)
        )

    normed_own = lax.dynamic_slice_in_dim(normed, pair_i * (model // 2), model // 2, 1)
    both_normed = jnp.concatenate([normed_own, swap_half(normed)])

    grad_quarter = lax.dynamic_slice_in_dim(upstream, quarter_first, quarter)
    up_blocks = gather_sp(grad_quarter)

    row_start_low = own_starts[0]
    row_start_high = own_starts[-1]

    def block_info(k):
        shards = [(ring_i - k) * 2 + pair_i, (ring_i - k) * 2 + (1 - pair_i)]
        entries = [own_first] + [shard * rows_dev for shard in shards]
        live = []
        full = []
        for shard in shards:
            token = shard * rows_dev
            live.append((shard >= 0) & (shard <= sp_i) & (token + rows_dev - 1 >= row_start_low))
            full.append((token >= row_start_high) & (shard < sp_i))
        return jnp.stack(entries + [v.astype(jnp.int32) for v in live + full]).astype(jnp.int32)

    infos = [block_info(k) for k in range(reach + 1)]
    starts_column = own_starts[:, None]
    starts_row = own_starts[None, :]
    carried = None
    for k in range(reach + 1):
        carried = attn_forward(
            infos[k], starts_column, queries, kv_blocks[k][0], kv_blocks[k][1], carried, scale
        )
    mix_acc, mix_sum = carried
    mixed = mix_acc / mix_sum
    lse = jnp.log2(mix_sum.reshape(rows_dev, heads, head_width)[:, :, 0])
    lse_rows = lse.T.reshape(groups, per_group, rows_dev)
    gate_sig = jax.nn.sigmoid(gate_raw)
    gated = (mixed * gate_sig).astype(BF16)
    gated_other = pair(gated)

    def scatter_tp(part):
        part = part.reshape(sides, 2, quarter, model)
        keep = lax.dynamic_index_in_dim(part, core_i, 1, keepdims=False)
        send = lax.dynamic_index_in_dim(part, 1 - core_i, 1, keepdims=False)
        keep = keep + core(send.astype(BF16)).astype(F32)
        mine = lax.dynamic_index_in_dim(keep, side_i, 0, keepdims=False)
        other = lax.dynamic_index_in_dim(keep, 1 - side_i, 0, keepdims=False)
        return mine + side(other.astype(BF16)).astype(F32)

    def gather_tp(block):
        far = side(block)
        swap_side = side_i == 1
        two = jnp.where(swap_side, jnp.stack([far, block]), jnp.stack([block, far]))
        near = core(two)
        swap_core = core_i == 1
        full = jnp.where(
            swap_core, jnp.stack([near, two], axis=1), jnp.stack([two, near], axis=1)
        )
        return full.reshape((rows_dev,) + block.shape[1:])

    fused = outer * quarter <= 512 and outer > 1 and tp_n == 4
    if fused:
        middle, grad_middle_quarter, ffn_gain_sum, branch, inner_rows, *ffn_parts = middle_layer(
            gated,
            output_proj,
            lax.dynamic_slice_in_dim(hidden, quarter_first, quarter),
            ffn_norm[None, :],
            ffn_gate,
            ffn_up,
            ffn_down,
            [block for both in up_blocks for block in both],
            outer,
            sides,
        )
        grad_branch = branch.reshape(rows_dev, model)
        ffn_gain_sum = ffn_gain_sum[0]
        inner_list = [
            inner_rows[k * 2 * quarter : (k + 1) * 2 * quarter] for k in range(outer)
        ]
    else:
        attn_quarter = scatter_tp(matmul(gated, output_proj))
        hidden_quarter = lax.dynamic_slice_in_dim(hidden, quarter_first, quarter).astype(F32)
        middle = hidden_quarter + attn_quarter
        normed_two_full, ffn_scales = norm_rows(middle, ffn_norm)
        normed_two = normed_two_full.astype(BF16)

        two_blocks = gather_sp(normed_two)
        rows_list, up_list, inner_list, gate_list, grad_up_list = [None] * outer, [None] * outer, [None] * outer, [None] * outer, [None] * outer
        grad_parts = [None] * outer
        for k in list(range(1, outer)) + [0]:
            rows_k = jnp.concatenate(two_blocks[k])
            up_k = jnp.concatenate(up_blocks[k])
            gate_vals = matmul(rows_k, ffn_gate)
            up_vals = matmul(rows_k, ffn_up)
            sig = jax.nn.sigmoid(gate_vals)
            grad_inner = times_transpose(up_k, ffn_down)
            grad_gate = (grad_inner * up_vals * (sig * (1.0 + gate_vals * (1.0 - sig)))).astype(BF16)
            grad_up = (grad_inner * (gate_vals * sig)).astype(BF16)
            inner = (gate_vals * sig * up_vals).astype(BF16)
            grad_parts[k] = (
                times_transpose(grad_gate, ffn_gate) + times_transpose(grad_up, ffn_up)
            ).reshape(2, quarter, model)
            rows_list[k], up_list[k], inner_list[k] = rows_k, up_k, inner
            gate_list[k], grad_up_list[k] = grad_gate, grad_up
        grad_two = scatter_sp(grad_parts)

        norm_grad_two, ffn_gain_terms = norm_back(middle, ffn_scales, ffn_norm, grad_two)
        grad_middle_quarter = grad_quarter.astype(F32) + norm_grad_two
        grad_branch = gather_tp(grad_middle_quarter.astype(BF16))
        ffn_gain_sum = jnp.sum(ffn_gain_terms, axis=0)

    mlp_parts = [matmul(inner_list[k], ffn_down).reshape(2, quarter, model) for k in range(outer)]
    mlp_quarter = scatter_sp(mlp_parts)
    layer_out = gather_tp((middle + mlp_quarter).astype(BF16))

    if not fused:
        rows_all = jnp.concatenate(rows_list)
        up_all = jnp.concatenate(up_list)
        inner_all = jnp.concatenate(inner_list)
        gate_all = jnp.concatenate(gate_list)
        grad_up_all = jnp.concatenate(grad_up_list)
        ffn_parts = [
            jnp.stack([outer_sum(rows_all, gate_all), outer_sum(rows_all, grad_up_all)]),
            outer_sum(inner_all, up_all),
        ]
    ffn_parts = [part.astype(BF16) for part in ffn_parts]

    branch_other = swap_half(grad_branch)
    branch_own = lax.dynamic_slice_in_dim(grad_branch, pair_i * (model // 2), model // 2, 1)
    output_half = outer_sum(
        jnp.concatenate([gated, gated_other]), jnp.concatenate([branch_own, branch_other])
    )
    grad_gated = times_transpose(grad_branch, output_proj)
    grad_mixed = (grad_gated * gate_sig).astype(BF16)
    grad_gate_raw = (grad_gated * mixed * (gate_sig * (1.0 - gate_sig))).astype(BF16)
    gate_half = outer_sum(both_normed, jnp.concatenate([grad_gate_raw, pair(grad_gate_raw)]))
    deltas = jnp.sum(
        (grad_mixed.astype(F32) * mixed).reshape(rows_dev, heads, head_width), axis=-1
    )
    delta_rows = deltas.T.reshape(groups, per_group, rows_dev)

    def down_pairs(step):
        return [(b, a) for a, b in up_pairs(step)]

    query_acc = None
    travelling = None
    for k in list(range(reach, -1, -1)):
        query_acc, grad_a, grad_b = attn_backward(
            infos[k], starts_row, lse_rows, delta_rows, queries, grad_mixed,
            kv_blocks[k][0], kv_blocks[k][1], query_acc, k == 0, scale,
        )
        total = grad_a.astype(F32) + pair(grad_b).astype(F32)
        if travelling is not None:
            total = total + travelling.astype(F32)
        if k > 0:
            travelling = lax.ppermute(total.astype(BF16), "sp", down_pairs(k))
    grad_key_rot = total[0].reshape(rows_dev, groups, head_width)
    grad_value_low = total[1].astype(BF16)
    grad_query_rot = (query_acc * scale).reshape(rows_dev, heads, head_width)
    grad_query_raw, query_gain_terms = norm_back(
        query_raw, query_scales, query_norm, rotary_back(grad_query_rot, cosine, sine)
    )
    grad_key_raw, key_gain_terms = norm_back(
        key_raw, key_scales, key_norm, rotary_back(grad_key_rot, cosine, sine)
    )
    grad_query_low = grad_query_raw.reshape(rows_dev, heads * head_width).astype(BF16)
    grad_key_low = grad_key_raw.reshape(rows_dev, group_width).astype(BF16)
    grad_kv_low = jnp.concatenate([grad_key_low, grad_value_low], axis=1)

    both_queries = jnp.concatenate([grad_query_low, pair(grad_query_low)])
    both_kv = jnp.concatenate([grad_kv_low, pair(grad_kv_low)])
    parts = [
        output_half.astype(BF16),
        gate_half.astype(BF16),
        outer_sum(both_normed, both_queries).astype(BF16),
        outer_sum(both_normed, both_kv).astype(BF16),
    ]

    grad_normed_part = (
        times_transpose(grad_query_low, query_proj)
        + times_transpose(grad_key_low, key_proj)
        + times_transpose(grad_value_low, value_proj)
        + times_transpose(grad_gate_raw, gate_proj)
    )
    gains = jnp.concatenate(
        [
            jnp.sum(grad_normed_part * hidden_full * attn_scales, axis=0),
            ffn_gain_sum,
            jnp.sum(query_gain_terms, axis=(0, 1)),
            jnp.sum(key_gain_terms, axis=(0, 1)),
        ]
    )
    gains_at = 2 * model + 2 * head_width
    gains = jnp.pad(gains, (0, -gains_at % 1024)).reshape(-1, 128)
    scales_quarter = lax.dynamic_slice_in_dim(attn_scales, quarter_first, quarter)
    finished = finish(
        parts,
        grad_normed_part.astype(BF16).reshape(sides, 2, quarter, model),
        lax.dynamic_slice_in_dim(hidden, quarter_first, quarter),
        scales_quarter,
        attn_norm[None, :],
        grad_middle_quarter,
        gains,
        ffn_parts,
        outer,
        sp_n,
        tp_n,
    )
    output_all, gate_all_w, query_all, kv_all, input_all, gains, ffn_both, ffn_last = finished
    output_grad = jnp.concatenate([output_all[0], output_all[1]], axis=1).astype(F32)
    gate_grad = gate_all_w.reshape(model, heads * head_width).astype(F32)
    query_grad = query_all.reshape(model, heads * head_width).astype(F32)
    kv_all = kv_all.reshape(model, 2 * group_width)
    key_grad = kv_all[:, :group_width].astype(F32)
    value_grad = kv_all[:, group_width:].astype(F32)
    hidden_grad = input_all.reshape(rows_dev, model).astype(F32)
    gains = gains.reshape(-1)
    return (
        layer_out,
        hidden_grad,
        gains[:model],
        query_grad,
        key_grad,
        value_grad,
        gate_grad,
        output_grad,
        gains[2 * model : 2 * model + head_width],
        gains[2 * model + head_width : gains_at],
        gains[model : 2 * model],
        ffn_both[0].astype(F32),
        ffn_both[1].astype(F32),
        ffn_last.astype(F32),
    )


def solution(mesh):
    placed = (
        P("sp", None),
        P(),
        P(),
        P(None, "tp"),
        P(None, "tp"),
        P(None, "tp"),
        P(None, "tp"),
        P("tp", None),
        P(),
        P(),
        P(),
        P(None, "sp"),
        P(None, "sp"),
        P("sp", None),
        P("sp", None),
    )
    return jax.shard_map(
        body,
        mesh=mesh,
        in_specs=placed,
        out_specs=(
            P("sp", None),
            P("sp", None),
            P(),
            P(None, "tp"),
            P(None, "tp"),
            P(None, "tp"),
            P(None, "tp"),
            P("tp", None),
            P(),
            P(),
            P(),
            P(None, "sp"),
            P(None, "sp"),
            P("sp", None),
        ),
        check_vma=False,
    )
```

```python
import functools
import math

import jax
import jax.numpy as jnp
from jax import lax
from jax.experimental import pallas as pl
from jax.experimental.pallas import tpu as pltpu
from jax.sharding import PartitionSpec as P

EPSILON = 1e-06
THETA = 1000000.0
LOG2E = 1.4426950408889634
F32 = jnp.float32
BF16 = jnp.bfloat16


def norm_scales(values):
    return lax.rsqrt(jnp.mean(values * values, axis=-1, keepdims=True) + EPSILON)


def norm_rows(values, gain):
    scales = norm_scales(values)
    return (values * scales * gain, scales)


def norm_back(values, scales, gain, incoming):
    weighted = incoming * gain
    inner_sum = jnp.sum(weighted * values, axis=-1, keepdims=True)
    grad_values = (
        scales * weighted - values * (scales * scales * scales) * inner_sum / values.shape[-1]
    )
    return (grad_values, incoming * values * scales)


def rotary(values, cosine, sine):
    half_width = values.shape[-1] // 2
    front_half = values[..., :half_width]
    back_half = values[..., half_width:]
    return jnp.concatenate(
        [front_half * cosine - back_half * sine, back_half * cosine + front_half * sine], axis=-1
    )


def rotary_back(grads, cosine, sine):
    half_width = grads.shape[-1] // 2
    front_half = grads[..., :half_width]
    back_half = grads[..., half_width:]
    return jnp.concatenate(
        [front_half * cosine + back_half * sine, back_half * cosine - front_half * sine], axis=-1
    )


def matmul(left, right):
    return jnp.dot(left, right, preferred_element_type=F32)


def outer_sum(left, right):
    return lax.dot_general(left, right, (((0,), (0,)), ((), ())), preferred_element_type=F32)


def times_transpose(left, right):
    return lax.dot_general(left, right, (((1,), (1,)), ((), ())), preferred_element_type=F32)


def attn_forward_kernel(first, diagonal, scale, info, starts, queries, kv_a, kv_b, *rest):
    if first:
        acc_out, sum_out = rest
    else:
        acc_in, sum_in, acc_out, sum_out = rest
    rows = queries.shape[0]
    keys_n = kv_a.shape[1]
    per_group = queries.shape[1] // kv_a.shape[2]
    width = kv_a.shape[2]
    if first:
        acc_out[...] = jnp.zeros_like(acc_out)
        sum_out[...] = jnp.zeros_like(sum_out)
    else:
        acc_out[...] = acc_in[...]
        sum_out[...] = sum_in[...]
    own_first = info[0]
    for slot, block in enumerate((kv_a, kv_b)):
        key_first = info[1 + slot]
        live = info[3 + slot] > 0

        def work(masked, causal):
            ones = jnp.ones((keys_n, width), BF16)
            values = jnp.concatenate([block[1], ones], axis=1)
            keys = block[0]
            if masked:
                key_index = key_first + lax.broadcasted_iota(jnp.int32, (rows, keys_n), 1)
                allowed = key_index >= starts[...]
                if causal:
                    row_index = own_first + lax.broadcasted_iota(jnp.int32, (rows, keys_n), 0)
                    allowed = allowed & (key_index <= row_index)
            for head in range(per_group):
                cols = slice(head * width, (head + 1) * width)
                scores = times_transpose(queries[:, cols], keys)
                weights = jnp.exp2(scores * (scale * LOG2E))
                if masked:
                    weights = jnp.where(allowed, weights, 0.0)
                both = matmul(weights.astype(BF16), values)
                acc_out[:, cols] += both[:, :width]
                sum_out[:, cols] += both[:, width:]

        if diagonal and slot == 0:
            work(True, True)
        else:
            full = info[5 + slot] > 0
            pl.when(live & full)(functools.partial(work, False, False))
            pl.when(live & jnp.logical_not(full))(functools.partial(work, True, False))


def attn_forward(info, starts, queries, kv_a, kv_b, carried, scale):
    rows, all_width = queries.shape
    width = 128
    groups = kv_a.shape[2] // width
    group_width = all_width // groups
    keys_n = kv_a.shape[1]
    first = carried is None
    spec_q = pl.BlockSpec((rows, group_width), lambda g, info: (0, g))
    spec_kv = pl.BlockSpec((2, keys_n, width), lambda g, info: (0, 0, g))
    specs = [pl.BlockSpec((rows, 1), lambda g, info: (0, 0)), spec_q, spec_kv, spec_kv]
    operands = [starts, queries, kv_a, kv_b]
    if not first:
        specs += [spec_q, spec_q]
        operands += list(carried)
    return pl.pallas_call(
        functools.partial(attn_forward_kernel, first, first, scale),
        grid_spec=pltpu.PrefetchScalarGridSpec(
            num_scalar_prefetch=1,
            grid=(groups,),
            in_specs=specs,
            out_specs=[spec_q, spec_q],
        ),
        out_shape=[jax.ShapeDtypeStruct((rows, all_width), F32)] * 2,
        compiler_params=pltpu.CompilerParams(dimension_semantics=("arbitrary",)),
        cost_estimate=pl.CostEstimate(
            flops=16 * rows * keys_n * all_width,
            transcendentals=2 * rows * keys_n * all_width // width,
            bytes_accessed=8 * rows * all_width,
        ),
        name="attn_forward",
    )(info, *operands)


def attn_backward_kernel(first, diagonal, scale, info, starts, lse, deltas, queries, grads, kv_a, kv_b, *rest):
    if first:
        grad_q, grad_a, grad_b = rest
    else:
        grad_in, grad_q, grad_a, grad_b = rest
    rows = queries.shape[0]
    keys_n = kv_a.shape[1]
    width = kv_a.shape[2]
    per_group = queries.shape[1] // width
    if first:
        grad_q[...] = jnp.zeros_like(grad_q)
    else:
        grad_q[...] = grad_in[...]
    own_first = info[0]
    for slot, (block, out) in enumerate(((kv_a, grad_a), (kv_b, grad_b))):
        key_first = info[1 + slot]
        live = info[3 + slot] > 0

        def work(masked, causal):
            keys = block[0]
            values = block[1]
            keys_t = keys.T
            if masked:
                key_index = key_first + lax.broadcasted_iota(jnp.int32, (keys_n, rows), 0)
                allowed = key_index >= starts[...]
                if causal:
                    row_index = own_first + lax.broadcasted_iota(jnp.int32, (keys_n, rows), 1)
                    allowed = allowed & (key_index <= row_index)
            total_k = jnp.zeros((keys_n, width), F32)
            total_v = jnp.zeros((keys_n, width), F32)
            for head in range(per_group):
                cols = slice(head * width, (head + 1) * width)
                q_head = queries[:, cols]
                g_head = grads[:, cols]
                scores = times_transpose(keys, q_head)
                probs = jnp.exp2(scores * (scale * LOG2E) - lse[0, head : head + 1, :])
                if masked:
                    probs = jnp.where(allowed, probs, 0.0)
                grad_probs = times_transpose(values, g_head)
                grad_scores = (probs * (grad_probs - deltas[0, head : head + 1, :])).astype(BF16)
                total_v += matmul(probs.astype(BF16), g_head)
                total_k += matmul(grad_scores, q_head)
                grad_q[:, cols] += matmul(keys_t, grad_scores).T
            out[0] = (total_k * scale).astype(BF16)
            out[1] = total_v.astype(BF16)

        if diagonal and slot == 0:
            work(True, True)
        else:
            full = info[5 + slot] > 0
            pl.when(live & full)(functools.partial(work, False, False))
            pl.when(live & jnp.logical_not(full))(functools.partial(work, True, False))

            @pl.when(jnp.logical_not(live))
            def _():
                out[...] = jnp.zeros_like(out)


def attn_backward(info, starts_row, lse, deltas, queries, grads, kv_a, kv_b, carried, diagonal, scale):
    rows, all_width = queries.shape
    width = 128
    groups = kv_a.shape[2] // width
    group_width = all_width // groups
    per_group = group_width // width
    keys_n = kv_a.shape[1]
    first = carried is None
    spec_q = pl.BlockSpec((rows, group_width), lambda g, info: (0, g))
    spec_kv = pl.BlockSpec((2, keys_n, width), lambda g, info: (0, 0, g))
    spec_row = pl.BlockSpec((1, per_group, rows), lambda g, info: (g, 0, 0))
    specs = [
        pl.BlockSpec((1, rows), lambda g, info: (0, 0)),
        spec_row,
        spec_row,
        spec_q,
        spec_q,
        spec_kv,
        spec_kv,
    ]
    operands = [starts_row, lse, deltas, queries, grads, kv_a, kv_b]
    if not first:
        specs.append(spec_q)
        operands.append(carried)
    return pl.pallas_call(
        functools.partial(attn_backward_kernel, first, diagonal, scale),
        grid_spec=pltpu.PrefetchScalarGridSpec(
            num_scalar_prefetch=1,
            grid=(groups,),
            in_specs=specs,
            out_specs=[spec_q, spec_kv, spec_kv],
        ),
        out_shape=[
            jax.ShapeDtypeStruct((rows, all_width), F32),
            jax.ShapeDtypeStruct(kv_a.shape, BF16),
            jax.ShapeDtypeStruct(kv_a.shape, BF16),
        ],
        compiler_params=pltpu.CompilerParams(dimension_semantics=("arbitrary",)),
        cost_estimate=pl.CostEstimate(
            flops=20 * rows * keys_n * all_width,
            transcendentals=2 * rows * keys_n * all_width // width,
            bytes_accessed=8 * rows * all_width,
        ),
        name="attn_backward",
    )(info, *operands)


def middle_kernel(outer, *refs):
    MESH = pl.DeviceIdType.MESH
    blocks = 2 * outer
    (gated, out_proj, hidden_ref, gain_ref, gate_in, up_in, down_in) = refs[:7]
    ups_in = refs[7 : 7 + blocks]
    (layer_out, grad_out, gain_out, branch, dw_both, dw_down) = refs[7 + blocks : 13 + blocks]
    (
        w_gate, w_up, w_down, ups, rows, inner, grad_gate, grad_up,
        near_buf, far_stage, far_got, middle_buf,
        keep, y_stage, y_got, z_stage, z_got, part_got, part_far,
        load_sem, store_sem, tp_send, tp_recv, zs, zr, ys, yr, rys, ryr, rzs, rzr,
        p_near_send, p_near_recv, p_far_send, p_far_recv, p_out_send, p_out_recv,
    ) = refs[13 + blocks :]
    stage_gate, stage_up, stage_down = w_gate, w_up, rows
    far_keep, own_keep = grad_out, middle_buf
    units = w_down.shape[0]
    quarter, model = hidden_ref.shape
    group = 2 * quarter
    chunk = model // outer
    last = outer - 1

    sp_i = lax.axis_index("sp")
    tp_i = lax.axis_index("tp")
    line = sp_i // 2
    half = sp_i % 2
    side = tp_i // 2
    core = tp_i % 2

    def sp_at(z, y):
        return (tp_i, z * 2 + y)

    pair_dev = sp_at(line, 1 - half)
    core_dev = (side * 2 + (1 - core), sp_i)
    side_dev = ((1 - side) * 2 + core, sp_i)
    nexts = (sp_at(jnp.minimum(line + 1, last), half), sp_at(jnp.maximum(line - 1, 0), half))

    loads = [
        pltpu.make_async_copy(src, dst, load_sem.at[index])
        for index, (src, dst) in enumerate(
            [(down_in, w_down)]
            + [(ups_in[b], ups.at[pl.ds(b * quarter, quarter), :]) for b in range(blocks)]
            + [(gate_in, w_gate), (up_in, w_up)]
        )
    ]
    for load in loads:
        load.start()

    barrier = pltpu.get_barrier_semaphore()
    greeted = [
        sp_at((line + 1) % outer, half), sp_at((line + outer - 1) % outer, half),
        pair_dev, core_dev, side_dev,
    ]
    for device in greeted:
        pl.semaphore_signal(barrier, inc=1, device_id=device, device_id_type=MESH)
    pl.semaphore_wait(barrier, len(greeted))

    def remote(src, dst, send, recv, device):
        return pltpu.make_async_remote_copy(
            src_ref=src, dst_ref=dst, send_sem=send, recv_sem=recv,
            device_id=device, device_id_type=MESH,
        )

    def aligned(index, count):
        return pl.ds(pl.multiple_of(index * count, count), count)

    def near_copy(j):
        return remote(near_buf.at[j], near_buf.at[2 + j], tp_send.at[j], tp_recv.at[j], core_dev)

    def far_copy():
        return remote(far_stage, far_got, tp_send.at[2], tp_recv.at[2], side_dev)

    def projected(s, c):
        return matmul(gated[aligned(s * 2 + c, quarter), :], out_proj[...])

    near_buf[0] = projected(1 - side, 1 - core).astype(BF16)
    near_copy(0).start()
    near_buf[1] = projected(side, 1 - core).astype(BF16)
    near_copy(1).start()
    far_keep[...] = projected(1 - side, core)
    near_copy(0).wait_recv()
    far_stage[...] = (far_keep[...] + near_buf[2].astype(F32)).astype(BF16)
    far_copy().start()
    own_keep[...] = projected(side, core)

    near_copy(1).wait_recv()
    far_copy().wait_recv()
    middle = hidden_ref[...].astype(F32) + (
        own_keep[...] + near_buf[3].astype(F32) + far_got[...].astype(F32)
    )
    middle_buf[...] = middle
    rows[0:quarter, :] = (middle * norm_scales(middle) * gain_ref[...]).astype(BF16)

    def entry(k, j):
        return pl.ds(pl.multiple_of((k * 2 + j) * quarter, quarter), quarter)

    def wrap(k):
        return (k + outer) % outer

    def z_copy(way, k):
        to = wrap(k + 1 - 2 * way)
        return remote(
            rows.at[entry(k, 0), :], rows.at[entry(to, 0), :], zs.at[way, k], zr.at[to], nexts[way]
        )

    def z_arrived(k):
        return remote(
            rows.at[entry(k, 0), :], rows.at[entry(k, 0), :], zs.at[0, k], zr.at[k], nexts[0]
        )

    def y_copy(k):
        return remote(
            rows.at[entry(k, 0), :], rows.at[entry(k, 1), :], ys.at[k], yr.at[k], pair_dev
        )

    short = jnp.minimum(line, last - line)

    def delta_of(i):
        near = jnp.where(i % 2 == 1, -((i + 1) // 2), (i + 1) // 2)
        far = jnp.where(line < last - line, i - short, short - i)
        return jnp.where(i <= 2 * short, near, far)

    def slot_of(delta):
        return jnp.where(delta <= 0, -delta, outer - delta)

    for way, exists in ((0, line < last), (1, line > 0)):
        pl.when(exists)(z_copy(way, 0).start)
    y_copy(0).start()

    def goes_on(delta):
        return ((delta < 0) & (line < last), (delta > 0) & (line > 0))

    def forward(i):
        delta = delta_of(i)
        k = slot_of(delta)
        z_arrived(k).wait_recv()
        for way, exists in enumerate(goes_on(delta)):
            pl.when(exists)(z_copy(way, k).start)
        y_copy(k).start()

    for load in loads:
        load.wait()
    forward(1)

    def turn_forward(i, carry):
        @pl.when(i + 2 < outer)
        def _():
            forward(i + 2)

        k = slot_of(delta_of(i))
        y_copy(k).wait_recv()
        at = aligned(k, group)
        rows_k = rows[at, :]
        gate_vals = matmul(rows_k, w_gate[...])
        up_vals = matmul(rows_k, w_up[...])
        incoming = times_transpose(ups[at, :], w_down[...])
        sig = jax.nn.sigmoid(gate_vals)
        silu = gate_vals * sig
        grad_gate[at, :] = (incoming * up_vals * (sig * (1.0 + gate_vals * (1.0 - sig)))).astype(BF16)
        grad_up[at, :] = (incoming * silu).astype(BF16)
        inner[at, :] = (silu * up_vals).astype(BF16)
        return carry

    lax.fori_loop(0, outer, turn_forward, 0)

    near_copy(0).wait_send()
    near_copy(1).wait_send()

    def y_sum(which, k):
        at = aligned(k, quarter)
        src = y_stage.at[at, :] if which == 0 else near_buf.at[k]
        got = y_got.at[aligned(which * outer + k, quarter), :]
        return remote(src, got, rys.at[which, k], ryr.at[which, k], pair_dev)

    def half_rows(k, j):
        return pl.ds(pl.multiple_of((k * 2 + j) * quarter, quarter), quarter)

    def turn_parts(step, carry):
        k = slot_of(delta_of(last - step))
        part = times_transpose(grad_gate[half_rows(k, 1), :], w_gate[...]) + times_transpose(
            grad_up[half_rows(k, 1), :], w_up[...]
        )
        y_stage[aligned(k, quarter), :] = part.astype(BF16)
        y_sum(0, k).start()
        return carry

    def turn_outputs(step, carry):
        k = slot_of(delta_of(last - step))
        near_buf[k] = matmul(inner[half_rows(k, 1), :], w_down[...]).astype(BF16)
        y_sum(1, k).start()
        part = times_transpose(grad_gate[half_rows(k, 0), :], w_gate[...]) + times_transpose(
            grad_up[half_rows(k, 0), :], w_up[...]
        )
        keep[aligned(k, quarter), :] = part.astype(BF16)
        return carry

    lax.fori_loop(0, outer, turn_parts, 0)
    lax.fori_loop(0, outer, turn_outputs, 0)

    def z_got_rows(which, way, k):
        return aligned((which * 2 + way) * outer + k, quarter)

    def z_sum(which, way, k):
        to = wrap(k + 1 - 2 * way)
        return remote(
            z_stage.at[aligned(k, quarter), :], z_got.at[z_got_rows(which, way, to), :],
            rzs.at[which, k], rzr.at[which, way, to], nexts[way],
        )

    def z_got_at(which, way, k):
        return z_got[z_got_rows(which, way, k), :].astype(F32)

    def z_sum_arrived(which, way, k):
        return remote(
            z_stage.at[aligned(k, quarter), :], z_got.at[z_got_rows(which, way, k), :],
            rzs.at[which, k], rzr.at[which, way, k], nexts[way],
        )

    def own_share(which, k):
        if which == 0:
            share = keep[aligned(k, quarter), :].astype(F32)
        else:
            share = matmul(inner[half_rows(k, 0), :], w_down[...])
        return share + y_got[aligned(which * outer + k, quarter), :].astype(F32)

    def chain(which, step):
        delta = delta_of(last - step)
        k = slot_of(delta)
        at = aligned(k, quarter)
        y_sum(which, k).wait_recv()
        own = own_share(which, k)
        if which == 1:
            z_sum(0, 0, k).wait_send()
        for way, (here, before) in enumerate(((delta > 0, line > 0), (delta < 0, line < last))):

            @pl.when(here & before)
            def _():
                z_sum_arrived(which, way, k).wait_recv()
                z_stage[at, :] = (own + z_got_at(which, way, k)).astype(BF16)

            @pl.when(here & jnp.logical_not(before))
            def _():
                z_stage[at, :] = own.astype(BF16)

            pl.when(here)(z_sum(which, way, k).start)

    def chain_end(which):
        y_sum(which, 0).wait_recv()
        own = own_share(which, 0)
        for way, exists in ((0, line > 0), (1, line < last)):
            pl.when(exists)(z_sum_arrived(which, way, 0).wait_recv)
        below = jnp.where(line > 0, z_got_at(which, 0, 0), 0.0)
        above = jnp.where(line < last, z_got_at(which, 1, 0), 0.0)
        return own + below + above

    half_model = model // 2
    piece = half_model // 2

    def stage_rows(owner, r):
        return pl.ds(pl.multiple_of(owner * half_model + r * piece, piece), piece)

    stages = (stage_gate, stage_up)

    def piece_at(ref, a, r):
        return ref.at[a, pl.ds(r * piece, piece), :]

    def piece_near(a, r):
        return remote(
            stages[a].at[stage_rows(1 - core, r), :], piece_at(part_got, a, r),
            p_near_send.at[a, r], p_near_recv.at[a, r], core_dev,
        )

    def piece_far(a, r):
        return remote(
            stages[a].at[stage_rows(core, r), :], piece_at(part_far, a, r),
            p_far_send.at[a, r], p_far_recv.at[a, r], side_dev,
        )

    def piece_store(a, r):
        return pltpu.make_async_copy(
            piece_at(part_got, a, r), dw_both.at[a, stage_rows(core, r), :], store_sem.at[1 + 2 * a + r]
        )

    def piece_out(a, r):
        return remote(
            piece_at(part_got, a, r), dw_both.at[a, stage_rows(core, r), :],
            p_out_send.at[a, r], p_out_recv.at[a, r], core_dev,
        )

    def pieces(mine, r):
        at = stage_rows(core if mine else 1 - core, r)
        some = rows[:, at]
        for a, grads in enumerate((grad_gate, grad_up)):
            stages[a][at, :] = outer_sum(some, grads[...]).astype(BF16)
            if not mine:
                piece_near(a, r).start()

    def pieces_sum(r):
        at = stage_rows(core, r)
        for a in range(2):
            piece_near(a, r).wait_recv()
            stages[a][at, :] = (
                stages[a][at, :].astype(F32) + piece_at(part_got, a, r)[...].astype(F32)
            ).astype(BF16)
            piece_far(a, r).start()

    def pieces_total(r):
        for a in range(2):
            piece_far(a, r).wait_recv()
            total = stages[a][stage_rows(core, r), :].astype(F32) + piece_at(part_far, a, r)[
                ...
            ].astype(F32)
            piece_at(part_got, a, r)[...] = total.astype(BF16)
            piece_store(a, r).start()
            piece_out(a, r).start()

    work = [
        functools.partial(pieces, False, 0), functools.partial(pieces, True, 0),
        functools.partial(pieces_sum, 0), functools.partial(pieces, False, 1),
        functools.partial(pieces, True, 1), functools.partial(pieces_sum, 1),
    ]
    for step in range(last):
        for _ in range(2):
            if work:
                work.pop(0)()
        chain(0, step)
    for some_work in work:
        some_work()
    grad_two = chain_end(0)

    values = middle_buf[...]
    back, gain_terms = norm_back(values, norm_scales(values), gain_ref[...], grad_two)
    grads = ups[0:quarter, :].astype(F32) + back
    branch[side, core] = grads.astype(BF16)

    def spread_copy(slot, s, device):
        block = branch.at[s, core]
        return remote(block, block, tp_send.at[3 + slot], tp_recv.at[3 + slot], device)

    spread_copy(0, side, side_dev).start()
    spread_copy(1, side, core_dev).start()
    grad_out[...] = grads
    gain_out[...] = jnp.sum(gain_terms, axis=0, keepdims=True)

    for way, exists in ((0, line < last), (1, line > 0)):
        pl.when(exists)(z_copy(way, 0).wait_send)

    def turn_sent(i, carry):
        delta = delta_of(i)
        k = slot_of(delta)
        y_copy(k).wait_send()
        for way, exists in enumerate(goes_on(delta)):
            pl.when(exists)(z_copy(way, k).wait_send)
        return carry

    lax.fori_loop(0, outer, turn_sent, 0)

    def turn_down(c, carry):
        at = aligned(c, chunk)
        stage_down[0:units, at] = outer_sum(inner[...], ups[:, at]).astype(BF16)
        return carry

    chain(1, 0)
    lax.fori_loop(0, outer, turn_down, 0)
    down_store = pltpu.make_async_copy(stage_down.at[pl.ds(0, units), :], dw_down, store_sem.at[0])
    down_store.start()
    for step in range(1, last):
        chain(1, step)
    spread_copy(0, side, side_dev).wait_recv()
    spread_copy(2, 1 - side, core_dev).start()
    pieces_total(0)
    layer_out[...] = (middle_buf[...] + chain_end(1)).astype(BF16)
    pieces_total(1)
    spread_copy(1, side, core_dev).wait_recv()

    down_store.wait()
    far_copy().wait_send()

    def turn_drain(i, carry):
        k = slot_of(delta_of(i))
        for which in range(2):
            y_sum(which, k).wait_send()
        pl.when(i > 0)(z_sum(1, 0, k).wait_send)
        return carry

    lax.fori_loop(0, outer, turn_drain, 0)
    for a in range(2):
        for r in range(2):
            piece_near(a, r).wait_send()
            piece_far(a, r).wait_send()
            piece_store(a, r).wait()
            piece_out(a, r).wait()
    spread_copy(0, side, side_dev).wait_send()
    spread_copy(1, side, core_dev).wait_send()
    spread_copy(2, 1 - side, core_dev).wait()


def middle_layer(gated, out_proj, hidden, gain, w_gate, w_up, w_down, ups, outer, sides):
    quarter, model = hidden.shape
    units = w_down.shape[0]
    rows_n = 2 * outer * quarter
    vmem = pl.BlockSpec(memory_space=pltpu.VMEM)
    anywhere = pl.BlockSpec(memory_space=pl.ANY)
    dma = pltpu.SemaphoreType.DMA
    line_rows = outer * quarter
    half = (2, model // 2, units)
    return pl.pallas_call(
        functools.partial(middle_kernel, outer),
        out_shape=[
            jax.ShapeDtypeStruct((quarter, model), BF16),
            jax.ShapeDtypeStruct((quarter, model), F32),
            jax.ShapeDtypeStruct((1, model), F32),
            jax.ShapeDtypeStruct((sides, 2, quarter, model), BF16),
            jax.ShapeDtypeStruct((2, model, units), BF16),
            jax.ShapeDtypeStruct((units, model), BF16),
        ],
        in_specs=[vmem] * 4 + [anywhere] * (3 + len(ups)),
        out_specs=[vmem] * 4 + [anywhere] * 2,
        scratch_shapes=[
            pltpu.VMEM((model, units), BF16),
            pltpu.VMEM((model, units), BF16),
            pltpu.VMEM((units, model), BF16),
            pltpu.VMEM((rows_n, model), BF16),
            pltpu.VMEM((rows_n, model), BF16),
            pltpu.VMEM((rows_n, units), BF16),
            pltpu.VMEM((rows_n, units), BF16),
            pltpu.VMEM((rows_n, units), BF16),
            pltpu.VMEM((4, quarter, model), BF16),
            pltpu.VMEM((quarter, model), BF16),
            pltpu.VMEM((quarter, model), BF16),
            pltpu.VMEM((quarter, model), F32),
            pltpu.VMEM((line_rows, model), BF16),
            pltpu.VMEM((line_rows, model), BF16),
            pltpu.VMEM((2 * line_rows, model), BF16),
            pltpu.VMEM((line_rows, model), BF16),
            pltpu.VMEM((4 * line_rows, model), BF16),
            pltpu.VMEM(half, BF16),
            pltpu.VMEM(half, BF16),
            dma((3 + len(ups),)),
            dma((5,)),
            dma((6,)),
            dma((6,)),
            dma((2, outer)),
            dma((outer,)),
            dma((outer,)),
            dma((outer,)),
            dma((2, outer)),
            dma((2, outer)),
            dma((2, outer)),
            dma((2, 2, outer)),
        ]
        + [dma((2, 2))] * 6,
        compiler_params=pltpu.CompilerParams(
            collective_id=2, has_side_effects=True, vmem_limit_bytes=63 * 1024 * 1024
        ),
        cost_estimate=pl.CostEstimate(flops=3 * 10**10, bytes_accessed=4 * 10**7, transcendentals=0),
        name="middle",
    )(gated, out_proj, hidden, gain, w_gate, w_up, w_down, *ups)


FFN_CHUNKS = 2


def finish_kernel(
    outer, sides, sp_n, tp_n, streams, width_scale,
    *refs,
):
    MESH = pl.DeviceIdType.MESH
    parts = refs[:streams]
    (part_ref, hidden_ref, scale_ref, gain_ref, middle_ref, sums_ref) = refs[streams : streams + 6]
    last_in, layer_ref = refs[streams + 6 : streams + 8]
    outs = refs[streams + 8 : 2 * streams + 8]
    grad_out, sums_out, last_out, layer_out = refs[2 * streams + 8 : 2 * streams + 12]
    rest = refs[2 * streams + 12 :]
    got = rest[:streams]
    staged = rest[streams : 2 * streams]
    (near_got, far_got, keep_buf, far_stage, sums_got, sums_stage) = rest[2 * streams : 2 * streams + 6]
    rest = rest[2 * streams + 6 :]
    (last_keep, last_got, last_far, layer_send, layer_recv) = rest[:5]
    (f_load, f_near_send, f_near_recv, f_far_send, f_far_recv, f_store, f_out_send, f_out_recv) = rest[5:13]
    (reduce_send, reduce_recv, gather_send, gather_recv, pair_send, pair_recv) = rest[13:19]
    tp_send, tp_recv, sums_send, sums_recv = rest[19:]

    sp_i = lax.axis_index("sp")
    tp_i = lax.axis_index("tp")
    line = sp_i // 2
    half = sp_i % 2
    side = tp_i // 2
    core = tp_i % 2
    last = outer - 1

    def sp_at(z, y):
        return (tp_i, z * 2 + y)

    pair_dev = sp_at(line, 1 - half)
    core_dev = (side * 2 + (1 - core), sp_i)
    side_dev = ((1 - side) * 2 + core, sp_i)

    tp_bits = []
    bit = 1
    while bit < tp_n:
        tp_bits.append(bit)
        bit *= 2
    sp_bits = []
    bit = 1
    while bit < sp_n:
        sp_bits.append(bit)
        bit *= 2

    def flip(value, bit):
        return value + bit - 2 * bit * ((value // bit) % 2)

    sum_devs = [(flip(tp_i, b), sp_i) for b in tp_bits] + [(tp_i, flip(sp_i, b)) for b in sp_bits]

    barrier = pltpu.get_barrier_semaphore()
    greeted = [sp_at((line + 1) % outer, half), sp_at((line + outer - 1) % outer, half)] + sum_devs
    for device in greeted:
        pl.semaphore_signal(barrier, inc=1, device_id=device, device_id_type=MESH)
    pl.semaphore_wait(barrier, len(greeted))

    def remote(src, dst, send, recv, device):
        return pltpu.make_async_remote_copy(
            src_ref=src, dst_ref=dst, send_sem=send, recv_sem=recv,
            device_id=device, device_id_type=MESH,
        )

    places = (line, last - line)
    nexts = (sp_at(jnp.minimum(line + 1, last), half), sp_at(jnp.maximum(line - 1, 0), half))
    signs = (1, -1)

    def rows_of(stream, index):
        count = parts[stream].shape[0] // outer
        return pl.ds(pl.multiple_of(index * count, count), count)

    def reduce_copy(stream, way, step, src):
        return remote(
            src, got[stream].at[way, step - 1], reduce_send.at[stream, way, step - 1],
            reduce_recv.at[stream, way, step - 1], nexts[way],
        )

    def clamp(index):
        return jnp.clip(index, 0, last)

    def reduce_step(stream, step):
        for way in range(2):
            place, sign = places[way], signs[way]
            target = clamp(line + sign * (outer - step))
            own = parts[stream].at[rows_of(stream, target), :]

            @pl.when(place == 0)
            def _():
                reduce_copy(stream, way, step, own).start()

            if step > 1:

                @pl.when((place > 0) & (place <= step - 1))
                def _():
                    reduce_copy(stream, way, step - 1, own).wait_recv()
                    stage = staged[stream].at[way, step - 2]
                    stage[...] = (
                        got[stream][way, step - 2].astype(F32) + own[...].astype(F32)
                    ).astype(BF16)
                    reduce_copy(stream, way, step, stage).start()

    def gather_copy(stream, way, step, origin):
        block = outs[stream].at[half, rows_of(stream, origin), :]
        return remote(
            block, block, gather_send.at[stream, way, step - 1],
            gather_recv.at[stream, way, step - 1], nexts[way],
        )

    def pair_copy(stream, slot, origin):
        block = outs[stream].at[half, rows_of(stream, origin), :]
        return remote(block, block, pair_send.at[stream, slot], pair_recv.at[stream, slot], pair_dev)

    def reduce_final(stream):
        own = parts[stream].at[rows_of(stream, line), :]
        block = outs[stream].at[half, rows_of(stream, line), :]
        for way in range(2):

            @pl.when(places[way] > 0)
            def _():
                reduce_copy(stream, way, last, own).wait_recv()

        up = jnp.where(line > 0, got[stream][0, last - 1].astype(F32), 0.0)
        down = jnp.where(line < last, got[stream][1, last - 1].astype(F32), 0.0)
        block[...] = (own[...].astype(F32) + up + down).astype(BF16)
        for way in range(2):

            @pl.when(places[way] < last)
            def _():
                gather_copy(stream, way, 1, line).start()

        pair_copy(stream, 0, line).start()

    def gather_step(stream, step):
        for way in range(2):
            place, sign = places[way], signs[way]
            origin = clamp(line - sign * step)

            @pl.when(place >= step)
            def _():
                gather_copy(stream, way, step, origin).wait_recv()
                if step < last:

                    @pl.when(place < last)
                    def _():
                        gather_copy(stream, way, step + 1, origin).start()

                pair_copy(stream, 1 + way * last + step - 1, origin).start()

    def drain(stream):
        pair_copy(stream, 0, line).wait()
        for way in range(2):
            place, sign = places[way], signs[way]
            for step in range(1, outer):
                origin = clamp(line - sign * step)

                @pl.when(place <= step - 1)
                def _():
                    reduce_copy(stream, way, step, parts[stream].at[rows_of(stream, 0), :]).wait_send()

                @pl.when((place >= step - 1) & (place < last))
                def _():
                    gather_copy(stream, way, step, origin).wait_send()

                @pl.when(place >= step)
                def _():
                    pair_copy(stream, 1 + way * last + step - 1, origin).wait()

    def near_copy(index):
        return remote(
            part_ref.at[index, 1 - core], near_got.at[index], tp_send.at[index], tp_recv.at[index],
            core_dev,
        )

    def far_copy():
        return remote(far_stage, far_got, tp_send.at[sides], tp_recv.at[sides], side_dev)

    def spread_copy(slot, s, device):
        block = grad_out.at[s, core]
        return remote(block, block, tp_send.at[sides + slot], tp_recv.at[sides + slot], device)

    def input_step(step):
        if step == 0:
            for index in range(sides):
                near_copy(index).start()
        if step == 1:
            for index in range(sides):
                near_copy(index).wait_recv()
            keep_buf[...] = part_ref[side, core].astype(F32) + near_got[side].astype(F32)
            far_stage[...] = (
                part_ref[1 - side, core].astype(F32) + near_got[1 - side].astype(F32)
            ).astype(BF16)
            far_copy().start()
        if step == 2:
            far_copy().wait_recv()
            incoming = keep_buf[...] + far_got[...].astype(F32)
            values = hidden_ref[...].astype(F32)
            scales = scale_ref[...]
            weighted = incoming * gain_ref[...]
            inner_sum = jnp.sum(weighted * values, axis=-1, keepdims=True)
            grads = scales * weighted - values * (scales * scales * scales) * inner_sum * width_scale
            grad_out[side, core] = (middle_ref[...] + grads).astype(BF16)
            spread_copy(1, side, side_dev).start()
            spread_copy(2, side, core_dev).start()
        if step == 3:
            spread_copy(1, side, side_dev).wait_recv()
            spread_copy(3, 1 - side, core_dev).start()
        if step == 4:
            spread_copy(2, side, core_dev).wait_recv()
            spread_copy(3, 1 - side, core_dev).wait_recv()
            for index in range(sides):
                near_copy(index).wait_send()
            far_copy().wait_send()
            spread_copy(1, side, side_dev).wait_send()
            spread_copy(2, side, core_dev).wait_send()
            spread_copy(3, 1 - side, core_dev).wait_send()

    last_half = last_keep.shape[0]

    def ffn_at(j, ref, whole, owner):
        count = last_half // FFN_CHUNKS
        start = j * count
        if whole:
            start = pl.multiple_of(owner * last_half + start, count)
        return ref.at[pl.ds(start, count), :]

    def ffn_keep(j):
        return ffn_at(j, last_keep, False, 0)

    def ffn_got(j):
        return ffn_at(j, last_got, False, 0)

    def ffn_far(j):
        return ffn_at(j, last_far, False, 0)

    def ffn_load(j):
        return pltpu.make_async_copy(ffn_at(j, last_in, True, core), ffn_keep(j), f_load.at[j])

    def ffn_near_copy(j):
        return remote(
            ffn_at(j, last_in, True, 1 - core), ffn_got(j), f_near_send.at[j], f_near_recv.at[j], core_dev
        )

    def ffn_far_copy(j):
        return remote(ffn_keep(j), ffn_far(j), f_far_send.at[j], f_far_recv.at[j], side_dev)

    def ffn_store(j):
        return pltpu.make_async_copy(ffn_got(j), ffn_at(j, last_out, True, core), f_store.at[j])

    def ffn_out_copy(j):
        return remote(
            ffn_got(j), ffn_at(j, last_out, True, core), f_out_send.at[j], f_out_recv.at[j], core_dev
        )

    def ffn_sum(j):
        ffn_load(j).wait()
        ffn_near_copy(j).wait_recv()
        keep = ffn_keep(j)
        keep[...] = (keep[...].astype(F32) + ffn_got(j)[...].astype(F32)).astype(BF16)
        ffn_far_copy(j).start()

    def ffn_total(j):
        ffn_far_copy(j).wait_recv()
        total = ffn_keep(j)[...].astype(F32) + ffn_far(j)[...].astype(F32)
        ffn_got(j)[...] = total.astype(BF16)
        ffn_store(j).start()
        ffn_out_copy(j).start()

    def ffn_drain(j):
        ffn_near_copy(j).wait_send()
        ffn_far_copy(j).wait_send()
        ffn_store(j).wait()
        ffn_out_copy(j).wait()

    rounds = len(sum_devs)

    def sums_copy(step):
        src = sums_ref if step == 0 else sums_stage.at[step - 1]
        return remote(
            src, sums_got.at[step], sums_send.at[step], sums_recv.at[step], sum_devs[step]
        )

    def sums_step(step):
        if step > 0:
            sums_copy(step - 1).wait_recv()
            before = sums_ref[...] if step == 1 else sums_stage[step - 2]
            total = before + sums_got[step - 1]
            if step == rounds:
                sums_out[...] = total
            else:
                sums_stage[step - 1] = total
        if step < rounds:
            sums_copy(step).start()
        if step == rounds:
            for index in range(rounds):
                sums_copy(index).wait_send()

    def later(do, *args):
        return functools.partial(do, *args)

    def layer_copy(slot, s, device):
        block = layer_out.at[s, core]
        src = block if slot == 2 else layer_ref
        return remote(src, block, layer_send.at[slot], layer_recv.at[slot], device)

    def layer_own():
        return pltpu.make_async_copy(layer_ref, layer_out.at[side, core], layer_send.at[3])

    def layer_step(step):
        if step == 0:
            layer_copy(0, side, side_dev).start()
            layer_copy(1, side, core_dev).start()
            layer_own().start()
        if step == 1:
            layer_copy(0, 1 - side, side_dev).wait_recv()
            layer_copy(2, 1 - side, core_dev).start()
        if step == 2:
            layer_copy(1, side, core_dev).wait_recv()
            layer_own().wait()
            layer_copy(0, side, side_dev).wait_send()
            layer_copy(1, side, core_dev).wait_send()
            layer_copy(2, 1 - side, core_dev).wait()

    extra = [
        later(input_step, 0), later(input_step, 1), later(layer_step, 0), later(ffn_sum, 0),
        later(ffn_sum, 1), later(sums_step, 0), later(input_step, 2), later(sums_step, 1),
        later(layer_step, 1), later(sums_step, 2), later(input_step, 3), later(sums_step, 3),
        later(ffn_total, 0), later(sums_step, 4), later(layer_step, 2), later(input_step, 4),
        later(ffn_total, 1),
    ]
    extra += [later(sums_step, index) for index in range(5, rounds + 1)]
    for index in range(FFN_CHUNKS):
        ffn_near_copy(index).start()
        ffn_load(index).start()
    for turn in range(streams + 1):
        for step in range(1, outer + 1):
            if turn < streams:
                if step < outer:
                    reduce_step(turn, step)
                else:
                    reduce_final(turn)
            if turn > 0 and step < outer:
                gather_step(turn - 1, step)
            if extra:
                extra.pop(0)()
    for step in extra:
        step()
    for stream in range(streams):
        drain(stream)
    for index in range(FFN_CHUNKS):
        ffn_drain(index)


def finish(parts, part, hidden, scales, gain, middle, sums, ffn_last, layer, outer, sp_n, tp_n):
    streams = len(parts)
    sides = tp_n // 2
    quarter, model = hidden.shape
    last = outer - 1
    rounds = (tp_n - 1).bit_length() + (sp_n - 1).bit_length()
    vmem = pl.BlockSpec(memory_space=pltpu.VMEM)
    anywhere = pl.BlockSpec(memory_space=pl.ANY)
    chunk = [(2, last, p.shape[0] // outer, p.shape[1]) for p in parts]
    dma = pltpu.SemaphoreType.DMA
    return pl.pallas_call(
        functools.partial(finish_kernel, outer, sides, sp_n, tp_n, streams, 1.0 / model),
        out_shape=[jax.ShapeDtypeStruct((2,) + p.shape, BF16) for p in parts]
        + [
            jax.ShapeDtypeStruct((sides, 2, quarter, model), BF16),
            jax.ShapeDtypeStruct(sums.shape, F32),
        ]
        + [
            jax.ShapeDtypeStruct(ffn_last.shape, BF16),
            jax.ShapeDtypeStruct((sides, 2, quarter, model), BF16),
        ],
        in_specs=[vmem] * (streams + 6) + [anywhere, vmem],
        out_specs=[vmem] * (streams + 2) + [anywhere, vmem],
        scratch_shapes=[pltpu.VMEM(c, BF16) for c in chunk]
        + [pltpu.VMEM(c, BF16) for c in chunk]
        + [
            pltpu.VMEM((sides, quarter, model), BF16),
            pltpu.VMEM((quarter, model), BF16),
            pltpu.VMEM((quarter, model), F32),
            pltpu.VMEM((quarter, model), BF16),
            pltpu.VMEM((rounds,) + sums.shape, F32),
            pltpu.VMEM((rounds,) + sums.shape, F32),
        ]
        + [pltpu.VMEM((ffn_last.shape[0] // 2, ffn_last.shape[1]), BF16)] * 3
        + [dma((4,))] * 2
        + [dma((FFN_CHUNKS,))] * 8
        + [dma((streams, 2, last))] * 4
        + [dma((streams, 1 + 2 * last))] * 2
        + [dma((sides + 4,))] * 2
        + [dma((rounds,))] * 2,
        compiler_params=pltpu.CompilerParams(
            collective_id=1, has_side_effects=True, vmem_limit_bytes=60 * 1024 * 1024
        ),
        cost_estimate=pl.CostEstimate(flops=10**9, bytes_accessed=10**8, transcendentals=0),
        name="finish",
    )(*parts, part, hidden, scales, gain, middle, sums, ffn_last, layer)


def body(
    hidden,
    segment_ids,
    attn_norm,
    query_proj,
    key_proj,
    value_proj,
    gate_proj,
    output_proj,
    query_norm,
    key_norm,
    ffn_norm,
    ffn_gate,
    ffn_up,
    ffn_down,
    upstream,
):
    rows_dev, model = hidden.shape
    head_width = query_norm.shape[0]
    heads = query_proj.shape[1] // head_width
    groups = key_proj.shape[1] // head_width
    per_group = heads // groups
    group_width = groups * head_width
    sp_n = lax.axis_size("sp")
    tp_n = lax.axis_size("tp")
    outer = sp_n // 2
    sides = tp_n // 2
    quarter = rows_dev // tp_n
    tp_i = lax.axis_index("tp")
    sp_i = lax.axis_index("sp")
    ring_i = sp_i // 2
    pair_i = sp_i % 2
    side_i = tp_i // 2
    core_i = tp_i % 2
    own_first = sp_i * rows_dev
    quarter_first = tp_i * quarter
    scale = 1.0 / math.sqrt(head_width)

    ring_pairs = [(z * 2 + y, ((z + 1) % outer) * 2 + y) for z in range(outer) for y in range(2)]
    pair_pairs = [(i, i ^ 1) for i in range(sp_n)]
    side_pairs = [(i, i ^ 2) for i in range(tp_n)]
    core_pairs = [(i, i ^ 1) for i in range(tp_n)]

    def ring(value):
        return lax.ppermute(value, "sp", ring_pairs)

    def pair(value):
        return lax.ppermute(value, "sp", pair_pairs)

    def side(value):
        return lax.ppermute(value, "tp", side_pairs)

    def core(value):
        return lax.ppermute(value, "tp", core_pairs)

    def gather_sp(block):
        blocks = []
        for k in range(outer):
            blocks.append((block, pair(block)))
            if k < outer - 1:
                block = ring(block)
        return blocks

    def scatter_sp(parts):
        def paired(k):
            return parts[k][0] + pair(parts[k][1].astype(BF16)).astype(F32)

        total = paired(1 % outer)
        for k in range(2, outer + 1):
            total = ring(total.astype(BF16)).astype(F32) + paired(k % outer)
        return total

    first_id = segment_ids[0]
    second_start = jnp.sum((segment_ids == first_id).astype(jnp.int32))
    own_index = own_first + jnp.arange(rows_dev, dtype=jnp.int32)
    own_starts = jnp.where(own_index < second_start, 0, second_start)
    steps_half = jnp.arange(head_width // 2, dtype=F32)
    frequencies = jnp.exp(steps_half * (-2.0 * math.log(THETA) / head_width))
    angles = (own_index - own_starts).astype(F32)[:, None] * frequencies[None, :]
    cosine = jnp.cos(angles)[:, None, :]
    sine = jnp.sin(angles)[:, None, :]

    hidden_full = hidden.astype(F32)
    normed_full, attn_scales = norm_rows(hidden_full, attn_norm)
    normed = normed_full.astype(BF16)
    key_raw = matmul(normed, key_proj).reshape(rows_dev, groups, head_width)
    value_rows = matmul(normed, value_proj).astype(BF16)
    key_normed, key_scales = norm_rows(key_raw, key_norm)
    key_rot = rotary(key_normed, cosine, sine).astype(BF16).reshape(rows_dev, group_width)
    kv_own = jnp.stack([key_rot, value_rows])

    low, high = (outer // 4, 3 * outer // 4) if outer % 4 == 0 else (0, outer)
    reach = high - 1 if low else outer - 1

    def up_pairs(step):
        return [
            (z * 2 + y, (z + 1) * 2 + y)
            for z in range(outer - 1)
            for y in range(2)
            if z + 1 - step >= 0 and (z + 1 - step >= low or z + 1 < high)
        ]

    kv_blocks = []
    travelling = kv_own
    for k in range(reach + 1):
        kv_blocks.append((travelling, pair(travelling)))
        if k < reach:
            travelling = lax.ppermute(travelling, "sp", up_pairs(k + 1))

    query_raw = matmul(normed, query_proj).reshape(rows_dev, heads, head_width)
    gate_raw = matmul(normed, gate_proj)
    query_normed, query_scales = norm_rows(query_raw, query_norm)
    queries = rotary(query_normed, cosine, sine).astype(BF16).reshape(rows_dev, heads * head_width)

    def swap_half(value):
        piece = model // 4
        mine = pair(lax.dynamic_slice_in_dim(value, ((1 - pair_i) * 2 + core_i) * piece, piece, 1))
        near = core(mine)
        return jnp.where(
            core_i == 1, jnp.concatenate([near, mine], 1), jnp.concatenate([mine, near], 1)
        )

    normed_own = lax.dynamic_slice_in_dim(normed, pair_i * (model // 2), model // 2, 1)
    both_normed = jnp.concatenate([normed_own, swap_half(normed)])

    grad_quarter = lax.dynamic_slice_in_dim(upstream, quarter_first, quarter)
    up_blocks = gather_sp(grad_quarter)

    row_start_low = own_starts[0]
    row_start_high = own_starts[-1]

    def block_info(k):
        shards = [(ring_i - k) * 2 + pair_i, (ring_i - k) * 2 + (1 - pair_i)]
        entries = [own_first] + [shard * rows_dev for shard in shards]
        live = []
        full = []
        for shard in shards:
            token = shard * rows_dev
            live.append((shard >= 0) & (shard <= sp_i) & (token + rows_dev - 1 >= row_start_low))
            full.append((token >= row_start_high) & (shard < sp_i))
        return jnp.stack(entries + [v.astype(jnp.int32) for v in live + full]).astype(jnp.int32)

    infos = [block_info(k) for k in range(reach + 1)]
    starts_column = own_starts[:, None]
    starts_row = own_starts[None, :]
    carried = None
    for k in range(reach + 1):
        carried = attn_forward(
            infos[k], starts_column, queries, kv_blocks[k][0], kv_blocks[k][1], carried, scale
        )
    mix_acc, mix_sum = carried
    mixed = mix_acc / mix_sum
    lse = jnp.log2(mix_sum.reshape(rows_dev, heads, head_width)[:, :, 0])
    lse_rows = lse.T.reshape(groups, per_group, rows_dev)
    gate_sig = jax.nn.sigmoid(gate_raw)
    gated = (mixed * gate_sig).astype(BF16)
    gated_other = pair(gated)

    def scatter_tp(part):
        part = part.reshape(sides, 2, quarter, model)
        keep = lax.dynamic_index_in_dim(part, core_i, 1, keepdims=False)
        send = lax.dynamic_index_in_dim(part, 1 - core_i, 1, keepdims=False)
        keep = keep + core(send.astype(BF16)).astype(F32)
        mine = lax.dynamic_index_in_dim(keep, side_i, 0, keepdims=False)
        other = lax.dynamic_index_in_dim(keep, 1 - side_i, 0, keepdims=False)
        return mine + side(other.astype(BF16)).astype(F32)

    def gather_tp(block):
        far = side(block)
        swap_side = side_i == 1
        two = jnp.where(swap_side, jnp.stack([far, block]), jnp.stack([block, far]))
        near = core(two)
        swap_core = core_i == 1
        full = jnp.where(
            swap_core, jnp.stack([near, two], axis=1), jnp.stack([two, near], axis=1)
        )
        return full.reshape((rows_dev,) + block.shape[1:])

    fused = outer * quarter <= 512 and outer > 1 and tp_n == 4
    if fused:
        layer_quarter, grad_middle_quarter, ffn_gain_sum, branch, *ffn_parts = middle_layer(
            gated,
            output_proj,
            lax.dynamic_slice_in_dim(hidden, quarter_first, quarter),
            ffn_norm[None, :],
            ffn_gate,
            ffn_up,
            ffn_down,
            [block for both in up_blocks for block in both],
            outer,
            sides,
        )
        grad_branch = branch.reshape(rows_dev, model)
        ffn_gain_sum = ffn_gain_sum[0]
    else:
        attn_quarter = scatter_tp(matmul(gated, output_proj))
        hidden_quarter = lax.dynamic_slice_in_dim(hidden, quarter_first, quarter).astype(F32)
        middle = hidden_quarter + attn_quarter
        normed_two_full, ffn_scales = norm_rows(middle, ffn_norm)
        normed_two = normed_two_full.astype(BF16)

        two_blocks = gather_sp(normed_two)
        rows_list, up_list, inner_list, gate_list, grad_up_list = [None] * outer, [None] * outer, [None] * outer, [None] * outer, [None] * outer
        grad_parts = [None] * outer
        for k in list(range(1, outer)) + [0]:
            rows_k = jnp.concatenate(two_blocks[k])
            up_k = jnp.concatenate(up_blocks[k])
            gate_vals = matmul(rows_k, ffn_gate)
            up_vals = matmul(rows_k, ffn_up)
            sig = jax.nn.sigmoid(gate_vals)
            grad_inner = times_transpose(up_k, ffn_down)
            grad_gate = (grad_inner * up_vals * (sig * (1.0 + gate_vals * (1.0 - sig)))).astype(BF16)
            grad_up = (grad_inner * (gate_vals * sig)).astype(BF16)
            inner = (gate_vals * sig * up_vals).astype(BF16)
            grad_parts[k] = (
                times_transpose(grad_gate, ffn_gate) + times_transpose(grad_up, ffn_up)
            ).reshape(2, quarter, model)
            rows_list[k], up_list[k], inner_list[k] = rows_k, up_k, inner
            gate_list[k], grad_up_list[k] = grad_gate, grad_up
        grad_two = scatter_sp(grad_parts)

        norm_grad_two, ffn_gain_terms = norm_back(middle, ffn_scales, ffn_norm, grad_two)
        grad_middle_quarter = grad_quarter.astype(F32) + norm_grad_two
        grad_branch = gather_tp(grad_middle_quarter.astype(BF16))
        ffn_gain_sum = jnp.sum(ffn_gain_terms, axis=0)
        mlp_parts = [
            matmul(inner_list[k], ffn_down).reshape(2, quarter, model) for k in range(outer)
        ]
        layer_quarter = (middle + scatter_sp(mlp_parts)).astype(BF16)

    def sum_tp(part):
        total = part.astype(BF16).astype(F32)
        total = total + core(total.astype(BF16)).astype(F32)
        low = total.astype(BF16)
        return (low.astype(F32) + side(low).astype(F32)).astype(BF16)

    if not fused:
        rows_all = jnp.concatenate(rows_list)
        up_all = jnp.concatenate(up_list)
        inner_all = jnp.concatenate(inner_list)
        gate_all = jnp.concatenate(gate_list)
        grad_up_all = jnp.concatenate(grad_up_list)
        ffn_parts = [
            jnp.stack([outer_sum(rows_all, gate_all), outer_sum(rows_all, grad_up_all)]),
            outer_sum(inner_all, up_all),
        ]
        ffn_parts = [sum_tp(ffn_parts[0]), ffn_parts[1].astype(BF16)]
    ffn_both, ffn_last = ffn_parts

    branch_other = swap_half(grad_branch)
    branch_own = lax.dynamic_slice_in_dim(grad_branch, pair_i * (model // 2), model // 2, 1)
    output_half = outer_sum(
        jnp.concatenate([gated, gated_other]), jnp.concatenate([branch_own, branch_other])
    )
    grad_gated = times_transpose(grad_branch, output_proj)
    grad_mixed = (grad_gated * gate_sig).astype(BF16)
    grad_gate_raw = (grad_gated * mixed * (gate_sig * (1.0 - gate_sig))).astype(BF16)
    gate_half = outer_sum(both_normed, jnp.concatenate([grad_gate_raw, pair(grad_gate_raw)]))
    deltas = jnp.sum(
        (grad_mixed.astype(F32) * mixed).reshape(rows_dev, heads, head_width), axis=-1
    )
    delta_rows = deltas.T.reshape(groups, per_group, rows_dev)

    def down_pairs(step):
        return [(b, a) for a, b in up_pairs(step)]

    query_acc = None
    travelling = None
    for k in list(range(reach, -1, -1)):
        query_acc, grad_a, grad_b = attn_backward(
            infos[k], starts_row, lse_rows, delta_rows, queries, grad_mixed,
            kv_blocks[k][0], kv_blocks[k][1], query_acc, k == 0, scale,
        )
        total = grad_a.astype(F32) + pair(grad_b).astype(F32)
        if travelling is not None:
            total = total + travelling.astype(F32)
        if k > 0:
            travelling = lax.ppermute(total.astype(BF16), "sp", down_pairs(k))
    grad_key_rot = total[0].reshape(rows_dev, groups, head_width)
    grad_value_low = total[1].astype(BF16)
    grad_query_rot = (query_acc * scale).reshape(rows_dev, heads, head_width)
    grad_query_raw, query_gain_terms = norm_back(
        query_raw, query_scales, query_norm, rotary_back(grad_query_rot, cosine, sine)
    )
    grad_key_raw, key_gain_terms = norm_back(
        key_raw, key_scales, key_norm, rotary_back(grad_key_rot, cosine, sine)
    )
    grad_query_low = grad_query_raw.reshape(rows_dev, heads * head_width).astype(BF16)
    grad_key_low = grad_key_raw.reshape(rows_dev, group_width).astype(BF16)
    grad_kv_low = jnp.concatenate([grad_key_low, grad_value_low], axis=1)

    both_queries = jnp.concatenate([grad_query_low, pair(grad_query_low)])
    both_kv = jnp.concatenate([grad_kv_low, pair(grad_kv_low)])
    parts = [
        output_half.astype(BF16),
        gate_half.astype(BF16),
        outer_sum(both_normed, both_queries).astype(BF16),
        outer_sum(both_normed, both_kv).astype(BF16),
    ]

    grad_normed_part = (
        times_transpose(grad_query_low, query_proj)
        + times_transpose(grad_key_low, key_proj)
        + times_transpose(grad_value_low, value_proj)
        + times_transpose(grad_gate_raw, gate_proj)
    )
    gains = jnp.concatenate(
        [
            jnp.sum(grad_normed_part * hidden_full * attn_scales, axis=0),
            ffn_gain_sum,
            jnp.sum(query_gain_terms, axis=(0, 1)),
            jnp.sum(key_gain_terms, axis=(0, 1)),
        ]
    )
    gains_at = 2 * model + 2 * head_width
    gains = jnp.pad(gains, (0, -gains_at % 1024)).reshape(-1, 128)
    scales_quarter = lax.dynamic_slice_in_dim(attn_scales, quarter_first, quarter)
    finished = finish(
        parts,
        grad_normed_part.astype(BF16).reshape(sides, 2, quarter, model),
        lax.dynamic_slice_in_dim(hidden, quarter_first, quarter),
        scales_quarter,
        attn_norm[None, :],
        grad_middle_quarter,
        gains,
        ffn_last,
        layer_quarter,
        outer,
        sp_n,
        tp_n,
    )
    output_all, gate_all_w, query_all, kv_all, input_all, gains, ffn_last, layer_all = finished
    output_grad = jnp.concatenate([output_all[0], output_all[1]], axis=1).astype(F32)
    gate_grad = gate_all_w.reshape(model, heads * head_width).astype(F32)
    query_grad = query_all.reshape(model, heads * head_width).astype(F32)
    kv_all = kv_all.reshape(model, 2 * group_width)
    key_grad = kv_all[:, :group_width].astype(F32)
    value_grad = kv_all[:, group_width:].astype(F32)
    hidden_grad = input_all.reshape(rows_dev, model).astype(F32)
    gains = gains.reshape(-1)
    return (
        layer_all.reshape(rows_dev, model),
        hidden_grad,
        gains[:model],
        query_grad,
        key_grad,
        value_grad,
        gate_grad,
        output_grad,
        gains[2 * model : 2 * model + head_width],
        gains[2 * model + head_width : gains_at],
        gains[model : 2 * model],
        ffn_both[0].astype(F32),
        ffn_both[1].astype(F32),
        ffn_last.astype(F32),
    )


def solution(mesh):
    placed = (
        P("sp", None),
        P(),
        P(),
        P(None, "tp"),
        P(None, "tp"),
        P(None, "tp"),
        P(None, "tp"),
        P("tp", None),
        P(),
        P(),
        P(),
        P(None, "sp"),
        P(None, "sp"),
        P("sp", None),
        P("sp", None),
    )
    return jax.shard_map(
        body,
        mesh=mesh,
        in_specs=placed,
        out_specs=(
            P("sp", None),
            P("sp", None),
            P(),
            P(None, "tp"),
            P(None, "tp"),
            P(None, "tp"),
            P(None, "tp"),
            P("tp", None),
            P(),
            P(),
            P(),
            P(None, "sp"),
            P(None, "sp"),
            P("sp", None),
        ),
        check_vma=False,
    )
```

```python
import functools
import math

import jax
import jax.numpy as jnp
from jax import lax
from jax.experimental import pallas as pl
from jax.experimental.pallas import tpu as pltpu
from jax.sharding import PartitionSpec as P

EPSILON = 1e-06
THETA = 1000000.0
LOG2E = 1.4426950408889634
F32 = jnp.float32
BF16 = jnp.bfloat16


def norm_scales(values):
    return lax.rsqrt(jnp.mean(values * values, axis=-1, keepdims=True) + EPSILON)


def norm_rows(values, gain):
    scales = norm_scales(values)
    return (values * scales * gain, scales)


def norm_back(values, scales, gain, incoming):
    weighted = incoming * gain
    inner_sum = jnp.sum(weighted * values, axis=-1, keepdims=True)
    grad_values = (
        scales * weighted - values * (scales * scales * scales) * inner_sum / values.shape[-1]
    )
    return (grad_values, incoming * values * scales)


def rotary(values, cosine, sine):
    half_width = values.shape[-1] // 2
    front_half = values[..., :half_width]
    back_half = values[..., half_width:]
    return jnp.concatenate(
        [front_half * cosine - back_half * sine, back_half * cosine + front_half * sine], axis=-1
    )


def rotary_back(grads, cosine, sine):
    half_width = grads.shape[-1] // 2
    front_half = grads[..., :half_width]
    back_half = grads[..., half_width:]
    return jnp.concatenate(
        [front_half * cosine + back_half * sine, back_half * cosine - front_half * sine], axis=-1
    )


def matmul(left, right):
    return jnp.dot(left, right, preferred_element_type=F32)


def outer_sum(left, right):
    return lax.dot_general(left, right, (((0,), (0,)), ((), ())), preferred_element_type=F32)


def times_transpose(left, right):
    return lax.dot_general(left, right, (((1,), (1,)), ((), ())), preferred_element_type=F32)


def attn_forward_kernel(first, diagonal, scale, info, starts, queries, kv_a, kv_b, *rest):
    if first:
        acc_out, sum_out = rest
    else:
        acc_in, sum_in, acc_out, sum_out = rest
    rows = queries.shape[0]
    keys_n = kv_a.shape[1]
    per_group = queries.shape[1] // kv_a.shape[2]
    width = kv_a.shape[2]
    if first:
        acc_out[...] = jnp.zeros_like(acc_out)
        sum_out[...] = jnp.zeros_like(sum_out)
    else:
        acc_out[...] = acc_in[...]
        sum_out[...] = sum_in[...]
    own_first = info[0]
    for slot, block in enumerate((kv_a, kv_b)):
        key_first = info[1 + slot]
        live = info[3 + slot] > 0

        def work(masked, causal):
            ones = jnp.ones((keys_n, width), BF16)
            values = jnp.concatenate([block[1], ones], axis=1)
            keys = block[0]
            if masked:
                key_index = key_first + lax.broadcasted_iota(jnp.int32, (rows, keys_n), 1)
                allowed = key_index >= starts[...]
                if causal:
                    row_index = own_first + lax.broadcasted_iota(jnp.int32, (rows, keys_n), 0)
                    allowed = allowed & (key_index <= row_index)
            for head in range(per_group):
                cols = slice(head * width, (head + 1) * width)
                scores = times_transpose(queries[:, cols], keys)
                weights = jnp.exp2(scores * (scale * LOG2E))
                if masked:
                    weights = jnp.where(allowed, weights, 0.0)
                both = matmul(weights.astype(BF16), values)
                acc_out[:, cols] += both[:, :width]
                sum_out[:, cols] += both[:, width:]

        if diagonal and slot == 0:
            work(True, True)
        else:
            full = info[5 + slot] > 0
            pl.when(live & full)(functools.partial(work, False, False))
            pl.when(live & jnp.logical_not(full))(functools.partial(work, True, False))


def attn_forward(info, starts, queries, kv_a, kv_b, carried, scale):
    rows, all_width = queries.shape
    width = 128
    groups = kv_a.shape[2] // width
    group_width = all_width // groups
    keys_n = kv_a.shape[1]
    first = carried is None
    spec_q = pl.BlockSpec((rows, group_width), lambda g, info: (0, g))
    spec_kv = pl.BlockSpec((2, keys_n, width), lambda g, info: (0, 0, g))
    specs = [pl.BlockSpec((rows, 1), lambda g, info: (0, 0)), spec_q, spec_kv, spec_kv]
    operands = [starts, queries, kv_a, kv_b]
    if not first:
        specs += [spec_q, spec_q]
        operands += list(carried)
    return pl.pallas_call(
        functools.partial(attn_forward_kernel, first, first, scale),
        grid_spec=pltpu.PrefetchScalarGridSpec(
            num_scalar_prefetch=1,
            grid=(groups,),
            in_specs=specs,
            out_specs=[spec_q, spec_q],
        ),
        out_shape=[jax.ShapeDtypeStruct((rows, all_width), F32)] * 2,
        compiler_params=pltpu.CompilerParams(dimension_semantics=("arbitrary",)),
        cost_estimate=pl.CostEstimate(
            flops=16 * rows * keys_n * all_width,
            transcendentals=2 * rows * keys_n * all_width // width,
            bytes_accessed=8 * rows * all_width,
        ),
        name="attn_forward",
    )(info, *operands)


def attn_backward_kernel(first, diagonal, scale, info, starts, lse, deltas, queries, grads, kv_a, kv_b, *rest):
    if first:
        grad_q, grad_a, grad_b = rest
    else:
        grad_in, grad_q, grad_a, grad_b = rest
    rows = queries.shape[0]
    keys_n = kv_a.shape[1]
    width = kv_a.shape[2]
    per_group = queries.shape[1] // width
    if first:
        grad_q[...] = jnp.zeros_like(grad_q)
    else:
        grad_q[...] = grad_in[...]
    own_first = info[0]
    for slot, (block, out) in enumerate(((kv_a, grad_a), (kv_b, grad_b))):
        key_first = info[1 + slot]
        live = info[3 + slot] > 0

        def work(masked, causal):
            keys = block[0]
            values = block[1]
            keys_t = keys.T
            if masked:
                key_index = key_first + lax.broadcasted_iota(jnp.int32, (keys_n, rows), 0)
                allowed = key_index >= starts[...]
                if causal:
                    row_index = own_first + lax.broadcasted_iota(jnp.int32, (keys_n, rows), 1)
                    allowed = allowed & (key_index <= row_index)
            total_k = jnp.zeros((keys_n, width), F32)
            total_v = jnp.zeros((keys_n, width), F32)
            for head in range(per_group):
                cols = slice(head * width, (head + 1) * width)
                q_head = queries[:, cols]
                g_head = grads[:, cols]
                scores = times_transpose(keys, q_head)
                probs = jnp.exp2(scores * (scale * LOG2E) - lse[0, head : head + 1, :])
                if masked:
                    probs = jnp.where(allowed, probs, 0.0)
                grad_probs = times_transpose(values, g_head)
                grad_scores = (probs * (grad_probs - deltas[0, head : head + 1, :])).astype(BF16)
                total_v += matmul(probs.astype(BF16), g_head)
                total_k += matmul(grad_scores, q_head)
                grad_q[:, cols] += matmul(keys_t, grad_scores).T
            out[0] = (total_k * scale).astype(BF16)
            out[1] = total_v.astype(BF16)

        if diagonal and slot == 0:
            work(True, True)
        else:
            full = info[5 + slot] > 0
            pl.when(live & full)(functools.partial(work, False, False))
            pl.when(live & jnp.logical_not(full))(functools.partial(work, True, False))

            @pl.when(jnp.logical_not(live))
            def _():
                out[...] = jnp.zeros_like(out)


def attn_backward(info, starts_row, lse, deltas, queries, grads, kv_a, kv_b, carried, diagonal, scale):
    rows, all_width = queries.shape
    width = 128
    groups = kv_a.shape[2] // width
    group_width = all_width // groups
    per_group = group_width // width
    keys_n = kv_a.shape[1]
    first = carried is None
    spec_q = pl.BlockSpec((rows, group_width), lambda g, info: (0, g))
    spec_kv = pl.BlockSpec((2, keys_n, width), lambda g, info: (0, 0, g))
    spec_row = pl.BlockSpec((1, per_group, rows), lambda g, info: (g, 0, 0))
    specs = [
        pl.BlockSpec((1, rows), lambda g, info: (0, 0)),
        spec_row,
        spec_row,
        spec_q,
        spec_q,
        spec_kv,
        spec_kv,
    ]
    operands = [starts_row, lse, deltas, queries, grads, kv_a, kv_b]
    if not first:
        specs.append(spec_q)
        operands.append(carried)
    return pl.pallas_call(
        functools.partial(attn_backward_kernel, first, diagonal, scale),
        grid_spec=pltpu.PrefetchScalarGridSpec(
            num_scalar_prefetch=1,
            grid=(groups,),
            in_specs=specs,
            out_specs=[spec_q, spec_kv, spec_kv],
        ),
        out_shape=[
            jax.ShapeDtypeStruct((rows, all_width), F32),
            jax.ShapeDtypeStruct(kv_a.shape, BF16),
            jax.ShapeDtypeStruct(kv_a.shape, BF16),
        ],
        compiler_params=pltpu.CompilerParams(dimension_semantics=("arbitrary",)),
        cost_estimate=pl.CostEstimate(
            flops=20 * rows * keys_n * all_width,
            transcendentals=2 * rows * keys_n * all_width // width,
            bytes_accessed=8 * rows * all_width,
        ),
        name="attn_backward",
    )(info, *operands)


LATE_BLOCKS = 2


def middle_kernel(outer, *refs):
    MESH = pl.DeviceIdType.MESH
    blocks = 2 * outer - LATE_BLOCKS
    (gated, out_proj, hidden_ref, gain_ref, gate_in, up_in, down_in) = refs[:7]
    ups_in = refs[7 : 7 + blocks]
    (layer_out, grad_out, gain_out, branch, dw_both, dw_down) = refs[7 + blocks : 13 + blocks]
    (
        w_gate, w_up, w_down, ups, rows, inner, grad_gate, grad_up,
        near_buf, far_stage, far_got, middle_buf,
        keep, y_stage, y_got, z_stage, z_got, part_got, part_far,
        load_sem, store_sem, tp_send, tp_recv, zs, zr, ys, yr, rys, ryr, rzs, rzr,
        p_near_send, p_near_recv, p_far_send, p_far_recv, p_out_send, p_out_recv, us, ur,
    ) = refs[13 + blocks :]
    stage_gate, stage_up, stage_down = w_gate, w_up, rows
    far_keep, own_keep = grad_out, middle_buf
    units = w_down.shape[0]
    quarter, model = hidden_ref.shape
    group = 2 * quarter
    chunk = model // outer
    last = outer - 1

    sp_i = lax.axis_index("sp")
    tp_i = lax.axis_index("tp")
    line = sp_i // 2
    half = sp_i % 2
    side = tp_i // 2
    core = tp_i % 2

    def sp_at(z, y):
        return (tp_i, z * 2 + y)

    pair_dev = sp_at(line, 1 - half)
    core_dev = (side * 2 + (1 - core), sp_i)
    side_dev = ((1 - side) * 2 + core, sp_i)
    nexts = (sp_at(jnp.minimum(line + 1, last), half), sp_at(jnp.maximum(line - 1, 0), half))

    late = list(range(outer - LATE_BLOCKS, outer))
    ups_at = [at for at in range(2 * outer) if at % 2 == 0 or at // 2 not in late]
    loads = [
        pltpu.make_async_copy(src, dst, load_sem.at[index])
        for index, (src, dst) in enumerate(
            [(down_in, w_down)]
            + [(src, ups.at[pl.ds(at * quarter, quarter), :]) for at, src in zip(ups_at, ups_in)]
            + [(gate_in, w_gate), (up_in, w_up)]
        )
    ]
    for load in loads:
        load.start()

    barrier = pltpu.get_barrier_semaphore()
    greeted = [
        sp_at((line + 1) % outer, half), sp_at((line + outer - 1) % outer, half),
        pair_dev, core_dev, side_dev,
    ]
    for device in greeted:
        pl.semaphore_signal(barrier, inc=1, device_id=device, device_id_type=MESH)
    pl.semaphore_wait(barrier, len(greeted))

    def remote(src, dst, send, recv, device):
        return pltpu.make_async_remote_copy(
            src_ref=src, dst_ref=dst, send_sem=send, recv_sem=recv,
            device_id=device, device_id_type=MESH,
        )

    def aligned(index, count):
        return pl.ds(pl.multiple_of(index * count, count), count)

    def late_copy(index):
        at = late[index] * 2
        return remote(
            ups.at[pl.ds(at * quarter, quarter), :], ups.at[pl.ds((at + 1) * quarter, quarter), :],
            us.at[index], ur.at[index], pair_dev,
        )

    def near_copy(j):
        return remote(near_buf.at[j], near_buf.at[2 + j], tp_send.at[j], tp_recv.at[j], core_dev)

    def far_copy():
        return remote(far_stage, far_got, tp_send.at[2], tp_recv.at[2], side_dev)

    def projected(s, c):
        return matmul(gated[aligned(s * 2 + c, quarter), :], out_proj[...])

    near_buf[0] = projected(1 - side, 1 - core).astype(BF16)
    near_copy(0).start()
    near_buf[1] = projected(side, 1 - core).astype(BF16)
    near_copy(1).start()
    for index in range(LATE_BLOCKS):
        loads[1 + ups_at.index(late[index] * 2)].wait()
        late_copy(index).start()
    far_keep[...] = projected(1 - side, core)
    near_copy(0).wait_recv()
    far_stage[...] = (far_keep[...] + near_buf[2].astype(F32)).astype(BF16)
    far_copy().start()
    own_keep[...] = projected(side, core)

    near_copy(1).wait_recv()
    far_copy().wait_recv()
    middle = hidden_ref[...].astype(F32) + (
        own_keep[...] + near_buf[3].astype(F32) + far_got[...].astype(F32)
    )
    middle_buf[...] = middle
    rows[0:quarter, :] = (middle * norm_scales(middle) * gain_ref[...]).astype(BF16)

    def entry(k, j):
        return pl.ds(pl.multiple_of((k * 2 + j) * quarter, quarter), quarter)

    def wrap(k):
        return (k + outer) % outer

    def z_copy(way, k):
        to = wrap(k + 1 - 2 * way)
        return remote(
            rows.at[entry(k, 0), :], rows.at[entry(to, 0), :], zs.at[way, k], zr.at[to], nexts[way]
        )

    def z_arrived(k):
        return remote(
            rows.at[entry(k, 0), :], rows.at[entry(k, 0), :], zs.at[0, k], zr.at[k], nexts[0]
        )

    def y_copy(k):
        return remote(
            rows.at[entry(k, 0), :], rows.at[entry(k, 1), :], ys.at[k], yr.at[k], pair_dev
        )

    short = jnp.minimum(line, last - line)

    def delta_of(i):
        near = jnp.where(i % 2 == 1, -((i + 1) // 2), (i + 1) // 2)
        far = jnp.where(line < last - line, i - short, short - i)
        return jnp.where(i <= 2 * short, near, far)

    def slot_of(delta):
        return jnp.where(delta <= 0, -delta, outer - delta)

    for way, exists in ((0, line < last), (1, line > 0)):
        pl.when(exists)(z_copy(way, 0).start)
    y_copy(0).start()

    def goes_on(delta):
        return ((delta < 0) & (line < last), (delta > 0) & (line > 0))

    def forward(i):
        delta = delta_of(i)
        k = slot_of(delta)
        z_arrived(k).wait_recv()
        for way, exists in enumerate(goes_on(delta)):
            pl.when(exists)(z_copy(way, k).start)
        y_copy(k).start()

    waited = [1 + ups_at.index(k * 2) for k in late]
    for index, load in enumerate(loads):
        if index not in waited:
            load.wait()
    for index in range(LATE_BLOCKS):
        late_copy(index).wait_recv()
    forward(1)

    def turn_forward(i, carry):
        @pl.when(i + 2 < outer)
        def _():
            forward(i + 2)

        k = slot_of(delta_of(i))
        y_copy(k).wait_recv()
        at = aligned(k, group)
        rows_k = rows[at, :]
        gate_vals = matmul(rows_k, w_gate[...])
        up_vals = matmul(rows_k, w_up[...])
        incoming = times_transpose(ups[at, :], w_down[...])
        sig = jax.nn.sigmoid(gate_vals)
        silu = gate_vals * sig
        grad_gate[at, :] = (incoming * up_vals * (sig * (1.0 + gate_vals * (1.0 - sig)))).astype(BF16)
        grad_up[at, :] = (incoming * silu).astype(BF16)
        inner[at, :] = (silu * up_vals).astype(BF16)
        return carry

    lax.fori_loop(0, outer, turn_forward, 0)

    near_copy(0).wait_send()
    near_copy(1).wait_send()

    def y_sum(which, k):
        at = aligned(k, quarter)
        src = y_stage.at[at, :] if which == 0 else near_buf.at[k]
        got = y_got.at[aligned(which * outer + k, quarter), :]
        return remote(src, got, rys.at[which, k], ryr.at[which, k], pair_dev)

    def half_rows(k, j):
        return pl.ds(pl.multiple_of((k * 2 + j) * quarter, quarter), quarter)

    def turn_parts(step, carry):
        k = slot_of(delta_of(last - step))
        part = times_transpose(grad_gate[half_rows(k, 1), :], w_gate[...]) + times_transpose(
            grad_up[half_rows(k, 1), :], w_up[...]
        )
        y_stage[aligned(k, quarter), :] = part.astype(BF16)
        y_sum(0, k).start()
        return carry

    def turn_outputs(step, carry):
        k = slot_of(delta_of(last - step))
        near_buf[k] = matmul(inner[half_rows(k, 1), :], w_down[...]).astype(BF16)
        y_sum(1, k).start()
        return carry

    def turn_keep(step, carry):
        k = slot_of(delta_of(last - step))
        part = times_transpose(grad_gate[half_rows(k, 0), :], w_gate[...]) + times_transpose(
            grad_up[half_rows(k, 0), :], w_up[...]
        )
        keep[aligned(k, quarter), :] = part.astype(BF16)
        return carry

    lax.fori_loop(0, outer, turn_parts, 0)
    lax.fori_loop(0, outer, turn_keep, 0)

    def z_got_rows(which, way, k):
        return aligned((which * 2 + way) * outer + k, quarter)

    def z_sum(which, way, k):
        to = wrap(k + 1 - 2 * way)
        return remote(
            z_stage.at[aligned(k, quarter), :], z_got.at[z_got_rows(which, way, to), :],
            rzs.at[which, k], rzr.at[which, way, to], nexts[way],
        )

    def z_got_at(which, way, k):
        return z_got[z_got_rows(which, way, k), :].astype(F32)

    def z_sum_arrived(which, way, k):
        return remote(
            z_stage.at[aligned(k, quarter), :], z_got.at[z_got_rows(which, way, k), :],
            rzs.at[which, k], rzr.at[which, way, k], nexts[way],
        )

    def own_share(which, k):
        if which == 0:
            share = keep[aligned(k, quarter), :].astype(F32)
        else:
            share = matmul(inner[half_rows(k, 0), :], w_down[...])
        return share + y_got[aligned(which * outer + k, quarter), :].astype(F32)

    def chain(which, step):
        delta = delta_of(last - step)
        k = slot_of(delta)
        at = aligned(k, quarter)
        y_sum(which, k).wait_recv()
        own = own_share(which, k)
        if which == 1:
            z_sum(0, 0, k).wait_send()
        for way, (here, before) in enumerate(((delta > 0, line > 0), (delta < 0, line < last))):

            @pl.when(here & before)
            def _():
                z_sum_arrived(which, way, k).wait_recv()
                z_stage[at, :] = (own + z_got_at(which, way, k)).astype(BF16)

            @pl.when(here & jnp.logical_not(before))
            def _():
                z_stage[at, :] = own.astype(BF16)

            pl.when(here)(z_sum(which, way, k).start)

    def chain_end(which):
        y_sum(which, 0).wait_recv()
        own = own_share(which, 0)
        for way, exists in ((0, line > 0), (1, line < last)):
            pl.when(exists)(z_sum_arrived(which, way, 0).wait_recv)
        below = jnp.where(line > 0, z_got_at(which, 0, 0), 0.0)
        above = jnp.where(line < last, z_got_at(which, 1, 0), 0.0)
        return own + below + above

    half_model = model // 2
    piece = half_model // 2

    def stage_rows(owner, r):
        return pl.ds(pl.multiple_of(owner * half_model + r * piece, piece), piece)

    stages = (stage_gate, stage_up)

    def piece_at(ref, a, r):
        return ref.at[a, pl.ds(r * piece, piece), :]

    def piece_near(a, r):
        return remote(
            stages[a].at[stage_rows(1 - core, r), :], piece_at(part_got, a, r),
            p_near_send.at[a, r], p_near_recv.at[a, r], core_dev,
        )

    def piece_far(a, r):
        return remote(
            stages[a].at[stage_rows(core, r), :], piece_at(part_far, a, r),
            p_far_send.at[a, r], p_far_recv.at[a, r], side_dev,
        )

    def piece_store(a, r):
        return pltpu.make_async_copy(
            piece_at(part_got, a, r), dw_both.at[a, stage_rows(core, r), :], store_sem.at[1 + 2 * a + r]
        )

    def piece_out(a, r):
        return remote(
            piece_at(part_got, a, r), dw_both.at[a, stage_rows(core, r), :],
            p_out_send.at[a, r], p_out_recv.at[a, r], core_dev,
        )

    def pieces(mine, r):
        at = stage_rows(core if mine else 1 - core, r)
        some = rows[:, at]
        for a, grads in enumerate((grad_gate, grad_up)):
            stages[a][at, :] = outer_sum(some, grads[...]).astype(BF16)
            if not mine:
                piece_near(a, r).start()

    def pieces_sum(r):
        at = stage_rows(core, r)
        for a in range(2):
            piece_near(a, r).wait_recv()
            stages[a][at, :] = (
                stages[a][at, :].astype(F32) + piece_at(part_got, a, r)[...].astype(F32)
            ).astype(BF16)
            piece_far(a, r).start()

    def pieces_total(r):
        for a in range(2):
            piece_far(a, r).wait_recv()
            total = stages[a][stage_rows(core, r), :].astype(F32) + piece_at(part_far, a, r)[
                ...
            ].astype(F32)
            piece_at(part_got, a, r)[...] = total.astype(BF16)
            piece_store(a, r).start()
            piece_out(a, r).start()

    pieces(False, 0)
    pieces(True, 0)
    pieces_sum(0)
    lax.fori_loop(0, outer, turn_outputs, 0)
    chain(0, 0)
    pieces(False, 1)
    pieces(True, 1)
    pieces_sum(1)
    for step in range(1, last):
        chain(0, step)
    grad_two = chain_end(0)

    values = middle_buf[...]
    back, gain_terms = norm_back(values, norm_scales(values), gain_ref[...], grad_two)
    grads = ups[0:quarter, :].astype(F32) + back
    branch[side, core] = grads.astype(BF16)

    def spread_copy(slot, s, device):
        block = branch.at[s, core]
        return remote(block, block, tp_send.at[3 + slot], tp_recv.at[3 + slot], device)

    spread_copy(0, side, side_dev).start()
    spread_copy(1, side, core_dev).start()
    grad_out[...] = grads
    gain_out[...] = jnp.sum(gain_terms, axis=0, keepdims=True)

    for way, exists in ((0, line < last), (1, line > 0)):
        pl.when(exists)(z_copy(way, 0).wait_send)

    def turn_sent(i, carry):
        delta = delta_of(i)
        k = slot_of(delta)
        y_copy(k).wait_send()
        for way, exists in enumerate(goes_on(delta)):
            pl.when(exists)(z_copy(way, k).wait_send)
        return carry

    lax.fori_loop(0, outer, turn_sent, 0)

    def turn_down(c, carry):
        at = aligned(c, chunk)
        stage_down[0:units, at] = outer_sum(inner[...], ups[:, at]).astype(BF16)
        return carry

    chain(1, 0)
    lax.fori_loop(0, outer, turn_down, 0)
    down_store = pltpu.make_async_copy(stage_down.at[pl.ds(0, units), :], dw_down, store_sem.at[0])
    down_store.start()
    for step in range(1, last):
        chain(1, step)
    spread_copy(0, side, side_dev).wait_recv()
    spread_copy(2, 1 - side, core_dev).start()
    pieces_total(0)
    layer_out[...] = (middle_buf[...] + chain_end(1)).astype(BF16)
    pieces_total(1)
    spread_copy(1, side, core_dev).wait_recv()

    down_store.wait()
    far_copy().wait_send()
    for index in range(LATE_BLOCKS):
        late_copy(index).wait_send()

    def turn_drain(i, carry):
        k = slot_of(delta_of(i))
        for which in range(2):
            y_sum(which, k).wait_send()
        pl.when(i > 0)(z_sum(1, 0, k).wait_send)
        return carry

    lax.fori_loop(0, outer, turn_drain, 0)
    for a in range(2):
        for r in range(2):
            piece_near(a, r).wait_send()
            piece_far(a, r).wait_send()
            piece_store(a, r).wait()
            piece_out(a, r).wait()
    spread_copy(0, side, side_dev).wait_send()
    spread_copy(1, side, core_dev).wait_send()
    spread_copy(2, 1 - side, core_dev).wait()


def middle_layer(gated, out_proj, hidden, gain, w_gate, w_up, w_down, ups, outer, sides):
    quarter, model = hidden.shape
    units = w_down.shape[0]
    rows_n = 2 * outer * quarter
    vmem = pl.BlockSpec(memory_space=pltpu.VMEM)
    anywhere = pl.BlockSpec(memory_space=pl.ANY)
    dma = pltpu.SemaphoreType.DMA
    line_rows = outer * quarter
    half = (2, model // 2, units)
    return pl.pallas_call(
        functools.partial(middle_kernel, outer),
        out_shape=[
            jax.ShapeDtypeStruct((quarter, model), BF16),
            jax.ShapeDtypeStruct((quarter, model), F32),
            jax.ShapeDtypeStruct((1, model), F32),
            jax.ShapeDtypeStruct((sides, 2, quarter, model), BF16),
            jax.ShapeDtypeStruct((2, model, units), BF16),
            jax.ShapeDtypeStruct((units, model), BF16),
        ],
        in_specs=[vmem] * 4 + [anywhere] * (3 + len(ups)),
        out_specs=[vmem] * 4 + [anywhere] * 2,
        scratch_shapes=[
            pltpu.VMEM((model, units), BF16),
            pltpu.VMEM((model, units), BF16),
            pltpu.VMEM((units, model), BF16),
            pltpu.VMEM((rows_n, model), BF16),
            pltpu.VMEM((rows_n, model), BF16),
            pltpu.VMEM((rows_n, units), BF16),
            pltpu.VMEM((rows_n, units), BF16),
            pltpu.VMEM((rows_n, units), BF16),
            pltpu.VMEM((4, quarter, model), BF16),
            pltpu.VMEM((quarter, model), BF16),
            pltpu.VMEM((quarter, model), BF16),
            pltpu.VMEM((quarter, model), F32),
            pltpu.VMEM((line_rows, model), BF16),
            pltpu.VMEM((line_rows, model), BF16),
            pltpu.VMEM((2 * line_rows, model), BF16),
            pltpu.VMEM((line_rows, model), BF16),
            pltpu.VMEM((4 * line_rows, model), BF16),
            pltpu.VMEM(half, BF16),
            pltpu.VMEM(half, BF16),
            dma((3 + len(ups),)),
            dma((5,)),
            dma((6,)),
            dma((6,)),
            dma((2, outer)),
            dma((outer,)),
            dma((outer,)),
            dma((outer,)),
            dma((2, outer)),
            dma((2, outer)),
            dma((2, outer)),
            dma((2, 2, outer)),
        ]
        + [dma((2, 2))] * 6
        + [dma((LATE_BLOCKS,))] * 2,
        compiler_params=pltpu.CompilerParams(
            collective_id=2, has_side_effects=True, vmem_limit_bytes=63 * 1024 * 1024
        ),
        cost_estimate=pl.CostEstimate(flops=3 * 10**10, bytes_accessed=4 * 10**7, transcendentals=0),
        name="middle",
    )(gated, out_proj, hidden, gain, w_gate, w_up, w_down, *ups)


FFN_CHUNKS = 2


def finish_kernel(
    outer, sides, sp_n, tp_n, streams, width_scale,
    *refs,
):
    MESH = pl.DeviceIdType.MESH
    parts = refs[:streams]
    (part_ref, hidden_ref, scale_ref, gain_ref, middle_ref, sums_ref) = refs[streams : streams + 6]
    last_in, layer_ref = refs[streams + 6 : streams + 8]
    outs = refs[streams + 8 : 2 * streams + 8]
    grad_out, sums_out, last_out, layer_out = refs[2 * streams + 8 : 2 * streams + 12]
    rest = refs[2 * streams + 12 :]
    got = rest[:streams]
    staged = rest[streams : 2 * streams]
    (near_got, far_got, keep_buf, far_stage, sums_got, sums_stage) = rest[2 * streams : 2 * streams + 6]
    rest = rest[2 * streams + 6 :]
    (last_keep, last_got, last_far, layer_send, layer_recv) = rest[:5]
    (f_load, f_near_send, f_near_recv, f_far_send, f_far_recv, f_store, f_out_send, f_out_recv) = rest[5:13]
    (reduce_send, reduce_recv, gather_send, gather_recv, pair_send, pair_recv) = rest[13:19]
    tp_send, tp_recv, sums_send, sums_recv = rest[19:]

    sp_i = lax.axis_index("sp")
    tp_i = lax.axis_index("tp")
    line = sp_i // 2
    half = sp_i % 2
    side = tp_i // 2
    core = tp_i % 2
    last = outer - 1

    def sp_at(z, y):
        return (tp_i, z * 2 + y)

    pair_dev = sp_at(line, 1 - half)
    core_dev = (side * 2 + (1 - core), sp_i)
    side_dev = ((1 - side) * 2 + core, sp_i)

    tp_bits = []
    bit = 1
    while bit < tp_n:
        tp_bits.append(bit)
        bit *= 2
    sp_bits = []
    bit = 1
    while bit < sp_n:
        sp_bits.append(bit)
        bit *= 2

    def flip(value, bit):
        return value + bit - 2 * bit * ((value // bit) % 2)

    sum_devs = [(flip(tp_i, b), sp_i) for b in tp_bits] + [(tp_i, flip(sp_i, b)) for b in sp_bits]

    barrier = pltpu.get_barrier_semaphore()
    greeted = [sp_at((line + 1) % outer, half), sp_at((line + outer - 1) % outer, half)] + sum_devs
    for device in greeted:
        pl.semaphore_signal(barrier, inc=1, device_id=device, device_id_type=MESH)
    pl.semaphore_wait(barrier, len(greeted))

    def remote(src, dst, send, recv, device):
        return pltpu.make_async_remote_copy(
            src_ref=src, dst_ref=dst, send_sem=send, recv_sem=recv,
            device_id=device, device_id_type=MESH,
        )

    places = (line, last - line)
    nexts = (sp_at(jnp.minimum(line + 1, last), half), sp_at(jnp.maximum(line - 1, 0), half))
    signs = (1, -1)

    def rows_of(stream, index):
        count = parts[stream].shape[0] // outer
        return pl.ds(pl.multiple_of(index * count, count), count)

    def reduce_copy(stream, way, step, src):
        return remote(
            src, got[stream].at[way, step - 1], reduce_send.at[stream, way, step - 1],
            reduce_recv.at[stream, way, step - 1], nexts[way],
        )

    def clamp(index):
        return jnp.clip(index, 0, last)

    def reduce_step(stream, step):
        for way in range(2):
            place, sign = places[way], signs[way]
            target = clamp(line + sign * (outer - step))
            own = parts[stream].at[rows_of(stream, target), :]

            @pl.when(place == 0)
            def _():
                reduce_copy(stream, way, step, own).start()

            if step > 1:

                @pl.when((place > 0) & (place <= step - 1))
                def _():
                    reduce_copy(stream, way, step - 1, own).wait_recv()
                    stage = staged[stream].at[way, step - 2]
                    stage[...] = (
                        got[stream][way, step - 2].astype(F32) + own[...].astype(F32)
                    ).astype(BF16)
                    reduce_copy(stream, way, step, stage).start()

    def gather_copy(stream, way, step, origin):
        block = outs[stream].at[half, rows_of(stream, origin), :]
        return remote(
            block, block, gather_send.at[stream, way, step - 1],
            gather_recv.at[stream, way, step - 1], nexts[way],
        )

    def pair_copy(stream, slot, origin):
        block = outs[stream].at[half, rows_of(stream, origin), :]
        return remote(block, block, pair_send.at[stream, slot], pair_recv.at[stream, slot], pair_dev)

    def reduce_final(stream):
        own = parts[stream].at[rows_of(stream, line), :]
        block = outs[stream].at[half, rows_of(stream, line), :]
        for way in range(2):

            @pl.when(places[way] > 0)
            def _():
                reduce_copy(stream, way, last, own).wait_recv()

        up = jnp.where(line > 0, got[stream][0, last - 1].astype(F32), 0.0)
        down = jnp.where(line < last, got[stream][1, last - 1].astype(F32), 0.0)
        block[...] = (own[...].astype(F32) + up + down).astype(BF16)
        for way in range(2):

            @pl.when(places[way] < last)
            def _():
                gather_copy(stream, way, 1, line).start()

        pair_copy(stream, 0, line).start()

    def gather_step(stream, step):
        for way in range(2):
            place, sign = places[way], signs[way]
            origin = clamp(line - sign * step)

            @pl.when(place >= step)
            def _():
                gather_copy(stream, way, step, origin).wait_recv()
                if step < last:

                    @pl.when(place < last)
                    def _():
                        gather_copy(stream, way, step + 1, origin).start()

                pair_copy(stream, 1 + way * last + step - 1, origin).start()

    def drain(stream):
        pair_copy(stream, 0, line).wait()
        for way in range(2):
            place, sign = places[way], signs[way]
            for step in range(1, outer):
                origin = clamp(line - sign * step)

                @pl.when(place <= step - 1)
                def _():
                    reduce_copy(stream, way, step, parts[stream].at[rows_of(stream, 0), :]).wait_send()

                @pl.when((place >= step - 1) & (place < last))
                def _():
                    gather_copy(stream, way, step, origin).wait_send()

                @pl.when(place >= step)
                def _():
                    pair_copy(stream, 1 + way * last + step - 1, origin).wait()

    def near_copy(index):
        return remote(
            part_ref.at[index, 1 - core], near_got.at[index], tp_send.at[index], tp_recv.at[index],
            core_dev,
        )

    def far_copy():
        return remote(far_stage, far_got, tp_send.at[sides], tp_recv.at[sides], side_dev)

    def spread_copy(slot, s, device):
        block = grad_out.at[s, core]
        return remote(block, block, tp_send.at[sides + slot], tp_recv.at[sides + slot], device)

    def input_step(step):
        if step == 0:
            for index in range(sides):
                near_copy(index).start()
        if step == 1:
            for index in range(sides):
                near_copy(index).wait_recv()
            keep_buf[...] = part_ref[side, core].astype(F32) + near_got[side].astype(F32)
            far_stage[...] = (
                part_ref[1 - side, core].astype(F32) + near_got[1 - side].astype(F32)
            ).astype(BF16)
            far_copy().start()
        if step == 2:
            far_copy().wait_recv()
            incoming = keep_buf[...] + far_got[...].astype(F32)
            values = hidden_ref[...].astype(F32)
            scales = scale_ref[...]
            weighted = incoming * gain_ref[...]
            inner_sum = jnp.sum(weighted * values, axis=-1, keepdims=True)
            grads = scales * weighted - values * (scales * scales * scales) * inner_sum * width_scale
            grad_out[side, core] = (middle_ref[...] + grads).astype(BF16)
            spread_copy(1, side, side_dev).start()
            spread_copy(2, side, core_dev).start()
        if step == 3:
            spread_copy(1, side, side_dev).wait_recv()
            spread_copy(3, 1 - side, core_dev).start()
        if step == 4:
            spread_copy(2, side, core_dev).wait_recv()
            spread_copy(3, 1 - side, core_dev).wait_recv()
            for index in range(sides):
                near_copy(index).wait_send()
            far_copy().wait_send()
            spread_copy(1, side, side_dev).wait_send()
            spread_copy(2, side, core_dev).wait_send()
            spread_copy(3, 1 - side, core_dev).wait_send()

    last_half = last_keep.shape[0]

    def ffn_at(j, ref, whole, owner):
        count = last_half // FFN_CHUNKS
        start = j * count
        if whole:
            start = pl.multiple_of(owner * last_half + start, count)
        return ref.at[pl.ds(start, count), :]

    def ffn_keep(j):
        return ffn_at(j, last_keep, False, 0)

    def ffn_got(j):
        return ffn_at(j, last_got, False, 0)

    def ffn_far(j):
        return ffn_at(j, last_far, False, 0)

    def ffn_load(j):
        return pltpu.make_async_copy(ffn_at(j, last_in, True, core), ffn_keep(j), f_load.at[j])

    def ffn_near_copy(j):
        return remote(
            ffn_at(j, last_in, True, 1 - core), ffn_got(j), f_near_send.at[j], f_near_recv.at[j], core_dev
        )

    def ffn_far_copy(j):
        return remote(ffn_keep(j), ffn_far(j), f_far_send.at[j], f_far_recv.at[j], side_dev)

    def ffn_store(j):
        return pltpu.make_async_copy(ffn_got(j), ffn_at(j, last_out, True, core), f_store.at[j])

    def ffn_out_copy(j):
        return remote(
            ffn_got(j), ffn_at(j, last_out, True, core), f_out_send.at[j], f_out_recv.at[j], core_dev
        )

    def ffn_sum(j):
        ffn_load(j).wait()
        ffn_near_copy(j).wait_recv()
        keep = ffn_keep(j)
        keep[...] = (keep[...].astype(F32) + ffn_got(j)[...].astype(F32)).astype(BF16)
        ffn_far_copy(j).start()

    def ffn_total(j):
        ffn_far_copy(j).wait_recv()
        total = ffn_keep(j)[...].astype(F32) + ffn_far(j)[...].astype(F32)
        ffn_got(j)[...] = total.astype(BF16)
        ffn_store(j).start()
        ffn_out_copy(j).start()

    def ffn_drain(j):
        ffn_near_copy(j).wait_send()
        ffn_far_copy(j).wait_send()
        ffn_store(j).wait()
        ffn_out_copy(j).wait()

    rounds = len(sum_devs)

    def sums_copy(step):
        src = sums_ref if step == 0 else sums_stage.at[step - 1]
        return remote(
            src, sums_got.at[step], sums_send.at[step], sums_recv.at[step], sum_devs[step]
        )

    def sums_step(step):
        if step > 0:
            sums_copy(step - 1).wait_recv()
            before = sums_ref[...] if step == 1 else sums_stage[step - 2]
            total = before + sums_got[step - 1]
            if step == rounds:
                sums_out[...] = total
            else:
                sums_stage[step - 1] = total
        if step < rounds:
            sums_copy(step).start()
        if step == rounds:
            for index in range(rounds):
                sums_copy(index).wait_send()

    def later(do, *args):
        return functools.partial(do, *args)

    def layer_copy(slot, s, device):
        block = layer_out.at[s, core]
        src = block if slot == 2 else layer_ref
        return remote(src, block, layer_send.at[slot], layer_recv.at[slot], device)

    def layer_own():
        return pltpu.make_async_copy(layer_ref, layer_out.at[side, core], layer_send.at[3])

    def layer_step(step):
        if step == 0:
            layer_copy(0, side, side_dev).start()
            layer_copy(1, side, core_dev).start()
            layer_own().start()
        if step == 1:
            layer_copy(0, 1 - side, side_dev).wait_recv()
            layer_copy(2, 1 - side, core_dev).start()
        if step == 2:
            layer_copy(1, side, core_dev).wait_recv()
            layer_own().wait()
            layer_copy(0, side, side_dev).wait_send()
            layer_copy(1, side, core_dev).wait_send()
            layer_copy(2, 1 - side, core_dev).wait()

    extra = [
        later(input_step, 0), later(input_step, 1), later(layer_step, 0), later(ffn_sum, 0),
        later(ffn_sum, 1), later(sums_step, 0), later(input_step, 2), later(sums_step, 1),
        later(layer_step, 1), later(sums_step, 2), later(input_step, 3), later(sums_step, 3),
        later(ffn_total, 0), later(sums_step, 4), later(layer_step, 2), later(input_step, 4),
        later(ffn_total, 1),
    ]
    extra += [later(sums_step, index) for index in range(5, rounds + 1)]
    for index in range(FFN_CHUNKS):
        ffn_near_copy(index).start()
        ffn_load(index).start()
    for turn in range(streams + 1):
        for step in range(1, outer + 1):
            if turn < streams:
                if step < outer:
                    reduce_step(turn, step)
                else:
                    reduce_final(turn)
            if turn > 0 and step < outer:
                gather_step(turn - 1, step)
            if extra:
                extra.pop(0)()
    for step in extra:
        step()
    for stream in range(streams):
        drain(stream)
    for index in range(FFN_CHUNKS):
        ffn_drain(index)


def finish(parts, part, hidden, scales, gain, middle, sums, ffn_last, layer, outer, sp_n, tp_n):
    streams = len(parts)
    sides = tp_n // 2
    quarter, model = hidden.shape
    last = outer - 1
    rounds = (tp_n - 1).bit_length() + (sp_n - 1).bit_length()
    vmem = pl.BlockSpec(memory_space=pltpu.VMEM)
    anywhere = pl.BlockSpec(memory_space=pl.ANY)
    chunk = [(2, last, p.shape[0] // outer, p.shape[1]) for p in parts]
    dma = pltpu.SemaphoreType.DMA
    return pl.pallas_call(
        functools.partial(finish_kernel, outer, sides, sp_n, tp_n, streams, 1.0 / model),
        out_shape=[jax.ShapeDtypeStruct((2,) + p.shape, BF16) for p in parts]
        + [
            jax.ShapeDtypeStruct((sides, 2, quarter, model), BF16),
            jax.ShapeDtypeStruct(sums.shape, F32),
        ]
        + [
            jax.ShapeDtypeStruct(ffn_last.shape, BF16),
            jax.ShapeDtypeStruct((sides, 2, quarter, model), BF16),
        ],
        in_specs=[vmem] * (streams + 6) + [anywhere, vmem],
        out_specs=[vmem] * (streams + 2) + [anywhere, vmem],
        scratch_shapes=[pltpu.VMEM(c, BF16) for c in chunk]
        + [pltpu.VMEM(c, BF16) for c in chunk]
        + [
            pltpu.VMEM((sides, quarter, model), BF16),
            pltpu.VMEM((quarter, model), BF16),
            pltpu.VMEM((quarter, model), F32),
            pltpu.VMEM((quarter, model), BF16),
            pltpu.VMEM((rounds,) + sums.shape, F32),
            pltpu.VMEM((rounds,) + sums.shape, F32),
        ]
        + [pltpu.VMEM((ffn_last.shape[0] // 2, ffn_last.shape[1]), BF16)] * 3
        + [dma((4,))] * 2
        + [dma((FFN_CHUNKS,))] * 8
        + [dma((streams, 2, last))] * 4
        + [dma((streams, 1 + 2 * last))] * 2
        + [dma((sides + 4,))] * 2
        + [dma((rounds,))] * 2,
        compiler_params=pltpu.CompilerParams(
            collective_id=1, has_side_effects=True, vmem_limit_bytes=60 * 1024 * 1024
        ),
        cost_estimate=pl.CostEstimate(flops=10**9, bytes_accessed=10**8, transcendentals=0),
        name="finish",
    )(*parts, part, hidden, scales, gain, middle, sums, ffn_last, layer)


def body(
    hidden,
    segment_ids,
    attn_norm,
    query_proj,
    key_proj,
    value_proj,
    gate_proj,
    output_proj,
    query_norm,
    key_norm,
    ffn_norm,
    ffn_gate,
    ffn_up,
    ffn_down,
    upstream,
):
    rows_dev, model = hidden.shape
    head_width = query_norm.shape[0]
    heads = query_proj.shape[1] // head_width
    groups = key_proj.shape[1] // head_width
    per_group = heads // groups
    group_width = groups * head_width
    sp_n = lax.axis_size("sp")
    tp_n = lax.axis_size("tp")
    outer = sp_n // 2
    sides = tp_n // 2
    quarter = rows_dev // tp_n
    tp_i = lax.axis_index("tp")
    sp_i = lax.axis_index("sp")
    ring_i = sp_i // 2
    pair_i = sp_i % 2
    side_i = tp_i // 2
    core_i = tp_i % 2
    own_first = sp_i * rows_dev
    quarter_first = tp_i * quarter
    scale = 1.0 / math.sqrt(head_width)

    ring_pairs = [(z * 2 + y, ((z + 1) % outer) * 2 + y) for z in range(outer) for y in range(2)]
    pair_pairs = [(i, i ^ 1) for i in range(sp_n)]
    side_pairs = [(i, i ^ 2) for i in range(tp_n)]
    core_pairs = [(i, i ^ 1) for i in range(tp_n)]

    def ring(value):
        return lax.ppermute(value, "sp", ring_pairs)

    def pair(value):
        return lax.ppermute(value, "sp", pair_pairs)

    def side(value):
        return lax.ppermute(value, "tp", side_pairs)

    def core(value):
        return lax.ppermute(value, "tp", core_pairs)

    def gather_sp(block, paired):
        blocks = []
        for k in range(outer):
            blocks.append((block, pair(block)) if k < paired else (block,))
            if k < outer - 1:
                block = ring(block)
        return blocks

    def scatter_sp(parts):
        def paired(k):
            return parts[k][0] + pair(parts[k][1].astype(BF16)).astype(F32)

        total = paired(1 % outer)
        for k in range(2, outer + 1):
            total = ring(total.astype(BF16)).astype(F32) + paired(k % outer)
        return total

    first_id = segment_ids[0]
    second_start = jnp.sum((segment_ids == first_id).astype(jnp.int32))
    own_index = own_first + jnp.arange(rows_dev, dtype=jnp.int32)
    own_starts = jnp.where(own_index < second_start, 0, second_start)
    steps_half = jnp.arange(head_width // 2, dtype=F32)
    frequencies = jnp.exp(steps_half * (-2.0 * math.log(THETA) / head_width))
    angles = (own_index - own_starts).astype(F32)[:, None] * frequencies[None, :]
    cosine = jnp.cos(angles)[:, None, :]
    sine = jnp.sin(angles)[:, None, :]

    hidden_full = hidden.astype(F32)
    normed_full, attn_scales = norm_rows(hidden_full, attn_norm)
    normed = normed_full.astype(BF16)
    key_raw = matmul(normed, key_proj).reshape(rows_dev, groups, head_width)
    value_rows = matmul(normed, value_proj).astype(BF16)
    key_normed, key_scales = norm_rows(key_raw, key_norm)
    key_rot = rotary(key_normed, cosine, sine).astype(BF16).reshape(rows_dev, group_width)
    kv_own = jnp.stack([key_rot, value_rows])

    low, high = (outer // 4, 3 * outer // 4) if outer % 4 == 0 else (0, outer)
    reach = high - 1 if low else outer - 1

    def up_pairs(step):
        return [
            (z * 2 + y, (z + 1) * 2 + y)
            for z in range(outer - 1)
            for y in range(2)
            if z + 1 - step >= 0 and (z + 1 - step >= low or z + 1 < high)
        ]

    kv_blocks = []
    travelling = kv_own
    for k in range(reach + 1):
        kv_blocks.append((travelling, pair(travelling)))
        if k < reach:
            travelling = lax.ppermute(travelling, "sp", up_pairs(k + 1))

    query_raw = matmul(normed, query_proj).reshape(rows_dev, heads, head_width)
    gate_raw = matmul(normed, gate_proj)
    query_normed, query_scales = norm_rows(query_raw, query_norm)
    queries = rotary(query_normed, cosine, sine).astype(BF16).reshape(rows_dev, heads * head_width)

    def swap_half(value):
        piece = model // 4
        mine = pair(lax.dynamic_slice_in_dim(value, ((1 - pair_i) * 2 + core_i) * piece, piece, 1))
        near = core(mine)
        return jnp.where(
            core_i == 1, jnp.concatenate([near, mine], 1), jnp.concatenate([mine, near], 1)
        )

    normed_own = lax.dynamic_slice_in_dim(normed, pair_i * (model // 2), model // 2, 1)
    both_normed = jnp.concatenate([normed_own, swap_half(normed)])

    grad_quarter = lax.dynamic_slice_in_dim(upstream, quarter_first, quarter)
    fused = 2 < outer and outer * quarter <= 512 and tp_n == 4
    up_blocks = gather_sp(grad_quarter, outer - LATE_BLOCKS if fused else outer)

    row_start_low = own_starts[0]
    row_start_high = own_starts[-1]

    def block_info(k):
        shards = [(ring_i - k) * 2 + pair_i, (ring_i - k) * 2 + (1 - pair_i)]
        entries = [own_first] + [shard * rows_dev for shard in shards]
        live = []
        full = []
        for shard in shards:
            token = shard * rows_dev
            live.append((shard >= 0) & (shard <= sp_i) & (token + rows_dev - 1 >= row_start_low))
            full.append((token >= row_start_high) & (shard < sp_i))
        return jnp.stack(entries + [v.astype(jnp.int32) for v in live + full]).astype(jnp.int32)

    infos = [block_info(k) for k in range(reach + 1)]
    starts_column = own_starts[:, None]
    starts_row = own_starts[None, :]
    carried = None
    for k in range(reach + 1):
        carried = attn_forward(
            infos[k], starts_column, queries, kv_blocks[k][0], kv_blocks[k][1], carried, scale
        )
    mix_acc, mix_sum = carried
    mixed = mix_acc / mix_sum
    lse = jnp.log2(mix_sum.reshape(rows_dev, heads, head_width)[:, :, 0])
    lse_rows = lse.T.reshape(groups, per_group, rows_dev)
    gate_sig = jax.nn.sigmoid(gate_raw)
    gated = (mixed * gate_sig).astype(BF16)
    gated_other = pair(gated)

    def scatter_tp(part):
        part = part.reshape(sides, 2, quarter, model)
        keep = lax.dynamic_index_in_dim(part, core_i, 1, keepdims=False)
        send = lax.dynamic_index_in_dim(part, 1 - core_i, 1, keepdims=False)
        keep = keep + core(send.astype(BF16)).astype(F32)
        mine = lax.dynamic_index_in_dim(keep, side_i, 0, keepdims=False)
        other = lax.dynamic_index_in_dim(keep, 1 - side_i, 0, keepdims=False)
        return mine + side(other.astype(BF16)).astype(F32)

    def gather_tp(block):
        far = side(block)
        swap_side = side_i == 1
        two = jnp.where(swap_side, jnp.stack([far, block]), jnp.stack([block, far]))
        near = core(two)
        swap_core = core_i == 1
        full = jnp.where(
            swap_core, jnp.stack([near, two], axis=1), jnp.stack([two, near], axis=1)
        )
        return full.reshape((rows_dev,) + block.shape[1:])

    if fused:
        layer_quarter, grad_middle_quarter, ffn_gain_sum, branch, *ffn_parts = middle_layer(
            gated,
            output_proj,
            lax.dynamic_slice_in_dim(hidden, quarter_first, quarter),
            ffn_norm[None, :],
            ffn_gate,
            ffn_up,
            ffn_down,
            [block for both in up_blocks for block in both],
            outer,
            sides,
        )
        grad_branch = branch.reshape(rows_dev, model)
        ffn_gain_sum = ffn_gain_sum[0]
    else:
        attn_quarter = scatter_tp(matmul(gated, output_proj))
        hidden_quarter = lax.dynamic_slice_in_dim(hidden, quarter_first, quarter).astype(F32)
        middle = hidden_quarter + attn_quarter
        normed_two_full, ffn_scales = norm_rows(middle, ffn_norm)
        normed_two = normed_two_full.astype(BF16)

        two_blocks = gather_sp(normed_two, outer)
        rows_list, up_list, inner_list, gate_list, grad_up_list = [None] * outer, [None] * outer, [None] * outer, [None] * outer, [None] * outer
        grad_parts = [None] * outer
        for k in list(range(1, outer)) + [0]:
            rows_k = jnp.concatenate(two_blocks[k])
            up_k = jnp.concatenate(up_blocks[k])
            gate_vals = matmul(rows_k, ffn_gate)
            up_vals = matmul(rows_k, ffn_up)
            sig = jax.nn.sigmoid(gate_vals)
            grad_inner = times_transpose(up_k, ffn_down)
            grad_gate = (grad_inner * up_vals * (sig * (1.0 + gate_vals * (1.0 - sig)))).astype(BF16)
            grad_up = (grad_inner * (gate_vals * sig)).astype(BF16)
            inner = (gate_vals * sig * up_vals).astype(BF16)
            grad_parts[k] = (
                times_transpose(grad_gate, ffn_gate) + times_transpose(grad_up, ffn_up)
            ).reshape(2, quarter, model)
            rows_list[k], up_list[k], inner_list[k] = rows_k, up_k, inner
            gate_list[k], grad_up_list[k] = grad_gate, grad_up
        grad_two = scatter_sp(grad_parts)

        norm_grad_two, ffn_gain_terms = norm_back(middle, ffn_scales, ffn_norm, grad_two)
        grad_middle_quarter = grad_quarter.astype(F32) + norm_grad_two
        grad_branch = gather_tp(grad_middle_quarter.astype(BF16))
        ffn_gain_sum = jnp.sum(ffn_gain_terms, axis=0)
        mlp_parts = [
            matmul(inner_list[k], ffn_down).reshape(2, quarter, model) for k in range(outer)
        ]
        layer_quarter = (middle + scatter_sp(mlp_parts)).astype(BF16)

    def sum_tp(part):
        total = part.astype(BF16).astype(F32)
        total = total + core(total.astype(BF16)).astype(F32)
        low = total.astype(BF16)
        return (low.astype(F32) + side(low).astype(F32)).astype(BF16)

    if not fused:
        rows_all = jnp.concatenate(rows_list)
        up_all = jnp.concatenate(up_list)
        inner_all = jnp.concatenate(inner_list)
        gate_all = jnp.concatenate(gate_list)
        grad_up_all = jnp.concatenate(grad_up_list)
        ffn_parts = [
            jnp.stack([outer_sum(rows_all, gate_all), outer_sum(rows_all, grad_up_all)]),
            outer_sum(inner_all, up_all),
        ]
        ffn_parts = [sum_tp(ffn_parts[0]), ffn_parts[1].astype(BF16)]
    ffn_both, ffn_last = ffn_parts

    branch_other = swap_half(grad_branch)
    branch_own = lax.dynamic_slice_in_dim(grad_branch, pair_i * (model // 2), model // 2, 1)
    output_half = outer_sum(
        jnp.concatenate([gated, gated_other]), jnp.concatenate([branch_own, branch_other])
    )
    grad_gated = times_transpose(grad_branch, output_proj)
    grad_mixed = (grad_gated * gate_sig).astype(BF16)
    grad_gate_raw = (grad_gated * mixed * (gate_sig * (1.0 - gate_sig))).astype(BF16)
    gate_half = outer_sum(both_normed, jnp.concatenate([grad_gate_raw, pair(grad_gate_raw)]))
    deltas = jnp.sum(
        (grad_mixed.astype(F32) * mixed).reshape(rows_dev, heads, head_width), axis=-1
    )
    delta_rows = deltas.T.reshape(groups, per_group, rows_dev)

    def down_pairs(step):
        return [(b, a) for a, b in up_pairs(step)]

    query_acc = None
    travelling = None
    for k in list(range(reach, -1, -1)):
        query_acc, grad_a, grad_b = attn_backward(
            infos[k], starts_row, lse_rows, delta_rows, queries, grad_mixed,
            kv_blocks[k][0], kv_blocks[k][1], query_acc, k == 0, scale,
        )
        total = grad_a.astype(F32) + pair(grad_b).astype(F32)
        if travelling is not None:
            total = total + travelling.astype(F32)
        if k > 0:
            travelling = lax.ppermute(total.astype(BF16), "sp", down_pairs(k))
    grad_key_rot = total[0].reshape(rows_dev, groups, head_width)
    grad_value_low = total[1].astype(BF16)
    grad_query_rot = (query_acc * scale).reshape(rows_dev, heads, head_width)
    grad_query_raw, query_gain_terms = norm_back(
        query_raw, query_scales, query_norm, rotary_back(grad_query_rot, cosine, sine)
    )
    grad_key_raw, key_gain_terms = norm_back(
        key_raw, key_scales, key_norm, rotary_back(grad_key_rot, cosine, sine)
    )
    grad_query_low = grad_query_raw.reshape(rows_dev, heads * head_width).astype(BF16)
    grad_key_low = grad_key_raw.reshape(rows_dev, group_width).astype(BF16)
    grad_kv_low = jnp.concatenate([grad_key_low, grad_value_low], axis=1)

    both_queries = jnp.concatenate([grad_query_low, pair(grad_query_low)])
    both_kv = jnp.concatenate([grad_kv_low, pair(grad_kv_low)])
    parts = [
        output_half.astype(BF16),
        gate_half.astype(BF16),
        outer_sum(both_normed, both_queries).astype(BF16),
        outer_sum(both_normed, both_kv).astype(BF16),
    ]

    grad_normed_part = (
        times_transpose(grad_query_low, query_proj)
        + times_transpose(grad_key_low, key_proj)
        + times_transpose(grad_value_low, value_proj)
        + times_transpose(grad_gate_raw, gate_proj)
    )
    gains = jnp.concatenate(
        [
            jnp.sum(grad_normed_part * hidden_full * attn_scales, axis=0),
            ffn_gain_sum,
            jnp.sum(query_gain_terms, axis=(0, 1)),
            jnp.sum(key_gain_terms, axis=(0, 1)),
        ]
    )
    gains_at = 2 * model + 2 * head_width
    gains = jnp.pad(gains, (0, -gains_at % 1024)).reshape(-1, 128)
    scales_quarter = lax.dynamic_slice_in_dim(attn_scales, quarter_first, quarter)
    finished = finish(
        parts,
        grad_normed_part.astype(BF16).reshape(sides, 2, quarter, model),
        lax.dynamic_slice_in_dim(hidden, quarter_first, quarter),
        scales_quarter,
        attn_norm[None, :],
        grad_middle_quarter,
        gains,
        ffn_last,
        layer_quarter,
        outer,
        sp_n,
        tp_n,
    )
    output_all, gate_all_w, query_all, kv_all, input_all, gains, ffn_last, layer_all = finished
    output_grad = jnp.concatenate([output_all[0], output_all[1]], axis=1).astype(F32)
    gate_grad = gate_all_w.reshape(model, heads * head_width).astype(F32)
    query_grad = query_all.reshape(model, heads * head_width).astype(F32)
    kv_all = kv_all.reshape(model, 2 * group_width)
    key_grad = kv_all[:, :group_width].astype(F32)
    value_grad = kv_all[:, group_width:].astype(F32)
    hidden_grad = input_all.reshape(rows_dev, model).astype(F32)
    gains = gains.reshape(-1)
    return (
        layer_all.reshape(rows_dev, model),
        hidden_grad,
        gains[:model],
        query_grad,
        key_grad,
        value_grad,
        gate_grad,
        output_grad,
        gains[2 * model : 2 * model + head_width],
        gains[2 * model + head_width : gains_at],
        gains[model : 2 * model],
        ffn_both[0].astype(F32),
        ffn_both[1].astype(F32),
        ffn_last.astype(F32),
    )


def solution(mesh):
    placed = (
        P("sp", None),
        P(),
        P(),
        P(None, "tp"),
        P(None, "tp"),
        P(None, "tp"),
        P(None, "tp"),
        P("tp", None),
        P(),
        P(),
        P(),
        P(None, "sp"),
        P(None, "sp"),
        P("sp", None),
        P("sp", None),
    )
    return jax.shard_map(
        body,
        mesh=mesh,
        in_specs=placed,
        out_specs=(
            P("sp", None),
            P("sp", None),
            P(),
            P(None, "tp"),
            P(None, "tp"),
            P(None, "tp"),
            P(None, "tp"),
            P("tp", None),
            P(),
            P(),
            P(),
            P(None, "sp"),
            P(None, "sp"),
            P("sp", None),
        ),
        check_vma=False,
    )
```

```python
import functools
import math

import jax
import jax.numpy as jnp
from jax import lax
from jax.experimental import pallas as pl
from jax.experimental.pallas import tpu as pltpu
from jax.sharding import PartitionSpec as P

EPSILON = 1e-06
THETA = 1000000.0
LOG2E = 1.4426950408889634
F32 = jnp.float32
BF16 = jnp.bfloat16


def norm_scales(values):
    return lax.rsqrt(jnp.mean(values * values, axis=-1, keepdims=True) + EPSILON)


def norm_rows(values, gain):
    scales = norm_scales(values)
    return (values * scales * gain, scales)


def norm_back(values, scales, gain, incoming):
    weighted = incoming * gain
    inner_sum = jnp.sum(weighted * values, axis=-1, keepdims=True)
    grad_values = (
        scales * weighted - values * (scales * scales * scales) * inner_sum / values.shape[-1]
    )
    return (grad_values, incoming * values * scales)


def rotary(values, cosine, sine):
    half_width = values.shape[-1] // 2
    front_half = values[..., :half_width]
    back_half = values[..., half_width:]
    return jnp.concatenate(
        [front_half * cosine - back_half * sine, back_half * cosine + front_half * sine], axis=-1
    )


def rotary_back(grads, cosine, sine):
    half_width = grads.shape[-1] // 2
    front_half = grads[..., :half_width]
    back_half = grads[..., half_width:]
    return jnp.concatenate(
        [front_half * cosine + back_half * sine, back_half * cosine - front_half * sine], axis=-1
    )


def matmul(left, right):
    return jnp.dot(left, right, preferred_element_type=F32)


def outer_sum(left, right):
    return lax.dot_general(left, right, (((0,), (0,)), ((), ())), preferred_element_type=F32)


def times_transpose(left, right):
    return lax.dot_general(left, right, (((1,), (1,)), ((), ())), preferred_element_type=F32)


def attn_forward_kernel(first, diagonal, scale, info, starts, queries, kv_a, kv_b, *rest):
    if first:
        acc_out, sum_out = rest
    else:
        acc_in, sum_in, acc_out, sum_out = rest
    rows = queries.shape[0]
    keys_n = kv_a.shape[1]
    per_group = queries.shape[1] // kv_a.shape[2]
    width = kv_a.shape[2]
    if first:
        acc_out[...] = jnp.zeros_like(acc_out)
        sum_out[...] = jnp.zeros_like(sum_out)
    else:
        acc_out[...] = acc_in[...]
        sum_out[...] = sum_in[...]
    own_first = info[0]
    for slot, block in enumerate((kv_a, kv_b)):
        key_first = info[1 + slot]
        live = info[3 + slot] > 0

        def work(masked, causal):
            ones = jnp.ones((keys_n, width), BF16)
            values = jnp.concatenate([block[1], ones], axis=1)
            keys = block[0]
            if masked:
                key_index = key_first + lax.broadcasted_iota(jnp.int32, (rows, keys_n), 1)
                allowed = key_index >= starts[...]
                if causal:
                    row_index = own_first + lax.broadcasted_iota(jnp.int32, (rows, keys_n), 0)
                    allowed = allowed & (key_index <= row_index)
            for head in range(per_group):
                cols = slice(head * width, (head + 1) * width)
                scores = times_transpose(queries[:, cols], keys)
                weights = jnp.exp2(scores * (scale * LOG2E))
                if masked:
                    weights = jnp.where(allowed, weights, 0.0)
                both = matmul(weights.astype(BF16), values)
                acc_out[:, cols] += both[:, :width]
                sum_out[:, cols] += both[:, width:]

        if diagonal and slot == 0:
            work(True, True)
        else:
            full = info[5 + slot] > 0
            pl.when(live & full)(functools.partial(work, False, False))
            pl.when(live & jnp.logical_not(full))(functools.partial(work, True, False))


def attn_forward(info, starts, queries, kv_a, kv_b, carried, scale):
    rows, all_width = queries.shape
    width = 128
    groups = kv_a.shape[2] // width
    group_width = all_width // groups
    keys_n = kv_a.shape[1]
    first = carried is None
    spec_q = pl.BlockSpec((rows, group_width), lambda g, info: (0, g))
    spec_kv = pl.BlockSpec((2, keys_n, width), lambda g, info: (0, 0, g))
    specs = [pl.BlockSpec((rows, 1), lambda g, info: (0, 0)), spec_q, spec_kv, spec_kv]
    operands = [starts, queries, kv_a, kv_b]
    if not first:
        specs += [spec_q, spec_q]
        operands += list(carried)
    return pl.pallas_call(
        functools.partial(attn_forward_kernel, first, first, scale),
        grid_spec=pltpu.PrefetchScalarGridSpec(
            num_scalar_prefetch=1,
            grid=(groups,),
            in_specs=specs,
            out_specs=[spec_q, spec_q],
        ),
        out_shape=[jax.ShapeDtypeStruct((rows, all_width), F32)] * 2,
        compiler_params=pltpu.CompilerParams(dimension_semantics=("arbitrary",)),
        cost_estimate=pl.CostEstimate(
            flops=16 * rows * keys_n * all_width,
            transcendentals=2 * rows * keys_n * all_width // width,
            bytes_accessed=8 * rows * all_width,
        ),
        name="attn_forward",
    )(info, *operands)


def attn_backward_kernel(first, diagonal, scale, info, starts, lse, deltas, queries, grads, kv_a, kv_b, *rest):
    if first:
        grad_q, grad_a, grad_b = rest
    else:
        grad_in, grad_q, grad_a, grad_b = rest
    rows = queries.shape[0]
    keys_n = kv_a.shape[1]
    width = kv_a.shape[2]
    per_group = queries.shape[1] // width
    if first:
        grad_q[...] = jnp.zeros_like(grad_q)
    else:
        grad_q[...] = grad_in[...]
    own_first = info[0]
    for slot, (block, out) in enumerate(((kv_a, grad_a), (kv_b, grad_b))):
        key_first = info[1 + slot]
        live = info[3 + slot] > 0

        def work(masked, causal):
            keys = block[0]
            values = block[1]
            keys_t = keys.T
            if masked:
                key_index = key_first + lax.broadcasted_iota(jnp.int32, (keys_n, rows), 0)
                allowed = key_index >= starts[...]
                if causal:
                    row_index = own_first + lax.broadcasted_iota(jnp.int32, (keys_n, rows), 1)
                    allowed = allowed & (key_index <= row_index)
            total_k = jnp.zeros((keys_n, width), F32)
            total_v = jnp.zeros((keys_n, width), F32)
            for head in range(per_group):
                cols = slice(head * width, (head + 1) * width)
                q_head = queries[:, cols]
                g_head = grads[:, cols]
                scores = times_transpose(keys, q_head)
                probs = jnp.exp2(scores * (scale * LOG2E) - lse[0, head : head + 1, :])
                if masked:
                    probs = jnp.where(allowed, probs, 0.0)
                grad_probs = times_transpose(values, g_head)
                grad_scores = (probs * (grad_probs - deltas[0, head : head + 1, :])).astype(BF16)
                total_v += matmul(probs.astype(BF16), g_head)
                total_k += matmul(grad_scores, q_head)
                grad_q[:, cols] += matmul(keys_t, grad_scores).T
            out[0] = (total_k * scale).astype(BF16)
            out[1] = total_v.astype(BF16)

        if diagonal and slot == 0:
            work(True, True)
        else:
            full = info[5 + slot] > 0
            pl.when(live & full)(functools.partial(work, False, False))
            pl.when(live & jnp.logical_not(full))(functools.partial(work, True, False))

            @pl.when(jnp.logical_not(live))
            def _():
                out[...] = jnp.zeros_like(out)


def attn_backward(info, starts_row, lse, deltas, queries, grads, kv_a, kv_b, carried, diagonal, scale):
    rows, all_width = queries.shape
    width = 128
    groups = kv_a.shape[2] // width
    group_width = all_width // groups
    per_group = group_width // width
    keys_n = kv_a.shape[1]
    first = carried is None
    spec_q = pl.BlockSpec((rows, group_width), lambda g, info: (0, g))
    spec_kv = pl.BlockSpec((2, keys_n, width), lambda g, info: (0, 0, g))
    spec_row = pl.BlockSpec((1, per_group, rows), lambda g, info: (g, 0, 0))
    specs = [
        pl.BlockSpec((1, rows), lambda g, info: (0, 0)),
        spec_row,
        spec_row,
        spec_q,
        spec_q,
        spec_kv,
        spec_kv,
    ]
    operands = [starts_row, lse, deltas, queries, grads, kv_a, kv_b]
    if not first:
        specs.append(spec_q)
        operands.append(carried)
    return pl.pallas_call(
        functools.partial(attn_backward_kernel, first, diagonal, scale),
        grid_spec=pltpu.PrefetchScalarGridSpec(
            num_scalar_prefetch=1,
            grid=(groups,),
            in_specs=specs,
            out_specs=[spec_q, spec_kv, spec_kv],
        ),
        out_shape=[
            jax.ShapeDtypeStruct((rows, all_width), F32),
            jax.ShapeDtypeStruct(kv_a.shape, BF16),
            jax.ShapeDtypeStruct(kv_a.shape, BF16),
        ],
        compiler_params=pltpu.CompilerParams(dimension_semantics=("arbitrary",)),
        cost_estimate=pl.CostEstimate(
            flops=20 * rows * keys_n * all_width,
            transcendentals=2 * rows * keys_n * all_width // width,
            bytes_accessed=8 * rows * all_width,
        ),
        name="attn_backward",
    )(info, *operands)


LATE_BLOCKS = 2


def middle_kernel(outer, *refs):
    MESH = pl.DeviceIdType.MESH
    blocks = 2 * outer - LATE_BLOCKS
    (gated, out_proj, hidden_ref, gain_ref, gate_in, up_in, down_in) = refs[:7]
    ups_in = refs[7 : 7 + blocks]
    (layer_out, grad_out, gain_out, branch, dw_both, dw_down) = refs[7 + blocks : 13 + blocks]
    (
        w_gate, w_up, w_down, ups, rows, inner, grad_gate, grad_up,
        near_buf, far_stage, far_got, middle_buf,
        keep, y_stage, y_got, z_stage, z_got, part_got, part_far,
        load_sem, store_sem, tp_send, tp_recv, zs, zr, ys, yr, rys, ryr, rzs, rzr,
        p_near_send, p_near_recv, p_far_send, p_far_recv, p_out_send, p_out_recv, us, ur,
    ) = refs[13 + blocks :]
    stage_gate, stage_up, stage_down = w_gate, w_up, rows
    far_keep, own_keep = grad_out, middle_buf
    units = w_down.shape[0]
    quarter, model = hidden_ref.shape
    group = 2 * quarter
    chunk = model // outer
    last = outer - 1

    sp_i = lax.axis_index("sp")
    tp_i = lax.axis_index("tp")
    line = sp_i // 2
    half = sp_i % 2
    side = tp_i // 2
    core = tp_i % 2

    def sp_at(z, y):
        return (tp_i, z * 2 + y)

    pair_dev = sp_at(line, 1 - half)
    core_dev = (side * 2 + (1 - core), sp_i)
    side_dev = ((1 - side) * 2 + core, sp_i)
    nexts = (sp_at(jnp.minimum(line + 1, last), half), sp_at(jnp.maximum(line - 1, 0), half))

    late = list(range(outer - LATE_BLOCKS, outer))
    ups_at = [at for at in range(2 * outer) if at % 2 == 0 or at // 2 not in late]
    loads = [
        pltpu.make_async_copy(src, dst, load_sem.at[index])
        for index, (src, dst) in enumerate(
            [(down_in, w_down)]
            + [(src, ups.at[pl.ds(at * quarter, quarter), :]) for at, src in zip(ups_at, ups_in)]
            + [(gate_in, w_gate), (up_in, w_up)]
        )
    ]
    for load in loads:
        load.start()

    barrier = pltpu.get_barrier_semaphore()
    greeted = [
        sp_at((line + 1) % outer, half), sp_at((line + outer - 1) % outer, half),
        pair_dev, core_dev, side_dev,
    ]
    for device in greeted:
        pl.semaphore_signal(barrier, inc=1, device_id=device, device_id_type=MESH)
    pl.semaphore_wait(barrier, len(greeted))

    def remote(src, dst, send, recv, device):
        return pltpu.make_async_remote_copy(
            src_ref=src, dst_ref=dst, send_sem=send, recv_sem=recv,
            device_id=device, device_id_type=MESH,
        )

    def aligned(index, count):
        return pl.ds(pl.multiple_of(index * count, count), count)

    def late_copy(index):
        at = late[index] * 2
        return remote(
            ups.at[pl.ds(at * quarter, quarter), :], ups.at[pl.ds((at + 1) * quarter, quarter), :],
            us.at[index], ur.at[index], pair_dev,
        )

    def near_copy(j):
        return remote(near_buf.at[j], near_buf.at[2 + j], tp_send.at[j], tp_recv.at[j], core_dev)

    def far_copy():
        return remote(far_stage, far_got, tp_send.at[2], tp_recv.at[2], side_dev)

    def projected(s, c):
        return matmul(gated[aligned(s * 2 + c, quarter), :], out_proj[...])

    near_buf[0] = projected(1 - side, 1 - core).astype(BF16)
    near_copy(0).start()
    near_buf[1] = projected(side, 1 - core).astype(BF16)
    near_copy(1).start()
    for index in range(LATE_BLOCKS):
        loads[1 + ups_at.index(late[index] * 2)].wait()
        late_copy(index).start()
    far_keep[...] = projected(1 - side, core)
    near_copy(0).wait_recv()
    far_stage[...] = (far_keep[...] + near_buf[2].astype(F32)).astype(BF16)
    far_copy().start()
    own_keep[...] = projected(side, core)

    near_copy(1).wait_recv()
    far_copy().wait_recv()
    middle = hidden_ref[...].astype(F32) + (
        own_keep[...] + near_buf[3].astype(F32) + far_got[...].astype(F32)
    )
    middle_buf[...] = middle
    rows[0:quarter, :] = (middle * norm_scales(middle) * gain_ref[...]).astype(BF16)

    def entry(k, j):
        return pl.ds(pl.multiple_of((k * 2 + j) * quarter, quarter), quarter)

    def wrap(k):
        return (k + outer) % outer

    def z_copy(way, k):
        to = wrap(k + 1 - 2 * way)
        return remote(
            rows.at[entry(k, 0), :], rows.at[entry(to, 0), :], zs.at[way, k], zr.at[to], nexts[way]
        )

    def z_arrived(k):
        return remote(
            rows.at[entry(k, 0), :], rows.at[entry(k, 0), :], zs.at[0, k], zr.at[k], nexts[0]
        )

    def y_copy(k):
        return remote(
            rows.at[entry(k, 0), :], rows.at[entry(k, 1), :], ys.at[k], yr.at[k], pair_dev
        )

    short = jnp.minimum(line, last - line)

    def delta_of(i):
        near = jnp.where(i % 2 == 1, -((i + 1) // 2), (i + 1) // 2)
        far = jnp.where(line < last - line, i - short, short - i)
        return jnp.where(i <= 2 * short, near, far)

    def slot_of(delta):
        return jnp.where(delta <= 0, -delta, outer - delta)

    for way, exists in ((0, line < last), (1, line > 0)):
        pl.when(exists)(z_copy(way, 0).start)
    y_copy(0).start()

    def goes_on(delta):
        return ((delta < 0) & (line < last), (delta > 0) & (line > 0))

    def forward(i):
        delta = delta_of(i)
        k = slot_of(delta)
        z_arrived(k).wait_recv()
        for way, exists in enumerate(goes_on(delta)):
            pl.when(exists)(z_copy(way, k).start)
        y_copy(k).start()

    waited = [1 + ups_at.index(k * 2) for k in late]
    for index, load in enumerate(loads):
        if index not in waited:
            load.wait()
    for index in range(LATE_BLOCKS):
        late_copy(index).wait_recv()
    forward(1)

    def turn_forward(i, carry):
        @pl.when(i + 2 < outer)
        def _():
            forward(i + 2)

        k = slot_of(delta_of(i))
        y_copy(k).wait_recv()
        at = aligned(k, group)
        rows_k = rows[at, :]
        gate_vals = matmul(rows_k, w_gate[...])
        up_vals = matmul(rows_k, w_up[...])
        incoming = times_transpose(ups[at, :], w_down[...])
        sig = jax.nn.sigmoid(gate_vals)
        silu = gate_vals * sig
        grad_gate[at, :] = (incoming * up_vals * (sig * (1.0 + gate_vals * (1.0 - sig)))).astype(BF16)
        grad_up[at, :] = (incoming * silu).astype(BF16)
        inner[at, :] = (silu * up_vals).astype(BF16)
        return carry

    lax.fori_loop(0, outer, turn_forward, 0)

    near_copy(0).wait_send()
    near_copy(1).wait_send()

    def y_sum(which, k):
        at = aligned(k, quarter)
        src = y_stage.at[at, :] if which == 0 else near_buf.at[k]
        got = y_got.at[aligned(which * outer + k, quarter), :]
        return remote(src, got, rys.at[which, k], ryr.at[which, k], pair_dev)

    def half_rows(k, j):
        return pl.ds(pl.multiple_of((k * 2 + j) * quarter, quarter), quarter)

    def turn_parts(step, carry):
        k = slot_of(delta_of(last - step))
        part = times_transpose(grad_gate[half_rows(k, 1), :], w_gate[...]) + times_transpose(
            grad_up[half_rows(k, 1), :], w_up[...]
        )
        y_stage[aligned(k, quarter), :] = part.astype(BF16)
        y_sum(0, k).start()
        return carry

    def turn_outputs(step, carry):
        k = slot_of(delta_of(last - step))
        near_buf[k] = matmul(inner[half_rows(k, 1), :], w_down[...]).astype(BF16)
        y_sum(1, k).start()
        return carry

    def turn_keep(step, carry):
        k = slot_of(delta_of(last - step))
        part = times_transpose(grad_gate[half_rows(k, 0), :], w_gate[...]) + times_transpose(
            grad_up[half_rows(k, 0), :], w_up[...]
        )
        keep[aligned(k, quarter), :] = part.astype(BF16)
        return carry

    lax.fori_loop(0, outer, turn_parts, 0)
    lax.fori_loop(0, outer, turn_keep, 0)

    def z_got_rows(which, way, k):
        return aligned((which * 2 + way) * outer + k, quarter)

    def z_sum(which, way, k):
        to = wrap(k + 1 - 2 * way)
        return remote(
            z_stage.at[aligned(k, quarter), :], z_got.at[z_got_rows(which, way, to), :],
            rzs.at[which, k], rzr.at[which, way, to], nexts[way],
        )

    def z_got_at(which, way, k):
        return z_got[z_got_rows(which, way, k), :].astype(F32)

    def z_sum_arrived(which, way, k):
        return remote(
            z_stage.at[aligned(k, quarter), :], z_got.at[z_got_rows(which, way, k), :],
            rzs.at[which, k], rzr.at[which, way, k], nexts[way],
        )

    def own_share(which, k):
        if which == 0:
            share = keep[aligned(k, quarter), :].astype(F32)
        else:
            share = matmul(inner[half_rows(k, 0), :], w_down[...])
        return share + y_got[aligned(which * outer + k, quarter), :].astype(F32)

    def chain(which, step):
        delta = delta_of(last - step)
        k = slot_of(delta)
        at = aligned(k, quarter)
        y_sum(which, k).wait_recv()
        own = own_share(which, k)
        if which == 1:
            z_sum(0, 0, k).wait_send()
        for way, (here, before) in enumerate(((delta > 0, line > 0), (delta < 0, line < last))):

            @pl.when(here & before)
            def _():
                z_sum_arrived(which, way, k).wait_recv()
                z_stage[at, :] = (own + z_got_at(which, way, k)).astype(BF16)

            @pl.when(here & jnp.logical_not(before))
            def _():
                z_stage[at, :] = own.astype(BF16)

            pl.when(here)(z_sum(which, way, k).start)

    def chain_end(which):
        y_sum(which, 0).wait_recv()
        own = own_share(which, 0)
        for way, exists in ((0, line > 0), (1, line < last)):
            pl.when(exists)(z_sum_arrived(which, way, 0).wait_recv)
        below = jnp.where(line > 0, z_got_at(which, 0, 0), 0.0)
        above = jnp.where(line < last, z_got_at(which, 1, 0), 0.0)
        return own + below + above

    half_model = model // 2
    piece = half_model // 2

    def stage_rows(owner, r):
        return pl.ds(pl.multiple_of(owner * half_model + r * piece, piece), piece)

    stages = (stage_gate, stage_up)

    def piece_at(ref, a, r):
        return ref.at[a, pl.ds(r * piece, piece), :]

    def piece_near(a, r):
        return remote(
            stages[a].at[stage_rows(1 - core, r), :], piece_at(part_got, a, r),
            p_near_send.at[a, r], p_near_recv.at[a, r], core_dev,
        )

    def piece_far(a, r):
        return remote(
            stages[a].at[stage_rows(core, r), :], piece_at(part_far, a, r),
            p_far_send.at[a, r], p_far_recv.at[a, r], side_dev,
        )

    def piece_store(a, r):
        return pltpu.make_async_copy(
            piece_at(part_got, a, r), dw_both.at[a, stage_rows(core, r), :], store_sem.at[1 + 2 * a + r]
        )

    def piece_out(a, r):
        return remote(
            piece_at(part_got, a, r), dw_both.at[a, stage_rows(core, r), :],
            p_out_send.at[a, r], p_out_recv.at[a, r], core_dev,
        )

    def pieces(mine, r):
        at = stage_rows(core if mine else 1 - core, r)
        some = rows[:, at]
        for a, grads in enumerate((grad_gate, grad_up)):
            stages[a][at, :] = outer_sum(some, grads[...]).astype(BF16)
            if not mine:
                piece_near(a, r).start()

    def pieces_sum(r):
        at = stage_rows(core, r)
        for a in range(2):
            piece_near(a, r).wait_recv()
            stages[a][at, :] = (
                stages[a][at, :].astype(F32) + piece_at(part_got, a, r)[...].astype(F32)
            ).astype(BF16)
            piece_far(a, r).start()

    def pieces_total(r):
        for a in range(2):
            piece_far(a, r).wait_recv()
            total = stages[a][stage_rows(core, r), :].astype(F32) + piece_at(part_far, a, r)[
                ...
            ].astype(F32)
            piece_at(part_got, a, r)[...] = total.astype(BF16)
            piece_store(a, r).start()
            piece_out(a, r).start()

    pieces(False, 0)
    pieces(True, 0)
    pieces_sum(0)
    lax.fori_loop(0, outer, turn_outputs, 0)
    chain(0, 0)
    pieces(False, 1)
    pieces(True, 1)
    pieces_sum(1)
    for step in range(1, last):
        chain(0, step)
    grad_two = chain_end(0)

    values = middle_buf[...]
    back, gain_terms = norm_back(values, norm_scales(values), gain_ref[...], grad_two)
    grads = ups[0:quarter, :].astype(F32) + back
    branch[side, core] = grads.astype(BF16)

    def spread_copy(slot, s, device):
        block = branch.at[s, core]
        return remote(block, block, tp_send.at[3 + slot], tp_recv.at[3 + slot], device)

    spread_copy(0, side, side_dev).start()
    spread_copy(1, side, core_dev).start()
    grad_out[...] = grads
    gain_out[...] = jnp.sum(gain_terms, axis=0, keepdims=True)

    for way, exists in ((0, line < last), (1, line > 0)):
        pl.when(exists)(z_copy(way, 0).wait_send)

    def turn_sent(i, carry):
        delta = delta_of(i)
        k = slot_of(delta)
        y_copy(k).wait_send()
        for way, exists in enumerate(goes_on(delta)):
            pl.when(exists)(z_copy(way, k).wait_send)
        return carry

    lax.fori_loop(0, outer, turn_sent, 0)

    def turn_down(c, carry):
        at = aligned(c, chunk)
        stage_down[0:units, at] = outer_sum(inner[...], ups[:, at]).astype(BF16)
        return carry

    chain(1, 0)
    lax.fori_loop(0, outer, turn_down, 0)
    down_store = pltpu.make_async_copy(stage_down.at[pl.ds(0, units), :], dw_down, store_sem.at[0])
    down_store.start()
    for step in range(1, last):
        chain(1, step)
    spread_copy(0, side, side_dev).wait_recv()
    spread_copy(2, 1 - side, core_dev).start()
    pieces_total(0)
    layer_out[...] = (middle_buf[...] + chain_end(1)).astype(BF16)
    pieces_total(1)
    spread_copy(1, side, core_dev).wait_recv()

    down_store.wait()
    far_copy().wait_send()
    for index in range(LATE_BLOCKS):
        late_copy(index).wait_send()

    def turn_drain(i, carry):
        k = slot_of(delta_of(i))
        for which in range(2):
            y_sum(which, k).wait_send()
        pl.when(i > 0)(z_sum(1, 0, k).wait_send)
        return carry

    lax.fori_loop(0, outer, turn_drain, 0)
    for a in range(2):
        for r in range(2):
            piece_near(a, r).wait_send()
            piece_far(a, r).wait_send()
            piece_store(a, r).wait()
            piece_out(a, r).wait()
    spread_copy(0, side, side_dev).wait_send()
    spread_copy(1, side, core_dev).wait_send()
    spread_copy(2, 1 - side, core_dev).wait()


def middle_layer(gated, out_proj, hidden, gain, w_gate, w_up, w_down, ups, outer, sides):
    quarter, model = hidden.shape
    units = w_down.shape[0]
    rows_n = 2 * outer * quarter
    vmem = pl.BlockSpec(memory_space=pltpu.VMEM)
    anywhere = pl.BlockSpec(memory_space=pl.ANY)
    dma = pltpu.SemaphoreType.DMA
    line_rows = outer * quarter
    half = (2, model // 2, units)
    return pl.pallas_call(
        functools.partial(middle_kernel, outer),
        out_shape=[
            jax.ShapeDtypeStruct((quarter, model), BF16),
            jax.ShapeDtypeStruct((quarter, model), F32),
            jax.ShapeDtypeStruct((1, model), F32),
            jax.ShapeDtypeStruct((sides, 2, quarter, model), BF16),
            jax.ShapeDtypeStruct((2, model, units), BF16),
            jax.ShapeDtypeStruct((units, model), BF16),
        ],
        in_specs=[vmem] * 4 + [anywhere] * (3 + len(ups)),
        out_specs=[vmem] * 4 + [anywhere] * 2,
        scratch_shapes=[
            pltpu.VMEM((model, units), BF16),
            pltpu.VMEM((model, units), BF16),
            pltpu.VMEM((units, model), BF16),
            pltpu.VMEM((rows_n, model), BF16),
            pltpu.VMEM((rows_n, model), BF16),
            pltpu.VMEM((rows_n, units), BF16),
            pltpu.VMEM((rows_n, units), BF16),
            pltpu.VMEM((rows_n, units), BF16),
            pltpu.VMEM((4, quarter, model), BF16),
            pltpu.VMEM((quarter, model), BF16),
            pltpu.VMEM((quarter, model), BF16),
            pltpu.VMEM((quarter, model), F32),
            pltpu.VMEM((line_rows, model), BF16),
            pltpu.VMEM((line_rows, model), BF16),
            pltpu.VMEM((2 * line_rows, model), BF16),
            pltpu.VMEM((line_rows, model), BF16),
            pltpu.VMEM((4 * line_rows, model), BF16),
            pltpu.VMEM(half, BF16),
            pltpu.VMEM(half, BF16),
            dma((3 + len(ups),)),
            dma((5,)),
            dma((6,)),
            dma((6,)),
            dma((2, outer)),
            dma((outer,)),
            dma((outer,)),
            dma((outer,)),
            dma((2, outer)),
            dma((2, outer)),
            dma((2, outer)),
            dma((2, 2, outer)),
        ]
        + [dma((2, 2))] * 6
        + [dma((LATE_BLOCKS,))] * 2,
        compiler_params=pltpu.CompilerParams(
            collective_id=2, has_side_effects=True, vmem_limit_bytes=63 * 1024 * 1024
        ),
        cost_estimate=pl.CostEstimate(flops=3 * 10**10, bytes_accessed=4 * 10**7, transcendentals=0),
        name="middle",
    )(gated, out_proj, hidden, gain, w_gate, w_up, w_down, *ups)


FFN_CHUNKS = 2


def finish_kernel(
    outer, sides, sp_n, tp_n, streams, width_scale,
    *refs,
):
    MESH = pl.DeviceIdType.MESH
    parts = refs[:streams]
    (part_ref, hidden_ref, scale_ref, gain_ref, middle_ref, sums_ref) = refs[streams : streams + 6]
    last_in, layer_ref = refs[streams + 6 : streams + 8]
    outs = refs[streams + 8 : 2 * streams + 8]
    grad_out, sums_out, last_out, layer_out = refs[2 * streams + 8 : 2 * streams + 12]
    rest = refs[2 * streams + 12 :]
    got = rest[:streams]
    staged = rest[streams : 2 * streams]
    (near_got, far_got, keep_buf, far_stage, sums_got, sums_stage) = rest[2 * streams : 2 * streams + 6]
    rest = rest[2 * streams + 6 :]
    (last_keep, last_got, last_far, layer_send, layer_recv) = rest[:5]
    (f_load, f_near_send, f_near_recv, f_far_send, f_far_recv, f_store, f_out_send, f_out_recv) = rest[5:13]
    (reduce_send, reduce_recv, gather_send, gather_recv, pair_send, pair_recv) = rest[13:19]
    tp_send, tp_recv, sums_send, sums_recv = rest[19:]

    sp_i = lax.axis_index("sp")
    tp_i = lax.axis_index("tp")
    line = sp_i // 2
    half = sp_i % 2
    side = tp_i // 2
    core = tp_i % 2
    last = outer - 1

    def sp_at(z, y):
        return (tp_i, z * 2 + y)

    pair_dev = sp_at(line, 1 - half)
    core_dev = (side * 2 + (1 - core), sp_i)
    side_dev = ((1 - side) * 2 + core, sp_i)

    tp_bits = []
    bit = 1
    while bit < tp_n:
        tp_bits.append(bit)
        bit *= 2
    sp_bits = []
    bit = 1
    while bit < sp_n:
        sp_bits.append(bit)
        bit *= 2

    def flip(value, bit):
        return value + bit - 2 * bit * ((value // bit) % 2)

    sum_devs = [(flip(tp_i, b), sp_i) for b in tp_bits] + [(tp_i, flip(sp_i, b)) for b in sp_bits]

    barrier = pltpu.get_barrier_semaphore()
    greeted = [sp_at((line + 1) % outer, half), sp_at((line + outer - 1) % outer, half)] + sum_devs
    for device in greeted:
        pl.semaphore_signal(barrier, inc=1, device_id=device, device_id_type=MESH)
    pl.semaphore_wait(barrier, len(greeted))

    def remote(src, dst, send, recv, device):
        return pltpu.make_async_remote_copy(
            src_ref=src, dst_ref=dst, send_sem=send, recv_sem=recv,
            device_id=device, device_id_type=MESH,
        )

    places = (line, last - line)
    nexts = (sp_at(jnp.minimum(line + 1, last), half), sp_at(jnp.maximum(line - 1, 0), half))
    signs = (1, -1)

    def rows_of(stream, index):
        count = parts[stream].shape[0] // outer
        return pl.ds(pl.multiple_of(index * count, count), count)

    def reduce_copy(stream, way, step, src):
        return remote(
            src, got[stream].at[way, step - 1], reduce_send.at[stream, way, step - 1],
            reduce_recv.at[stream, way, step - 1], nexts[way],
        )

    def clamp(index):
        return jnp.clip(index, 0, last)

    def reduce_step(stream, step):
        for way in range(2):
            place, sign = places[way], signs[way]
            target = clamp(line + sign * (outer - step))
            own = parts[stream].at[rows_of(stream, target), :]

            @pl.when(place == 0)
            def _():
                reduce_copy(stream, way, step, own).start()

            if step > 1:

                @pl.when((place > 0) & (place <= step - 1))
                def _():
                    reduce_copy(stream, way, step - 1, own).wait_recv()
                    stage = staged[stream].at[way, step - 2]
                    stage[...] = (
                        got[stream][way, step - 2].astype(F32) + own[...].astype(F32)
                    ).astype(BF16)
                    reduce_copy(stream, way, step, stage).start()

    def gather_copy(stream, way, step, origin):
        block = outs[stream].at[half, rows_of(stream, origin), :]
        return remote(
            block, block, gather_send.at[stream, way, step - 1],
            gather_recv.at[stream, way, step - 1], nexts[way],
        )

    def pair_copy(stream, slot, origin):
        block = outs[stream].at[half, rows_of(stream, origin), :]
        return remote(block, block, pair_send.at[stream, slot], pair_recv.at[stream, slot], pair_dev)

    def reduce_final(stream):
        own = parts[stream].at[rows_of(stream, line), :]
        block = outs[stream].at[half, rows_of(stream, line), :]
        for way in range(2):

            @pl.when(places[way] > 0)
            def _():
                reduce_copy(stream, way, last, own).wait_recv()

        up = jnp.where(line > 0, got[stream][0, last - 1].astype(F32), 0.0)
        down = jnp.where(line < last, got[stream][1, last - 1].astype(F32), 0.0)
        block[...] = (own[...].astype(F32) + up + down).astype(BF16)
        for way in range(2):

            @pl.when(places[way] < last)
            def _():
                gather_copy(stream, way, 1, line).start()

        pair_copy(stream, 0, line).start()

    def gather_step(stream, step):
        for way in range(2):
            place, sign = places[way], signs[way]
            origin = clamp(line - sign * step)

            @pl.when(place >= step)
            def _():
                gather_copy(stream, way, step, origin).wait_recv()
                if step < last:

                    @pl.when(place < last)
                    def _():
                        gather_copy(stream, way, step + 1, origin).start()

                pair_copy(stream, 1 + way * last + step - 1, origin).start()

    def drain(stream):
        pair_copy(stream, 0, line).wait()
        for way in range(2):
            place, sign = places[way], signs[way]
            for step in range(1, outer):
                origin = clamp(line - sign * step)

                @pl.when(place <= step - 1)
                def _():
                    reduce_copy(stream, way, step, parts[stream].at[rows_of(stream, 0), :]).wait_send()

                @pl.when((place >= step - 1) & (place < last))
                def _():
                    gather_copy(stream, way, step, origin).wait_send()

                @pl.when(place >= step)
                def _():
                    pair_copy(stream, 1 + way * last + step - 1, origin).wait()

    def near_copy(index):
        return remote(
            part_ref.at[index, 1 - core], near_got.at[index], tp_send.at[index], tp_recv.at[index],
            core_dev,
        )

    def far_copy():
        return remote(far_stage, far_got, tp_send.at[sides], tp_recv.at[sides], side_dev)

    def spread_copy(slot, s, device):
        block = grad_out.at[s, core]
        return remote(block, block, tp_send.at[sides + slot], tp_recv.at[sides + slot], device)

    def input_step(step):
        if step == 0:
            for index in range(sides):
                near_copy(index).start()
        if step == 1:
            for index in range(sides):
                near_copy(index).wait_recv()
            keep_buf[...] = part_ref[side, core].astype(F32) + near_got[side].astype(F32)
            far_stage[...] = (
                part_ref[1 - side, core].astype(F32) + near_got[1 - side].astype(F32)
            ).astype(BF16)
            far_copy().start()
        if step == 2:
            far_copy().wait_recv()
            incoming = keep_buf[...] + far_got[...].astype(F32)
            values = hidden_ref[...].astype(F32)
            scales = scale_ref[...]
            weighted = incoming * gain_ref[...]
            inner_sum = jnp.sum(weighted * values, axis=-1, keepdims=True)
            grads = scales * weighted - values * (scales * scales * scales) * inner_sum * width_scale
            grad_out[side, core] = (middle_ref[...] + grads).astype(BF16)
            spread_copy(1, side, side_dev).start()
            spread_copy(2, side, core_dev).start()
        if step == 3:
            spread_copy(1, side, side_dev).wait_recv()
            spread_copy(3, 1 - side, core_dev).start()
        if step == 4:
            spread_copy(2, side, core_dev).wait_recv()
            spread_copy(3, 1 - side, core_dev).wait_recv()
            for index in range(sides):
                near_copy(index).wait_send()
            far_copy().wait_send()
            spread_copy(1, side, side_dev).wait_send()
            spread_copy(2, side, core_dev).wait_send()
            spread_copy(3, 1 - side, core_dev).wait_send()

    last_half = last_keep.shape[0]

    def ffn_at(j, ref, whole, owner):
        count = last_half // FFN_CHUNKS
        start = j * count
        if whole:
            start = pl.multiple_of(owner * last_half + start, count)
        return ref.at[pl.ds(start, count), :]

    def ffn_keep(j):
        return ffn_at(j, last_keep, False, 0)

    def ffn_got(j):
        return ffn_at(j, last_got, False, 0)

    def ffn_far(j):
        return ffn_at(j, last_far, False, 0)

    def ffn_load(j):
        return pltpu.make_async_copy(ffn_at(j, last_in, True, core), ffn_keep(j), f_load.at[j])

    def ffn_near_copy(j):
        return remote(
            ffn_at(j, last_in, True, 1 - core), ffn_got(j), f_near_send.at[j], f_near_recv.at[j], core_dev
        )

    def ffn_far_copy(j):
        return remote(ffn_keep(j), ffn_far(j), f_far_send.at[j], f_far_recv.at[j], side_dev)

    def ffn_store(j):
        return pltpu.make_async_copy(ffn_got(j), ffn_at(j, last_out, True, core), f_store.at[j])

    def ffn_out_copy(j):
        return remote(
            ffn_got(j), ffn_at(j, last_out, True, core), f_out_send.at[j], f_out_recv.at[j], core_dev
        )

    def ffn_sum(j):
        ffn_load(j).wait()
        ffn_near_copy(j).wait_recv()
        keep = ffn_keep(j)
        keep[...] = (keep[...].astype(F32) + ffn_got(j)[...].astype(F32)).astype(BF16)
        ffn_far_copy(j).start()

    def ffn_total(j):
        ffn_far_copy(j).wait_recv()
        total = ffn_keep(j)[...].astype(F32) + ffn_far(j)[...].astype(F32)
        ffn_got(j)[...] = total.astype(BF16)
        ffn_store(j).start()
        ffn_out_copy(j).start()

    def ffn_drain(j):
        ffn_near_copy(j).wait_send()
        ffn_far_copy(j).wait_send()
        ffn_store(j).wait()
        ffn_out_copy(j).wait()

    rounds = len(sum_devs)

    def sums_copy(step):
        src = sums_ref if step == 0 else sums_stage.at[step - 1]
        return remote(
            src, sums_got.at[step], sums_send.at[step], sums_recv.at[step], sum_devs[step]
        )

    def sums_step(step):
        if step > 0:
            sums_copy(step - 1).wait_recv()
            before = sums_ref[...] if step == 1 else sums_stage[step - 2]
            total = before + sums_got[step - 1]
            if step == rounds:
                sums_out[...] = total
            else:
                sums_stage[step - 1] = total
        if step < rounds:
            sums_copy(step).start()
        if step == rounds:
            for index in range(rounds):
                sums_copy(index).wait_send()

    def later(do, *args):
        return functools.partial(do, *args)

    def layer_copy(slot, s, device):
        block = layer_out.at[s, core]
        src = block if slot == 2 else layer_ref
        return remote(src, block, layer_send.at[slot], layer_recv.at[slot], device)

    def layer_own():
        return pltpu.make_async_copy(layer_ref, layer_out.at[side, core], layer_send.at[3])

    def layer_step(step):
        if step == 0:
            layer_copy(0, side, side_dev).start()
            layer_copy(1, side, core_dev).start()
            layer_own().start()
        if step == 1:
            layer_copy(0, 1 - side, side_dev).wait_recv()
            layer_copy(2, 1 - side, core_dev).start()
        if step == 2:
            layer_copy(1, side, core_dev).wait_recv()
            layer_own().wait()
            layer_copy(0, side, side_dev).wait_send()
            layer_copy(1, side, core_dev).wait_send()
            layer_copy(2, 1 - side, core_dev).wait()

    extra = [
        later(input_step, 0), later(input_step, 1), later(layer_step, 0), later(ffn_sum, 0),
        later(ffn_sum, 1), later(sums_step, 0), later(input_step, 2), later(sums_step, 1),
        later(layer_step, 1), later(sums_step, 2), later(input_step, 3), later(sums_step, 3),
        later(ffn_total, 0), later(sums_step, 4), later(layer_step, 2), later(input_step, 4),
        later(ffn_total, 1),
    ]
    extra += [later(sums_step, index) for index in range(5, rounds + 1)]
    for index in range(FFN_CHUNKS):
        ffn_near_copy(index).start()
        ffn_load(index).start()
    for turn in range(streams + 1):
        for step in range(1, outer + 1):
            if turn < streams:
                if step < outer:
                    reduce_step(turn, step)
                else:
                    reduce_final(turn)
            if turn > 0 and step < outer:
                gather_step(turn - 1, step)
            if extra:
                extra.pop(0)()
    for step in extra:
        step()
    for stream in range(streams):
        drain(stream)
    for index in range(FFN_CHUNKS):
        ffn_drain(index)


def finish(parts, part, hidden, scales, gain, middle, sums, ffn_last, layer, outer, sp_n, tp_n):
    streams = len(parts)
    sides = tp_n // 2
    quarter, model = hidden.shape
    last = outer - 1
    rounds = (tp_n - 1).bit_length() + (sp_n - 1).bit_length()
    vmem = pl.BlockSpec(memory_space=pltpu.VMEM)
    anywhere = pl.BlockSpec(memory_space=pl.ANY)
    chunk = [(2, last, p.shape[0] // outer, p.shape[1]) for p in parts]
    dma = pltpu.SemaphoreType.DMA
    return pl.pallas_call(
        functools.partial(finish_kernel, outer, sides, sp_n, tp_n, streams, 1.0 / model),
        out_shape=[jax.ShapeDtypeStruct((2,) + p.shape, BF16) for p in parts]
        + [
            jax.ShapeDtypeStruct((sides, 2, quarter, model), BF16),
            jax.ShapeDtypeStruct(sums.shape, F32),
        ]
        + [
            jax.ShapeDtypeStruct(ffn_last.shape, BF16),
            jax.ShapeDtypeStruct((sides, 2, quarter, model), BF16),
        ],
        in_specs=[vmem] * (streams + 6) + [anywhere, vmem],
        out_specs=[vmem] * (streams + 2) + [anywhere, vmem],
        scratch_shapes=[pltpu.VMEM(c, BF16) for c in chunk]
        + [pltpu.VMEM(c, BF16) for c in chunk]
        + [
            pltpu.VMEM((sides, quarter, model), BF16),
            pltpu.VMEM((quarter, model), BF16),
            pltpu.VMEM((quarter, model), F32),
            pltpu.VMEM((quarter, model), BF16),
            pltpu.VMEM((rounds,) + sums.shape, F32),
            pltpu.VMEM((rounds,) + sums.shape, F32),
        ]
        + [pltpu.VMEM((ffn_last.shape[0] // 2, ffn_last.shape[1]), BF16)] * 3
        + [dma((4,))] * 2
        + [dma((FFN_CHUNKS,))] * 8
        + [dma((streams, 2, last))] * 4
        + [dma((streams, 1 + 2 * last))] * 2
        + [dma((sides + 4,))] * 2
        + [dma((rounds,))] * 2,
        compiler_params=pltpu.CompilerParams(
            collective_id=1, has_side_effects=True, vmem_limit_bytes=60 * 1024 * 1024
        ),
        cost_estimate=pl.CostEstimate(flops=10**9, bytes_accessed=10**8, transcendentals=0),
        name="finish",
    )(*parts, part, hidden, scales, gain, middle, sums, ffn_last, layer)


def body(
    hidden,
    segment_ids,
    attn_norm,
    query_proj,
    key_proj,
    value_proj,
    gate_proj,
    output_proj,
    query_norm,
    key_norm,
    ffn_norm,
    ffn_gate,
    ffn_up,
    ffn_down,
    upstream,
):
    rows_dev, model = hidden.shape
    head_width = query_norm.shape[0]
    heads = query_proj.shape[1] // head_width
    groups = key_proj.shape[1] // head_width
    per_group = heads // groups
    group_width = groups * head_width
    sp_n = lax.axis_size("sp")
    tp_n = lax.axis_size("tp")
    outer = sp_n // 2
    sides = tp_n // 2
    quarter = rows_dev // tp_n
    tp_i = lax.axis_index("tp")
    sp_i = lax.axis_index("sp")
    ring_i = sp_i // 2
    pair_i = sp_i % 2
    side_i = tp_i // 2
    core_i = tp_i % 2
    own_first = sp_i * rows_dev
    quarter_first = tp_i * quarter
    scale = 1.0 / math.sqrt(head_width)

    ring_pairs = [(z * 2 + y, ((z + 1) % outer) * 2 + y) for z in range(outer) for y in range(2)]
    pair_pairs = [(i, i ^ 1) for i in range(sp_n)]
    side_pairs = [(i, i ^ 2) for i in range(tp_n)]
    core_pairs = [(i, i ^ 1) for i in range(tp_n)]

    def ring(value):
        return lax.ppermute(value, "sp", ring_pairs)

    def far(value, step):
        pairs = [(z * 2 + y, ((z + step) % outer) * 2 + y) for z in range(outer) for y in range(2)]
        return lax.ppermute(value, "sp", pairs)

    def pair(value):
        return lax.ppermute(value, "sp", pair_pairs)

    def side(value):
        return lax.ppermute(value, "tp", side_pairs)

    def core(value):
        return lax.ppermute(value, "tp", core_pairs)

    def gather_sp(block, paired):
        blocks = []
        first = block
        for k in range(outer):
            blocks.append((block, pair(block)) if k < paired else (block,))
            if k < outer - 1:
                block = ring(block) if paired == outer else far(first, k + 1)
        return blocks

    def scatter_sp(parts):
        def paired(k):
            return parts[k][0] + pair(parts[k][1].astype(BF16)).astype(F32)

        total = paired(1 % outer)
        for k in range(2, outer + 1):
            total = ring(total.astype(BF16)).astype(F32) + paired(k % outer)
        return total

    first_id = segment_ids[0]
    second_start = jnp.sum((segment_ids == first_id).astype(jnp.int32))
    own_index = own_first + jnp.arange(rows_dev, dtype=jnp.int32)
    own_starts = jnp.where(own_index < second_start, 0, second_start)
    steps_half = jnp.arange(head_width // 2, dtype=F32)
    frequencies = jnp.exp(steps_half * (-2.0 * math.log(THETA) / head_width))
    angles = (own_index - own_starts).astype(F32)[:, None] * frequencies[None, :]
    cosine = jnp.cos(angles)[:, None, :]
    sine = jnp.sin(angles)[:, None, :]

    hidden_full = hidden.astype(F32)
    normed_full, attn_scales = norm_rows(hidden_full, attn_norm)
    normed = normed_full.astype(BF16)
    key_raw = matmul(normed, key_proj).reshape(rows_dev, groups, head_width)
    value_rows = matmul(normed, value_proj).astype(BF16)
    key_normed, key_scales = norm_rows(key_raw, key_norm)
    key_rot = rotary(key_normed, cosine, sine).astype(BF16).reshape(rows_dev, group_width)
    kv_own = jnp.stack([key_rot, value_rows])

    low, high = (outer // 4, 3 * outer // 4) if outer % 4 == 0 else (0, outer)
    reach = high - 1 if low else outer - 1

    def up_pairs(step):
        return [
            (z * 2 + y, (z + 1) * 2 + y)
            for z in range(outer - 1)
            for y in range(2)
            if z + 1 - step >= 0 and (z + 1 - step >= low or z + 1 < high)
        ]

    def far_pairs(step):
        return [
            (z * 2 + y, (z + step) * 2 + y)
            for z in range(outer - step)
            for y in range(2)
            if z >= low or z + step < high
        ]

    kv_blocks = []
    travelling = kv_own
    for k in range(reach + 1):
        if k > 0 and reach <= 2:
            travelling = lax.ppermute(kv_own, "sp", far_pairs(k))
        elif k > 0:
            travelling = lax.ppermute(travelling, "sp", up_pairs(k))
        kv_blocks.append((travelling, pair(travelling)))

    query_raw = matmul(normed, query_proj).reshape(rows_dev, heads, head_width)
    gate_raw = matmul(normed, gate_proj)
    query_normed, query_scales = norm_rows(query_raw, query_norm)
    queries = rotary(query_normed, cosine, sine).astype(BF16).reshape(rows_dev, heads * head_width)

    def swap_half(value):
        piece = model // 4
        mine = pair(lax.dynamic_slice_in_dim(value, ((1 - pair_i) * 2 + core_i) * piece, piece, 1))
        near = core(mine)
        return jnp.where(
            core_i == 1, jnp.concatenate([near, mine], 1), jnp.concatenate([mine, near], 1)
        )

    normed_own = lax.dynamic_slice_in_dim(normed, pair_i * (model // 2), model // 2, 1)
    both_normed = jnp.concatenate([normed_own, swap_half(normed)])

    grad_quarter = lax.dynamic_slice_in_dim(upstream, quarter_first, quarter)
    fused = 2 < outer and outer * quarter <= 512 and tp_n == 4
    up_blocks = gather_sp(grad_quarter, outer - LATE_BLOCKS if fused else outer)

    row_start_low = own_starts[0]
    row_start_high = own_starts[-1]

    def block_info(k):
        shards = [(ring_i - k) * 2 + pair_i, (ring_i - k) * 2 + (1 - pair_i)]
        entries = [own_first] + [shard * rows_dev for shard in shards]
        live = []
        full = []
        for shard in shards:
            token = shard * rows_dev
            live.append((shard >= 0) & (shard <= sp_i) & (token + rows_dev - 1 >= row_start_low))
            full.append((token >= row_start_high) & (shard < sp_i))
        return jnp.stack(entries + [v.astype(jnp.int32) for v in live + full]).astype(jnp.int32)

    infos = [block_info(k) for k in range(reach + 1)]
    starts_column = own_starts[:, None]
    starts_row = own_starts[None, :]
    carried = None
    for k in range(reach + 1):
        if fused and k == reach:
            carried, up_blocks = lax.optimization_barrier((carried, up_blocks))
        carried = attn_forward(
            infos[k], starts_column, queries, kv_blocks[k][0], kv_blocks[k][1], carried, scale
        )
    mix_acc, mix_sum = carried
    mixed = mix_acc / mix_sum
    lse = jnp.log2(mix_sum.reshape(rows_dev, heads, head_width)[:, :, 0])
    lse_rows = lse.T.reshape(groups, per_group, rows_dev)
    gate_sig = jax.nn.sigmoid(gate_raw)
    gated = (mixed * gate_sig).astype(BF16)
    gated_other = pair(gated)

    def scatter_tp(part):
        part = part.reshape(sides, 2, quarter, model)
        keep = lax.dynamic_index_in_dim(part, core_i, 1, keepdims=False)
        send = lax.dynamic_index_in_dim(part, 1 - core_i, 1, keepdims=False)
        keep = keep + core(send.astype(BF16)).astype(F32)
        mine = lax.dynamic_index_in_dim(keep, side_i, 0, keepdims=False)
        other = lax.dynamic_index_in_dim(keep, 1 - side_i, 0, keepdims=False)
        return mine + side(other.astype(BF16)).astype(F32)

    def gather_tp(block):
        far = side(block)
        swap_side = side_i == 1
        two = jnp.where(swap_side, jnp.stack([far, block]), jnp.stack([block, far]))
        near = core(two)
        swap_core = core_i == 1
        full = jnp.where(
            swap_core, jnp.stack([near, two], axis=1), jnp.stack([two, near], axis=1)
        )
        return full.reshape((rows_dev,) + block.shape[1:])

    if fused:
        layer_quarter, grad_middle_quarter, ffn_gain_sum, branch, *ffn_parts = middle_layer(
            gated,
            output_proj,
            lax.dynamic_slice_in_dim(hidden, quarter_first, quarter),
            ffn_norm[None, :],
            ffn_gate,
            ffn_up,
            ffn_down,
            [block for both in up_blocks for block in both],
            outer,
            sides,
        )
        grad_branch = branch.reshape(rows_dev, model)
        ffn_gain_sum = ffn_gain_sum[0]
    else:
        attn_quarter = scatter_tp(matmul(gated, output_proj))
        hidden_quarter = lax.dynamic_slice_in_dim(hidden, quarter_first, quarter).astype(F32)
        middle = hidden_quarter + attn_quarter
        normed_two_full, ffn_scales = norm_rows(middle, ffn_norm)
        normed_two = normed_two_full.astype(BF16)

        two_blocks = gather_sp(normed_two, outer)
        rows_list, up_list, inner_list, gate_list, grad_up_list = [None] * outer, [None] * outer, [None] * outer, [None] * outer, [None] * outer
        grad_parts = [None] * outer
        for k in list(range(1, outer)) + [0]:
            rows_k = jnp.concatenate(two_blocks[k])
            up_k = jnp.concatenate(up_blocks[k])
            gate_vals = matmul(rows_k, ffn_gate)
            up_vals = matmul(rows_k, ffn_up)
            sig = jax.nn.sigmoid(gate_vals)
            grad_inner = times_transpose(up_k, ffn_down)
            grad_gate = (grad_inner * up_vals * (sig * (1.0 + gate_vals * (1.0 - sig)))).astype(BF16)
            grad_up = (grad_inner * (gate_vals * sig)).astype(BF16)
            inner = (gate_vals * sig * up_vals).astype(BF16)
            grad_parts[k] = (
                times_transpose(grad_gate, ffn_gate) + times_transpose(grad_up, ffn_up)
            ).reshape(2, quarter, model)
            rows_list[k], up_list[k], inner_list[k] = rows_k, up_k, inner
            gate_list[k], grad_up_list[k] = grad_gate, grad_up
        grad_two = scatter_sp(grad_parts)

        norm_grad_two, ffn_gain_terms = norm_back(middle, ffn_scales, ffn_norm, grad_two)
        grad_middle_quarter = grad_quarter.astype(F32) + norm_grad_two
        grad_branch = gather_tp(grad_middle_quarter.astype(BF16))
        ffn_gain_sum = jnp.sum(ffn_gain_terms, axis=0)
        mlp_parts = [
            matmul(inner_list[k], ffn_down).reshape(2, quarter, model) for k in range(outer)
        ]
        layer_quarter = (middle + scatter_sp(mlp_parts)).astype(BF16)

    def sum_tp(part):
        total = part.astype(BF16).astype(F32)
        total = total + core(total.astype(BF16)).astype(F32)
        low = total.astype(BF16)
        return (low.astype(F32) + side(low).astype(F32)).astype(BF16)

    if not fused:
        rows_all = jnp.concatenate(rows_list)
        up_all = jnp.concatenate(up_list)
        inner_all = jnp.concatenate(inner_list)
        gate_all = jnp.concatenate(gate_list)
        grad_up_all = jnp.concatenate(grad_up_list)
        ffn_parts = [
            jnp.stack([outer_sum(rows_all, gate_all), outer_sum(rows_all, grad_up_all)]),
            outer_sum(inner_all, up_all),
        ]
        ffn_parts = [sum_tp(ffn_parts[0]), ffn_parts[1].astype(BF16)]
    ffn_both, ffn_last = ffn_parts

    branch_other = swap_half(grad_branch)
    branch_own = lax.dynamic_slice_in_dim(grad_branch, pair_i * (model // 2), model // 2, 1)
    output_half = outer_sum(
        jnp.concatenate([gated, gated_other]), jnp.concatenate([branch_own, branch_other])
    )
    grad_gated = times_transpose(grad_branch, output_proj)
    grad_mixed = (grad_gated * gate_sig).astype(BF16)
    grad_gate_raw = (grad_gated * mixed * (gate_sig * (1.0 - gate_sig))).astype(BF16)
    gate_half = outer_sum(both_normed, jnp.concatenate([grad_gate_raw, pair(grad_gate_raw)]))
    deltas = jnp.sum(
        (grad_mixed.astype(F32) * mixed).reshape(rows_dev, heads, head_width), axis=-1
    )
    delta_rows = deltas.T.reshape(groups, per_group, rows_dev)

    def down_pairs(step):
        return [(b, a) for a, b in up_pairs(step)]

    query_acc = None
    travelling = None
    for k in list(range(reach, -1, -1)):
        query_acc, grad_a, grad_b = attn_backward(
            infos[k], starts_row, lse_rows, delta_rows, queries, grad_mixed,
            kv_blocks[k][0], kv_blocks[k][1], query_acc, k == 0, scale,
        )
        total = grad_a.astype(F32) + pair(grad_b).astype(F32)
        if travelling is not None:
            total = total + travelling.astype(F32)
        if k > 0:
            travelling = lax.ppermute(total.astype(BF16), "sp", down_pairs(k))
    grad_key_rot = total[0].reshape(rows_dev, groups, head_width)
    grad_value_low = total[1].astype(BF16)
    grad_query_rot = (query_acc * scale).reshape(rows_dev, heads, head_width)
    grad_query_raw, query_gain_terms = norm_back(
        query_raw, query_scales, query_norm, rotary_back(grad_query_rot, cosine, sine)
    )
    grad_key_raw, key_gain_terms = norm_back(
        key_raw, key_scales, key_norm, rotary_back(grad_key_rot, cosine, sine)
    )
    grad_query_low = grad_query_raw.reshape(rows_dev, heads * head_width).astype(BF16)
    grad_key_low = grad_key_raw.reshape(rows_dev, group_width).astype(BF16)
    grad_kv_low = jnp.concatenate([grad_key_low, grad_value_low], axis=1)

    both_queries = jnp.concatenate([grad_query_low, pair(grad_query_low)])
    both_kv = jnp.concatenate([grad_kv_low, pair(grad_kv_low)])
    parts = [
        output_half.astype(BF16),
        gate_half.astype(BF16),
        outer_sum(both_normed, both_queries).astype(BF16),
        outer_sum(both_normed, both_kv).astype(BF16),
    ]

    grad_normed_part = (
        times_transpose(grad_query_low, query_proj)
        + times_transpose(grad_key_low, key_proj)
        + times_transpose(grad_value_low, value_proj)
        + times_transpose(grad_gate_raw, gate_proj)
    )
    gains = jnp.concatenate(
        [
            jnp.sum(grad_normed_part * hidden_full * attn_scales, axis=0),
            ffn_gain_sum,
            jnp.sum(query_gain_terms, axis=(0, 1)),
            jnp.sum(key_gain_terms, axis=(0, 1)),
        ]
    )
    gains_at = 2 * model + 2 * head_width
    gains = jnp.pad(gains, (0, -gains_at % 1024)).reshape(-1, 128)
    scales_quarter = lax.dynamic_slice_in_dim(attn_scales, quarter_first, quarter)
    finished = finish(
        parts,
        grad_normed_part.astype(BF16).reshape(sides, 2, quarter, model),
        lax.dynamic_slice_in_dim(hidden, quarter_first, quarter),
        scales_quarter,
        attn_norm[None, :],
        grad_middle_quarter,
        gains,
        ffn_last,
        layer_quarter,
        outer,
        sp_n,
        tp_n,
    )
    output_all, gate_all_w, query_all, kv_all, input_all, gains, ffn_last, layer_all = finished
    output_grad = jnp.concatenate([output_all[0], output_all[1]], axis=1).astype(F32)
    gate_grad = gate_all_w.reshape(model, heads * head_width).astype(F32)
    query_grad = query_all.reshape(model, heads * head_width).astype(F32)
    kv_all = kv_all.reshape(model, 2 * group_width)
    key_grad = kv_all[:, :group_width].astype(F32)
    value_grad = kv_all[:, group_width:].astype(F32)
    hidden_grad = input_all.reshape(rows_dev, model).astype(F32)
    gains = gains.reshape(-1)
    return (
        layer_all.reshape(rows_dev, model),
        hidden_grad,
        gains[:model],
        query_grad,
        key_grad,
        value_grad,
        gate_grad,
        output_grad,
        gains[2 * model : 2 * model + head_width],
        gains[2 * model + head_width : gains_at],
        gains[model : 2 * model],
        ffn_both[0].astype(F32),
        ffn_both[1].astype(F32),
        ffn_last.astype(F32),
    )


def solution(mesh):
    placed = (
        P("sp", None),
        P(),
        P(),
        P(None, "tp"),
        P(None, "tp"),
        P(None, "tp"),
        P(None, "tp"),
        P("tp", None),
        P(),
        P(),
        P(),
        P(None, "sp"),
        P(None, "sp"),
        P("sp", None),
        P("sp", None),
    )
    return jax.shard_map(
        body,
        mesh=mesh,
        in_specs=placed,
        out_specs=(
            P("sp", None),
            P("sp", None),
            P(),
            P(None, "tp"),
            P(None, "tp"),
            P(None, "tp"),
            P(None, "tp"),
            P("tp", None),
            P(),
            P(),
            P(),
            P(None, "sp"),
            P(None, "sp"),
            P("sp", None),
        ),
        check_vma=False,
    )
```

```python
import functools
import math

import jax
import jax.numpy as jnp
from jax import lax
from jax.experimental import pallas as pl
from jax.experimental.pallas import tpu as pltpu
from jax.sharding import PartitionSpec as P

EPSILON = 1e-06
THETA = 1000000.0
LOG2E = 1.4426950408889634
F32 = jnp.float32
BF16 = jnp.bfloat16


def norm_scales(values):
    return lax.rsqrt(jnp.mean(values * values, axis=-1, keepdims=True) + EPSILON)


def norm_rows(values, gain):
    scales = norm_scales(values)
    return (values * scales * gain, scales)


def norm_back(values, scales, gain, incoming):
    weighted = incoming * gain
    inner_sum = jnp.sum(weighted * values, axis=-1, keepdims=True)
    grad_values = (
        scales * weighted - values * (scales * scales * scales) * inner_sum / values.shape[-1]
    )
    return (grad_values, incoming * values * scales)


def rotary(values, cosine, sine):
    half_width = values.shape[-1] // 2
    front_half = values[..., :half_width]
    back_half = values[..., half_width:]
    return jnp.concatenate(
        [front_half * cosine - back_half * sine, back_half * cosine + front_half * sine], axis=-1
    )


def rotary_back(grads, cosine, sine):
    half_width = grads.shape[-1] // 2
    front_half = grads[..., :half_width]
    back_half = grads[..., half_width:]
    return jnp.concatenate(
        [front_half * cosine + back_half * sine, back_half * cosine - front_half * sine], axis=-1
    )


def matmul(left, right):
    return jnp.dot(left, right, preferred_element_type=F32)


def outer_sum(left, right):
    return lax.dot_general(left, right, (((0,), (0,)), ((), ())), preferred_element_type=F32)


def times_transpose(left, right):
    return lax.dot_general(left, right, (((1,), (1,)), ((), ())), preferred_element_type=F32)


def attn_forward_kernel(first, diagonal, scale, info, starts, queries, kv_a, kv_b, *rest):
    if first:
        acc_out, sum_out = rest
    else:
        acc_in, sum_in, acc_out, sum_out = rest
    rows = queries.shape[0]
    keys_n = kv_a.shape[1]
    per_group = queries.shape[1] // kv_a.shape[2]
    width = kv_a.shape[2]
    if first:
        acc_out[...] = jnp.zeros_like(acc_out)
        sum_out[...] = jnp.zeros_like(sum_out)
    else:
        acc_out[...] = acc_in[...]
        sum_out[...] = sum_in[...]
    own_first = info[0]
    for slot, block in enumerate((kv_a, kv_b)):
        key_first = info[1 + slot]
        live = info[3 + slot] > 0

        def work(masked, causal):
            ones = jnp.ones((keys_n, width), BF16)
            values = jnp.concatenate([block[1], ones], axis=1)
            keys = block[0]
            if masked:
                key_index = key_first + lax.broadcasted_iota(jnp.int32, (rows, keys_n), 1)
                allowed = key_index >= starts[...]
                if causal:
                    row_index = own_first + lax.broadcasted_iota(jnp.int32, (rows, keys_n), 0)
                    allowed = allowed & (key_index <= row_index)
            for head in range(per_group):
                cols = slice(head * width, (head + 1) * width)
                scores = times_transpose(queries[:, cols], keys)
                weights = jnp.exp2(scores * (scale * LOG2E))
                if masked:
                    weights = jnp.where(allowed, weights, 0.0)
                both = matmul(weights.astype(BF16), values)
                acc_out[:, cols] += both[:, :width]
                sum_out[:, cols] += both[:, width:]

        if diagonal and slot == 0:
            work(True, True)
        else:
            full = info[5 + slot] > 0
            pl.when(live & full)(functools.partial(work, False, False))
            pl.when(live & jnp.logical_not(full))(functools.partial(work, True, False))


def attn_forward(info, starts, queries, kv_a, kv_b, carried, scale):
    rows, all_width = queries.shape
    width = 128
    groups = kv_a.shape[2] // width
    group_width = all_width // groups
    keys_n = kv_a.shape[1]
    first = carried is None
    spec_q = pl.BlockSpec((rows, group_width), lambda g, info: (0, g))
    spec_kv = pl.BlockSpec((2, keys_n, width), lambda g, info: (0, 0, g))
    specs = [pl.BlockSpec((rows, 1), lambda g, info: (0, 0)), spec_q, spec_kv, spec_kv]
    operands = [starts, queries, kv_a, kv_b]
    if not first:
        specs += [spec_q, spec_q]
        operands += list(carried)
    return pl.pallas_call(
        functools.partial(attn_forward_kernel, first, first, scale),
        grid_spec=pltpu.PrefetchScalarGridSpec(
            num_scalar_prefetch=1,
            grid=(groups,),
            in_specs=specs,
            out_specs=[spec_q, spec_q],
        ),
        out_shape=[jax.ShapeDtypeStruct((rows, all_width), F32)] * 2,
        compiler_params=pltpu.CompilerParams(dimension_semantics=("arbitrary",)),
        cost_estimate=pl.CostEstimate(
            flops=16 * rows * keys_n * all_width,
            transcendentals=2 * rows * keys_n * all_width // width,
            bytes_accessed=8 * rows * all_width,
        ),
        name="attn_forward",
    )(info, *operands)


def attn_backward_kernel(first, diagonal, scale, info, starts, lse, deltas, queries, grads, kv_a, kv_b, *rest):
    if first:
        grad_q, grad_a, grad_b = rest
    else:
        grad_in, grad_q, grad_a, grad_b = rest
    rows = queries.shape[0]
    keys_n = kv_a.shape[1]
    width = kv_a.shape[2]
    per_group = queries.shape[1] // width
    if first:
        grad_q[...] = jnp.zeros_like(grad_q)
    else:
        grad_q[...] = grad_in[...]
    own_first = info[0]
    for slot, (block, out) in enumerate(((kv_a, grad_a), (kv_b, grad_b))):
        key_first = info[1 + slot]
        live = info[3 + slot] > 0

        def work(masked, causal):
            keys = block[0]
            values = block[1]
            keys_t = keys.T
            if masked:
                key_index = key_first + lax.broadcasted_iota(jnp.int32, (keys_n, rows), 0)
                allowed = key_index >= starts[...]
                if causal:
                    row_index = own_first + lax.broadcasted_iota(jnp.int32, (keys_n, rows), 1)
                    allowed = allowed & (key_index <= row_index)
            total_k = jnp.zeros((keys_n, width), F32)
            total_v = jnp.zeros((keys_n, width), F32)
            for head in range(per_group):
                cols = slice(head * width, (head + 1) * width)
                q_head = queries[:, cols]
                g_head = grads[:, cols]
                scores = times_transpose(keys, q_head)
                probs = jnp.exp2(scores * (scale * LOG2E) - lse[0, head : head + 1, :])
                if masked:
                    probs = jnp.where(allowed, probs, 0.0)
                grad_probs = times_transpose(values, g_head)
                grad_scores = (probs * (grad_probs - deltas[0, head : head + 1, :])).astype(BF16)
                total_v += matmul(probs.astype(BF16), g_head)
                total_k += matmul(grad_scores, q_head)
                grad_q[:, cols] += matmul(keys_t, grad_scores).T
            out[0] = (total_k * scale).astype(BF16)
            out[1] = total_v.astype(BF16)

        if diagonal and slot == 0:
            work(True, True)
        else:
            full = info[5 + slot] > 0
            pl.when(live & full)(functools.partial(work, False, False))
            pl.when(live & jnp.logical_not(full))(functools.partial(work, True, False))

            @pl.when(jnp.logical_not(live))
            def _():
                out[...] = jnp.zeros_like(out)


def attn_backward(info, starts_row, lse, deltas, queries, grads, kv_a, kv_b, carried, diagonal, scale):
    rows, all_width = queries.shape
    width = 128
    groups = kv_a.shape[2] // width
    group_width = all_width // groups
    per_group = group_width // width
    keys_n = kv_a.shape[1]
    first = carried is None
    spec_q = pl.BlockSpec((rows, group_width), lambda g, info: (0, g))
    spec_kv = pl.BlockSpec((2, keys_n, width), lambda g, info: (0, 0, g))
    spec_row = pl.BlockSpec((1, per_group, rows), lambda g, info: (g, 0, 0))
    specs = [
        pl.BlockSpec((1, rows), lambda g, info: (0, 0)),
        spec_row,
        spec_row,
        spec_q,
        spec_q,
        spec_kv,
        spec_kv,
    ]
    operands = [starts_row, lse, deltas, queries, grads, kv_a, kv_b]
    if not first:
        specs.append(spec_q)
        operands.append(carried)
    return pl.pallas_call(
        functools.partial(attn_backward_kernel, first, diagonal, scale),
        grid_spec=pltpu.PrefetchScalarGridSpec(
            num_scalar_prefetch=1,
            grid=(groups,),
            in_specs=specs,
            out_specs=[spec_q, spec_kv, spec_kv],
        ),
        out_shape=[
            jax.ShapeDtypeStruct((rows, all_width), F32),
            jax.ShapeDtypeStruct(kv_a.shape, BF16),
            jax.ShapeDtypeStruct(kv_a.shape, BF16),
        ],
        compiler_params=pltpu.CompilerParams(dimension_semantics=("arbitrary",)),
        cost_estimate=pl.CostEstimate(
            flops=20 * rows * keys_n * all_width,
            transcendentals=2 * rows * keys_n * all_width // width,
            bytes_accessed=8 * rows * all_width,
        ),
        name="attn_backward",
    )(info, *operands)


LATE_BLOCKS = 2


def middle_kernel(outer, *refs):
    MESH = pl.DeviceIdType.MESH
    blocks = 2 * outer - LATE_BLOCKS
    (gated, out_proj, hidden_ref, gain_ref, gate_in, up_in, down_in) = refs[:7]
    ups_in = refs[7 : 7 + blocks]
    (layer_out, grad_out, gain_out, branch, dw_both, dw_down) = refs[7 + blocks : 13 + blocks]
    (
        w_gate, w_up, w_down, ups, rows, inner, grad_gate, grad_up,
        near_buf, far_stage, far_got, middle_buf,
        keep, y_stage, y_got, z_stage, z_got, part_got, part_far,
        load_sem, store_sem, tp_send, tp_recv, zs, zr, ys, yr, rys, ryr, rzs, rzr,
        p_near_send, p_near_recv, p_far_send, p_far_recv, p_out_send, p_out_recv, us, ur,
    ) = refs[13 + blocks :]
    stage_gate, stage_up, stage_down = w_gate, w_up, rows
    far_keep, own_keep = grad_out, middle_buf
    units = w_down.shape[0]
    quarter, model = hidden_ref.shape
    group = 2 * quarter
    chunk = model // outer
    last = outer - 1

    sp_i = lax.axis_index("sp")
    tp_i = lax.axis_index("tp")
    line = sp_i // 2
    half = sp_i % 2
    side = tp_i // 2
    core = tp_i % 2

    def sp_at(z, y):
        return (tp_i, z * 2 + y)

    pair_dev = sp_at(line, 1 - half)
    core_dev = (side * 2 + (1 - core), sp_i)
    side_dev = ((1 - side) * 2 + core, sp_i)
    nexts = (sp_at(jnp.minimum(line + 1, last), half), sp_at(jnp.maximum(line - 1, 0), half))

    late = list(range(outer - LATE_BLOCKS, outer))
    ups_at = [at for at in range(2 * outer) if at % 2 == 0 or at // 2 not in late]
    loads = [
        pltpu.make_async_copy(src, dst, load_sem.at[index])
        for index, (src, dst) in enumerate(
            [(down_in, w_down)]
            + [(src, ups.at[pl.ds(at * quarter, quarter), :]) for at, src in zip(ups_at, ups_in)]
            + [(gate_in, w_gate), (up_in, w_up)]
        )
    ]
    for load in loads:
        load.start()

    barrier = pltpu.get_barrier_semaphore()
    greeted = [
        sp_at((line + 1) % outer, half), sp_at((line + outer - 1) % outer, half),
        pair_dev, core_dev, side_dev,
    ]
    for device in greeted:
        pl.semaphore_signal(barrier, inc=1, device_id=device, device_id_type=MESH)
    pl.semaphore_wait(barrier, len(greeted))

    def remote(src, dst, send, recv, device):
        return pltpu.make_async_remote_copy(
            src_ref=src, dst_ref=dst, send_sem=send, recv_sem=recv,
            device_id=device, device_id_type=MESH,
        )

    def aligned(index, count):
        return pl.ds(pl.multiple_of(index * count, count), count)

    def late_copy(index):
        at = late[index] * 2
        return remote(
            ups.at[pl.ds(at * quarter, quarter), :], ups.at[pl.ds((at + 1) * quarter, quarter), :],
            us.at[index], ur.at[index], pair_dev,
        )

    def near_copy(j):
        return remote(near_buf.at[j], near_buf.at[2 + j], tp_send.at[j], tp_recv.at[j], core_dev)

    def far_copy():
        return remote(far_stage, far_got, tp_send.at[2], tp_recv.at[2], side_dev)

    def projected(s, c):
        return matmul(gated[aligned(s * 2 + c, quarter), :], out_proj[...])

    near_buf[0] = projected(1 - side, 1 - core).astype(BF16)
    near_copy(0).start()
    near_buf[1] = projected(side, 1 - core).astype(BF16)
    near_copy(1).start()
    for index in range(LATE_BLOCKS):
        loads[1 + ups_at.index(late[index] * 2)].wait()
        late_copy(index).start()
    far_keep[...] = projected(1 - side, core)
    near_copy(0).wait_recv()
    far_stage[...] = (far_keep[...] + near_buf[2].astype(F32)).astype(BF16)
    far_copy().start()
    own_keep[...] = projected(side, core)

    near_copy(1).wait_recv()
    far_copy().wait_recv()
    middle = hidden_ref[...].astype(F32) + (
        own_keep[...] + near_buf[3].astype(F32) + far_got[...].astype(F32)
    )
    middle_buf[...] = middle
    rows[0:quarter, :] = (middle * norm_scales(middle) * gain_ref[...]).astype(BF16)

    def entry(k, j):
        return pl.ds(pl.multiple_of((k * 2 + j) * quarter, quarter), quarter)

    def wrap(k):
        return (k + outer) % outer

    def z_copy(way, k):
        to = wrap(k + 1 - 2 * way)
        return remote(
            rows.at[entry(k, 0), :], rows.at[entry(to, 0), :], zs.at[way, k], zr.at[to], nexts[way]
        )

    def z_arrived(k):
        return remote(
            rows.at[entry(k, 0), :], rows.at[entry(k, 0), :], zs.at[0, k], zr.at[k], nexts[0]
        )

    def y_copy(k):
        return remote(
            rows.at[entry(k, 0), :], rows.at[entry(k, 1), :], ys.at[k], yr.at[k], pair_dev
        )

    short = jnp.minimum(line, last - line)

    def delta_of(i):
        near = jnp.where(i % 2 == 1, -((i + 1) // 2), (i + 1) // 2)
        far = jnp.where(line < last - line, i - short, short - i)
        return jnp.where(i <= 2 * short, near, far)

    def slot_of(delta):
        return jnp.where(delta <= 0, -delta, outer - delta)

    for way, exists in ((0, line < last), (1, line > 0)):
        pl.when(exists)(z_copy(way, 0).start)
    y_copy(0).start()

    def goes_on(delta):
        return ((delta < 0) & (line < last), (delta > 0) & (line > 0))

    def forward(i):
        delta = delta_of(i)
        k = slot_of(delta)
        z_arrived(k).wait_recv()
        for way, exists in enumerate(goes_on(delta)):
            pl.when(exists)(z_copy(way, k).start)
        y_copy(k).start()

    waited = [1 + ups_at.index(k * 2) for k in late]
    for index, load in enumerate(loads):
        if index not in waited:
            load.wait()
    for index in range(LATE_BLOCKS):
        late_copy(index).wait_recv()
    forward(1)

    def turn_forward(i, carry):
        @pl.when(i + 2 < outer)
        def _():
            forward(i + 2)

        k = slot_of(delta_of(i))
        y_copy(k).wait_recv()
        at = aligned(k, group)
        rows_k = rows[at, :]
        gate_vals = matmul(rows_k, w_gate[...])
        up_vals = matmul(rows_k, w_up[...])
        incoming = times_transpose(ups[at, :], w_down[...])
        sig = jax.nn.sigmoid(gate_vals)
        silu = gate_vals * sig
        grad_gate[at, :] = (incoming * up_vals * (sig * (1.0 + gate_vals * (1.0 - sig)))).astype(BF16)
        grad_up[at, :] = (incoming * silu).astype(BF16)
        inner[at, :] = (silu * up_vals).astype(BF16)
        return carry

    lax.fori_loop(0, outer, turn_forward, 0)

    near_copy(0).wait_send()
    near_copy(1).wait_send()

    def y_sum(which, k):
        at = aligned(k, quarter)
        src = y_stage.at[at, :] if which == 0 else near_buf.at[k]
        got = y_got.at[aligned(which * outer + k, quarter), :]
        return remote(src, got, rys.at[which, k], ryr.at[which, k], pair_dev)

    def half_rows(k, j):
        return pl.ds(pl.multiple_of((k * 2 + j) * quarter, quarter), quarter)

    def turn_parts(step, carry):
        k = slot_of(delta_of(last - step))
        part = times_transpose(grad_gate[half_rows(k, 1), :], w_gate[...]) + times_transpose(
            grad_up[half_rows(k, 1), :], w_up[...]
        )
        y_stage[aligned(k, quarter), :] = part.astype(BF16)
        y_sum(0, k).start()
        return carry

    def turn_outputs(step, carry):
        k = slot_of(delta_of(last - step))
        near_buf[k] = matmul(inner[half_rows(k, 1), :], w_down[...]).astype(BF16)
        y_sum(1, k).start()
        return carry

    def turn_keep(step, carry):
        k = slot_of(delta_of(last - step))
        part = times_transpose(grad_gate[half_rows(k, 0), :], w_gate[...]) + times_transpose(
            grad_up[half_rows(k, 0), :], w_up[...]
        )
        keep[aligned(k, quarter), :] = part.astype(BF16)
        return carry

    lax.fori_loop(0, outer, turn_parts, 0)
    lax.fori_loop(0, outer, turn_keep, 0)

    def z_got_rows(which, way, k):
        return aligned((which * 2 + way) * outer + k, quarter)

    def z_sum(which, way, k):
        to = wrap(k + 1 - 2 * way)
        return remote(
            z_stage.at[aligned(k, quarter), :], z_got.at[z_got_rows(which, way, to), :],
            rzs.at[which, k], rzr.at[which, way, to], nexts[way],
        )

    def z_got_at(which, way, k):
        return z_got[z_got_rows(which, way, k), :].astype(F32)

    def z_sum_arrived(which, way, k):
        return remote(
            z_stage.at[aligned(k, quarter), :], z_got.at[z_got_rows(which, way, k), :],
            rzs.at[which, k], rzr.at[which, way, k], nexts[way],
        )

    def own_share(which, k):
        if which == 0:
            share = keep[aligned(k, quarter), :].astype(F32)
        else:
            share = matmul(inner[half_rows(k, 0), :], w_down[...])
        return share + y_got[aligned(which * outer + k, quarter), :].astype(F32)

    def chain(which, step):
        delta = delta_of(last - step)
        k = slot_of(delta)
        at = aligned(k, quarter)
        y_sum(which, k).wait_recv()
        own = own_share(which, k)
        if which == 1:
            z_sum(0, 0, k).wait_send()
        for way, (here, before) in enumerate(((delta > 0, line > 0), (delta < 0, line < last))):

            @pl.when(here & before)
            def _():
                z_sum_arrived(which, way, k).wait_recv()
                z_stage[at, :] = (own + z_got_at(which, way, k)).astype(BF16)

            @pl.when(here & jnp.logical_not(before))
            def _():
                z_stage[at, :] = own.astype(BF16)

            pl.when(here)(z_sum(which, way, k).start)

    def chain_end(which):
        y_sum(which, 0).wait_recv()
        own = own_share(which, 0)
        for way, exists in ((0, line > 0), (1, line < last)):
            pl.when(exists)(z_sum_arrived(which, way, 0).wait_recv)
        below = jnp.where(line > 0, z_got_at(which, 0, 0), 0.0)
        above = jnp.where(line < last, z_got_at(which, 1, 0), 0.0)
        return own + below + above

    half_model = model // 2
    piece = half_model // 2

    def stage_rows(owner, r):
        return pl.ds(pl.multiple_of(owner * half_model + r * piece, piece), piece)

    stages = (stage_gate, stage_up)

    def piece_at(ref, a, r):
        return ref.at[a, pl.ds(r * piece, piece), :]

    def piece_near(a, r):
        return remote(
            stages[a].at[stage_rows(1 - core, r), :], piece_at(part_got, a, r),
            p_near_send.at[a, r], p_near_recv.at[a, r], core_dev,
        )

    def piece_far(a, r):
        return remote(
            stages[a].at[stage_rows(core, r), :], piece_at(part_far, a, r),
            p_far_send.at[a, r], p_far_recv.at[a, r], side_dev,
        )

    def piece_store(a, r):
        return pltpu.make_async_copy(
            piece_at(part_got, a, r), dw_both.at[a, stage_rows(core, r), :], store_sem.at[1 + 2 * a + r]
        )

    def piece_out(a, r):
        return remote(
            piece_at(part_got, a, r), dw_both.at[a, stage_rows(core, r), :],
            p_out_send.at[a, r], p_out_recv.at[a, r], core_dev,
        )

    def pieces(mine, r):
        at = stage_rows(core if mine else 1 - core, r)
        some = rows[:, at]
        for a, grads in enumerate((grad_gate, grad_up)):
            stages[a][at, :] = outer_sum(some, grads[...]).astype(BF16)
            if not mine:
                piece_near(a, r).start()

    def pieces_sum(r):
        at = stage_rows(core, r)
        for a in range(2):
            piece_near(a, r).wait_recv()
            stages[a][at, :] = (
                stages[a][at, :].astype(F32) + piece_at(part_got, a, r)[...].astype(F32)
            ).astype(BF16)
            piece_far(a, r).start()

    def pieces_total(r):
        for a in range(2):
            piece_far(a, r).wait_recv()
            total = stages[a][stage_rows(core, r), :].astype(F32) + piece_at(part_far, a, r)[
                ...
            ].astype(F32)
            piece_at(part_got, a, r)[...] = total.astype(BF16)
            piece_store(a, r).start()
            piece_out(a, r).start()

    pieces(False, 0)
    pieces(True, 0)
    pieces_sum(0)
    lax.fori_loop(0, outer, turn_outputs, 0)
    chain(0, 0)
    pieces(False, 1)
    pieces(True, 1)
    pieces_sum(1)
    for step in range(1, last):
        chain(0, step)
    grad_two = chain_end(0)

    values = middle_buf[...]
    back, gain_terms = norm_back(values, norm_scales(values), gain_ref[...], grad_two)
    grads = ups[0:quarter, :].astype(F32) + back
    branch[side, core] = grads.astype(BF16)

    def spread_copy(slot, s, device):
        block = branch.at[s, core]
        return remote(block, block, tp_send.at[3 + slot], tp_recv.at[3 + slot], device)

    spread_copy(0, side, side_dev).start()
    spread_copy(1, side, core_dev).start()
    grad_out[...] = grads
    gain_out[...] = jnp.sum(gain_terms, axis=0, keepdims=True)

    for way, exists in ((0, line < last), (1, line > 0)):
        pl.when(exists)(z_copy(way, 0).wait_send)

    def turn_sent(i, carry):
        delta = delta_of(i)
        k = slot_of(delta)
        y_copy(k).wait_send()
        for way, exists in enumerate(goes_on(delta)):
            pl.when(exists)(z_copy(way, k).wait_send)
        return carry

    lax.fori_loop(0, outer, turn_sent, 0)

    def turn_down(c, carry):
        at = aligned(c, chunk)
        stage_down[0:units, at] = outer_sum(inner[...], ups[:, at]).astype(BF16)
        return carry

    chain(1, 0)
    lax.fori_loop(0, outer, turn_down, 0)
    down_store = pltpu.make_async_copy(stage_down.at[pl.ds(0, units), :], dw_down, store_sem.at[0])
    down_store.start()
    for step in range(1, last):
        chain(1, step)
    spread_copy(0, side, side_dev).wait_recv()
    spread_copy(2, 1 - side, core_dev).start()
    pieces_total(0)
    layer_out[...] = (middle_buf[...] + chain_end(1)).astype(BF16)
    pieces_total(1)
    spread_copy(1, side, core_dev).wait_recv()

    down_store.wait()
    far_copy().wait_send()
    for index in range(LATE_BLOCKS):
        late_copy(index).wait_send()

    def turn_drain(i, carry):
        k = slot_of(delta_of(i))
        for which in range(2):
            y_sum(which, k).wait_send()
        pl.when(i > 0)(z_sum(1, 0, k).wait_send)
        return carry

    lax.fori_loop(0, outer, turn_drain, 0)
    for a in range(2):
        for r in range(2):
            piece_near(a, r).wait_send()
            piece_far(a, r).wait_send()
            piece_store(a, r).wait()
            piece_out(a, r).wait()
    spread_copy(0, side, side_dev).wait_send()
    spread_copy(1, side, core_dev).wait_send()
    spread_copy(2, 1 - side, core_dev).wait()


def middle_layer(gated, out_proj, hidden, gain, w_gate, w_up, w_down, ups, outer, sides):
    quarter, model = hidden.shape
    units = w_down.shape[0]
    rows_n = 2 * outer * quarter
    vmem = pl.BlockSpec(memory_space=pltpu.VMEM)
    anywhere = pl.BlockSpec(memory_space=pl.ANY)
    dma = pltpu.SemaphoreType.DMA
    line_rows = outer * quarter
    half = (2, model // 2, units)
    return pl.pallas_call(
        functools.partial(middle_kernel, outer),
        out_shape=[
            jax.ShapeDtypeStruct((quarter, model), BF16),
            jax.ShapeDtypeStruct((quarter, model), F32),
            jax.ShapeDtypeStruct((1, model), F32),
            jax.ShapeDtypeStruct((sides, 2, quarter, model), BF16),
            jax.ShapeDtypeStruct((2, model, units), BF16),
            jax.ShapeDtypeStruct((units, model), BF16),
        ],
        in_specs=[vmem] * 4 + [anywhere] * (3 + len(ups)),
        out_specs=[vmem] * 4 + [anywhere] * 2,
        scratch_shapes=[
            pltpu.VMEM((model, units), BF16),
            pltpu.VMEM((model, units), BF16),
            pltpu.VMEM((units, model), BF16),
            pltpu.VMEM((rows_n, model), BF16),
            pltpu.VMEM((rows_n, model), BF16),
            pltpu.VMEM((rows_n, units), BF16),
            pltpu.VMEM((rows_n, units), BF16),
            pltpu.VMEM((rows_n, units), BF16),
            pltpu.VMEM((4, quarter, model), BF16),
            pltpu.VMEM((quarter, model), BF16),
            pltpu.VMEM((quarter, model), BF16),
            pltpu.VMEM((quarter, model), F32),
            pltpu.VMEM((line_rows, model), BF16),
            pltpu.VMEM((line_rows, model), BF16),
            pltpu.VMEM((2 * line_rows, model), BF16),
            pltpu.VMEM((line_rows, model), BF16),
            pltpu.VMEM((4 * line_rows, model), BF16),
            pltpu.VMEM(half, BF16),
            pltpu.VMEM(half, BF16),
            dma((3 + len(ups),)),
            dma((5,)),
            dma((6,)),
            dma((6,)),
            dma((2, outer)),
            dma((outer,)),
            dma((outer,)),
            dma((outer,)),
            dma((2, outer)),
            dma((2, outer)),
            dma((2, outer)),
            dma((2, 2, outer)),
        ]
        + [dma((2, 2))] * 6
        + [dma((LATE_BLOCKS,))] * 2,
        compiler_params=pltpu.CompilerParams(
            collective_id=2, has_side_effects=True, vmem_limit_bytes=63 * 1024 * 1024
        ),
        cost_estimate=pl.CostEstimate(flops=3 * 10**10, bytes_accessed=4 * 10**7, transcendentals=0),
        name="middle",
    )(gated, out_proj, hidden, gain, w_gate, w_up, w_down, *ups)


FFN_CHUNKS = 2


def finish_kernel(
    outer, sides, sp_n, tp_n, streams, width_scale,
    *refs,
):
    MESH = pl.DeviceIdType.MESH
    parts = refs[:streams]
    (part_ref, hidden_ref, scale_ref, gain_ref, middle_ref, sums_ref) = refs[streams : streams + 6]
    last_in, layer_ref = refs[streams + 6 : streams + 8]
    outs = refs[streams + 8 : 2 * streams + 8]
    grad_out, sums_out, last_out, layer_out = refs[2 * streams + 8 : 2 * streams + 12]
    rest = refs[2 * streams + 12 :]
    got = rest[:streams]
    staged = rest[streams : 2 * streams]
    (near_got, far_got, keep_buf, far_stage, sums_got, sums_stage) = rest[2 * streams : 2 * streams + 6]
    rest = rest[2 * streams + 6 :]
    (last_keep, last_got, last_far, layer_send, layer_recv) = rest[:5]
    (f_load, f_near_send, f_near_recv, f_far_send, f_far_recv, f_store, f_out_send, f_out_recv) = rest[5:13]
    (reduce_send, reduce_recv, gather_send, gather_recv, pair_send, pair_recv) = rest[13:19]
    tp_send, tp_recv, sums_send, sums_recv = rest[19:]

    sp_i = lax.axis_index("sp")
    tp_i = lax.axis_index("tp")
    line = sp_i // 2
    half = sp_i % 2
    side = tp_i // 2
    core = tp_i % 2
    last = outer - 1

    def sp_at(z, y):
        return (tp_i, z * 2 + y)

    pair_dev = sp_at(line, 1 - half)
    core_dev = (side * 2 + (1 - core), sp_i)
    side_dev = ((1 - side) * 2 + core, sp_i)

    tp_bits = []
    bit = 1
    while bit < tp_n:
        tp_bits.append(bit)
        bit *= 2
    sp_bits = []
    bit = 1
    while bit < sp_n:
        sp_bits.append(bit)
        bit *= 2

    def flip(value, bit):
        return value + bit - 2 * bit * ((value // bit) % 2)

    sum_devs = [(flip(tp_i, b), sp_i) for b in tp_bits] + [(tp_i, flip(sp_i, b)) for b in sp_bits]

    barrier = pltpu.get_barrier_semaphore()
    greeted = [sp_at((line + 1) % outer, half), sp_at((line + outer - 1) % outer, half)] + sum_devs
    for device in greeted:
        pl.semaphore_signal(barrier, inc=1, device_id=device, device_id_type=MESH)
    pl.semaphore_wait(barrier, len(greeted))

    def remote(src, dst, send, recv, device):
        return pltpu.make_async_remote_copy(
            src_ref=src, dst_ref=dst, send_sem=send, recv_sem=recv,
            device_id=device, device_id_type=MESH,
        )

    places = (line, last - line)
    nexts = (sp_at(jnp.minimum(line + 1, last), half), sp_at(jnp.maximum(line - 1, 0), half))
    signs = (1, -1)

    def rows_of(stream, index):
        count = parts[stream].shape[0] // outer
        return pl.ds(pl.multiple_of(index * count, count), count)

    def reduce_copy(stream, way, step, src):
        return remote(
            src, got[stream].at[way, step - 1], reduce_send.at[stream, way, step - 1],
            reduce_recv.at[stream, way, step - 1], nexts[way],
        )

    def clamp(index):
        return jnp.clip(index, 0, last)

    def reduce_step(stream, step):
        for way in range(2):
            place, sign = places[way], signs[way]
            target = clamp(line + sign * (outer - step))
            own = parts[stream].at[rows_of(stream, target), :]

            @pl.when(place == 0)
            def _():
                reduce_copy(stream, way, step, own).start()

            if step > 1:

                @pl.when((place > 0) & (place <= step - 1))
                def _():
                    reduce_copy(stream, way, step - 1, own).wait_recv()
                    stage = staged[stream].at[way, step - 2]
                    stage[...] = (
                        got[stream][way, step - 2].astype(F32) + own[...].astype(F32)
                    ).astype(BF16)
                    reduce_copy(stream, way, step, stage).start()

    def gather_copy(stream, way, step, origin):
        block = outs[stream].at[half, rows_of(stream, origin), :]
        return remote(
            block, block, gather_send.at[stream, way, step - 1],
            gather_recv.at[stream, way, step - 1], nexts[way],
        )

    def pair_copy(stream, slot, origin):
        block = outs[stream].at[half, rows_of(stream, origin), :]
        return remote(block, block, pair_send.at[stream, slot], pair_recv.at[stream, slot], pair_dev)

    def reduce_final(stream):
        own = parts[stream].at[rows_of(stream, line), :]
        block = outs[stream].at[half, rows_of(stream, line), :]
        for way in range(2):

            @pl.when(places[way] > 0)
            def _():
                reduce_copy(stream, way, last, own).wait_recv()

        up = jnp.where(line > 0, got[stream][0, last - 1].astype(F32), 0.0)
        down = jnp.where(line < last, got[stream][1, last - 1].astype(F32), 0.0)
        block[...] = (own[...].astype(F32) + up + down).astype(BF16)
        for way in range(2):

            @pl.when(places[way] < last)
            def _():
                gather_copy(stream, way, 1, line).start()

        pair_copy(stream, 0, line).start()

    def gather_step(stream, step):
        for way in range(2):
            place, sign = places[way], signs[way]
            origin = clamp(line - sign * step)

            @pl.when(place >= step)
            def _():
                gather_copy(stream, way, step, origin).wait_recv()
                if step < last:

                    @pl.when(place < last)
                    def _():
                        gather_copy(stream, way, step + 1, origin).start()

                pair_copy(stream, 1 + way * last + step - 1, origin).start()

    def drain(stream):
        pair_copy(stream, 0, line).wait()
        for way in range(2):
            place, sign = places[way], signs[way]
            for step in range(1, outer):
                origin = clamp(line - sign * step)

                @pl.when(place <= step - 1)
                def _():
                    reduce_copy(stream, way, step, parts[stream].at[rows_of(stream, 0), :]).wait_send()

                @pl.when((place >= step - 1) & (place < last))
                def _():
                    gather_copy(stream, way, step, origin).wait_send()

                @pl.when(place >= step)
                def _():
                    pair_copy(stream, 1 + way * last + step - 1, origin).wait()

    def near_copy(index):
        return remote(
            part_ref.at[index, 1 - core], near_got.at[index], tp_send.at[index], tp_recv.at[index],
            core_dev,
        )

    def far_copy():
        return remote(far_stage, far_got, tp_send.at[sides], tp_recv.at[sides], side_dev)

    def spread_copy(slot, s, device):
        block = grad_out.at[s, core]
        return remote(block, block, tp_send.at[sides + slot], tp_recv.at[sides + slot], device)

    def input_step(step):
        if step == 0:
            for index in range(sides):
                near_copy(index).start()
        if step == 1:
            for index in range(sides):
                near_copy(index).wait_recv()
            keep_buf[...] = part_ref[side, core].astype(F32) + near_got[side].astype(F32)
            far_stage[...] = (
                part_ref[1 - side, core].astype(F32) + near_got[1 - side].astype(F32)
            ).astype(BF16)
            far_copy().start()
        if step == 2:
            far_copy().wait_recv()
            incoming = keep_buf[...] + far_got[...].astype(F32)
            values = hidden_ref[...].astype(F32)
            scales = scale_ref[...]
            weighted = incoming * gain_ref[...]
            inner_sum = jnp.sum(weighted * values, axis=-1, keepdims=True)
            grads = scales * weighted - values * (scales * scales * scales) * inner_sum * width_scale
            grad_out[side, core] = (middle_ref[...] + grads).astype(BF16)
            spread_copy(1, side, side_dev).start()
            spread_copy(2, side, core_dev).start()
        if step == 3:
            spread_copy(1, side, side_dev).wait_recv()
            spread_copy(3, 1 - side, core_dev).start()
        if step == 4:
            spread_copy(2, side, core_dev).wait_recv()
            spread_copy(3, 1 - side, core_dev).wait_recv()
            for index in range(sides):
                near_copy(index).wait_send()
            far_copy().wait_send()
            spread_copy(1, side, side_dev).wait_send()
            spread_copy(2, side, core_dev).wait_send()
            spread_copy(3, 1 - side, core_dev).wait_send()

    last_half = last_keep.shape[0]

    def ffn_at(j, ref, whole, owner):
        count = last_half // FFN_CHUNKS
        start = j * count
        if whole:
            start = pl.multiple_of(owner * last_half + start, count)
        return ref.at[pl.ds(start, count), :]

    def ffn_keep(j):
        return ffn_at(j, last_keep, False, 0)

    def ffn_got(j):
        return ffn_at(j, last_got, False, 0)

    def ffn_far(j):
        return ffn_at(j, last_far, False, 0)

    def ffn_load(j):
        return pltpu.make_async_copy(ffn_at(j, last_in, True, core), ffn_keep(j), f_load.at[j])

    def ffn_near_copy(j):
        return remote(
            ffn_at(j, last_in, True, 1 - core), ffn_got(j), f_near_send.at[j], f_near_recv.at[j], core_dev
        )

    def ffn_far_copy(j):
        return remote(ffn_keep(j), ffn_far(j), f_far_send.at[j], f_far_recv.at[j], side_dev)

    def ffn_store(j):
        return pltpu.make_async_copy(ffn_got(j), ffn_at(j, last_out, True, core), f_store.at[j])

    def ffn_out_copy(j):
        return remote(
            ffn_got(j), ffn_at(j, last_out, True, core), f_out_send.at[j], f_out_recv.at[j], core_dev
        )

    def ffn_sum(j):
        ffn_load(j).wait()
        ffn_near_copy(j).wait_recv()
        keep = ffn_keep(j)
        keep[...] = (keep[...].astype(F32) + ffn_got(j)[...].astype(F32)).astype(BF16)
        ffn_far_copy(j).start()

    def ffn_total(j):
        ffn_far_copy(j).wait_recv()
        total = ffn_keep(j)[...].astype(F32) + ffn_far(j)[...].astype(F32)
        ffn_got(j)[...] = total.astype(BF16)
        ffn_store(j).start()
        ffn_out_copy(j).start()

    def ffn_drain(j):
        ffn_near_copy(j).wait_send()
        ffn_far_copy(j).wait_send()
        ffn_store(j).wait()
        ffn_out_copy(j).wait()

    rounds = len(sum_devs)

    def sums_copy(step):
        src = sums_ref if step == 0 else sums_stage.at[step - 1]
        return remote(
            src, sums_got.at[step], sums_send.at[step], sums_recv.at[step], sum_devs[step]
        )

    def sums_step(step):
        if step > 0:
            sums_copy(step - 1).wait_recv()
            before = sums_ref[...] if step == 1 else sums_stage[step - 2]
            total = before + sums_got[step - 1]
            if step == rounds:
                sums_out[...] = total
            else:
                sums_stage[step - 1] = total
        if step < rounds:
            sums_copy(step).start()
        if step == rounds:
            for index in range(rounds):
                sums_copy(index).wait_send()

    def later(do, *args):
        return functools.partial(do, *args)

    def layer_copy(slot, s, device):
        block = layer_out.at[s, core]
        src = block if slot == 2 else layer_ref
        return remote(src, block, layer_send.at[slot], layer_recv.at[slot], device)

    def layer_own():
        return pltpu.make_async_copy(layer_ref, layer_out.at[side, core], layer_send.at[3])

    def layer_step(step):
        if step == 0:
            layer_copy(0, side, side_dev).start()
            layer_copy(1, side, core_dev).start()
            layer_own().start()
        if step == 1:
            layer_copy(0, 1 - side, side_dev).wait_recv()
            layer_copy(2, 1 - side, core_dev).start()
        if step == 2:
            layer_copy(1, side, core_dev).wait_recv()
            layer_own().wait()
            layer_copy(0, side, side_dev).wait_send()
            layer_copy(1, side, core_dev).wait_send()
            layer_copy(2, 1 - side, core_dev).wait()

    extra = [
        later(input_step, 0), later(sums_step, 0), later(input_step, 1), later(layer_step, 0),
        later(ffn_sum, 0), later(ffn_sum, 1), later(lambda: None), later(lambda: None), later(input_step, 2),
        later(sums_step, 1), later(lambda: None), later(sums_step, 2), later(lambda: None), later(sums_step, 3),
        later(layer_step, 1), later(lambda: None), later(sums_step, 4), later(input_step, 3),
        later(lambda: None), later(sums_step, 5), later(ffn_total, 0), later(ffn_total, 1),
        later(layer_step, 2), later(input_step, 4),
    ]
    extra += [later(sums_step, index) for index in range(6, rounds + 1)]
    for index in range(FFN_CHUNKS):
        ffn_near_copy(index).start()
        ffn_load(index).start()
    for turn in range(streams + 1):
        for step in range(1, outer + 1):
            if turn < streams:
                if step < outer:
                    reduce_step(turn, step)
                else:
                    reduce_final(turn)
            if turn > 0 and step < outer:
                gather_step(turn - 1, step)
            if extra:
                extra.pop(0)()
    for step in extra:
        step()
    for stream in range(streams):
        drain(stream)
    for index in range(FFN_CHUNKS):
        ffn_drain(index)


def finish(parts, part, hidden, scales, gain, middle, sums, ffn_last, layer, outer, sp_n, tp_n):
    streams = len(parts)
    sides = tp_n // 2
    quarter, model = hidden.shape
    last = outer - 1
    rounds = (tp_n - 1).bit_length() + (sp_n - 1).bit_length()
    vmem = pl.BlockSpec(memory_space=pltpu.VMEM)
    anywhere = pl.BlockSpec(memory_space=pl.ANY)
    chunk = [(2, last, p.shape[0] // outer, p.shape[1]) for p in parts]
    dma = pltpu.SemaphoreType.DMA
    return pl.pallas_call(
        functools.partial(finish_kernel, outer, sides, sp_n, tp_n, streams, 1.0 / model),
        out_shape=[jax.ShapeDtypeStruct((2,) + p.shape, BF16) for p in parts]
        + [
            jax.ShapeDtypeStruct((sides, 2, quarter, model), BF16),
            jax.ShapeDtypeStruct(sums.shape, F32),
        ]
        + [
            jax.ShapeDtypeStruct(ffn_last.shape, BF16),
            jax.ShapeDtypeStruct((sides, 2, quarter, model), BF16),
        ],
        in_specs=[vmem] * (streams + 6) + [anywhere, vmem],
        out_specs=[vmem] * (streams + 2) + [anywhere, vmem],
        scratch_shapes=[pltpu.VMEM(c, BF16) for c in chunk]
        + [pltpu.VMEM(c, BF16) for c in chunk]
        + [
            pltpu.VMEM((sides, quarter, model), BF16),
            pltpu.VMEM((quarter, model), BF16),
            pltpu.VMEM((quarter, model), F32),
            pltpu.VMEM((quarter, model), BF16),
            pltpu.VMEM((rounds,) + sums.shape, F32),
            pltpu.VMEM((rounds,) + sums.shape, F32),
        ]
        + [pltpu.VMEM((ffn_last.shape[0] // 2, ffn_last.shape[1]), BF16)] * 3
        + [dma((4,))] * 2
        + [dma((FFN_CHUNKS,))] * 8
        + [dma((streams, 2, last))] * 4
        + [dma((streams, 1 + 2 * last))] * 2
        + [dma((sides + 4,))] * 2
        + [dma((rounds,))] * 2,
        compiler_params=pltpu.CompilerParams(
            collective_id=1, has_side_effects=True, vmem_limit_bytes=60 * 1024 * 1024
        ),
        cost_estimate=pl.CostEstimate(flops=10**9, bytes_accessed=10**8, transcendentals=0),
        name="finish",
    )(*parts, part, hidden, scales, gain, middle, sums, ffn_last, layer)


def body(
    hidden,
    segment_ids,
    attn_norm,
    query_proj,
    key_proj,
    value_proj,
    gate_proj,
    output_proj,
    query_norm,
    key_norm,
    ffn_norm,
    ffn_gate,
    ffn_up,
    ffn_down,
    upstream,
):
    rows_dev, model = hidden.shape
    head_width = query_norm.shape[0]
    heads = query_proj.shape[1] // head_width
    groups = key_proj.shape[1] // head_width
    per_group = heads // groups
    group_width = groups * head_width
    sp_n = lax.axis_size("sp")
    tp_n = lax.axis_size("tp")
    outer = sp_n // 2
    sides = tp_n // 2
    quarter = rows_dev // tp_n
    tp_i = lax.axis_index("tp")
    sp_i = lax.axis_index("sp")
    ring_i = sp_i // 2
    pair_i = sp_i % 2
    side_i = tp_i // 2
    core_i = tp_i % 2
    own_first = sp_i * rows_dev
    quarter_first = tp_i * quarter
    scale = 1.0 / math.sqrt(head_width)

    ring_pairs = [(z * 2 + y, ((z + 1) % outer) * 2 + y) for z in range(outer) for y in range(2)]
    pair_pairs = [(i, i ^ 1) for i in range(sp_n)]
    side_pairs = [(i, i ^ 2) for i in range(tp_n)]
    core_pairs = [(i, i ^ 1) for i in range(tp_n)]

    def ring(value):
        return lax.ppermute(value, "sp", ring_pairs)

    def far(value, step):
        pairs = [(z * 2 + y, ((z + step) % outer) * 2 + y) for z in range(outer) for y in range(2)]
        return lax.ppermute(value, "sp", pairs)

    def pair(value):
        return lax.ppermute(value, "sp", pair_pairs)

    def side(value):
        return lax.ppermute(value, "tp", side_pairs)

    def core(value):
        return lax.ppermute(value, "tp", core_pairs)

    def gather_sp(block, paired):
        blocks = []
        first = block
        for k in range(outer):
            blocks.append((block, pair(block)) if k < paired else (block,))
            if k < outer - 1:
                block = ring(block) if paired == outer else far(first, k + 1)
        return blocks

    def scatter_sp(parts):
        def paired(k):
            return parts[k][0] + pair(parts[k][1].astype(BF16)).astype(F32)

        total = paired(1 % outer)
        for k in range(2, outer + 1):
            total = ring(total.astype(BF16)).astype(F32) + paired(k % outer)
        return total

    first_id = segment_ids[0]
    second_start = jnp.sum((segment_ids == first_id).astype(jnp.int32))
    own_index = own_first + jnp.arange(rows_dev, dtype=jnp.int32)
    own_starts = jnp.where(own_index < second_start, 0, second_start)
    steps_half = jnp.arange(head_width // 2, dtype=F32)
    frequencies = jnp.exp(steps_half * (-2.0 * math.log(THETA) / head_width))
    angles = (own_index - own_starts).astype(F32)[:, None] * frequencies[None, :]
    cosine = jnp.cos(angles)[:, None, :]
    sine = jnp.sin(angles)[:, None, :]

    hidden_full = hidden.astype(F32)
    normed_full, attn_scales = norm_rows(hidden_full, attn_norm)
    normed = normed_full.astype(BF16)
    key_raw = matmul(normed, key_proj).reshape(rows_dev, groups, head_width)
    value_rows = matmul(normed, value_proj).astype(BF16)
    key_normed, key_scales = norm_rows(key_raw, key_norm)
    key_rot = rotary(key_normed, cosine, sine).astype(BF16).reshape(rows_dev, group_width)
    kv_own = jnp.stack([key_rot, value_rows])

    low, high = (outer // 4, 3 * outer // 4) if outer % 4 == 0 else (0, outer)
    reach = high - 1 if low else outer - 1

    def up_pairs(step):
        return [
            (z * 2 + y, (z + 1) * 2 + y)
            for z in range(outer - 1)
            for y in range(2)
            if z + 1 - step >= 0 and (z + 1 - step >= low or z + 1 < high)
        ]

    def far_pairs(step):
        return [
            (z * 2 + y, (z + step) * 2 + y)
            for z in range(outer - step)
            for y in range(2)
            if z >= low or z + step < high
        ]

    kv_blocks = []
    travelling = kv_own
    for k in range(reach + 1):
        if k > 0 and reach <= 2:
            travelling = lax.ppermute(kv_own, "sp", far_pairs(k))
        elif k > 0:
            travelling = lax.ppermute(travelling, "sp", up_pairs(k))
        kv_blocks.append((travelling, pair(travelling)))

    query_raw = matmul(normed, query_proj).reshape(rows_dev, heads, head_width)
    gate_raw = matmul(normed, gate_proj)
    query_normed, query_scales = norm_rows(query_raw, query_norm)
    queries = rotary(query_normed, cosine, sine).astype(BF16).reshape(rows_dev, heads * head_width)

    def swap_half(value):
        piece = model // 4
        mine = pair(lax.dynamic_slice_in_dim(value, ((1 - pair_i) * 2 + core_i) * piece, piece, 1))
        near = core(mine)
        return jnp.where(
            core_i == 1, jnp.concatenate([near, mine], 1), jnp.concatenate([mine, near], 1)
        )

    normed_own = lax.dynamic_slice_in_dim(normed, pair_i * (model // 2), model // 2, 1)
    both_normed = jnp.concatenate([normed_own, swap_half(normed)])

    grad_quarter = lax.dynamic_slice_in_dim(upstream, quarter_first, quarter)
    fused = 2 < outer and outer * quarter <= 512 and tp_n == 4
    up_blocks = gather_sp(grad_quarter, outer - LATE_BLOCKS if fused else outer)

    row_start_low = own_starts[0]
    row_start_high = own_starts[-1]

    def block_info(k):
        shards = [(ring_i - k) * 2 + pair_i, (ring_i - k) * 2 + (1 - pair_i)]
        entries = [own_first] + [shard * rows_dev for shard in shards]
        live = []
        full = []
        for shard in shards:
            token = shard * rows_dev
            live.append((shard >= 0) & (shard <= sp_i) & (token + rows_dev - 1 >= row_start_low))
            full.append((token >= row_start_high) & (shard < sp_i))
        return jnp.stack(entries + [v.astype(jnp.int32) for v in live + full]).astype(jnp.int32)

    infos = [block_info(k) for k in range(reach + 1)]
    starts_column = own_starts[:, None]
    starts_row = own_starts[None, :]
    carried = None
    for k in range(reach + 1):
        if fused and k == reach:
            carried, up_blocks = lax.optimization_barrier((carried, up_blocks))
        carried = attn_forward(
            infos[k], starts_column, queries, kv_blocks[k][0], kv_blocks[k][1], carried, scale
        )
    mix_acc, mix_sum = carried
    mixed = mix_acc / mix_sum
    lse = jnp.log2(mix_sum.reshape(rows_dev, heads, head_width)[:, :, 0])
    lse_rows = lse.T.reshape(groups, per_group, rows_dev)
    gate_sig = jax.nn.sigmoid(gate_raw)
    gated = (mixed * gate_sig).astype(BF16)
    gated_other = pair(gated)

    def scatter_tp(part):
        part = part.reshape(sides, 2, quarter, model)
        keep = lax.dynamic_index_in_dim(part, core_i, 1, keepdims=False)
        send = lax.dynamic_index_in_dim(part, 1 - core_i, 1, keepdims=False)
        keep = keep + core(send.astype(BF16)).astype(F32)
        mine = lax.dynamic_index_in_dim(keep, side_i, 0, keepdims=False)
        other = lax.dynamic_index_in_dim(keep, 1 - side_i, 0, keepdims=False)
        return mine + side(other.astype(BF16)).astype(F32)

    def gather_tp(block):
        far = side(block)
        swap_side = side_i == 1
        two = jnp.where(swap_side, jnp.stack([far, block]), jnp.stack([block, far]))
        near = core(two)
        swap_core = core_i == 1
        full = jnp.where(
            swap_core, jnp.stack([near, two], axis=1), jnp.stack([two, near], axis=1)
        )
        return full.reshape((rows_dev,) + block.shape[1:])

    if fused:
        layer_quarter, grad_middle_quarter, ffn_gain_sum, branch, *ffn_parts = middle_layer(
            gated,
            output_proj,
            lax.dynamic_slice_in_dim(hidden, quarter_first, quarter),
            ffn_norm[None, :],
            ffn_gate,
            ffn_up,
            ffn_down,
            [block for both in up_blocks for block in both],
            outer,
            sides,
        )
        grad_branch = branch.reshape(rows_dev, model)
        ffn_gain_sum = ffn_gain_sum[0]
    else:
        attn_quarter = scatter_tp(matmul(gated, output_proj))
        hidden_quarter = lax.dynamic_slice_in_dim(hidden, quarter_first, quarter).astype(F32)
        middle = hidden_quarter + attn_quarter
        normed_two_full, ffn_scales = norm_rows(middle, ffn_norm)
        normed_two = normed_two_full.astype(BF16)

        two_blocks = gather_sp(normed_two, outer)
        rows_list, up_list, inner_list, gate_list, grad_up_list = [None] * outer, [None] * outer, [None] * outer, [None] * outer, [None] * outer
        grad_parts = [None] * outer
        for k in list(range(1, outer)) + [0]:
            rows_k = jnp.concatenate(two_blocks[k])
            up_k = jnp.concatenate(up_blocks[k])
            gate_vals = matmul(rows_k, ffn_gate)
            up_vals = matmul(rows_k, ffn_up)
            sig = jax.nn.sigmoid(gate_vals)
            grad_inner = times_transpose(up_k, ffn_down)
            grad_gate = (grad_inner * up_vals * (sig * (1.0 + gate_vals * (1.0 - sig)))).astype(BF16)
            grad_up = (grad_inner * (gate_vals * sig)).astype(BF16)
            inner = (gate_vals * sig * up_vals).astype(BF16)
            grad_parts[k] = (
                times_transpose(grad_gate, ffn_gate) + times_transpose(grad_up, ffn_up)
            ).reshape(2, quarter, model)
            rows_list[k], up_list[k], inner_list[k] = rows_k, up_k, inner
            gate_list[k], grad_up_list[k] = grad_gate, grad_up
        grad_two = scatter_sp(grad_parts)

        norm_grad_two, ffn_gain_terms = norm_back(middle, ffn_scales, ffn_norm, grad_two)
        grad_middle_quarter = grad_quarter.astype(F32) + norm_grad_two
        grad_branch = gather_tp(grad_middle_quarter.astype(BF16))
        ffn_gain_sum = jnp.sum(ffn_gain_terms, axis=0)
        mlp_parts = [
            matmul(inner_list[k], ffn_down).reshape(2, quarter, model) for k in range(outer)
        ]
        layer_quarter = (middle + scatter_sp(mlp_parts)).astype(BF16)

    def sum_tp(part):
        total = part.astype(BF16).astype(F32)
        total = total + core(total.astype(BF16)).astype(F32)
        low = total.astype(BF16)
        return (low.astype(F32) + side(low).astype(F32)).astype(BF16)

    if not fused:
        rows_all = jnp.concatenate(rows_list)
        up_all = jnp.concatenate(up_list)
        inner_all = jnp.concatenate(inner_list)
        gate_all = jnp.concatenate(gate_list)
        grad_up_all = jnp.concatenate(grad_up_list)
        ffn_parts = [
            jnp.stack([outer_sum(rows_all, gate_all), outer_sum(rows_all, grad_up_all)]),
            outer_sum(inner_all, up_all),
        ]
        ffn_parts = [sum_tp(ffn_parts[0]), ffn_parts[1].astype(BF16)]
    ffn_both, ffn_last = ffn_parts

    branch_other = swap_half(grad_branch)
    branch_own = lax.dynamic_slice_in_dim(grad_branch, pair_i * (model // 2), model // 2, 1)
    grad_gated = times_transpose(grad_branch, output_proj)
    grad_mixed = (grad_gated * gate_sig).astype(BF16)
    grad_gate_raw = (grad_gated * mixed * (gate_sig * (1.0 - gate_sig))).astype(BF16)
    gate_other = pair(grad_gate_raw)
    deltas = jnp.sum(
        (grad_mixed.astype(F32) * mixed).reshape(rows_dev, heads, head_width), axis=-1
    )
    delta_rows = deltas.T.reshape(groups, per_group, rows_dev)

    def down_pairs(step):
        return [(b, a) for a, b in up_pairs(step)]

    query_acc = None
    travelling = None
    paired = {}
    for k in list(range(reach, -1, -1)):
        if k + 2 in paired:
            query_acc, paired[k + 2] = lax.optimization_barrier((query_acc, paired[k + 2]))
        query_acc, grad_a, grad_b = attn_backward(
            infos[k], starts_row, lse_rows, delta_rows, queries, grad_mixed,
            kv_blocks[k][0], kv_blocks[k][1], query_acc, k == 0, scale,
        )
        if k == reach:
            query_acc, grad_a, grad_b, gated_other, branch_other, gate_other = lax.optimization_barrier(
                (query_acc, grad_a, grad_b, gated_other, branch_other, gate_other)
            )
        paired[k] = pair(grad_b)
        total = grad_a.astype(F32) + paired[k].astype(F32)
        if travelling is not None:
            total = total + travelling.astype(F32)
        if k > 0:
            travelling = lax.ppermute(total.astype(BF16), "sp", down_pairs(k))
    output_half = outer_sum(
        jnp.concatenate([gated, gated_other]), jnp.concatenate([branch_own, branch_other])
    )
    gate_half = outer_sum(both_normed, jnp.concatenate([grad_gate_raw, gate_other]))
    grad_key_rot = total[0].reshape(rows_dev, groups, head_width)
    grad_value_low = total[1].astype(BF16)
    grad_query_rot = (query_acc * scale).reshape(rows_dev, heads, head_width)
    grad_query_raw, query_gain_terms = norm_back(
        query_raw, query_scales, query_norm, rotary_back(grad_query_rot, cosine, sine)
    )
    grad_key_raw, key_gain_terms = norm_back(
        key_raw, key_scales, key_norm, rotary_back(grad_key_rot, cosine, sine)
    )
    grad_query_low = grad_query_raw.reshape(rows_dev, heads * head_width).astype(BF16)
    grad_key_low = grad_key_raw.reshape(rows_dev, group_width).astype(BF16)
    grad_kv_low = jnp.concatenate([grad_key_low, grad_value_low], axis=1)

    both_queries = jnp.concatenate([grad_query_low, pair(grad_query_low)])
    both_kv = jnp.concatenate([grad_kv_low, pair(grad_kv_low)])
    parts = [
        output_half.astype(BF16),
        gate_half.astype(BF16),
        outer_sum(both_normed, both_queries).astype(BF16),
        outer_sum(both_normed, both_kv).astype(BF16),
    ]

    grad_normed_part = (
        times_transpose(grad_query_low, query_proj)
        + times_transpose(grad_key_low, key_proj)
        + times_transpose(grad_value_low, value_proj)
        + times_transpose(grad_gate_raw, gate_proj)
    )
    gains = jnp.concatenate(
        [
            jnp.sum(grad_normed_part * hidden_full * attn_scales, axis=0),
            ffn_gain_sum,
            jnp.sum(query_gain_terms, axis=(0, 1)),
            jnp.sum(key_gain_terms, axis=(0, 1)),
        ]
    )
    gains_at = 2 * model + 2 * head_width
    gains = jnp.pad(gains, (0, -gains_at % 1024)).reshape(-1, 128)
    scales_quarter = lax.dynamic_slice_in_dim(attn_scales, quarter_first, quarter)
    finished = finish(
        parts,
        grad_normed_part.astype(BF16).reshape(sides, 2, quarter, model),
        lax.dynamic_slice_in_dim(hidden, quarter_first, quarter),
        scales_quarter,
        attn_norm[None, :],
        grad_middle_quarter,
        gains,
        ffn_last,
        layer_quarter,
        outer,
        sp_n,
        tp_n,
    )
    output_all, gate_all_w, query_all, kv_all, input_all, gains, ffn_last, layer_all = finished
    output_grad = jnp.concatenate([output_all[0], output_all[1]], axis=1).astype(F32)
    gate_grad = gate_all_w.reshape(model, heads * head_width).astype(F32)
    query_grad = query_all.reshape(model, heads * head_width).astype(F32)
    kv_all = kv_all.reshape(model, 2 * group_width)
    key_grad = kv_all[:, :group_width].astype(F32)
    value_grad = kv_all[:, group_width:].astype(F32)
    hidden_grad = input_all.reshape(rows_dev, model).astype(F32)
    gains = gains.reshape(-1)
    return (
        layer_all.reshape(rows_dev, model),
        hidden_grad,
        gains[:model],
        query_grad,
        key_grad,
        value_grad,
        gate_grad,
        output_grad,
        gains[2 * model : 2 * model + head_width],
        gains[2 * model + head_width : gains_at],
        gains[model : 2 * model],
        ffn_both[0].astype(F32),
        ffn_both[1].astype(F32),
        ffn_last.astype(F32),
    )


def solution(mesh):
    placed = (
        P("sp", None),
        P(),
        P(),
        P(None, "tp"),
        P(None, "tp"),
        P(None, "tp"),
        P(None, "tp"),
        P("tp", None),
        P(),
        P(),
        P(),
        P(None, "sp"),
        P(None, "sp"),
        P("sp", None),
        P("sp", None),
    )
    return jax.shard_map(
        body,
        mesh=mesh,
        in_specs=placed,
        out_specs=(
            P("sp", None),
            P("sp", None),
            P(),
            P(None, "tp"),
            P(None, "tp"),
            P(None, "tp"),
            P(None, "tp"),
            P("tp", None),
            P(),
            P(),
            P(),
            P(None, "sp"),
            P(None, "sp"),
            P("sp", None),
        ),
        check_vma=False,
    )
```

```python
import functools
import math

import jax
import jax.numpy as jnp
from jax import lax
from jax.experimental import pallas as pl
from jax.experimental.pallas import tpu as pltpu
from jax.sharding import PartitionSpec as P

EPSILON = 1e-06
THETA = 1000000.0
LOG2E = 1.4426950408889634
F32 = jnp.float32
BF16 = jnp.bfloat16


def norm_scales(values):
    return lax.rsqrt(jnp.mean(values * values, axis=-1, keepdims=True) + EPSILON)


def norm_rows(values, gain):
    scales = norm_scales(values)
    return (values * scales * gain, scales)


def norm_back(values, scales, gain, incoming):
    weighted = incoming * gain
    inner_sum = jnp.sum(weighted * values, axis=-1, keepdims=True)
    grad_values = (
        scales * weighted - values * (scales * scales * scales) * inner_sum / values.shape[-1]
    )
    return (grad_values, incoming * values * scales)


def rotary(values, cosine, sine):
    half_width = values.shape[-1] // 2
    front_half = values[..., :half_width]
    back_half = values[..., half_width:]
    return jnp.concatenate(
        [front_half * cosine - back_half * sine, back_half * cosine + front_half * sine], axis=-1
    )


def rotary_back(grads, cosine, sine):
    half_width = grads.shape[-1] // 2
    front_half = grads[..., :half_width]
    back_half = grads[..., half_width:]
    return jnp.concatenate(
        [front_half * cosine + back_half * sine, back_half * cosine - front_half * sine], axis=-1
    )


def matmul(left, right):
    return jnp.dot(left, right, preferred_element_type=F32)


def outer_sum(left, right):
    return lax.dot_general(left, right, (((0,), (0,)), ((), ())), preferred_element_type=F32)


def times_transpose(left, right):
    return lax.dot_general(left, right, (((1,), (1,)), ((), ())), preferred_element_type=F32)


def attn_forward_kernel(first, diagonal, scale, info, starts, queries, kv_a, kv_b, *rest):
    if first:
        acc_out, sum_out = rest
    else:
        acc_in, sum_in, acc_out, sum_out = rest
    rows = queries.shape[0]
    keys_n = kv_a.shape[1]
    per_group = queries.shape[1] // kv_a.shape[2]
    width = kv_a.shape[2]
    if first:
        acc_out[...] = jnp.zeros_like(acc_out)
        sum_out[...] = jnp.zeros_like(sum_out)
    else:
        acc_out[...] = acc_in[...]
        sum_out[...] = sum_in[...]
    own_first = info[0]
    for slot, block in enumerate((kv_a, kv_b)):
        key_first = info[1 + slot]
        live = info[3 + slot] > 0

        def work(masked, causal):
            ones = jnp.ones((keys_n, width), BF16)
            values = jnp.concatenate([block[1], ones], axis=1)
            keys = block[0]
            if masked:
                key_index = key_first + lax.broadcasted_iota(jnp.int32, (rows, keys_n), 1)
                allowed = key_index >= starts[...]
                if causal:
                    row_index = own_first + lax.broadcasted_iota(jnp.int32, (rows, keys_n), 0)
                    allowed = allowed & (key_index <= row_index)
            for head in range(per_group):
                cols = slice(head * width, (head + 1) * width)
                scores = times_transpose(queries[:, cols], keys)
                weights = jnp.exp2(scores * (scale * LOG2E))
                if masked:
                    weights = jnp.where(allowed, weights, 0.0)
                both = matmul(weights.astype(BF16), values)
                acc_out[:, cols] += both[:, :width]
                sum_out[:, cols] += both[:, width:]

        if diagonal and slot == 0:
            work(True, True)
        else:
            full = info[5 + slot] > 0
            pl.when(live & full)(functools.partial(work, False, False))
            pl.when(live & jnp.logical_not(full))(functools.partial(work, True, False))


def attn_forward(info, starts, queries, kv_a, kv_b, carried, scale):
    rows, all_width = queries.shape
    width = 128
    groups = kv_a.shape[2] // width
    group_width = all_width // groups
    keys_n = kv_a.shape[1]
    first = carried is None
    spec_q = pl.BlockSpec((rows, group_width), lambda g, info: (0, g))
    spec_kv = pl.BlockSpec((2, keys_n, width), lambda g, info: (0, 0, g))
    specs = [pl.BlockSpec((rows, 1), lambda g, info: (0, 0)), spec_q, spec_kv, spec_kv]
    operands = [starts, queries, kv_a, kv_b]
    if not first:
        specs += [spec_q, spec_q]
        operands += list(carried)
    return pl.pallas_call(
        functools.partial(attn_forward_kernel, first, first, scale),
        grid_spec=pltpu.PrefetchScalarGridSpec(
            num_scalar_prefetch=1,
            grid=(groups,),
            in_specs=specs,
            out_specs=[spec_q, spec_q],
        ),
        out_shape=[jax.ShapeDtypeStruct((rows, all_width), F32)] * 2,
        compiler_params=pltpu.CompilerParams(dimension_semantics=("arbitrary",)),
        cost_estimate=pl.CostEstimate(
            flops=16 * rows * keys_n * all_width,
            transcendentals=2 * rows * keys_n * all_width // width,
            bytes_accessed=8 * rows * all_width,
        ),
        name="attn_forward",
    )(info, *operands)


def attn_backward_kernel(first, diagonal, scale, info, starts, lse, deltas, queries, grads, kv_a, kv_b, *rest):
    if first:
        grad_q, grad_a, grad_b = rest
    else:
        grad_in, grad_q, grad_a, grad_b = rest
    rows = queries.shape[0]
    keys_n = kv_a.shape[1]
    width = kv_a.shape[2]
    per_group = queries.shape[1] // width
    if first:
        grad_q[...] = jnp.zeros_like(grad_q)
    else:
        grad_q[...] = grad_in[...]
    own_first = info[0]
    for slot, (block, out) in enumerate(((kv_a, grad_a), (kv_b, grad_b))):
        key_first = info[1 + slot]
        live = info[3 + slot] > 0

        def work(masked, causal):
            keys = block[0]
            values = block[1]
            keys_t = keys.T
            if masked:
                key_index = key_first + lax.broadcasted_iota(jnp.int32, (keys_n, rows), 0)
                allowed = key_index >= starts[...]
                if causal:
                    row_index = own_first + lax.broadcasted_iota(jnp.int32, (keys_n, rows), 1)
                    allowed = allowed & (key_index <= row_index)
            total_k = jnp.zeros((keys_n, width), F32)
            total_v = jnp.zeros((keys_n, width), F32)
            for head in range(per_group):
                cols = slice(head * width, (head + 1) * width)
                q_head = queries[:, cols]
                g_head = grads[:, cols]
                scores = times_transpose(keys, q_head)
                probs = jnp.exp2(scores * (scale * LOG2E) - lse[0, head : head + 1, :])
                if masked:
                    probs = jnp.where(allowed, probs, 0.0)
                grad_probs = times_transpose(values, g_head)
                grad_scores = (probs * (grad_probs - deltas[0, head : head + 1, :])).astype(BF16)
                total_v += matmul(probs.astype(BF16), g_head)
                total_k += matmul(grad_scores, q_head)
                grad_q[:, cols] += matmul(keys_t, grad_scores).T
            out[0] = (total_k * scale).astype(BF16)
            out[1] = total_v.astype(BF16)

        if diagonal and slot == 0:
            work(True, True)
        else:
            full = info[5 + slot] > 0
            pl.when(live & full)(functools.partial(work, False, False))
            pl.when(live & jnp.logical_not(full))(functools.partial(work, True, False))

            @pl.when(jnp.logical_not(live))
            def _():
                out[...] = jnp.zeros_like(out)


def attn_backward(info, starts_row, lse, deltas, queries, grads, kv_a, kv_b, carried, diagonal, scale):
    rows, all_width = queries.shape
    width = 128
    groups = kv_a.shape[2] // width
    group_width = all_width // groups
    per_group = group_width // width
    keys_n = kv_a.shape[1]
    first = carried is None
    spec_q = pl.BlockSpec((rows, group_width), lambda g, info: (0, g))
    spec_kv = pl.BlockSpec((2, keys_n, width), lambda g, info: (0, 0, g))
    spec_row = pl.BlockSpec((1, per_group, rows), lambda g, info: (g, 0, 0))
    specs = [
        pl.BlockSpec((1, rows), lambda g, info: (0, 0)),
        spec_row,
        spec_row,
        spec_q,
        spec_q,
        spec_kv,
        spec_kv,
    ]
    operands = [starts_row, lse, deltas, queries, grads, kv_a, kv_b]
    if not first:
        specs.append(spec_q)
        operands.append(carried)
    return pl.pallas_call(
        functools.partial(attn_backward_kernel, first, diagonal, scale),
        grid_spec=pltpu.PrefetchScalarGridSpec(
            num_scalar_prefetch=1,
            grid=(groups,),
            in_specs=specs,
            out_specs=[spec_q, spec_kv, spec_kv],
        ),
        out_shape=[
            jax.ShapeDtypeStruct((rows, all_width), F32),
            jax.ShapeDtypeStruct(kv_a.shape, BF16),
            jax.ShapeDtypeStruct(kv_a.shape, BF16),
        ],
        compiler_params=pltpu.CompilerParams(dimension_semantics=("arbitrary",)),
        cost_estimate=pl.CostEstimate(
            flops=20 * rows * keys_n * all_width,
            transcendentals=2 * rows * keys_n * all_width // width,
            bytes_accessed=8 * rows * all_width,
        ),
        name="attn_backward",
    )(info, *operands)


LATE_BLOCKS = 2


def middle_kernel(outer, *refs):
    MESH = pl.DeviceIdType.MESH
    blocks = 2 * outer - LATE_BLOCKS
    (gated, out_proj, hidden_ref, gain_ref, gate_in, up_in, down_in) = refs[:7]
    ups_in = refs[7 : 7 + blocks]
    (layer_out, grad_out, gain_out, branch, dw_both, dw_down) = refs[7 + blocks : 13 + blocks]
    (
        w_gate, w_up, w_down, ups, rows, inner, grad_gate, grad_up,
        near_buf, far_stage, far_got, middle_buf,
        keep, y_stage, y_got, z_stage, z_got, part_got, part_far,
        load_sem, store_sem, tp_send, tp_recv, zs, zr, ys, yr, rys, ryr, rzs, rzr,
        p_near_send, p_near_recv, p_far_send, p_far_recv, p_out_send, p_out_recv, us, ur,
    ) = refs[13 + blocks :]
    stage_gate, stage_up, stage_down = w_gate, w_up, rows
    far_keep, own_keep = grad_out, middle_buf
    units = w_down.shape[0]
    quarter, model = hidden_ref.shape
    group = 2 * quarter
    chunk = model // outer
    last = outer - 1

    sp_i = lax.axis_index("sp")
    tp_i = lax.axis_index("tp")
    line = sp_i // 2
    half = sp_i % 2
    side = tp_i // 2
    core = tp_i % 2

    def sp_at(z, y):
        return (tp_i, z * 2 + y)

    pair_dev = sp_at(line, 1 - half)
    core_dev = (side * 2 + (1 - core), sp_i)
    side_dev = ((1 - side) * 2 + core, sp_i)
    nexts = (sp_at(jnp.minimum(line + 1, last), half), sp_at(jnp.maximum(line - 1, 0), half))

    late = list(range(outer - LATE_BLOCKS, outer))
    ups_at = [at for at in range(2 * outer) if at % 2 == 0 or at // 2 not in late]
    loads = [
        pltpu.make_async_copy(src, dst, load_sem.at[index])
        for index, (src, dst) in enumerate(
            [(down_in, w_down)]
            + [(src, ups.at[pl.ds(at * quarter, quarter), :]) for at, src in zip(ups_at, ups_in)]
            + [(gate_in, w_gate), (up_in, w_up)]
        )
    ]
    for load in loads:
        load.start()

    barrier = pltpu.get_barrier_semaphore()
    greeted = [
        sp_at((line + 1) % outer, half), sp_at((line + outer - 1) % outer, half),
        pair_dev, core_dev, side_dev,
    ]
    for device in greeted:
        pl.semaphore_signal(barrier, inc=1, device_id=device, device_id_type=MESH)
    pl.semaphore_wait(barrier, len(greeted))

    def remote(src, dst, send, recv, device):
        return pltpu.make_async_remote_copy(
            src_ref=src, dst_ref=dst, send_sem=send, recv_sem=recv,
            device_id=device, device_id_type=MESH,
        )

    def aligned(index, count):
        return pl.ds(pl.multiple_of(index * count, count), count)

    def late_copy(index):
        at = late[index] * 2
        return remote(
            ups.at[pl.ds(at * quarter, quarter), :], ups.at[pl.ds((at + 1) * quarter, quarter), :],
            us.at[index], ur.at[index], pair_dev,
        )

    def near_copy(j):
        return remote(near_buf.at[j], near_buf.at[2 + j], tp_send.at[j], tp_recv.at[j], core_dev)

    def far_copy():
        return remote(far_stage, far_got, tp_send.at[2], tp_recv.at[2], side_dev)

    def projected(s, c):
        return matmul(gated[aligned(s * 2 + c, quarter), :], out_proj[...])

    near_buf[0] = projected(1 - side, 1 - core).astype(BF16)
    near_copy(0).start()
    near_buf[1] = projected(side, 1 - core).astype(BF16)
    near_copy(1).start()
    for index in range(LATE_BLOCKS):
        loads[1 + ups_at.index(late[index] * 2)].wait()
        late_copy(index).start()
    far_keep[...] = projected(1 - side, core)
    near_copy(0).wait_recv()
    far_stage[...] = (far_keep[...] + near_buf[2].astype(F32)).astype(BF16)
    far_copy().start()
    own_keep[...] = projected(side, core)

    near_copy(1).wait_recv()
    far_copy().wait_recv()
    middle = hidden_ref[...].astype(F32) + (
        own_keep[...] + near_buf[3].astype(F32) + far_got[...].astype(F32)
    )
    middle_buf[...] = middle
    rows[0:quarter, :] = (middle * norm_scales(middle) * gain_ref[...]).astype(BF16)

    def entry(k, j):
        return pl.ds(pl.multiple_of((k * 2 + j) * quarter, quarter), quarter)

    def wrap(k):
        return (k + outer) % outer

    def z_copy(way, k):
        to = wrap(k + 1 - 2 * way)
        return remote(
            rows.at[entry(k, 0), :], rows.at[entry(to, 0), :], zs.at[way, k], zr.at[to], nexts[way]
        )

    def z_arrived(k):
        return remote(
            rows.at[entry(k, 0), :], rows.at[entry(k, 0), :], zs.at[0, k], zr.at[k], nexts[0]
        )

    def y_copy(k):
        return remote(
            rows.at[entry(k, 0), :], rows.at[entry(k, 1), :], ys.at[k], yr.at[k], pair_dev
        )

    short = jnp.minimum(line, last - line)

    def delta_of(i):
        near = jnp.where(i % 2 == 1, -((i + 1) // 2), (i + 1) // 2)
        far = jnp.where(line < last - line, i - short, short - i)
        return jnp.where(i <= 2 * short, near, far)

    def slot_of(delta):
        return jnp.where(delta <= 0, -delta, outer - delta)

    for way, exists in ((0, line < last), (1, line > 0)):
        pl.when(exists)(z_copy(way, 0).start)
    y_copy(0).start()

    def goes_on(delta):
        return ((delta < 0) & (line < last), (delta > 0) & (line > 0))

    def forward(i):
        delta = delta_of(i)
        k = slot_of(delta)
        z_arrived(k).wait_recv()
        for way, exists in enumerate(goes_on(delta)):
            pl.when(exists)(z_copy(way, k).start)
        y_copy(k).start()

    waited = [1 + ups_at.index(k * 2) for k in late]
    for index, load in enumerate(loads):
        if index not in waited:
            load.wait()
    for index in range(LATE_BLOCKS):
        late_copy(index).wait_recv()
    forward(1)

    def turn_forward(i, carry):
        @pl.when(i + 2 < outer)
        def _():
            forward(i + 2)

        k = slot_of(delta_of(i))
        y_copy(k).wait_recv()
        at = aligned(k, group)
        rows_k = rows[at, :]
        gate_vals = matmul(rows_k, w_gate[...])
        up_vals = matmul(rows_k, w_up[...])
        incoming = times_transpose(ups[at, :], w_down[...])
        sig = jax.nn.sigmoid(gate_vals)
        silu = gate_vals * sig
        grad_gate[at, :] = (incoming * up_vals * (sig * (1.0 + gate_vals * (1.0 - sig)))).astype(BF16)
        grad_up[at, :] = (incoming * silu).astype(BF16)
        inner[at, :] = (silu * up_vals).astype(BF16)
        return carry

    lax.fori_loop(0, outer, turn_forward, 0)

    near_copy(0).wait_send()
    near_copy(1).wait_send()

    def y_sum(which, k):
        at = aligned(k, quarter)
        src = y_stage.at[at, :] if which == 0 else near_buf.at[k]
        got = y_got.at[aligned(which * outer + k, quarter), :]
        return remote(src, got, rys.at[which, k], ryr.at[which, k], pair_dev)

    def half_rows(k, j):
        return pl.ds(pl.multiple_of((k * 2 + j) * quarter, quarter), quarter)

    def turn_parts(step, carry):
        k = slot_of(delta_of(last - step))
        part = times_transpose(grad_gate[half_rows(k, 1), :], w_gate[...]) + times_transpose(
            grad_up[half_rows(k, 1), :], w_up[...]
        )
        y_stage[aligned(k, quarter), :] = part.astype(BF16)
        y_sum(0, k).start()
        return carry

    def turn_outputs(step, carry):
        k = slot_of(delta_of(last - step))
        near_buf[k] = matmul(inner[half_rows(k, 1), :], w_down[...]).astype(BF16)
        y_sum(1, k).start()
        return carry

    def turn_keep(step, carry):
        k = slot_of(delta_of(last - step))
        part = times_transpose(grad_gate[half_rows(k, 0), :], w_gate[...]) + times_transpose(
            grad_up[half_rows(k, 0), :], w_up[...]
        )
        keep[aligned(k, quarter), :] = part.astype(BF16)
        return carry

    lax.fori_loop(0, outer, turn_parts, 0)
    lax.fori_loop(0, outer, turn_keep, 0)

    def z_got_rows(which, way, k):
        return aligned((which * 2 + way) * outer + k, quarter)

    def z_sum(which, way, k):
        to = wrap(k + 1 - 2 * way)
        return remote(
            z_stage.at[aligned(k, quarter), :], z_got.at[z_got_rows(which, way, to), :],
            rzs.at[which, k], rzr.at[which, way, to], nexts[way],
        )

    def z_got_at(which, way, k):
        return z_got[z_got_rows(which, way, k), :].astype(F32)

    def z_sum_arrived(which, way, k):
        return remote(
            z_stage.at[aligned(k, quarter), :], z_got.at[z_got_rows(which, way, k), :],
            rzs.at[which, k], rzr.at[which, way, k], nexts[way],
        )

    def own_share(which, k):
        if which == 0:
            share = keep[aligned(k, quarter), :].astype(F32)
        else:
            share = matmul(inner[half_rows(k, 0), :], w_down[...])
        return share + y_got[aligned(which * outer + k, quarter), :].astype(F32)

    def chain(which, step):
        delta = delta_of(last - step)
        k = slot_of(delta)
        at = aligned(k, quarter)
        y_sum(which, k).wait_recv()
        own = own_share(which, k)
        if which == 1:
            z_sum(0, 0, k).wait_send()
        for way, (here, before) in enumerate(((delta > 0, line > 0), (delta < 0, line < last))):

            @pl.when(here & before)
            def _():
                z_sum_arrived(which, way, k).wait_recv()
                z_stage[at, :] = (own + z_got_at(which, way, k)).astype(BF16)

            @pl.when(here & jnp.logical_not(before))
            def _():
                z_stage[at, :] = own.astype(BF16)

            pl.when(here)(z_sum(which, way, k).start)

    def chain_end(which):
        y_sum(which, 0).wait_recv()
        own = own_share(which, 0)
        for way, exists in ((0, line > 0), (1, line < last)):
            pl.when(exists)(z_sum_arrived(which, way, 0).wait_recv)
        below = jnp.where(line > 0, z_got_at(which, 0, 0), 0.0)
        above = jnp.where(line < last, z_got_at(which, 1, 0), 0.0)
        return own + below + above

    half_model = model // 2
    piece = half_model // 2

    def stage_rows(owner, r):
        return pl.ds(pl.multiple_of(owner * half_model + r * piece, piece), piece)

    stages = (stage_gate, stage_up)

    def piece_at(ref, a, r):
        return ref.at[a, pl.ds(r * piece, piece), :]

    def piece_near(a, r):
        return remote(
            stages[a].at[stage_rows(1 - core, r), :], piece_at(part_got, a, r),
            p_near_send.at[a, r], p_near_recv.at[a, r], core_dev,
        )

    def piece_far(a, r):
        return remote(
            stages[a].at[stage_rows(core, r), :], piece_at(part_far, a, r),
            p_far_send.at[a, r], p_far_recv.at[a, r], side_dev,
        )

    def piece_store(a, r):
        return pltpu.make_async_copy(
            piece_at(part_got, a, r), dw_both.at[a, stage_rows(core, r), :], store_sem.at[1 + 2 * a + r]
        )

    def piece_out(a, r):
        return remote(
            piece_at(part_got, a, r), dw_both.at[a, stage_rows(core, r), :],
            p_out_send.at[a, r], p_out_recv.at[a, r], core_dev,
        )

    def pieces(mine, r):
        at = stage_rows(core if mine else 1 - core, r)
        some = rows[:, at]
        for a, grads in enumerate((grad_gate, grad_up)):
            stages[a][at, :] = outer_sum(some, grads[...]).astype(BF16)
            if not mine:
                piece_near(a, r).start()

    def pieces_sum(r):
        at = stage_rows(core, r)
        for a in range(2):
            piece_near(a, r).wait_recv()
            stages[a][at, :] = (
                stages[a][at, :].astype(F32) + piece_at(part_got, a, r)[...].astype(F32)
            ).astype(BF16)
            piece_far(a, r).start()

    def pieces_total(r):
        for a in range(2):
            piece_far(a, r).wait_recv()
            total = stages[a][stage_rows(core, r), :].astype(F32) + piece_at(part_far, a, r)[
                ...
            ].astype(F32)
            piece_at(part_got, a, r)[...] = total.astype(BF16)
            piece_store(a, r).start()
            piece_out(a, r).start()

    pieces(False, 0)
    pieces(True, 0)
    pieces_sum(0)
    lax.fori_loop(0, outer, turn_outputs, 0)
    chain(0, 0)
    pieces(False, 1)
    pieces(True, 1)
    pieces_sum(1)
    for step in range(1, last):
        chain(0, step)
    grad_two = chain_end(0)

    values = middle_buf[...]
    back, gain_terms = norm_back(values, norm_scales(values), gain_ref[...], grad_two)
    grads = ups[0:quarter, :].astype(F32) + back
    branch[side, core] = grads.astype(BF16)

    def spread_copy(slot, s, device):
        block = branch.at[s, core]
        return remote(block, block, tp_send.at[3 + slot], tp_recv.at[3 + slot], device)

    spread_copy(0, side, side_dev).start()
    spread_copy(1, side, core_dev).start()
    grad_out[...] = grads
    gain_out[...] = jnp.sum(gain_terms, axis=0, keepdims=True)

    for way, exists in ((0, line < last), (1, line > 0)):
        pl.when(exists)(z_copy(way, 0).wait_send)

    def turn_sent(i, carry):
        delta = delta_of(i)
        k = slot_of(delta)
        y_copy(k).wait_send()
        for way, exists in enumerate(goes_on(delta)):
            pl.when(exists)(z_copy(way, k).wait_send)
        return carry

    lax.fori_loop(0, outer, turn_sent, 0)

    def turn_down(c, carry):
        at = aligned(c, chunk)
        stage_down[0:units, at] = outer_sum(inner[...], ups[:, at]).astype(BF16)
        return carry

    chain(1, 0)
    lax.fori_loop(0, outer, turn_down, 0)
    down_store = pltpu.make_async_copy(stage_down.at[pl.ds(0, units), :], dw_down, store_sem.at[0])
    down_store.start()
    for step in range(1, last):
        chain(1, step)
    spread_copy(0, side, side_dev).wait_recv()
    spread_copy(2, 1 - side, core_dev).start()
    pieces_total(0)
    layer_out[...] = (middle_buf[...] + chain_end(1)).astype(BF16)
    pieces_total(1)
    spread_copy(1, side, core_dev).wait_recv()

    down_store.wait()
    far_copy().wait_send()
    for index in range(LATE_BLOCKS):
        late_copy(index).wait_send()

    def turn_drain(i, carry):
        k = slot_of(delta_of(i))
        for which in range(2):
            y_sum(which, k).wait_send()
        pl.when(i > 0)(z_sum(1, 0, k).wait_send)
        return carry

    lax.fori_loop(0, outer, turn_drain, 0)
    for a in range(2):
        for r in range(2):
            piece_near(a, r).wait_send()
            piece_far(a, r).wait_send()
            piece_store(a, r).wait()
            piece_out(a, r).wait()
    spread_copy(0, side, side_dev).wait_send()
    spread_copy(1, side, core_dev).wait_send()
    spread_copy(2, 1 - side, core_dev).wait()


def middle_layer(gated, out_proj, hidden, gain, w_gate, w_up, w_down, ups, outer, sides):
    quarter, model = hidden.shape
    units = w_down.shape[0]
    rows_n = 2 * outer * quarter
    vmem = pl.BlockSpec(memory_space=pltpu.VMEM)
    anywhere = pl.BlockSpec(memory_space=pl.ANY)
    dma = pltpu.SemaphoreType.DMA
    line_rows = outer * quarter
    half = (2, model // 2, units)
    return pl.pallas_call(
        functools.partial(middle_kernel, outer),
        out_shape=[
            jax.ShapeDtypeStruct((quarter, model), BF16),
            jax.ShapeDtypeStruct((quarter, model), F32),
            jax.ShapeDtypeStruct((1, model), F32),
            jax.ShapeDtypeStruct((sides, 2, quarter, model), BF16),
            jax.ShapeDtypeStruct((2, model, units), BF16),
            jax.ShapeDtypeStruct((units, model), BF16),
        ],
        in_specs=[vmem] * 4 + [anywhere] * (3 + len(ups)),
        out_specs=[vmem] * 4 + [anywhere] * 2,
        scratch_shapes=[
            pltpu.VMEM((model, units), BF16),
            pltpu.VMEM((model, units), BF16),
            pltpu.VMEM((units, model), BF16),
            pltpu.VMEM((rows_n, model), BF16),
            pltpu.VMEM((rows_n, model), BF16),
            pltpu.VMEM((rows_n, units), BF16),
            pltpu.VMEM((rows_n, units), BF16),
            pltpu.VMEM((rows_n, units), BF16),
            pltpu.VMEM((4, quarter, model), BF16),
            pltpu.VMEM((quarter, model), BF16),
            pltpu.VMEM((quarter, model), BF16),
            pltpu.VMEM((quarter, model), F32),
            pltpu.VMEM((line_rows, model), BF16),
            pltpu.VMEM((line_rows, model), BF16),
            pltpu.VMEM((2 * line_rows, model), BF16),
            pltpu.VMEM((line_rows, model), BF16),
            pltpu.VMEM((4 * line_rows, model), BF16),
            pltpu.VMEM(half, BF16),
            pltpu.VMEM(half, BF16),
            dma((3 + len(ups),)),
            dma((5,)),
            dma((6,)),
            dma((6,)),
            dma((2, outer)),
            dma((outer,)),
            dma((outer,)),
            dma((outer,)),
            dma((2, outer)),
            dma((2, outer)),
            dma((2, outer)),
            dma((2, 2, outer)),
        ]
        + [dma((2, 2))] * 6
        + [dma((LATE_BLOCKS,))] * 2,
        compiler_params=pltpu.CompilerParams(
            collective_id=2, has_side_effects=True, vmem_limit_bytes=63 * 1024 * 1024
        ),
        cost_estimate=pl.CostEstimate(flops=3 * 10**10, bytes_accessed=4 * 10**7, transcendentals=0),
        name="middle",
    )(gated, out_proj, hidden, gain, w_gate, w_up, w_down, *ups)


FFN_CHUNKS = 2


def finish_kernel(
    outer, sides, sp_n, tp_n, streams, width_scale,
    *refs,
):
    MESH = pl.DeviceIdType.MESH
    parts = refs[:streams]
    (part_ref, hidden_ref, scale_ref, gain_ref, middle_ref, sums_ref) = refs[streams : streams + 6]
    last_in, layer_ref = refs[streams + 6 : streams + 8]
    outs = refs[streams + 8 : 2 * streams + 8]
    grad_out, sums_out, last_out, layer_out = refs[2 * streams + 8 : 2 * streams + 12]
    rest = refs[2 * streams + 12 :]
    got = rest[:streams]
    staged = rest[streams : 2 * streams]
    (near_got, far_got, keep_buf, far_stage, sums_got, sums_stage) = rest[2 * streams : 2 * streams + 6]
    rest = rest[2 * streams + 6 :]
    (last_keep, last_got, last_far, layer_send, layer_recv) = rest[:5]
    (f_load, f_near_send, f_near_recv, f_far_send, f_far_recv, f_store, f_out_send, f_out_recv) = rest[5:13]
    (reduce_send, reduce_recv, gather_send, gather_recv, pair_send, pair_recv) = rest[13:19]
    tp_send, tp_recv, sums_send, sums_recv = rest[19:]

    sp_i = lax.axis_index("sp")
    tp_i = lax.axis_index("tp")
    line = sp_i // 2
    half = sp_i % 2
    side = tp_i // 2
    core = tp_i % 2
    last = outer - 1

    def sp_at(z, y):
        return (tp_i, z * 2 + y)

    pair_dev = sp_at(line, 1 - half)
    core_dev = (side * 2 + (1 - core), sp_i)
    side_dev = ((1 - side) * 2 + core, sp_i)

    tp_bits = []
    bit = 1
    while bit < tp_n:
        tp_bits.append(bit)
        bit *= 2
    sp_bits = []
    bit = 1
    while bit < sp_n:
        sp_bits.append(bit)
        bit *= 2

    def flip(value, bit):
        return value + bit - 2 * bit * ((value // bit) % 2)

    sum_devs = [(flip(tp_i, b), sp_i) for b in tp_bits] + [(tp_i, flip(sp_i, b)) for b in sp_bits]

    barrier = pltpu.get_barrier_semaphore()
    greeted = [sp_at((line + 1) % outer, half), sp_at((line + outer - 1) % outer, half)] + sum_devs
    for device in greeted:
        pl.semaphore_signal(barrier, inc=1, device_id=device, device_id_type=MESH)
    pl.semaphore_wait(barrier, len(greeted))

    def remote(src, dst, send, recv, device):
        return pltpu.make_async_remote_copy(
            src_ref=src, dst_ref=dst, send_sem=send, recv_sem=recv,
            device_id=device, device_id_type=MESH,
        )

    places = (line, last - line)
    nexts = (sp_at(jnp.minimum(line + 1, last), half), sp_at(jnp.maximum(line - 1, 0), half))
    signs = (1, -1)

    def rows_of(stream, index):
        count = parts[stream].shape[0] // outer
        return pl.ds(pl.multiple_of(index * count, count), count)

    def reduce_copy(stream, way, step, src):
        return remote(
            src, got[stream].at[way, step - 1], reduce_send.at[stream, way, step - 1],
            reduce_recv.at[stream, way, step - 1], nexts[way],
        )

    def clamp(index):
        return jnp.clip(index, 0, last)

    def reduce_step(stream, step):
        for way in range(2):
            place, sign = places[way], signs[way]
            target = clamp(line + sign * (outer - step))
            own = parts[stream].at[rows_of(stream, target), :]

            @pl.when(place == 0)
            def _():
                reduce_copy(stream, way, step, own).start()

            if step > 1:

                @pl.when((place > 0) & (place <= step - 1))
                def _():
                    reduce_copy(stream, way, step - 1, own).wait_recv()
                    stage = staged[stream].at[way, step - 2]
                    stage[...] = (
                        got[stream][way, step - 2].astype(F32) + own[...].astype(F32)
                    ).astype(BF16)
                    reduce_copy(stream, way, step, stage).start()

    def gather_copy(stream, way, step, origin):
        block = outs[stream].at[half, rows_of(stream, origin), :]
        return remote(
            block, block, gather_send.at[stream, way, step - 1],
            gather_recv.at[stream, way, step - 1], nexts[way],
        )

    def pair_copy(stream, slot, origin):
        block = outs[stream].at[half, rows_of(stream, origin), :]
        return remote(block, block, pair_send.at[stream, slot], pair_recv.at[stream, slot], pair_dev)

    def reduce_final(stream):
        own = parts[stream].at[rows_of(stream, line), :]
        block = outs[stream].at[half, rows_of(stream, line), :]
        for way in range(2):

            @pl.when(places[way] > 0)
            def _():
                reduce_copy(stream, way, last, own).wait_recv()

        up = jnp.where(line > 0, got[stream][0, last - 1].astype(F32), 0.0)
        down = jnp.where(line < last, got[stream][1, last - 1].astype(F32), 0.0)
        block[...] = (own[...].astype(F32) + up + down).astype(BF16)
        for way in range(2):

            @pl.when(places[way] < last)
            def _():
                gather_copy(stream, way, 1, line).start()

        pair_copy(stream, 0, line).start()

    def gather_step(stream, step):
        for way in range(2):
            place, sign = places[way], signs[way]
            origin = clamp(line - sign * step)

            @pl.when(place >= step)
            def _():
                gather_copy(stream, way, step, origin).wait_recv()
                if step < last:

                    @pl.when(place < last)
                    def _():
                        gather_copy(stream, way, step + 1, origin).start()

                pair_copy(stream, 1 + way * last + step - 1, origin).start()

    def drain(stream):
        pair_copy(stream, 0, line).wait()
        for way in range(2):
            place, sign = places[way], signs[way]
            for step in range(1, outer):
                origin = clamp(line - sign * step)

                @pl.when(place <= step - 1)
                def _():
                    reduce_copy(stream, way, step, parts[stream].at[rows_of(stream, 0), :]).wait_send()

                @pl.when((place >= step - 1) & (place < last))
                def _():
                    gather_copy(stream, way, step, origin).wait_send()

                @pl.when(place >= step)
                def _():
                    pair_copy(stream, 1 + way * last + step - 1, origin).wait()

    def near_copy(index):
        return remote(
            part_ref.at[index, 1 - core], near_got.at[index], tp_send.at[index], tp_recv.at[index],
            core_dev,
        )

    def far_copy():
        return remote(far_stage, far_got, tp_send.at[sides], tp_recv.at[sides], side_dev)

    def spread_copy(slot, s, device):
        block = grad_out.at[s, core]
        return remote(block, block, tp_send.at[sides + slot], tp_recv.at[sides + slot], device)

    def input_step(step):
        if step == 0:
            for index in range(sides):
                near_copy(index).start()
        if step == 1:
            for index in range(sides):
                near_copy(index).wait_recv()
            keep_buf[...] = part_ref[side, core].astype(F32) + near_got[side].astype(F32)
            far_stage[...] = (
                part_ref[1 - side, core].astype(F32) + near_got[1 - side].astype(F32)
            ).astype(BF16)
            far_copy().start()
        if step == 2:
            far_copy().wait_recv()
            incoming = keep_buf[...] + far_got[...].astype(F32)
            values = hidden_ref[...].astype(F32)
            scales = scale_ref[...]
            weighted = incoming * gain_ref[...]
            inner_sum = jnp.sum(weighted * values, axis=-1, keepdims=True)
            grads = scales * weighted - values * (scales * scales * scales) * inner_sum * width_scale
            grad_out[side, core] = (middle_ref[...] + grads).astype(BF16)
            spread_copy(1, side, side_dev).start()
            spread_copy(2, side, core_dev).start()
        if step == 3:
            spread_copy(1, side, side_dev).wait_recv()
            spread_copy(3, 1 - side, core_dev).start()
        if step == 4:
            spread_copy(2, side, core_dev).wait_recv()
            spread_copy(3, 1 - side, core_dev).wait_recv()
            for index in range(sides):
                near_copy(index).wait_send()
            far_copy().wait_send()
            spread_copy(1, side, side_dev).wait_send()
            spread_copy(2, side, core_dev).wait_send()
            spread_copy(3, 1 - side, core_dev).wait_send()

    last_half = last_keep.shape[0]

    def ffn_at(j, ref, whole, owner):
        count = last_half // FFN_CHUNKS
        start = j * count
        if whole:
            start = pl.multiple_of(owner * last_half + start, count)
        return ref.at[pl.ds(start, count), :]

    def ffn_keep(j):
        return ffn_at(j, last_keep, False, 0)

    def ffn_got(j):
        return ffn_at(j, last_got, False, 0)

    def ffn_far(j):
        return ffn_at(j, last_far, False, 0)

    def ffn_load(j):
        return pltpu.make_async_copy(ffn_at(j, last_in, True, core), ffn_keep(j), f_load.at[j])

    def ffn_near_copy(j):
        return remote(
            ffn_at(j, last_in, True, 1 - core), ffn_got(j), f_near_send.at[j], f_near_recv.at[j], core_dev
        )

    def ffn_far_copy(j):
        return remote(ffn_keep(j), ffn_far(j), f_far_send.at[j], f_far_recv.at[j], side_dev)

    def ffn_store(j):
        return pltpu.make_async_copy(ffn_got(j), ffn_at(j, last_out, True, core), f_store.at[j])

    def ffn_out_copy(j):
        return remote(
            ffn_got(j), ffn_at(j, last_out, True, core), f_out_send.at[j], f_out_recv.at[j], core_dev
        )

    def ffn_sum(j):
        ffn_load(j).wait()
        ffn_near_copy(j).wait_recv()
        keep = ffn_keep(j)
        keep[...] = (keep[...].astype(F32) + ffn_got(j)[...].astype(F32)).astype(BF16)
        ffn_far_copy(j).start()

    def ffn_total(j):
        ffn_far_copy(j).wait_recv()
        total = ffn_keep(j)[...].astype(F32) + ffn_far(j)[...].astype(F32)
        ffn_got(j)[...] = total.astype(BF16)
        ffn_store(j).start()
        ffn_out_copy(j).start()

    def ffn_drain(j):
        ffn_near_copy(j).wait_send()
        ffn_far_copy(j).wait_send()
        ffn_store(j).wait()
        ffn_out_copy(j).wait()

    rounds = len(sum_devs)

    def sums_copy(step):
        src = sums_ref if step == 0 else sums_stage.at[step - 1]
        return remote(
            src, sums_got.at[step], sums_send.at[step], sums_recv.at[step], sum_devs[step]
        )

    def sums_step(step):
        if step > 0:
            sums_copy(step - 1).wait_recv()
            before = sums_ref[...] if step == 1 else sums_stage[step - 2]
            total = before + sums_got[step - 1]
            if step == rounds:
                sums_out[...] = total
            else:
                sums_stage[step - 1] = total
        if step < rounds:
            sums_copy(step).start()
        if step == rounds:
            for index in range(rounds):
                sums_copy(index).wait_send()

    def later(do, *args):
        return functools.partial(do, *args)

    def layer_copy(slot, s, device):
        block = layer_out.at[s, core]
        src = block if slot == 2 else layer_ref
        return remote(src, block, layer_send.at[slot], layer_recv.at[slot], device)

    def layer_own():
        return pltpu.make_async_copy(layer_ref, layer_out.at[side, core], layer_send.at[3])

    def layer_step(step):
        if step == 0:
            layer_copy(0, side, side_dev).start()
            layer_copy(1, side, core_dev).start()
            layer_own().start()
        if step == 1:
            layer_copy(0, 1 - side, side_dev).wait_recv()
            layer_copy(2, 1 - side, core_dev).start()
        if step == 2:
            layer_copy(1, side, core_dev).wait_recv()
            layer_own().wait()
            layer_copy(0, side, side_dev).wait_send()
            layer_copy(1, side, core_dev).wait_send()
            layer_copy(2, 1 - side, core_dev).wait()

    extra = [
        later(input_step, 0), later(sums_step, 0), later(input_step, 1), later(layer_step, 0),
        later(ffn_sum, 0), later(ffn_sum, 1), later(lambda: None), later(lambda: None), later(input_step, 2),
        later(sums_step, 1), later(lambda: None), later(sums_step, 2), later(lambda: None), later(sums_step, 3),
        later(layer_step, 1), later(lambda: None), later(sums_step, 4), later(input_step, 3),
        later(lambda: None), later(sums_step, 5), later(ffn_total, 0), later(ffn_total, 1),
        later(layer_step, 2), later(input_step, 4),
    ]
    extra += [later(sums_step, index) for index in range(6, rounds + 1)]
    for index in range(FFN_CHUNKS):
        ffn_near_copy(index).start()
        ffn_load(index).start()
    for turn in range(streams + 1):
        for step in range(1, outer + 1):
            if turn < streams:
                if step < outer:
                    reduce_step(turn, step)
                else:
                    reduce_final(turn)
            if turn > 0 and step < outer:
                gather_step(turn - 1, step)
            if extra:
                extra.pop(0)()
    for step in extra:
        step()
    for stream in range(streams):
        drain(stream)
    for index in range(FFN_CHUNKS):
        ffn_drain(index)


def finish(parts, part, hidden, scales, gain, middle, sums, ffn_last, layer, outer, sp_n, tp_n):
    streams = len(parts)
    sides = tp_n // 2
    quarter, model = hidden.shape
    last = outer - 1
    rounds = (tp_n - 1).bit_length() + (sp_n - 1).bit_length()
    vmem = pl.BlockSpec(memory_space=pltpu.VMEM)
    anywhere = pl.BlockSpec(memory_space=pl.ANY)
    chunk = [(2, last, p.shape[0] // outer, p.shape[1]) for p in parts]
    dma = pltpu.SemaphoreType.DMA
    return pl.pallas_call(
        functools.partial(finish_kernel, outer, sides, sp_n, tp_n, streams, 1.0 / model),
        out_shape=[jax.ShapeDtypeStruct((2,) + p.shape, BF16) for p in parts]
        + [
            jax.ShapeDtypeStruct((sides, 2, quarter, model), BF16),
            jax.ShapeDtypeStruct(sums.shape, F32),
        ]
        + [
            jax.ShapeDtypeStruct(ffn_last.shape, BF16),
            jax.ShapeDtypeStruct((sides, 2, quarter, model), BF16),
        ],
        in_specs=[vmem] * (streams + 6) + [anywhere, vmem],
        out_specs=[vmem] * (streams + 2) + [anywhere, vmem],
        scratch_shapes=[pltpu.VMEM(c, BF16) for c in chunk]
        + [pltpu.VMEM(c, BF16) for c in chunk]
        + [
            pltpu.VMEM((sides, quarter, model), BF16),
            pltpu.VMEM((quarter, model), BF16),
            pltpu.VMEM((quarter, model), F32),
            pltpu.VMEM((quarter, model), BF16),
            pltpu.VMEM((rounds,) + sums.shape, F32),
            pltpu.VMEM((rounds,) + sums.shape, F32),
        ]
        + [pltpu.VMEM((ffn_last.shape[0] // 2, ffn_last.shape[1]), BF16)] * 3
        + [dma((4,))] * 2
        + [dma((FFN_CHUNKS,))] * 8
        + [dma((streams, 2, last))] * 4
        + [dma((streams, 1 + 2 * last))] * 2
        + [dma((sides + 4,))] * 2
        + [dma((rounds,))] * 2,
        compiler_params=pltpu.CompilerParams(
            collective_id=1, has_side_effects=True, vmem_limit_bytes=60 * 1024 * 1024
        ),
        cost_estimate=pl.CostEstimate(flops=10**9, bytes_accessed=10**8, transcendentals=0),
        name="finish",
    )(*parts, part, hidden, scales, gain, middle, sums, ffn_last, layer)


def body(
    hidden,
    segment_ids,
    attn_norm,
    query_proj,
    key_proj,
    value_proj,
    gate_proj,
    output_proj,
    query_norm,
    key_norm,
    ffn_norm,
    ffn_gate,
    ffn_up,
    ffn_down,
    upstream,
):
    rows_dev, model = hidden.shape
    head_width = query_norm.shape[0]
    heads = query_proj.shape[1] // head_width
    groups = key_proj.shape[1] // head_width
    per_group = heads // groups
    group_width = groups * head_width
    sp_n = lax.axis_size("sp")
    tp_n = lax.axis_size("tp")
    outer = sp_n // 2
    sides = tp_n // 2
    quarter = rows_dev // tp_n
    tp_i = lax.axis_index("tp")
    sp_i = lax.axis_index("sp")
    ring_i = sp_i // 2
    pair_i = sp_i % 2
    side_i = tp_i // 2
    core_i = tp_i % 2
    own_first = sp_i * rows_dev
    quarter_first = tp_i * quarter
    scale = 1.0 / math.sqrt(head_width)

    ring_pairs = [(z * 2 + y, ((z + 1) % outer) * 2 + y) for z in range(outer) for y in range(2)]
    pair_pairs = [(i, i ^ 1) for i in range(sp_n)]
    side_pairs = [(i, i ^ 2) for i in range(tp_n)]
    core_pairs = [(i, i ^ 1) for i in range(tp_n)]

    def ring(value):
        return lax.ppermute(value, "sp", ring_pairs)

    def far(value, step):
        pairs = [(z * 2 + y, ((z + step) % outer) * 2 + y) for z in range(outer) for y in range(2)]
        return lax.ppermute(value, "sp", pairs)

    def pair(value):
        return lax.ppermute(value, "sp", pair_pairs)

    def side(value):
        return lax.ppermute(value, "tp", side_pairs)

    def core(value):
        return lax.ppermute(value, "tp", core_pairs)

    def gather_sp(block, paired):
        blocks = []
        first = block
        for k in range(outer):
            blocks.append((block, pair(block)) if k < paired else (block,))
            if k < outer - 1:
                block = ring(block) if paired == outer else far(first, k + 1)
        return blocks

    def scatter_sp(parts):
        def paired(k):
            return parts[k][0] + pair(parts[k][1].astype(BF16)).astype(F32)

        total = paired(1 % outer)
        for k in range(2, outer + 1):
            total = ring(total.astype(BF16)).astype(F32) + paired(k % outer)
        return total

    first_id = segment_ids[0]
    second_start = jnp.sum((segment_ids == first_id).astype(jnp.int32))
    own_index = own_first + jnp.arange(rows_dev, dtype=jnp.int32)
    own_starts = jnp.where(own_index < second_start, 0, second_start)
    steps_half = jnp.arange(head_width // 2, dtype=F32)
    frequencies = jnp.exp(steps_half * (-2.0 * math.log(THETA) / head_width))
    angles = (own_index - own_starts).astype(F32)[:, None] * frequencies[None, :]
    cosine = jnp.cos(angles)[:, None, :]
    sine = jnp.sin(angles)[:, None, :]

    hidden_full = hidden.astype(F32)
    normed_full, attn_scales = norm_rows(hidden_full, attn_norm)
    normed = normed_full.astype(BF16)
    key_raw = matmul(normed, key_proj).reshape(rows_dev, groups, head_width)
    value_rows = matmul(normed, value_proj).astype(BF16)
    key_normed, key_scales = norm_rows(key_raw, key_norm)
    key_rot = rotary(key_normed, cosine, sine).astype(BF16).reshape(rows_dev, group_width)
    kv_own = jnp.stack([key_rot, value_rows])

    low, high = (outer // 4, 3 * outer // 4) if outer % 4 == 0 else (0, outer)
    reach = high - 1 if low else outer - 1

    def up_pairs(step):
        return [
            (z * 2 + y, (z + 1) * 2 + y)
            for z in range(outer - 1)
            for y in range(2)
            if z + 1 - step >= 0 and (z + 1 - step >= low or z + 1 < high)
        ]

    def far_pairs(step):
        return [
            (z * 2 + y, (z + step) * 2 + y)
            for z in range(outer - step)
            for y in range(2)
            if z >= low or z + step < high
        ]

    kv_blocks = []
    travelling = kv_own
    for k in range(reach + 1):
        if k > 0 and reach <= 2:
            travelling = lax.ppermute(kv_own, "sp", far_pairs(k))
        elif k > 0:
            travelling = lax.ppermute(travelling, "sp", up_pairs(k))
        kv_blocks.append((travelling, pair(travelling)))

    query_raw = matmul(normed, query_proj).reshape(rows_dev, heads, head_width)
    gate_raw = matmul(normed, gate_proj)
    query_normed, query_scales = norm_rows(query_raw, query_norm)
    queries = rotary(query_normed, cosine, sine).astype(BF16).reshape(rows_dev, heads * head_width)

    def swap_half(value):
        piece = model // 4
        mine = pair(lax.dynamic_slice_in_dim(value, ((1 - pair_i) * 2 + core_i) * piece, piece, 1))
        near = core(mine)
        return jnp.where(
            core_i == 1, jnp.concatenate([near, mine], 1), jnp.concatenate([mine, near], 1)
        )

    normed_own = lax.dynamic_slice_in_dim(normed, pair_i * (model // 2), model // 2, 1)
    both_normed = jnp.concatenate([normed_own, swap_half(normed)])

    grad_quarter = lax.dynamic_slice_in_dim(upstream, quarter_first, quarter)
    fused = 2 < outer and outer * quarter <= 512 and tp_n == 4
    up_blocks = gather_sp(grad_quarter, outer - LATE_BLOCKS if fused else outer)

    row_start_low = own_starts[0]
    row_start_high = own_starts[-1]

    def block_info(k):
        shards = [(ring_i - k) * 2 + pair_i, (ring_i - k) * 2 + (1 - pair_i)]
        entries = [own_first] + [shard * rows_dev for shard in shards]
        live = []
        full = []
        for shard in shards:
            token = shard * rows_dev
            live.append((shard >= 0) & (shard <= sp_i) & (token + rows_dev - 1 >= row_start_low))
            full.append((token >= row_start_high) & (shard < sp_i))
        return jnp.stack(entries + [v.astype(jnp.int32) for v in live + full]).astype(jnp.int32)

    infos = [block_info(k) for k in range(reach + 1)]
    starts_column = own_starts[:, None]
    starts_row = own_starts[None, :]
    carried = None
    for k in range(reach + 1):
        if fused and k == reach:
            carried, up_blocks = lax.optimization_barrier((carried, up_blocks))
        carried = attn_forward(
            infos[k], starts_column, queries, kv_blocks[k][0], kv_blocks[k][1], carried, scale
        )
    mix_acc, mix_sum = carried
    mixed = mix_acc / mix_sum
    lse = jnp.log2(mix_sum.reshape(rows_dev, heads, head_width)[:, :, 0])
    lse_rows = lse.T.reshape(groups, per_group, rows_dev)
    gate_sig = jax.nn.sigmoid(gate_raw)
    gated = (mixed * gate_sig).astype(BF16)
    gated_other = pair(gated)

    def scatter_tp(part):
        part = part.reshape(sides, 2, quarter, model)
        keep = lax.dynamic_index_in_dim(part, core_i, 1, keepdims=False)
        send = lax.dynamic_index_in_dim(part, 1 - core_i, 1, keepdims=False)
        keep = keep + core(send.astype(BF16)).astype(F32)
        mine = lax.dynamic_index_in_dim(keep, side_i, 0, keepdims=False)
        other = lax.dynamic_index_in_dim(keep, 1 - side_i, 0, keepdims=False)
        return mine + side(other.astype(BF16)).astype(F32)

    def gather_tp(block):
        far = side(block)
        swap_side = side_i == 1
        two = jnp.where(swap_side, jnp.stack([far, block]), jnp.stack([block, far]))
        near = core(two)
        swap_core = core_i == 1
        full = jnp.where(
            swap_core, jnp.stack([near, two], axis=1), jnp.stack([two, near], axis=1)
        )
        return full.reshape((rows_dev,) + block.shape[1:])

    if fused:
        layer_quarter, grad_middle_quarter, ffn_gain_sum, branch, *ffn_parts = middle_layer(
            gated,
            output_proj,
            lax.dynamic_slice_in_dim(hidden, quarter_first, quarter),
            ffn_norm[None, :],
            ffn_gate,
            ffn_up,
            ffn_down,
            [block for both in up_blocks for block in both],
            outer,
            sides,
        )
        grad_branch = branch.reshape(rows_dev, model)
        ffn_gain_sum = ffn_gain_sum[0]
    else:
        attn_quarter = scatter_tp(matmul(gated, output_proj))
        hidden_quarter = lax.dynamic_slice_in_dim(hidden, quarter_first, quarter).astype(F32)
        middle = hidden_quarter + attn_quarter
        normed_two_full, ffn_scales = norm_rows(middle, ffn_norm)
        normed_two = normed_two_full.astype(BF16)

        two_blocks = gather_sp(normed_two, outer)
        rows_list, up_list, inner_list, gate_list, grad_up_list = [None] * outer, [None] * outer, [None] * outer, [None] * outer, [None] * outer
        grad_parts = [None] * outer
        for k in list(range(1, outer)) + [0]:
            rows_k = jnp.concatenate(two_blocks[k])
            up_k = jnp.concatenate(up_blocks[k])
            gate_vals = matmul(rows_k, ffn_gate)
            up_vals = matmul(rows_k, ffn_up)
            sig = jax.nn.sigmoid(gate_vals)
            grad_inner = times_transpose(up_k, ffn_down)
            grad_gate = (grad_inner * up_vals * (sig * (1.0 + gate_vals * (1.0 - sig)))).astype(BF16)
            grad_up = (grad_inner * (gate_vals * sig)).astype(BF16)
            inner = (gate_vals * sig * up_vals).astype(BF16)
            grad_parts[k] = (
                times_transpose(grad_gate, ffn_gate) + times_transpose(grad_up, ffn_up)
            ).reshape(2, quarter, model)
            rows_list[k], up_list[k], inner_list[k] = rows_k, up_k, inner
            gate_list[k], grad_up_list[k] = grad_gate, grad_up
        grad_two = scatter_sp(grad_parts)

        norm_grad_two, ffn_gain_terms = norm_back(middle, ffn_scales, ffn_norm, grad_two)
        grad_middle_quarter = grad_quarter.astype(F32) + norm_grad_two
        grad_branch = gather_tp(grad_middle_quarter.astype(BF16))
        ffn_gain_sum = jnp.sum(ffn_gain_terms, axis=0)
        mlp_parts = [
            matmul(inner_list[k], ffn_down).reshape(2, quarter, model) for k in range(outer)
        ]
        layer_quarter = (middle + scatter_sp(mlp_parts)).astype(BF16)

    def sum_tp(part):
        total = part.astype(BF16).astype(F32)
        total = total + core(total.astype(BF16)).astype(F32)
        low = total.astype(BF16)
        return (low.astype(F32) + side(low).astype(F32)).astype(BF16)

    if not fused:
        rows_all = jnp.concatenate(rows_list)
        up_all = jnp.concatenate(up_list)
        inner_all = jnp.concatenate(inner_list)
        gate_all = jnp.concatenate(gate_list)
        grad_up_all = jnp.concatenate(grad_up_list)
        ffn_parts = [
            jnp.stack([outer_sum(rows_all, gate_all), outer_sum(rows_all, grad_up_all)]),
            outer_sum(inner_all, up_all),
        ]
        ffn_parts = [sum_tp(ffn_parts[0]), ffn_parts[1].astype(BF16)]
    ffn_both, ffn_last = ffn_parts

    branch_other = swap_half(grad_branch)
    branch_own = lax.dynamic_slice_in_dim(grad_branch, pair_i * (model // 2), model // 2, 1)
    grad_gated = times_transpose(grad_branch, output_proj)
    grad_mixed = (grad_gated * gate_sig).astype(BF16)
    grad_gate_raw = (grad_gated * mixed * (gate_sig * (1.0 - gate_sig))).astype(BF16)
    gate_other = pair(grad_gate_raw)
    deltas = jnp.sum(
        (grad_mixed.astype(F32) * mixed).reshape(rows_dev, heads, head_width), axis=-1
    )
    delta_rows = deltas.T.reshape(groups, per_group, rows_dev)

    def down_pairs(step):
        return [(b, a) for a, b in up_pairs(step)]

    query_acc = None
    travelling = None
    paired = {}
    for k in list(range(reach, -1, -1)):
        if k + 2 in paired:
            query_acc, paired[k + 2] = lax.optimization_barrier((query_acc, paired[k + 2]))
        query_acc, grad_a, grad_b = attn_backward(
            infos[k], starts_row, lse_rows, delta_rows, queries, grad_mixed,
            kv_blocks[k][0], kv_blocks[k][1], query_acc, k == 0, scale,
        )
        if k == reach:
            query_acc, grad_a, grad_b, gated_other, branch_other, gate_other = lax.optimization_barrier(
                (query_acc, grad_a, grad_b, gated_other, branch_other, gate_other)
            )
        paired[k] = pair(grad_b)
        total = grad_a.astype(F32) + paired[k].astype(F32)
        if travelling is not None:
            total = total + travelling.astype(F32)
        if k > 0:
            travelling = lax.ppermute(total.astype(BF16), "sp", down_pairs(k))
    output_half = outer_sum(
        jnp.concatenate([gated, gated_other]), jnp.concatenate([branch_own, branch_other])
    )
    gate_half = outer_sum(both_normed, jnp.concatenate([grad_gate_raw, gate_other]))
    grad_key_rot = total[0].reshape(rows_dev, groups, head_width)
    grad_value_low = total[1].astype(BF16)
    grad_query_rot = (query_acc * scale).reshape(rows_dev, heads, head_width)
    grad_query_raw, query_gain_terms = norm_back(
        query_raw, query_scales, query_norm, rotary_back(grad_query_rot, cosine, sine)
    )
    grad_key_raw, key_gain_terms = norm_back(
        key_raw, key_scales, key_norm, rotary_back(grad_key_rot, cosine, sine)
    )
    grad_query_low = grad_query_raw.reshape(rows_dev, heads * head_width).astype(BF16)
    grad_key_low = grad_key_raw.reshape(rows_dev, group_width).astype(BF16)
    grad_kv_low = jnp.concatenate([grad_key_low, grad_value_low], axis=1)
    grad_kv_low, ffn_both = lax.optimization_barrier((grad_kv_low, ffn_both))
    ffn_gate_grad, ffn_up_grad = ffn_both[0].astype(F32), ffn_both[1].astype(F32)

    both_queries = jnp.concatenate([grad_query_low, pair(grad_query_low)])
    both_kv = jnp.concatenate([grad_kv_low, pair(grad_kv_low)])
    parts = [
        output_half.astype(BF16),
        gate_half.astype(BF16),
        outer_sum(both_normed, both_queries).astype(BF16),
        outer_sum(both_normed, both_kv).astype(BF16),
    ]

    grad_normed_part = (
        times_transpose(grad_query_low, query_proj)
        + times_transpose(grad_key_low, key_proj)
        + times_transpose(grad_value_low, value_proj)
        + times_transpose(grad_gate_raw, gate_proj)
    )
    gains = jnp.concatenate(
        [
            jnp.sum(grad_normed_part * hidden_full * attn_scales, axis=0),
            ffn_gain_sum,
            jnp.sum(query_gain_terms, axis=(0, 1)),
            jnp.sum(key_gain_terms, axis=(0, 1)),
        ]
    )
    gains, ffn_gate_grad, ffn_up_grad = lax.optimization_barrier((gains, ffn_gate_grad, ffn_up_grad))
    gains_at = 2 * model + 2 * head_width
    gains = jnp.pad(gains, (0, -gains_at % 1024)).reshape(-1, 128)
    scales_quarter = lax.dynamic_slice_in_dim(attn_scales, quarter_first, quarter)
    finished = finish(
        parts,
        grad_normed_part.astype(BF16).reshape(sides, 2, quarter, model),
        lax.dynamic_slice_in_dim(hidden, quarter_first, quarter),
        scales_quarter,
        attn_norm[None, :],
        grad_middle_quarter,
        gains,
        ffn_last,
        layer_quarter,
        outer,
        sp_n,
        tp_n,
    )
    output_all, gate_all_w, query_all, kv_all, input_all, gains, ffn_last, layer_all = finished
    output_grad = jnp.concatenate([output_all[0], output_all[1]], axis=1).astype(F32)
    gate_grad = gate_all_w.reshape(model, heads * head_width).astype(F32)
    query_grad = query_all.reshape(model, heads * head_width).astype(F32)
    kv_all = kv_all.reshape(model, 2 * group_width)
    key_grad = kv_all[:, :group_width].astype(F32)
    value_grad = kv_all[:, group_width:].astype(F32)
    hidden_grad = input_all.reshape(rows_dev, model).astype(F32)
    gains = gains.reshape(-1)
    return (
        layer_all.reshape(rows_dev, model),
        hidden_grad,
        gains[:model],
        query_grad,
        key_grad,
        value_grad,
        gate_grad,
        output_grad,
        gains[2 * model : 2 * model + head_width],
        gains[2 * model + head_width : gains_at],
        gains[model : 2 * model],
        ffn_gate_grad,
        ffn_up_grad,
        ffn_last.astype(F32),
    )


def solution(mesh):
    placed = (
        P("sp", None),
        P(),
        P(),
        P(None, "tp"),
        P(None, "tp"),
        P(None, "tp"),
        P(None, "tp"),
        P("tp", None),
        P(),
        P(),
        P(),
        P(None, "sp"),
        P(None, "sp"),
        P("sp", None),
        P("sp", None),
    )
    return jax.shard_map(
        body,
        mesh=mesh,
        in_specs=placed,
        out_specs=(
            P("sp", None),
            P("sp", None),
            P(),
            P(None, "tp"),
            P(None, "tp"),
            P(None, "tp"),
            P(None, "tp"),
            P("tp", None),
            P(),
            P(),
            P(),
            P(None, "sp"),
            P(None, "sp"),
            P("sp", None),
        ),
        check_vma=False,
    )
```

```python
import functools
import math

import jax
import jax.numpy as jnp
from jax import lax
from jax.experimental import pallas as pl
from jax.experimental.pallas import tpu as pltpu
from jax.sharding import PartitionSpec as P

EPSILON = 1e-06
THETA = 1000000.0
LOG2E = 1.4426950408889634
F32 = jnp.float32
BF16 = jnp.bfloat16


def norm_scales(values):
    return lax.rsqrt(jnp.mean(values * values, axis=-1, keepdims=True) + EPSILON)


def norm_rows(values, gain):
    scales = norm_scales(values)
    return (values * scales * gain, scales)


def norm_back(values, scales, gain, incoming):
    weighted = incoming * gain
    inner_sum = jnp.sum(weighted * values, axis=-1, keepdims=True)
    grad_values = (
        scales * weighted - values * (scales * scales * scales) * inner_sum / values.shape[-1]
    )
    return (grad_values, incoming * values * scales)


def rotary(values, cosine, sine):
    half_width = values.shape[-1] // 2
    front_half = values[..., :half_width]
    back_half = values[..., half_width:]
    return jnp.concatenate(
        [front_half * cosine - back_half * sine, back_half * cosine + front_half * sine], axis=-1
    )


def rotary_back(grads, cosine, sine):
    half_width = grads.shape[-1] // 2
    front_half = grads[..., :half_width]
    back_half = grads[..., half_width:]
    return jnp.concatenate(
        [front_half * cosine + back_half * sine, back_half * cosine - front_half * sine], axis=-1
    )


def matmul(left, right):
    return jnp.dot(left, right, preferred_element_type=F32)


def outer_sum(left, right):
    return lax.dot_general(left, right, (((0,), (0,)), ((), ())), preferred_element_type=F32)


def times_transpose(left, right):
    return lax.dot_general(left, right, (((1,), (1,)), ((), ())), preferred_element_type=F32)


def attn_forward_kernel(first, diagonal, scale, info, starts, queries, kv_a, kv_b, *rest):
    if first:
        acc_out, sum_out = rest
    else:
        acc_in, sum_in, acc_out, sum_out = rest
    rows = queries.shape[0]
    keys_n = kv_a.shape[1]
    per_group = queries.shape[1] // kv_a.shape[2]
    width = kv_a.shape[2]
    if first:
        acc_out[...] = jnp.zeros_like(acc_out)
        sum_out[...] = jnp.zeros_like(sum_out)
    else:
        acc_out[...] = acc_in[...]
        sum_out[...] = sum_in[...]
    own_first = info[0]
    for slot, block in enumerate((kv_a, kv_b)):
        key_first = info[1 + slot]
        live = info[3 + slot] > 0

        def work(masked, causal):
            ones = jnp.ones((keys_n, width), BF16)
            values = jnp.concatenate([block[1], ones], axis=1)
            keys = block[0]
            if masked:
                key_index = key_first + lax.broadcasted_iota(jnp.int32, (rows, keys_n), 1)
                allowed = key_index >= starts[...]
                if causal:
                    row_index = own_first + lax.broadcasted_iota(jnp.int32, (rows, keys_n), 0)
                    allowed = allowed & (key_index <= row_index)
            for head in range(per_group):
                cols = slice(head * width, (head + 1) * width)
                scores = times_transpose(queries[:, cols], keys)
                weights = jnp.exp2(scores * (scale * LOG2E))
                if masked:
                    weights = jnp.where(allowed, weights, 0.0)
                both = matmul(weights.astype(BF16), values)
                acc_out[:, cols] += both[:, :width]
                sum_out[:, cols] += both[:, width:]

        if diagonal and slot == 0:
            work(True, True)
        else:
            full = info[5 + slot] > 0
            pl.when(live & full)(functools.partial(work, False, False))
            pl.when(live & jnp.logical_not(full))(functools.partial(work, True, False))


def attn_forward(info, starts, queries, kv_a, kv_b, carried, scale):
    rows, all_width = queries.shape
    width = 128
    groups = kv_a.shape[2] // width
    group_width = all_width // groups
    keys_n = kv_a.shape[1]
    first = carried is None
    spec_q = pl.BlockSpec((rows, group_width), lambda g, info: (0, g))
    spec_kv = pl.BlockSpec((2, keys_n, width), lambda g, info: (0, 0, g))
    specs = [pl.BlockSpec((rows, 1), lambda g, info: (0, 0)), spec_q, spec_kv, spec_kv]
    operands = [starts, queries, kv_a, kv_b]
    if not first:
        specs += [spec_q, spec_q]
        operands += list(carried)
    return pl.pallas_call(
        functools.partial(attn_forward_kernel, first, first, scale),
        grid_spec=pltpu.PrefetchScalarGridSpec(
            num_scalar_prefetch=1,
            grid=(groups,),
            in_specs=specs,
            out_specs=[spec_q, spec_q],
        ),
        out_shape=[jax.ShapeDtypeStruct((rows, all_width), F32)] * 2,
        compiler_params=pltpu.CompilerParams(dimension_semantics=("arbitrary",)),
        cost_estimate=pl.CostEstimate(
            flops=16 * rows * keys_n * all_width,
            transcendentals=2 * rows * keys_n * all_width // width,
            bytes_accessed=8 * rows * all_width,
        ),
        name="attn_forward",
    )(info, *operands)


def attn_backward_kernel(first, diagonal, scale, info, starts, lse, deltas, queries, grads, kv_a, kv_b, *rest):
    if first:
        grad_q, grad_a, grad_b = rest
    else:
        grad_in, grad_q, grad_a, grad_b = rest
    rows = queries.shape[0]
    keys_n = kv_a.shape[1]
    width = kv_a.shape[2]
    per_group = queries.shape[1] // width
    if first:
        grad_q[...] = jnp.zeros_like(grad_q)
    else:
        grad_q[...] = grad_in[...]
    own_first = info[0]
    for slot, (block, out) in enumerate(((kv_a, grad_a), (kv_b, grad_b))):
        key_first = info[1 + slot]
        live = info[3 + slot] > 0

        def work(masked, causal):
            keys = block[0]
            values = block[1]
            keys_t = keys.T
            if masked:
                key_index = key_first + lax.broadcasted_iota(jnp.int32, (keys_n, rows), 0)
                allowed = key_index >= starts[...]
                if causal:
                    row_index = own_first + lax.broadcasted_iota(jnp.int32, (keys_n, rows), 1)
                    allowed = allowed & (key_index <= row_index)
            total_k = jnp.zeros((keys_n, width), F32)
            total_v = jnp.zeros((keys_n, width), F32)
            for head in range(per_group):
                cols = slice(head * width, (head + 1) * width)
                q_head = queries[:, cols]
                g_head = grads[:, cols]
                scores = times_transpose(keys, q_head)
                probs = jnp.exp2(scores * (scale * LOG2E) - lse[0, head : head + 1, :])
                if masked:
                    probs = jnp.where(allowed, probs, 0.0)
                grad_probs = times_transpose(values, g_head)
                grad_scores = (probs * (grad_probs - deltas[0, head : head + 1, :])).astype(BF16)
                total_v += matmul(probs.astype(BF16), g_head)
                total_k += matmul(grad_scores, q_head)
                grad_q[:, cols] += matmul(keys_t, grad_scores).T
            out[0] = (total_k * scale).astype(BF16)
            out[1] = total_v.astype(BF16)

        if diagonal and slot == 0:
            work(True, True)
        else:
            full = info[5 + slot] > 0
            pl.when(live & full)(functools.partial(work, False, False))
            pl.when(live & jnp.logical_not(full))(functools.partial(work, True, False))

            @pl.when(jnp.logical_not(live))
            def _():
                out[...] = jnp.zeros_like(out)


def attn_backward(info, starts_row, lse, deltas, queries, grads, kv_a, kv_b, carried, diagonal, scale):
    rows, all_width = queries.shape
    width = 128
    groups = kv_a.shape[2] // width
    group_width = all_width // groups
    per_group = group_width // width
    keys_n = kv_a.shape[1]
    first = carried is None
    spec_q = pl.BlockSpec((rows, group_width), lambda g, info: (0, g))
    spec_kv = pl.BlockSpec((2, keys_n, width), lambda g, info: (0, 0, g))
    spec_row = pl.BlockSpec((1, per_group, rows), lambda g, info: (g, 0, 0))
    specs = [
        pl.BlockSpec((1, rows), lambda g, info: (0, 0)),
        spec_row,
        spec_row,
        spec_q,
        spec_q,
        spec_kv,
        spec_kv,
    ]
    operands = [starts_row, lse, deltas, queries, grads, kv_a, kv_b]
    if not first:
        specs.append(spec_q)
        operands.append(carried)
    return pl.pallas_call(
        functools.partial(attn_backward_kernel, first, diagonal, scale),
        grid_spec=pltpu.PrefetchScalarGridSpec(
            num_scalar_prefetch=1,
            grid=(groups,),
            in_specs=specs,
            out_specs=[spec_q, spec_kv, spec_kv],
        ),
        out_shape=[
            jax.ShapeDtypeStruct((rows, all_width), F32),
            jax.ShapeDtypeStruct(kv_a.shape, BF16),
            jax.ShapeDtypeStruct(kv_a.shape, BF16),
        ],
        compiler_params=pltpu.CompilerParams(dimension_semantics=("arbitrary",)),
        cost_estimate=pl.CostEstimate(
            flops=20 * rows * keys_n * all_width,
            transcendentals=2 * rows * keys_n * all_width // width,
            bytes_accessed=8 * rows * all_width,
        ),
        name="attn_backward",
    )(info, *operands)


LATE_BLOCKS = 2


def middle_kernel(outer, *refs):
    MESH = pl.DeviceIdType.MESH
    blocks = 2 * outer - LATE_BLOCKS
    (gated, out_proj, hidden_ref, gain_ref, gate_in, up_in, down_in) = refs[:7]
    ups_in = refs[7 : 7 + blocks]
    (layer_out, grad_out, gain_out, branch, dw_both, dw_down) = refs[7 + blocks : 13 + blocks]
    (
        w_gate, w_up, w_down, ups, rows, inner, grad_gate, grad_up,
        near_buf, far_stage, far_got, middle_buf,
        keep, y_stage, y_got, z_stage, z_got, part_got, part_far,
        load_sem, store_sem, tp_send, tp_recv, zs, zr, ys, yr, rys, ryr, rzs, rzr,
        p_near_send, p_near_recv, p_far_send, p_far_recv, p_out_send, p_out_recv, us, ur,
    ) = refs[13 + blocks :]
    stage_gate, stage_up, stage_down = w_gate, w_up, rows
    far_keep, own_keep = grad_out, middle_buf
    units = w_down.shape[0]
    quarter, model = hidden_ref.shape
    group = 2 * quarter
    chunk = model // outer
    last = outer - 1

    sp_i = lax.axis_index("sp")
    tp_i = lax.axis_index("tp")
    line = sp_i // 2
    half = sp_i % 2
    side = tp_i // 2
    core = tp_i % 2

    def sp_at(z, y):
        return (tp_i, z * 2 + y)

    pair_dev = sp_at(line, 1 - half)
    core_dev = (side * 2 + (1 - core), sp_i)
    side_dev = ((1 - side) * 2 + core, sp_i)
    nexts = (sp_at(jnp.minimum(line + 1, last), half), sp_at(jnp.maximum(line - 1, 0), half))

    late = list(range(outer - LATE_BLOCKS, outer))
    ups_at = [at for at in range(2 * outer) if at % 2 == 0 or at // 2 not in late]
    loads = [
        pltpu.make_async_copy(src, dst, load_sem.at[index])
        for index, (src, dst) in enumerate(
            [(down_in, w_down)]
            + [(src, ups.at[pl.ds(at * quarter, quarter), :]) for at, src in zip(ups_at, ups_in)]
            + [(gate_in, w_gate), (up_in, w_up)]
        )
    ]
    for load in loads:
        load.start()

    barrier = pltpu.get_barrier_semaphore()
    greeted = [
        sp_at((line + 1) % outer, half), sp_at((line + outer - 1) % outer, half),
        pair_dev, core_dev, side_dev,
    ]
    for device in greeted:
        pl.semaphore_signal(barrier, inc=1, device_id=device, device_id_type=MESH)
    pl.semaphore_wait(barrier, len(greeted))

    def remote(src, dst, send, recv, device):
        return pltpu.make_async_remote_copy(
            src_ref=src, dst_ref=dst, send_sem=send, recv_sem=recv,
            device_id=device, device_id_type=MESH,
        )

    def aligned(index, count):
        return pl.ds(pl.multiple_of(index * count, count), count)

    def late_copy(index):
        at = late[index] * 2
        return remote(
            ups.at[pl.ds(at * quarter, quarter), :], ups.at[pl.ds((at + 1) * quarter, quarter), :],
            us.at[index], ur.at[index], pair_dev,
        )

    def near_copy(j):
        return remote(near_buf.at[j], near_buf.at[2 + j], tp_send.at[j], tp_recv.at[j], core_dev)

    def far_copy():
        return remote(far_stage, far_got, tp_send.at[2], tp_recv.at[2], side_dev)

    def projected(s, c):
        return matmul(gated[aligned(s * 2 + c, quarter), :], out_proj[...])

    near_buf[0] = projected(1 - side, 1 - core).astype(BF16)
    near_copy(0).start()
    near_buf[1] = projected(side, 1 - core).astype(BF16)
    near_copy(1).start()
    for index in range(LATE_BLOCKS):
        loads[1 + ups_at.index(late[index] * 2)].wait()
        late_copy(index).start()
    far_keep[...] = projected(1 - side, core)
    near_copy(0).wait_recv()
    far_stage[...] = (far_keep[...] + near_buf[2].astype(F32)).astype(BF16)
    far_copy().start()
    own_keep[...] = projected(side, core)

    near_copy(1).wait_recv()
    far_copy().wait_recv()
    middle = hidden_ref[...].astype(F32) + (
        own_keep[...] + near_buf[3].astype(F32) + far_got[...].astype(F32)
    )
    middle_buf[...] = middle
    rows[0:quarter, :] = (middle * norm_scales(middle) * gain_ref[...]).astype(BF16)

    def entry(k, j):
        return pl.ds(pl.multiple_of((k * 2 + j) * quarter, quarter), quarter)

    def wrap(k):
        return (k + outer) % outer

    def z_copy(way, k):
        to = wrap(k + 1 - 2 * way)
        return remote(
            rows.at[entry(k, 0), :], rows.at[entry(to, 0), :], zs.at[way, k], zr.at[to], nexts[way]
        )

    def z_arrived(k):
        return remote(
            rows.at[entry(k, 0), :], rows.at[entry(k, 0), :], zs.at[0, k], zr.at[k], nexts[0]
        )

    def y_copy(k):
        return remote(
            rows.at[entry(k, 0), :], rows.at[entry(k, 1), :], ys.at[k], yr.at[k], pair_dev
        )

    short = jnp.minimum(line, last - line)

    def delta_of(i):
        near = jnp.where(i % 2 == 1, -((i + 1) // 2), (i + 1) // 2)
        far = jnp.where(line < last - line, i - short, short - i)
        return jnp.where(i <= 2 * short, near, far)

    def slot_of(delta):
        return jnp.where(delta <= 0, -delta, outer - delta)

    for way, exists in ((0, line < last), (1, line > 0)):
        pl.when(exists)(z_copy(way, 0).start)
    y_copy(0).start()

    def goes_on(delta):
        return ((delta < 0) & (line < last), (delta > 0) & (line > 0))

    def forward(i):
        delta = delta_of(i)
        k = slot_of(delta)
        z_arrived(k).wait_recv()
        for way, exists in enumerate(goes_on(delta)):
            pl.when(exists)(z_copy(way, k).start)
        y_copy(k).start()

    waited = [1 + ups_at.index(k * 2) for k in late]
    for index, load in enumerate(loads):
        if index not in waited:
            load.wait()
    for index in range(LATE_BLOCKS):
        late_copy(index).wait_recv()
    forward(1)

    def turn_forward(i, carry):
        @pl.when(i + 2 < outer)
        def _():
            forward(i + 2)

        k = slot_of(delta_of(i))
        y_copy(k).wait_recv()
        at = aligned(k, group)
        rows_k = rows[at, :]
        gate_vals = matmul(rows_k, w_gate[...])
        up_vals = matmul(rows_k, w_up[...])
        incoming = times_transpose(ups[at, :], w_down[...])
        sig = jax.nn.sigmoid(gate_vals)
        silu = gate_vals * sig
        grad_gate[at, :] = (incoming * up_vals * (sig * (1.0 + gate_vals * (1.0 - sig)))).astype(BF16)
        grad_up[at, :] = (incoming * silu).astype(BF16)
        inner[at, :] = (silu * up_vals).astype(BF16)
        return carry

    lax.fori_loop(0, outer, turn_forward, 0)

    near_copy(0).wait_send()
    near_copy(1).wait_send()

    def y_sum(which, k):
        at = aligned(k, quarter)
        src = y_stage.at[at, :] if which == 0 else near_buf.at[k]
        got = y_got.at[aligned(which * outer + k, quarter), :]
        return remote(src, got, rys.at[which, k], ryr.at[which, k], pair_dev)

    def half_rows(k, j):
        return pl.ds(pl.multiple_of((k * 2 + j) * quarter, quarter), quarter)

    def turn_parts(step, carry):
        k = slot_of(delta_of(last - step))
        part = times_transpose(grad_gate[half_rows(k, 1), :], w_gate[...]) + times_transpose(
            grad_up[half_rows(k, 1), :], w_up[...]
        )
        y_stage[aligned(k, quarter), :] = part.astype(BF16)
        y_sum(0, k).start()
        return carry

    def turn_outputs(step, carry):
        k = slot_of(delta_of(last - step))
        near_buf[k] = matmul(inner[half_rows(k, 1), :], w_down[...]).astype(BF16)
        y_sum(1, k).start()
        return carry

    def turn_keep(step, carry):
        k = slot_of(delta_of(last - step))
        part = times_transpose(grad_gate[half_rows(k, 0), :], w_gate[...]) + times_transpose(
            grad_up[half_rows(k, 0), :], w_up[...]
        )
        keep[aligned(k, quarter), :] = part.astype(BF16)
        return carry

    lax.fori_loop(0, outer, turn_parts, 0)
    lax.fori_loop(0, outer, turn_keep, 0)

    def z_got_rows(which, way, k):
        return aligned((which * 2 + way) * outer + k, quarter)

    def z_sum(which, way, k):
        to = wrap(k + 1 - 2 * way)
        return remote(
            z_stage.at[aligned(k, quarter), :], z_got.at[z_got_rows(which, way, to), :],
            rzs.at[which, k], rzr.at[which, way, to], nexts[way],
        )

    def z_got_at(which, way, k):
        return z_got[z_got_rows(which, way, k), :].astype(F32)

    def z_sum_arrived(which, way, k):
        return remote(
            z_stage.at[aligned(k, quarter), :], z_got.at[z_got_rows(which, way, k), :],
            rzs.at[which, k], rzr.at[which, way, k], nexts[way],
        )

    def own_share(which, k):
        if which == 0:
            share = keep[aligned(k, quarter), :].astype(F32)
        else:
            share = matmul(inner[half_rows(k, 0), :], w_down[...])
        return share + y_got[aligned(which * outer + k, quarter), :].astype(F32)

    def chain(which, step):
        delta = delta_of(last - step)
        k = slot_of(delta)
        at = aligned(k, quarter)
        y_sum(which, k).wait_recv()
        own = own_share(which, k)
        if which == 1:
            z_sum(0, 0, k).wait_send()
        for way, (here, before) in enumerate(((delta > 0, line > 0), (delta < 0, line < last))):

            @pl.when(here & before)
            def _():
                z_sum_arrived(which, way, k).wait_recv()
                z_stage[at, :] = (own + z_got_at(which, way, k)).astype(BF16)

            @pl.when(here & jnp.logical_not(before))
            def _():
                z_stage[at, :] = own.astype(BF16)

            pl.when(here)(z_sum(which, way, k).start)

    def chain_end(which):
        y_sum(which, 0).wait_recv()
        own = own_share(which, 0)
        for way, exists in ((0, line > 0), (1, line < last)):
            pl.when(exists)(z_sum_arrived(which, way, 0).wait_recv)
        below = jnp.where(line > 0, z_got_at(which, 0, 0), 0.0)
        above = jnp.where(line < last, z_got_at(which, 1, 0), 0.0)
        return own + below + above

    half_model = model // 2
    piece = half_model // 2

    def stage_rows(owner, r):
        return pl.ds(pl.multiple_of(owner * half_model + r * piece, piece), piece)

    stages = (stage_gate, stage_up)

    def piece_at(ref, a, r):
        return ref.at[a, pl.ds(r * piece, piece), :]

    def piece_near(a, r):
        return remote(
            stages[a].at[stage_rows(1 - core, r), :], piece_at(part_got, a, r),
            p_near_send.at[a, r], p_near_recv.at[a, r], core_dev,
        )

    def piece_far(a, r):
        return remote(
            stages[a].at[stage_rows(core, r), :], piece_at(part_far, a, r),
            p_far_send.at[a, r], p_far_recv.at[a, r], side_dev,
        )

    def piece_store(a, r):
        return pltpu.make_async_copy(
            piece_at(part_got, a, r), dw_both.at[a, stage_rows(core, r), :], store_sem.at[1 + 2 * a + r]
        )

    def piece_out(a, r):
        return remote(
            piece_at(part_got, a, r), dw_both.at[a, stage_rows(core, r), :],
            p_out_send.at[a, r], p_out_recv.at[a, r], core_dev,
        )

    def pieces(mine, r):
        at = stage_rows(core if mine else 1 - core, r)
        some = rows[:, at]
        for a, grads in enumerate((grad_gate, grad_up)):
            stages[a][at, :] = outer_sum(some, grads[...]).astype(BF16)
            if not mine:
                piece_near(a, r).start()

    def pieces_sum(r):
        at = stage_rows(core, r)
        for a in range(2):
            piece_near(a, r).wait_recv()
            stages[a][at, :] = (
                stages[a][at, :].astype(F32) + piece_at(part_got, a, r)[...].astype(F32)
            ).astype(BF16)
            piece_far(a, r).start()

    def pieces_total(r):
        for a in range(2):
            piece_far(a, r).wait_recv()
            total = stages[a][stage_rows(core, r), :].astype(F32) + piece_at(part_far, a, r)[
                ...
            ].astype(F32)
            piece_at(part_got, a, r)[...] = total.astype(BF16)
            piece_store(a, r).start()
            piece_out(a, r).start()

    pieces(False, 0)
    pieces(True, 0)
    pieces_sum(0)
    lax.fori_loop(0, outer, turn_outputs, 0)
    chain(0, 0)
    pieces(False, 1)
    pieces(True, 1)
    pieces_sum(1)
    for step in range(1, last):
        chain(0, step)
    grad_two = chain_end(0)

    values = middle_buf[...]
    back, gain_terms = norm_back(values, norm_scales(values), gain_ref[...], grad_two)
    grads = ups[0:quarter, :].astype(F32) + back
    branch[side, core] = grads.astype(BF16)

    def spread_copy(slot, s, device):
        block = branch.at[s, core]
        return remote(block, block, tp_send.at[3 + slot], tp_recv.at[3 + slot], device)

    spread_copy(0, side, side_dev).start()
    spread_copy(1, side, core_dev).start()
    grad_out[...] = grads
    gain_out[...] = jnp.sum(gain_terms, axis=0, keepdims=True)

    for way, exists in ((0, line < last), (1, line > 0)):
        pl.when(exists)(z_copy(way, 0).wait_send)

    def turn_sent(i, carry):
        delta = delta_of(i)
        k = slot_of(delta)
        y_copy(k).wait_send()
        for way, exists in enumerate(goes_on(delta)):
            pl.when(exists)(z_copy(way, k).wait_send)
        return carry

    lax.fori_loop(0, outer, turn_sent, 0)

    def turn_down(c, carry):
        at = aligned(c, chunk)
        stage_down[0:units, at] = outer_sum(inner[...], ups[:, at]).astype(BF16)
        return carry

    chain(1, 0)
    lax.fori_loop(0, outer, turn_down, 0)
    down_store = pltpu.make_async_copy(stage_down.at[pl.ds(0, units), :], dw_down, store_sem.at[0])
    down_store.start()
    for step in range(1, last):
        chain(1, step)
    spread_copy(0, side, side_dev).wait_recv()
    spread_copy(2, 1 - side, core_dev).start()
    pieces_total(0)
    layer_out[...] = (middle_buf[...] + chain_end(1)).astype(BF16)
    pieces_total(1)
    spread_copy(1, side, core_dev).wait_recv()

    down_store.wait()
    far_copy().wait_send()
    for index in range(LATE_BLOCKS):
        late_copy(index).wait_send()

    def turn_drain(i, carry):
        k = slot_of(delta_of(i))
        for which in range(2):
            y_sum(which, k).wait_send()
        pl.when(i > 0)(z_sum(1, 0, k).wait_send)
        return carry

    lax.fori_loop(0, outer, turn_drain, 0)
    for a in range(2):
        for r in range(2):
            piece_near(a, r).wait_send()
            piece_far(a, r).wait_send()
            piece_store(a, r).wait()
            piece_out(a, r).wait()
    spread_copy(0, side, side_dev).wait_send()
    spread_copy(1, side, core_dev).wait_send()
    spread_copy(2, 1 - side, core_dev).wait()


def middle_layer(gated, out_proj, hidden, gain, w_gate, w_up, w_down, ups, outer, sides):
    quarter, model = hidden.shape
    units = w_down.shape[0]
    rows_n = 2 * outer * quarter
    vmem = pl.BlockSpec(memory_space=pltpu.VMEM)
    anywhere = pl.BlockSpec(memory_space=pl.ANY)
    dma = pltpu.SemaphoreType.DMA
    line_rows = outer * quarter
    half = (2, model // 2, units)
    return pl.pallas_call(
        functools.partial(middle_kernel, outer),
        out_shape=[
            jax.ShapeDtypeStruct((quarter, model), BF16),
            jax.ShapeDtypeStruct((quarter, model), F32),
            jax.ShapeDtypeStruct((1, model), F32),
            jax.ShapeDtypeStruct((sides, 2, quarter, model), BF16),
            jax.ShapeDtypeStruct((2, model, units), BF16),
            jax.ShapeDtypeStruct((units, model), BF16),
        ],
        in_specs=[vmem] * 4 + [anywhere] * (3 + len(ups)),
        out_specs=[vmem] * 4 + [anywhere] * 2,
        scratch_shapes=[
            pltpu.VMEM((model, units), BF16),
            pltpu.VMEM((model, units), BF16),
            pltpu.VMEM((units, model), BF16),
            pltpu.VMEM((rows_n, model), BF16),
            pltpu.VMEM((rows_n, model), BF16),
            pltpu.VMEM((rows_n, units), BF16),
            pltpu.VMEM((rows_n, units), BF16),
            pltpu.VMEM((rows_n, units), BF16),
            pltpu.VMEM((4, quarter, model), BF16),
            pltpu.VMEM((quarter, model), BF16),
            pltpu.VMEM((quarter, model), BF16),
            pltpu.VMEM((quarter, model), F32),
            pltpu.VMEM((line_rows, model), BF16),
            pltpu.VMEM((line_rows, model), BF16),
            pltpu.VMEM((2 * line_rows, model), BF16),
            pltpu.VMEM((line_rows, model), BF16),
            pltpu.VMEM((4 * line_rows, model), BF16),
            pltpu.VMEM(half, BF16),
            pltpu.VMEM(half, BF16),
            dma((3 + len(ups),)),
            dma((5,)),
            dma((6,)),
            dma((6,)),
            dma((2, outer)),
            dma((outer,)),
            dma((outer,)),
            dma((outer,)),
            dma((2, outer)),
            dma((2, outer)),
            dma((2, outer)),
            dma((2, 2, outer)),
        ]
        + [dma((2, 2))] * 6
        + [dma((LATE_BLOCKS,))] * 2,
        compiler_params=pltpu.CompilerParams(
            collective_id=2, has_side_effects=True, vmem_limit_bytes=63 * 1024 * 1024
        ),
        cost_estimate=pl.CostEstimate(flops=3 * 10**10, bytes_accessed=4 * 10**7, transcendentals=0),
        name="middle",
    )(gated, out_proj, hidden, gain, w_gate, w_up, w_down, *ups)


FFN_CHUNKS = 2


def finish_kernel(
    outer, sides, sp_n, tp_n, streams, width_scale,
    *refs,
):
    MESH = pl.DeviceIdType.MESH
    parts = refs[:streams]
    (part_ref, hidden_ref, scale_ref, gain_ref, middle_ref, sums_ref) = refs[streams : streams + 6]
    last_in, layer_ref = refs[streams + 6 : streams + 8]
    outs = refs[streams + 8 : 2 * streams + 8]
    grad_out, sums_out, last_out, layer_out = refs[2 * streams + 8 : 2 * streams + 12]
    rest = refs[2 * streams + 12 :]
    got = rest[:streams]
    staged = rest[streams : 2 * streams]
    (near_got, far_got, keep_buf, far_stage, sums_got, sums_stage) = rest[2 * streams : 2 * streams + 6]
    rest = rest[2 * streams + 6 :]
    (last_keep, last_got, last_far, layer_send, layer_recv) = rest[:5]
    (f_load, f_near_send, f_near_recv, f_far_send, f_far_recv, f_store, f_out_send, f_out_recv) = rest[5:13]
    (reduce_send, reduce_recv, gather_send, gather_recv, pair_send, pair_recv) = rest[13:19]
    tp_send, tp_recv, sums_send, sums_recv = rest[19:]

    sp_i = lax.axis_index("sp")
    tp_i = lax.axis_index("tp")
    line = sp_i // 2
    half = sp_i % 2
    side = tp_i // 2
    core = tp_i % 2
    last = outer - 1

    def sp_at(z, y):
        return (tp_i, z * 2 + y)

    pair_dev = sp_at(line, 1 - half)
    core_dev = (side * 2 + (1 - core), sp_i)
    side_dev = ((1 - side) * 2 + core, sp_i)

    tp_bits = []
    bit = 1
    while bit < tp_n:
        tp_bits.append(bit)
        bit *= 2
    sp_bits = []
    bit = 1
    while bit < sp_n:
        sp_bits.append(bit)
        bit *= 2

    def flip(value, bit):
        return value + bit - 2 * bit * ((value // bit) % 2)

    sum_devs = [(flip(tp_i, b), sp_i) for b in tp_bits] + [(tp_i, flip(sp_i, b)) for b in sp_bits]

    barrier = pltpu.get_barrier_semaphore()
    greeted = [sp_at((line + 1) % outer, half), sp_at((line + outer - 1) % outer, half)] + sum_devs
    for device in greeted:
        pl.semaphore_signal(barrier, inc=1, device_id=device, device_id_type=MESH)
    pl.semaphore_wait(barrier, len(greeted))

    def remote(src, dst, send, recv, device):
        return pltpu.make_async_remote_copy(
            src_ref=src, dst_ref=dst, send_sem=send, recv_sem=recv,
            device_id=device, device_id_type=MESH,
        )

    places = (line, last - line)
    nexts = (sp_at(jnp.minimum(line + 1, last), half), sp_at(jnp.maximum(line - 1, 0), half))
    signs = (1, -1)

    def rows_of(stream, index):
        count = parts[stream].shape[0] // outer
        return pl.ds(pl.multiple_of(index * count, count), count)

    def reduce_copy(stream, way, step, src):
        return remote(
            src, got[stream].at[way, step - 1], reduce_send.at[stream, way, step - 1],
            reduce_recv.at[stream, way, step - 1], nexts[way],
        )

    def clamp(index):
        return jnp.clip(index, 0, last)

    def reduce_step(stream, step):
        for way in range(2):
            place, sign = places[way], signs[way]
            target = clamp(line + sign * (outer - step))
            own = parts[stream].at[rows_of(stream, target), :]

            @pl.when(place == 0)
            def _():
                reduce_copy(stream, way, step, own).start()

            if step > 1:

                @pl.when((place > 0) & (place <= step - 1))
                def _():
                    reduce_copy(stream, way, step - 1, own).wait_recv()
                    stage = staged[stream].at[way, step - 2]
                    stage[...] = (
                        got[stream][way, step - 2].astype(F32) + own[...].astype(F32)
                    ).astype(BF16)
                    reduce_copy(stream, way, step, stage).start()

    def gather_copy(stream, way, step, origin):
        block = outs[stream].at[half, rows_of(stream, origin), :]
        return remote(
            block, block, gather_send.at[stream, way, step - 1],
            gather_recv.at[stream, way, step - 1], nexts[way],
        )

    def pair_copy(stream, slot, origin):
        block = outs[stream].at[half, rows_of(stream, origin), :]
        return remote(block, block, pair_send.at[stream, slot], pair_recv.at[stream, slot], pair_dev)

    def reduce_final(stream):
        own = parts[stream].at[rows_of(stream, line), :]
        block = outs[stream].at[half, rows_of(stream, line), :]
        for way in range(2):

            @pl.when(places[way] > 0)
            def _():
                reduce_copy(stream, way, last, own).wait_recv()

        up = jnp.where(line > 0, got[stream][0, last - 1].astype(F32), 0.0)
        down = jnp.where(line < last, got[stream][1, last - 1].astype(F32), 0.0)
        block[...] = (own[...].astype(F32) + up + down).astype(BF16)
        for way in range(2):

            @pl.when(places[way] < last)
            def _():
                gather_copy(stream, way, 1, line).start()

        pair_copy(stream, 0, line).start()

    def gather_step(stream, step):
        for way in range(2):
            place, sign = places[way], signs[way]
            origin = clamp(line - sign * step)

            @pl.when(place >= step)
            def _():
                gather_copy(stream, way, step, origin).wait_recv()
                if step < last:

                    @pl.when(place < last)
                    def _():
                        gather_copy(stream, way, step + 1, origin).start()

                pair_copy(stream, 1 + way * last + step - 1, origin).start()

    def drain(stream):
        pair_copy(stream, 0, line).wait()
        for way in range(2):
            place, sign = places[way], signs[way]
            for step in range(1, outer):
                origin = clamp(line - sign * step)

                @pl.when(place <= step - 1)
                def _():
                    reduce_copy(stream, way, step, parts[stream].at[rows_of(stream, 0), :]).wait_send()

                @pl.when((place >= step - 1) & (place < last))
                def _():
                    gather_copy(stream, way, step, origin).wait_send()

                @pl.when(place >= step)
                def _():
                    pair_copy(stream, 1 + way * last + step - 1, origin).wait()

    def near_copy(index):
        return remote(
            part_ref.at[index, 1 - core], near_got.at[index], tp_send.at[index], tp_recv.at[index],
            core_dev,
        )

    def far_copy():
        return remote(far_stage, far_got, tp_send.at[sides], tp_recv.at[sides], side_dev)

    def spread_copy(slot, s, device):
        block = grad_out.at[s, core]
        return remote(block, block, tp_send.at[sides + slot], tp_recv.at[sides + slot], device)

    def input_step(step):
        if step == 0:
            for index in range(sides):
                near_copy(index).start()
        if step == 1:
            for index in range(sides):
                near_copy(index).wait_recv()
            keep_buf[...] = part_ref[side, core].astype(F32) + near_got[side].astype(F32)
            far_stage[...] = (
                part_ref[1 - side, core].astype(F32) + near_got[1 - side].astype(F32)
            ).astype(BF16)
            far_copy().start()
        if step == 2:
            far_copy().wait_recv()
            incoming = keep_buf[...] + far_got[...].astype(F32)
            values = hidden_ref[...].astype(F32)
            scales = scale_ref[...]
            weighted = incoming * gain_ref[...]
            inner_sum = jnp.sum(weighted * values, axis=-1, keepdims=True)
            grads = scales * weighted - values * (scales * scales * scales) * inner_sum * width_scale
            grad_out[side, core] = (middle_ref[...] + grads).astype(BF16)
            spread_copy(1, side, side_dev).start()
            spread_copy(2, side, core_dev).start()
        if step == 3:
            spread_copy(1, side, side_dev).wait_recv()
            spread_copy(3, 1 - side, core_dev).start()
        if step == 4:
            spread_copy(2, side, core_dev).wait_recv()
            spread_copy(3, 1 - side, core_dev).wait_recv()
            for index in range(sides):
                near_copy(index).wait_send()
            far_copy().wait_send()
            spread_copy(1, side, side_dev).wait_send()
            spread_copy(2, side, core_dev).wait_send()
            spread_copy(3, 1 - side, core_dev).wait_send()

    last_half = last_keep.shape[0]

    def ffn_at(j, ref, whole, owner):
        count = last_half // FFN_CHUNKS
        start = j * count
        if whole:
            start = pl.multiple_of(owner * last_half + start, count)
        return ref.at[pl.ds(start, count), :]

    def ffn_keep(j):
        return ffn_at(j, last_keep, False, 0)

    def ffn_got(j):
        return ffn_at(j, last_got, False, 0)

    def ffn_far(j):
        return ffn_at(j, last_far, False, 0)

    def ffn_load(j):
        return pltpu.make_async_copy(ffn_at(j, last_in, True, core), ffn_keep(j), f_load.at[j])

    def ffn_near_copy(j):
        return remote(
            ffn_at(j, last_in, True, 1 - core), ffn_got(j), f_near_send.at[j], f_near_recv.at[j], core_dev
        )

    def ffn_far_copy(j):
        return remote(ffn_keep(j), ffn_far(j), f_far_send.at[j], f_far_recv.at[j], side_dev)

    def ffn_store(j):
        return pltpu.make_async_copy(ffn_got(j), ffn_at(j, last_out, True, core), f_store.at[j])

    def ffn_out_copy(j):
        return remote(
            ffn_got(j), ffn_at(j, last_out, True, core), f_out_send.at[j], f_out_recv.at[j], core_dev
        )

    def ffn_sum(j):
        ffn_load(j).wait()
        ffn_near_copy(j).wait_recv()
        keep = ffn_keep(j)
        keep[...] = (keep[...].astype(F32) + ffn_got(j)[...].astype(F32)).astype(BF16)
        ffn_far_copy(j).start()

    def ffn_total(j):
        ffn_far_copy(j).wait_recv()
        total = ffn_keep(j)[...].astype(F32) + ffn_far(j)[...].astype(F32)
        ffn_got(j)[...] = total.astype(BF16)
        ffn_store(j).start()
        ffn_out_copy(j).start()

    def ffn_drain(j):
        ffn_near_copy(j).wait_send()
        ffn_far_copy(j).wait_send()
        ffn_store(j).wait()
        ffn_out_copy(j).wait()

    rounds = len(sum_devs)

    def sums_copy(step):
        src = sums_ref if step == 0 else sums_stage.at[step - 1]
        return remote(
            src, sums_got.at[step], sums_send.at[step], sums_recv.at[step], sum_devs[step]
        )

    def sums_step(step):
        if step > 0:
            sums_copy(step - 1).wait_recv()
            before = sums_ref[...] if step == 1 else sums_stage[step - 2]
            total = before + sums_got[step - 1]
            if step == rounds:
                sums_out[...] = total
            else:
                sums_stage[step - 1] = total
        if step < rounds:
            sums_copy(step).start()
        if step == rounds:
            for index in range(rounds):
                sums_copy(index).wait_send()

    def later(do, *args):
        return functools.partial(do, *args)

    def layer_copy(slot, s, device):
        block = layer_out.at[s, core]
        src = block if slot == 2 else layer_ref
        return remote(src, block, layer_send.at[slot], layer_recv.at[slot], device)

    def layer_own():
        return pltpu.make_async_copy(layer_ref, layer_out.at[side, core], layer_send.at[3])

    def layer_step(step):
        if step == 0:
            layer_copy(0, side, side_dev).start()
            layer_copy(1, side, core_dev).start()
            layer_own().start()
        if step == 1:
            layer_copy(0, 1 - side, side_dev).wait_recv()
            layer_copy(2, 1 - side, core_dev).start()
        if step == 2:
            layer_copy(1, side, core_dev).wait_recv()
            layer_own().wait()
            layer_copy(0, side, side_dev).wait_send()
            layer_copy(1, side, core_dev).wait_send()
            layer_copy(2, 1 - side, core_dev).wait()

    extra = [
        later(input_step, 0), later(sums_step, 0), later(input_step, 1), later(layer_step, 0),
        later(ffn_sum, 0), later(ffn_sum, 1), later(lambda: None), later(lambda: None), later(input_step, 2),
        later(sums_step, 1), later(lambda: None), later(sums_step, 2), later(lambda: None), later(sums_step, 3),
        later(layer_step, 1), later(lambda: None), later(sums_step, 4), later(input_step, 3),
        later(lambda: None), later(sums_step, 5), later(ffn_total, 0), later(ffn_total, 1),
        later(layer_step, 2), later(input_step, 4),
    ]
    extra += [later(sums_step, index) for index in range(6, rounds + 1)]
    for index in range(FFN_CHUNKS):
        ffn_near_copy(index).start()
        ffn_load(index).start()
    for turn in range(streams + 1):
        for step in range(1, outer + 1):
            if turn < streams:
                if step < outer:
                    reduce_step(turn, step)
                else:
                    reduce_final(turn)
            if turn > 0 and step < outer:
                gather_step(turn - 1, step)
            if extra:
                extra.pop(0)()
    for step in extra:
        step()
    for stream in range(streams):
        drain(stream)
    for index in range(FFN_CHUNKS):
        ffn_drain(index)


def finish(parts, part, hidden, scales, gain, middle, sums, ffn_last, layer, outer, sp_n, tp_n):
    streams = len(parts)
    sides = tp_n // 2
    quarter, model = hidden.shape
    last = outer - 1
    rounds = (tp_n - 1).bit_length() + (sp_n - 1).bit_length()
    vmem = pl.BlockSpec(memory_space=pltpu.VMEM)
    anywhere = pl.BlockSpec(memory_space=pl.ANY)
    chunk = [(2, last, p.shape[0] // outer, p.shape[1]) for p in parts]
    dma = pltpu.SemaphoreType.DMA
    return pl.pallas_call(
        functools.partial(finish_kernel, outer, sides, sp_n, tp_n, streams, 1.0 / model),
        out_shape=[jax.ShapeDtypeStruct((2,) + p.shape, BF16) for p in parts]
        + [
            jax.ShapeDtypeStruct((sides, 2, quarter, model), BF16),
            jax.ShapeDtypeStruct(sums.shape, F32),
        ]
        + [
            jax.ShapeDtypeStruct(ffn_last.shape, BF16),
            jax.ShapeDtypeStruct((sides, 2, quarter, model), BF16),
        ],
        in_specs=[vmem] * (streams + 6) + [anywhere, vmem],
        out_specs=[vmem] * (streams + 2) + [anywhere, vmem],
        scratch_shapes=[pltpu.VMEM(c, BF16) for c in chunk]
        + [pltpu.VMEM(c, BF16) for c in chunk]
        + [
            pltpu.VMEM((sides, quarter, model), BF16),
            pltpu.VMEM((quarter, model), BF16),
            pltpu.VMEM((quarter, model), F32),
            pltpu.VMEM((quarter, model), BF16),
            pltpu.VMEM((rounds,) + sums.shape, F32),
            pltpu.VMEM((rounds,) + sums.shape, F32),
        ]
        + [pltpu.VMEM((ffn_last.shape[0] // 2, ffn_last.shape[1]), BF16)] * 3
        + [dma((4,))] * 2
        + [dma((FFN_CHUNKS,))] * 8
        + [dma((streams, 2, last))] * 4
        + [dma((streams, 1 + 2 * last))] * 2
        + [dma((sides + 4,))] * 2
        + [dma((rounds,))] * 2,
        compiler_params=pltpu.CompilerParams(
            collective_id=1, has_side_effects=True, vmem_limit_bytes=60 * 1024 * 1024
        ),
        cost_estimate=pl.CostEstimate(flops=10**9, bytes_accessed=10**8, transcendentals=0),
        name="finish",
    )(*parts, part, hidden, scales, gain, middle, sums, ffn_last, layer)


def body(
    hidden,
    segment_ids,
    attn_norm,
    query_proj,
    key_proj,
    value_proj,
    gate_proj,
    output_proj,
    query_norm,
    key_norm,
    ffn_norm,
    ffn_gate,
    ffn_up,
    ffn_down,
    upstream,
):
    rows_dev, model = hidden.shape
    head_width = query_norm.shape[0]
    heads = query_proj.shape[1] // head_width
    groups = key_proj.shape[1] // head_width
    per_group = heads // groups
    group_width = groups * head_width
    sp_n = lax.axis_size("sp")
    tp_n = lax.axis_size("tp")
    outer = sp_n // 2
    sides = tp_n // 2
    quarter = rows_dev // tp_n
    tp_i = lax.axis_index("tp")
    sp_i = lax.axis_index("sp")
    ring_i = sp_i // 2
    pair_i = sp_i % 2
    side_i = tp_i // 2
    core_i = tp_i % 2
    own_first = sp_i * rows_dev
    quarter_first = tp_i * quarter
    scale = 1.0 / math.sqrt(head_width)

    ring_pairs = [(z * 2 + y, ((z + 1) % outer) * 2 + y) for z in range(outer) for y in range(2)]
    pair_pairs = [(i, i ^ 1) for i in range(sp_n)]
    side_pairs = [(i, i ^ 2) for i in range(tp_n)]
    core_pairs = [(i, i ^ 1) for i in range(tp_n)]

    def ring(value):
        return lax.ppermute(value, "sp", ring_pairs)

    def far(value, step):
        pairs = [(z * 2 + y, ((z + step) % outer) * 2 + y) for z in range(outer) for y in range(2)]
        return lax.ppermute(value, "sp", pairs)

    def pair(value):
        return lax.ppermute(value, "sp", pair_pairs)

    def side(value):
        return lax.ppermute(value, "tp", side_pairs)

    def core(value):
        return lax.ppermute(value, "tp", core_pairs)

    def gather_sp(block, paired):
        blocks = []
        first = block
        for k in range(outer):
            blocks.append((block, pair(block)) if k < paired else (block,))
            if k < outer - 1:
                block = ring(block) if paired == outer else far(first, k + 1)
        return blocks

    def scatter_sp(parts):
        def paired(k):
            return parts[k][0] + pair(parts[k][1].astype(BF16)).astype(F32)

        total = paired(1 % outer)
        for k in range(2, outer + 1):
            total = ring(total.astype(BF16)).astype(F32) + paired(k % outer)
        return total

    first_id = segment_ids[0]
    second_start = jnp.sum((segment_ids == first_id).astype(jnp.int32))
    own_index = own_first + jnp.arange(rows_dev, dtype=jnp.int32)
    own_starts = jnp.where(own_index < second_start, 0, second_start)
    steps_half = jnp.arange(head_width // 2, dtype=F32)
    frequencies = jnp.exp(steps_half * (-2.0 * math.log(THETA) / head_width))
    angles = (own_index - own_starts).astype(F32)[:, None] * frequencies[None, :]
    cosine = jnp.cos(angles)[:, None, :]
    sine = jnp.sin(angles)[:, None, :]

    hidden_full = hidden.astype(F32)
    normed_full, attn_scales = norm_rows(hidden_full, attn_norm)
    normed = normed_full.astype(BF16)
    key_raw = matmul(normed, key_proj).reshape(rows_dev, groups, head_width)
    value_rows = matmul(normed, value_proj).astype(BF16)
    key_normed, key_scales = norm_rows(key_raw, key_norm)
    key_rot = rotary(key_normed, cosine, sine).astype(BF16).reshape(rows_dev, group_width)
    kv_own = jnp.stack([key_rot, value_rows])

    low, high = (outer // 4, 3 * outer // 4) if outer % 4 == 0 else (0, outer)
    reach = high - 1 if low else outer - 1

    def up_pairs(step):
        return [
            (z * 2 + y, (z + 1) * 2 + y)
            for z in range(outer - 1)
            for y in range(2)
            if z + 1 - step >= 0 and (z + 1 - step >= low or z + 1 < high)
        ]

    def far_pairs(step):
        return [
            (z * 2 + y, (z + step) * 2 + y)
            for z in range(outer - step)
            for y in range(2)
            if z >= low or z + step < high
        ]

    kv_blocks = []
    travelling = kv_own
    for k in range(reach + 1):
        if k > 0 and reach <= 2:
            travelling = lax.ppermute(kv_own, "sp", far_pairs(k))
        elif k > 0:
            travelling = lax.ppermute(travelling, "sp", up_pairs(k))
        kv_blocks.append((travelling, pair(travelling)))

    query_raw = matmul(normed, query_proj).reshape(rows_dev, heads, head_width)
    gate_raw = matmul(normed, gate_proj)
    query_normed, query_scales = norm_rows(query_raw, query_norm)
    queries = rotary(query_normed, cosine, sine).astype(BF16).reshape(rows_dev, heads * head_width)

    def swap_half(value):
        piece = model // 4
        mine = pair(lax.dynamic_slice_in_dim(value, ((1 - pair_i) * 2 + core_i) * piece, piece, 1))
        near = core(mine)
        return jnp.where(
            core_i == 1, jnp.concatenate([near, mine], 1), jnp.concatenate([mine, near], 1)
        )

    normed_own = lax.dynamic_slice_in_dim(normed, pair_i * (model // 2), model // 2, 1)
    both_normed = jnp.concatenate([normed_own, swap_half(normed)])

    grad_quarter = lax.dynamic_slice_in_dim(upstream, quarter_first, quarter)
    fused = 2 < outer and outer * quarter <= 512 and tp_n == 4
    up_blocks = gather_sp(grad_quarter, outer - LATE_BLOCKS if fused else outer)

    row_start_low = own_starts[0]
    row_start_high = own_starts[-1]

    def block_info(k):
        shards = [(ring_i - k) * 2 + pair_i, (ring_i - k) * 2 + (1 - pair_i)]
        entries = [own_first] + [shard * rows_dev for shard in shards]
        live = []
        full = []
        for shard in shards:
            token = shard * rows_dev
            live.append((shard >= 0) & (shard <= sp_i) & (token + rows_dev - 1 >= row_start_low))
            full.append((token >= row_start_high) & (shard < sp_i))
        return jnp.stack(entries + [v.astype(jnp.int32) for v in live + full]).astype(jnp.int32)

    infos = [block_info(k) for k in range(reach + 1)]
    starts_column = own_starts[:, None]
    starts_row = own_starts[None, :]
    carried = None
    for k in range(reach + 1):
        if fused and k == reach:
            carried, up_blocks = lax.optimization_barrier((carried, up_blocks))
        carried = attn_forward(
            infos[k], starts_column, queries, kv_blocks[k][0], kv_blocks[k][1], carried, scale
        )
    mix_acc, mix_sum = carried
    mixed = mix_acc / mix_sum
    lse = jnp.log2(mix_sum.reshape(rows_dev, heads, head_width)[:, :, 0])
    lse_rows = lse.T.reshape(groups, per_group, rows_dev)
    gate_sig = jax.nn.sigmoid(gate_raw)
    gated = (mixed * gate_sig).astype(BF16)
    gated_other = pair(gated)

    def scatter_tp(part):
        part = part.reshape(sides, 2, quarter, model)
        keep = lax.dynamic_index_in_dim(part, core_i, 1, keepdims=False)
        send = lax.dynamic_index_in_dim(part, 1 - core_i, 1, keepdims=False)
        keep = keep + core(send.astype(BF16)).astype(F32)
        mine = lax.dynamic_index_in_dim(keep, side_i, 0, keepdims=False)
        other = lax.dynamic_index_in_dim(keep, 1 - side_i, 0, keepdims=False)
        return mine + side(other.astype(BF16)).astype(F32)

    def gather_tp(block):
        far = side(block)
        swap_side = side_i == 1
        two = jnp.where(swap_side, jnp.stack([far, block]), jnp.stack([block, far]))
        near = core(two)
        swap_core = core_i == 1
        full = jnp.where(
            swap_core, jnp.stack([near, two], axis=1), jnp.stack([two, near], axis=1)
        )
        return full.reshape((rows_dev,) + block.shape[1:])

    if fused:
        layer_quarter, grad_middle_quarter, ffn_gain_sum, branch, *ffn_parts = middle_layer(
            gated,
            output_proj,
            lax.dynamic_slice_in_dim(hidden, quarter_first, quarter),
            ffn_norm[None, :],
            ffn_gate,
            ffn_up,
            ffn_down,
            [block for both in up_blocks for block in both],
            outer,
            sides,
        )
        grad_branch = branch.reshape(rows_dev, model)
        ffn_gain_sum = ffn_gain_sum[0]
    else:
        attn_quarter = scatter_tp(matmul(gated, output_proj))
        hidden_quarter = lax.dynamic_slice_in_dim(hidden, quarter_first, quarter).astype(F32)
        middle = hidden_quarter + attn_quarter
        normed_two_full, ffn_scales = norm_rows(middle, ffn_norm)
        normed_two = normed_two_full.astype(BF16)

        two_blocks = gather_sp(normed_two, outer)
        rows_list, up_list, inner_list, gate_list, grad_up_list = [None] * outer, [None] * outer, [None] * outer, [None] * outer, [None] * outer
        grad_parts = [None] * outer
        for k in list(range(1, outer)) + [0]:
            rows_k = jnp.concatenate(two_blocks[k])
            up_k = jnp.concatenate(up_blocks[k])
            gate_vals = matmul(rows_k, ffn_gate)
            up_vals = matmul(rows_k, ffn_up)
            sig = jax.nn.sigmoid(gate_vals)
            grad_inner = times_transpose(up_k, ffn_down)
            grad_gate = (grad_inner * up_vals * (sig * (1.0 + gate_vals * (1.0 - sig)))).astype(BF16)
            grad_up = (grad_inner * (gate_vals * sig)).astype(BF16)
            inner = (gate_vals * sig * up_vals).astype(BF16)
            grad_parts[k] = (
                times_transpose(grad_gate, ffn_gate) + times_transpose(grad_up, ffn_up)
            ).reshape(2, quarter, model)
            rows_list[k], up_list[k], inner_list[k] = rows_k, up_k, inner
            gate_list[k], grad_up_list[k] = grad_gate, grad_up
        grad_two = scatter_sp(grad_parts)

        norm_grad_two, ffn_gain_terms = norm_back(middle, ffn_scales, ffn_norm, grad_two)
        grad_middle_quarter = grad_quarter.astype(F32) + norm_grad_two
        grad_branch = gather_tp(grad_middle_quarter.astype(BF16))
        ffn_gain_sum = jnp.sum(ffn_gain_terms, axis=0)
        mlp_parts = [
            matmul(inner_list[k], ffn_down).reshape(2, quarter, model) for k in range(outer)
        ]
        layer_quarter = (middle + scatter_sp(mlp_parts)).astype(BF16)

    def sum_tp(part):
        total = part.astype(BF16).astype(F32)
        total = total + core(total.astype(BF16)).astype(F32)
        low = total.astype(BF16)
        return (low.astype(F32) + side(low).astype(F32)).astype(BF16)

    if not fused:
        rows_all = jnp.concatenate(rows_list)
        up_all = jnp.concatenate(up_list)
        inner_all = jnp.concatenate(inner_list)
        gate_all = jnp.concatenate(gate_list)
        grad_up_all = jnp.concatenate(grad_up_list)
        ffn_parts = [
            jnp.stack([outer_sum(rows_all, gate_all), outer_sum(rows_all, grad_up_all)]),
            outer_sum(inner_all, up_all),
        ]
        ffn_parts = [sum_tp(ffn_parts[0]), ffn_parts[1].astype(BF16)]
    ffn_both, ffn_last = ffn_parts

    branch_other = swap_half(grad_branch)
    branch_own = lax.dynamic_slice_in_dim(grad_branch, pair_i * (model // 2), model // 2, 1)
    grad_gated = times_transpose(grad_branch, output_proj)
    grad_mixed = (grad_gated * gate_sig).astype(BF16)
    grad_gate_raw = (grad_gated * mixed * (gate_sig * (1.0 - gate_sig))).astype(BF16)
    gate_other = pair(grad_gate_raw)
    deltas = jnp.sum(
        (grad_mixed.astype(F32) * mixed).reshape(rows_dev, heads, head_width), axis=-1
    )
    delta_rows = deltas.T.reshape(groups, per_group, rows_dev)

    def down_pairs(step):
        return [(b, a) for a, b in up_pairs(step)]

    query_acc = None
    travelling = None
    paired = {}
    for k in list(range(reach, -1, -1)):
        if k + 2 in paired:
            query_acc, paired[k + 2] = lax.optimization_barrier((query_acc, paired[k + 2]))
        query_acc, grad_a, grad_b = attn_backward(
            infos[k], starts_row, lse_rows, delta_rows, queries, grad_mixed,
            kv_blocks[k][0], kv_blocks[k][1], query_acc, k == 0, scale,
        )
        if k == reach:
            query_acc, grad_a, grad_b, gated_other, gate_other = lax.optimization_barrier(
                (query_acc, grad_a, grad_b, gated_other, gate_other)
            )
        paired[k] = pair(grad_b)
        total = grad_a.astype(F32) + paired[k].astype(F32)
        if travelling is not None:
            total = total + travelling.astype(F32)
        if k > 0:
            travelling = lax.ppermute(total.astype(BF16), "sp", down_pairs(k))
    output_half = outer_sum(
        jnp.concatenate([gated, gated_other]), jnp.concatenate([branch_own, branch_other])
    )
    gate_half = outer_sum(both_normed, jnp.concatenate([grad_gate_raw, gate_other]))
    grad_key_rot = total[0].reshape(rows_dev, groups, head_width)
    grad_value_low = total[1].astype(BF16)
    grad_query_rot = (query_acc * scale).reshape(rows_dev, heads, head_width)
    grad_query_raw, query_gain_terms = norm_back(
        query_raw, query_scales, query_norm, rotary_back(grad_query_rot, cosine, sine)
    )
    grad_key_raw, key_gain_terms = norm_back(
        key_raw, key_scales, key_norm, rotary_back(grad_key_rot, cosine, sine)
    )
    grad_query_low = grad_query_raw.reshape(rows_dev, heads * head_width).astype(BF16)
    grad_key_low = grad_key_raw.reshape(rows_dev, group_width).astype(BF16)
    grad_kv_low = jnp.concatenate([grad_key_low, grad_value_low], axis=1)
    grad_kv_low, ffn_both = lax.optimization_barrier((grad_kv_low, ffn_both))
    ffn_gate_grad, ffn_up_grad = ffn_both[0].astype(F32), ffn_both[1].astype(F32)

    both_queries = jnp.concatenate([grad_query_low, pair(grad_query_low)])
    both_kv = jnp.concatenate([grad_kv_low, pair(grad_kv_low)])
    parts = [
        output_half.astype(BF16),
        gate_half.astype(BF16),
        outer_sum(both_normed, both_queries).astype(BF16),
        outer_sum(both_normed, both_kv).astype(BF16),
    ]

    grad_normed_part = (
        times_transpose(grad_query_low, query_proj)
        + times_transpose(grad_key_low, key_proj)
        + times_transpose(grad_value_low, value_proj)
        + times_transpose(grad_gate_raw, gate_proj)
    )
    gains = jnp.concatenate(
        [
            jnp.sum(grad_normed_part * hidden_full * attn_scales, axis=0),
            ffn_gain_sum,
            jnp.sum(query_gain_terms, axis=(0, 1)),
            jnp.sum(key_gain_terms, axis=(0, 1)),
        ]
    )
    gains, ffn_gate_grad, ffn_up_grad = lax.optimization_barrier((gains, ffn_gate_grad, ffn_up_grad))
    gains_at = 2 * model + 2 * head_width
    gains = jnp.pad(gains, (0, -gains_at % 1024)).reshape(-1, 128)
    scales_quarter = lax.dynamic_slice_in_dim(attn_scales, quarter_first, quarter)
    finished = finish(
        parts,
        grad_normed_part.astype(BF16).reshape(sides, 2, quarter, model),
        lax.dynamic_slice_in_dim(hidden, quarter_first, quarter),
        scales_quarter,
        attn_norm[None, :],
        grad_middle_quarter,
        gains,
        ffn_last,
        layer_quarter,
        outer,
        sp_n,
        tp_n,
    )
    output_all, gate_all_w, query_all, kv_all, input_all, gains, ffn_last, layer_all = finished
    output_grad = jnp.concatenate([output_all[0], output_all[1]], axis=1).astype(F32)
    gate_grad = gate_all_w.reshape(model, heads * head_width).astype(F32)
    query_grad = query_all.reshape(model, heads * head_width).astype(F32)
    kv_all = kv_all.reshape(model, 2 * group_width)
    key_grad = kv_all[:, :group_width].astype(F32)
    value_grad = kv_all[:, group_width:].astype(F32)
    hidden_grad = input_all.reshape(rows_dev, model).astype(F32)
    gains = gains.reshape(-1)
    return (
        layer_all.reshape(rows_dev, model),
        hidden_grad,
        gains[:model],
        query_grad,
        key_grad,
        value_grad,
        gate_grad,
        output_grad,
        gains[2 * model : 2 * model + head_width],
        gains[2 * model + head_width : gains_at],
        gains[model : 2 * model],
        ffn_gate_grad,
        ffn_up_grad,
        ffn_last.astype(F32),
    )


def solution(mesh):
    placed = (
        P("sp", None),
        P(),
        P(),
        P(None, "tp"),
        P(None, "tp"),
        P(None, "tp"),
        P(None, "tp"),
        P("tp", None),
        P(),
        P(),
        P(),
        P(None, "sp"),
        P(None, "sp"),
        P("sp", None),
        P("sp", None),
    )
    return jax.shard_map(
        body,
        mesh=mesh,
        in_specs=placed,
        out_specs=(
            P("sp", None),
            P("sp", None),
            P(),
            P(None, "tp"),
            P(None, "tp"),
            P(None, "tp"),
            P(None, "tp"),
            P("tp", None),
            P(),
            P(),
            P(),
            P(None, "sp"),
            P(None, "sp"),
            P("sp", None),
        ),
        check_vma=False,
    )
```
